32 devices in a mesh: tm: 8 (over z, x), col: 4 (over y, core).
Axes of the slice: x: 2, y: 2, z: 4, core: 2. Of those that a mesh axis runs over, the one named last changes fastest.
Arguments:
- blocks: float32 [16, 512, 192], P('tm', 'col'), may hold values from -0.5 to 1.5, as said below
- pattern: int32 [8, 3], replicated, may hold values from 0 to 7, as said below
- drift: float32 [16, 512], P('tm', 'col'), may hold values from -6 to 6
- cov: float32 [16, 512, 512], P('tm', 'col'), may hold values from -0.5 to 2, as said below
- cost: float32 [16, 512, 512], P('tm', 'col'), may hold values from -0.5 to 2, as said below
- eta: float32 [16, 512], P('tm', 'col'), may hold values from -6 to 6
Outputs:
- dyn_out: float32 [16, 512, 512], P('tm', 'col')
- drift_out: float32 [16, 512], P('tm', 'col')
- cov_out: float32 [16, 512, 512], P('tm', 'col')
- cost_out: float32 [16, 512, 512], P('tm', 'col')
- eta_out: float32 [16, 512], P('tm', 'col')
The draws below stay inside these ranges and needn't reach their ends.
Inputs may be any that keep to these rules, and one draw needn't show every extreme that they name: `pattern`: row r lists r first, then two different block columns other than r. `blocks`: the first block of each row is the diagonal block. `cov`: each group's matrix is symmetric. `cost`: each group's matrix is symmetric.
All inputs are finite; a program needn't handle non-finite values.
Results may differ from the reference program's by a relative error of at most 0.00015.
Values sent between devices are 32-bit elements; how exact they have to be, the bound alone decides.
No kernel may reach another device: no remote copies, remote signals or barrier semaphores. Data moves between devices by JAX's collectives and lax.ppermute only.
A program may use at most 64 MiB of HBM per device.

```python
import math
import jax
import jax.numpy as jnp
from jax import lax

MODES = 512
BS = 64
LEVELS = 2
ELEM_DEV = 2
GROUPS = 16


def sym_field(key, scale):
    raw = jnp.clip(jax.random.normal(key, (GROUPS, MODES, MODES), jnp.float32), -4.0, 4.0)
    symmetric = 0.5 * (raw + jnp.swapaxes(raw, 1, 2)) * (scale / math.sqrt(MODES))
    diagonal = jax.random.uniform(jax.random.fold_in(key, 7), (GROUPS, MODES), jnp.float32, 0.5, 1.5)
    indices = jnp.arange(MODES)
    identity = (indices[:, None] == indices[None, :]).astype(jnp.float32)
    return symmetric + identity[None, :, :] * diagonal[:, :, None]


def draw_cov(key, part):
    return sym_field(jax.random.fold_in(key, 11), 0.7)


def draw_cost(key, part):
    return sym_field(jax.random.fold_in(key, 13), 0.7)


def draw_blocks(key, part):
    inner = jax.random.fold_in(key, 17)
    raw = jnp.clip(jax.random.normal(inner, (GROUPS, MODES, 3 * BS), jnp.float32), -4.0, 4.0)
    noise = raw * (0.5 / math.sqrt(3 * BS))
    position = jnp.arange(MODES) % BS
    placed = (jnp.arange(3 * BS)[None, :] == position[:, None]).astype(jnp.float32)
    rates = jax.random.uniform(jax.random.fold_in(key, 19), (GROUPS, MODES), jnp.float32, 0.5, 0.9)
    return noise + placed[None, :, :] * rates[:, :, None]


def draw_pattern(key, part):
    block_count = MODES // BS
    inner = jax.random.fold_in(key, 23)

    def one_row(row_index):
        shuffled = jax.random.permutation(jax.random.fold_in(inner, row_index), block_count - 1)[:2]
        others = shuffled + (shuffled >= row_index).astype(jnp.int32)
        return jnp.concatenate([jnp.reshape(row_index, (1,)), others]).astype(jnp.int32)
    return jax.vmap(one_row)(jnp.arange(block_count, dtype=jnp.int32))


def levels(key, shape, cuts, low, largest):
    gain, own = 1.0, jax.random.fold_in(key, 6)
    for axis_at, shards_of in cuts:
        heights = jnp.exp(jax.random.uniform(jax.random.fold_in(own, axis_at), (shards_of,), jnp.float32, low / len(cuts), largest / len(cuts)))
        gain = gain * jnp.repeat(heights, shape[axis_at] // shards_of).reshape([-1 if axis == axis_at else 1 for axis in range(len(shape))])
    return gain


def scatter_about(stream_key, shape, scale, most, shards=(), kind=jnp.bfloat16):
    array = jax.random.normal(stream_key, shape, jnp.float32) * scale
    if len(shards) > 0:
        array = levels(stream_key, shape, shards, -0.22, 0.18) * array
    return jnp.clip(array, min=-most, max=most).astype(kind)


def setup_inputs(seed: int = 0) -> dict:
    streams_of = jax.random.split(jax.random.key(seed), 7)
    return {
        "blocks": draw_blocks(jax.random.fold_in(streams_of[6], 71), 0),
        "pattern": draw_pattern(jax.random.fold_in(streams_of[6], 71), 0),
        "drift": scatter_about(streams_of[2], (GROUPS, MODES), 1.0, 6.0, ((0, 8), (1, 4)), jnp.float32),
        "cov": draw_cov(jax.random.fold_in(streams_of[6], 71), 0),
        "cost": draw_cost(jax.random.fold_in(streams_of[6], 71), 0),
        "eta": scatter_about(streams_of[5], (GROUPS, MODES), 1.0, 6.0, ((0, 8), (1, 4)), jnp.float32),
    }


HIGH = lax.Precision.HIGHEST


def product(form, left, right):
    return jnp.einsum(form, left, right, precision=HIGH)


def densify(row_blocks, row_ids, pattern, block_size):
    block_count = pattern.shape[0]
    row_block = row_ids // block_size
    chooser = (row_block[:, None] == jnp.arange(block_count, dtype=jnp.int32)[None, :]).astype(jnp.int32)
    columns = jnp.sum(chooser[:, :, None] * pattern[None, :, :], axis=1)
    matches = (columns[:, :, None] == jnp.arange(block_count, dtype=jnp.int32)[None, None, :]).astype(jnp.float32)
    pieces = row_blocks.reshape(row_blocks.shape[:-1] + (3, 1, block_size))
    filled = jnp.sum(matches[:, :, :, None] * pieces, axis=-3)
    return filled.reshape(row_blocks.shape[:-1] + (block_count * block_size,))


def combine_full(earlier, later):
    dyn_old, drift_old, cov_old, cost_old, eta_old = earlier
    dyn_new, drift_new, cov_new, cost_new, eta_new = later
    dyn_res = product("tij,tjk->tik", dyn_new, dyn_old)
    drift_res = product("tij,tj->ti", dyn_new, drift_old) + drift_new
    cov_res = product("tik,tjk->tij", product("tij,tjk->tik", dyn_new, cov_old), dyn_new) + cov_new
    value_rows = product("tij,tjk->tik", cost_new, dyn_old)
    cost_res = cost_old + product("tki,tkj->tij", dyn_old, value_rows)
    carried = eta_new + product("tij,tj->ti", cost_new, drift_old)
    eta_res = eta_old + product("tki,tk->ti", dyn_old, carried)
    return (dyn_res, drift_res, cov_res, cost_res, eta_res)


def reference(blocks, pattern, drift, cov, cost, eta):
    all_ids = jnp.arange(MODES, dtype=jnp.int32)
    dynamics = densify(blocks, all_ids, pattern, BS)
    current = (dynamics, drift, cov, cost, eta)
    for level_index in range(LEVELS):
        offset = ELEM_DEV * 2 ** level_index
        earlier = tuple(member[:-offset] for member in current)
        later = tuple(member[offset:] for member in current)
        merged = combine_full(earlier, later)
        current = tuple(jnp.concatenate([member[:offset], combined], axis=0) for member, combined in zip(current, merged))
    return (current[0], current[1], current[2], current[3], current[4])
```

```python
import functools

import jax
import jax.numpy as jnp
from jax import lax
from jax.experimental import pallas as pl
from jax.experimental.pallas import tpu as pltpu
from jax.sharding import PartitionSpec as P

HIGH = lax.Precision.HIGHEST
F32 = jnp.float32
BF16 = jnp.bfloat16


def shifted(block, axis, distance):
    devices = range(lax.axis_size(axis))
    route = [(i - distance, i) for i in devices if i - distance in devices]
    return lax.ppermute(block, axis, route)


def product(form, left, right):
    return jnp.einsum(form, left, right, precision=HIGH)


def densify(row_blocks, row_ids, pattern, block_size):
    block_count = pattern.shape[0]
    row_block = row_ids // block_size
    chooser = (row_block[:, None] == jnp.arange(block_count, dtype=jnp.int32)[None, :]).astype(
        jnp.int32
    )
    columns = jnp.sum(chooser[:, :, None] * pattern[None, :, :], axis=1)
    matches = (
        columns[:, :, None] == jnp.arange(block_count, dtype=jnp.int32)[None, None, :]
    ).astype(jnp.float32)
    pieces = row_blocks.reshape(row_blocks.shape[:-1] + (3, 1, block_size))
    filled = jnp.sum(matches[:, :, :, None] * pieces, axis=-3)
    return filled.reshape(row_blocks.shape[:-1] + (block_count * block_size,))


def combine_rows(
    dyn_prev_full,
    dyn_own_full,
    dyn_own,
    drift_prev_full,
    drift_own,
    cov_prev,
    cov_own,
    cost_prev,
    cost_own,
    eta_prev,
    eta_own,
    first_row,
):
    height = dyn_own.shape[1]
    dyn_res = product("tij,tjk->tik", dyn_own, dyn_prev_full)
    drift_res = product("tij,tj->ti", dyn_own, drift_prev_full) + drift_own
    carried = eta_own + product("tij,tj->ti", cost_own, drift_prev_full)
    value_rows = product("tij,tjk->tik", cost_own, dyn_prev_full)
    prev_columns = lax.dynamic_slice_in_dim(dyn_prev_full, first_row, height, 2)
    cov_full, carried_full, value_full = (
        lax.all_gather(cov_prev, "col", axis=1, tiled=True),
        lax.all_gather(carried, "col", axis=1, tiled=True),
        lax.all_gather(value_rows, "col", axis=1, tiled=True),
    )
    cost_res = cost_prev + product("tki,tkj->tij", prev_columns, value_full)
    cov_res = (
        product("tik,tjk->tij", product("tij,tjk->tik", dyn_own, cov_full), dyn_own_full) + cov_own
    )
    eta_res = eta_prev + product("tki,tk->ti", prev_columns, carried_full)
    return (dyn_res, drift_res, cov_res, cost_res, eta_res)


def choose(flag, combined, kept):
    return tuple(jnp.where(flag, new, old) for new, old in zip(combined, kept))


def per_device_general(blocks, pattern, drift, cov, cost, eta):
    height = cov.shape[1]
    modes = cov.shape[2]
    block_size = blocks.shape[2] // 3
    first_row = lax.axis_index("col") * height
    own_ids = first_row + jnp.arange(height, dtype=jnp.int32)
    all_ids = jnp.arange(modes, dtype=jnp.int32)
    position = lax.axis_index("tm")
    dyn_own = densify(blocks, own_ids, pattern, block_size)
    received = shifted((blocks, drift, cov, cost, eta), "tm", 1)
    blocks_prev, blocks_own, drift_prev_full = (
        lax.all_gather(received[0], "col", axis=1, tiled=True),
        lax.all_gather(blocks, "col", axis=1, tiled=True),
        lax.all_gather(received[1], "col", axis=1, tiled=True),
    )
    merged = combine_rows(
        densify(blocks_prev, all_ids, pattern, block_size),
        densify(blocks_own, all_ids, pattern, block_size),
        dyn_own,
        drift_prev_full,
        drift,
        received[2],
        cov,
        received[3],
        cost,
        received[4],
        eta,
        first_row,
    )
    current = choose(position >= 1, merged, (dyn_own, drift, cov, cost, eta))
    received = shifted(current, "tm", 2)
    dyn_prev_full = lax.all_gather(received[0], "col", axis=1, tiled=True)
    dyn_own_full = lax.all_gather(current[0], "col", axis=1, tiled=True)
    drift_prev_full = lax.all_gather(received[1], "col", axis=1, tiled=True)
    merged = combine_rows(
        dyn_prev_full,
        dyn_own_full,
        current[0],
        drift_prev_full,
        current[1],
        received[2],
        current[2],
        received[3],
        current[3],
        received[4],
        current[4],
        first_row,
    )
    return choose(position >= 2, merged, current)


def split(x):
    hi = x.astype(BF16)
    lo = (x - hi.astype(F32)).astype(BF16)
    return hi, lo


def dot(a, b):
    return jnp.dot(a, b, preferred_element_type=F32)


def dot3(ah, al, bh, bl):
    return dot(ah, bh) + (dot(ah, bl) + dot(al, bh))


def triangle(r):
    rows = lax.broadcasted_iota(jnp.int32, (r, r), 0)
    cols = lax.broadcasted_iota(jnp.int32, (r, r), 1)
    return rows, cols


def fold(first, second, r):
    rows, cols = triangle(r)
    return jnp.where(rows >= cols, first, second)


def diagonal(block, r):
    rows, cols = triangle(r)
    return jnp.sum(jnp.where(rows == cols, block, 0.0), axis=0, keepdims=True)


def unfold(folded, second_diag, r):
    rows, cols = triangle(r)
    turned = folded.T
    first = jnp.where(rows >= cols, folded, turned)
    second = jnp.where(rows < cols, folded, turned)
    second = jnp.where(rows == cols, jnp.broadcast_to(second_diag, (r, r)), second)
    return first, second


UPPER = ((0, 1), (0, 2), (0, 3), (1, 2), (1, 3), (2, 3))


def spread(packed, r, put):
    panel0, panel1, diags = packed[0:r], packed[r : 2 * r], packed[2 * r : 2 * r + 1]
    k00, k11 = unfold(panel0[:, 0:r], diags[:, 0:r], r)
    k22, k33 = unfold(panel1[:, 0:r], diags[:, r : 2 * r], r)
    for i, block in enumerate((k00, k11, k22, k33)):
        put(i, i, block)
    for at, (i, j) in enumerate(UPPER):
        panel = panel0 if at < 3 else panel1
        block = panel[:, (at % 3 + 1) * r : (at % 3 + 2) * r]
        put(i, j, block)
        put(j, i, block.T)


def column(row, r):
    rows, cols = triangle(r)
    pieces = []
    for at in range(row.shape[1] // r):
        piece = jnp.broadcast_to(row[:, at * r : (at + 1) * r], (r, r))
        pieces.append(jnp.sum(jnp.where(rows == cols, piece, 0.0), axis=1, keepdims=True))
    return jnp.concatenate(pieces, axis=0)


def row_times(row, matrix, r):
    return jnp.sum(column(row, r) * matrix, axis=0, keepdims=True)


def lanes(index, r):
    return pl.ds(pl.multiple_of(index * r, r), r)


def send_kernel(scal, cov, cost, turned, drift, eta, to_core, to_chip, to_far):
    q, y, c = scal[0], scal[1], scal[2]
    r = cov.shape[1]
    third = turned.shape[1] // 2

    def kind(which, element, col_block):
        at = lanes(col_block, r)
        return jnp.where(which == 0, cov[element, :, at], cost[element, :, at])

    def vectors(element):
        return drift[pl.ds(element, 1), :], eta[pl.ds(element, 1), :]

    b, e = vectors(y)
    for j in range(1, 4):
        to_core[0:r, (j - 1) * r : j * r] = kind(1 - c, y, (q ^ 1) ^ j)
    to_core[r : r + 1, 0:r] = b
    to_core[r : r + 1, r : 2 * r] = e
    b, e = vectors(1 - y)
    for j in range(2, 4):
        to_chip[0:r, (j - 2) * r : (j - 1) * r] = kind(c, 1 - y, (q ^ 2) ^ j)
    to_chip[r : r + 1, 0:r] = b
    to_chip[r : r + 1, r : 2 * r] = e
    to_chip[r + 8 :, 0:r] = turned[1 - y, 0:third, :]
    to_chip[r + 8 :, r : 2 * r] = turned[1 - y, third:, :]
    to_far[0:r, :] = kind(1 - c, 1 - y, q)
    to_far[r : r + 1, :] = b
    to_far[r + 1 : r + 2, :] = e


def pack_kernel(scal, cov, cost, turned, drift, eta, from_core, from_chip, from_far, packed):
    q, y, c = scal[0], scal[1], scal[2]
    r = cov.shape[1]
    third = turned.shape[1] // 2

    def own(j):
        at = lanes(q ^ j, r)
        return jnp.where(c == 0, cov[y, :, at], cost[y, :, at])

    k11 = from_core[0:r, 0:r]
    k33 = from_far[0:r, :]
    packed[0:r, 0:r] = fold(own(0), k11, r)
    for j in range(1, 4):
        packed[0:r, j * r : (j + 1) * r] = own(j)
    packed[r : 2 * r, 0:r] = fold(from_chip[0:r, 0:r], k33, r)
    packed[r : 2 * r, r : 3 * r] = from_core[0:r, r : 3 * r]
    packed[r : 2 * r, 3 * r :] = from_chip[0:r, r : 2 * r]
    base = 2 * r
    packed[base : base + 8, :] = jnp.zeros((8, packed.shape[1]), F32)
    packed[base : base + 1, 0:r] = diagonal(k11, r)
    packed[base : base + 1, r : 2 * r] = diagonal(k33, r)
    parts_b = (
        drift[pl.ds(y, 1), :],
        from_core[r : r + 1, 0:r],
        from_chip[r : r + 1, 0:r],
        from_far[r : r + 1, :],
    )
    parts_e = (
        eta[pl.ds(y, 1), :],
        from_core[r : r + 1, r : 2 * r],
        from_chip[r : r + 1, r : 2 * r],
        from_far[r + 1 : r + 2, :],
    )
    for j in range(4):
        packed[base + 1 : base + 2, j * r : (j + 1) * r] = parts_b[j]
        packed[base + 2 : base + 3, j * r : (j + 1) * r] = parts_e[j]
    packed[base + 8 :, 0:r] = turned[y, 0:third, :]
    packed[base + 8 :, r : 2 * r] = turned[y, third:, :]
    packed[base + 8 :, 2 * r :] = from_chip[r + 8 :, :]


def dense_turned(out, scal, pattern, own_half, core_half, flag, r, bs):
    q = scal[0]
    n = out.shape[0]
    lane = lax.broadcasted_iota(jnp.int32, (bs, r), 1) // bs
    rows = lax.broadcasted_iota(jnp.int32, (bs, r), 0)
    cols = lax.broadcasted_iota(jnp.int32, (bs, r), 1)
    per = r // bs
    for j in range(4):
        half = own_half if j % 2 == 0 else core_half
        at = (j // 2) * 2 * r
        full = jnp.concatenate([half[:, at : at + r], half[:, at + r : at + 2 * r]], axis=0)
        wanted = []
        for k in range(3):
            want = jnp.zeros((bs, r), jnp.int32)
            for h in range(per):
                block = pattern[(q ^ j) * per + h, k] ^ (q * per)
                want = jnp.where(lane == h, block, want)
            wanted.append(jnp.where(flag == 1, want, -1))
        for block in range(n // bs):
            value = jnp.where(
                jnp.logical_and(rows + block * bs == cols + j * r, flag == 0), 1.0, 0.0
            )
            for k in range(3):
                piece = full[k * bs : (k + 1) * bs, :]
                value = value + jnp.where(wanted[k] == block, piece, 0.0)
            out[block * bs : (block + 1) * bs, j * r : (j + 1) * r] = value


def put_split(hi_ref, lo_ref, rows, cols, value):
    hi, lo = split(value)
    hi_ref[rows, cols] = hi
    lo_ref[rows, cols] = lo


def transpose_split(hi_ref, lo_ref, source, r):
    n = source.shape[0]
    for i in range(n // r):
        for j in range(n // r):
            put_split(
                hi_ref,
                lo_ref,
                slice(j * r, (j + 1) * r),
                slice(i * r, (i + 1) * r),
                source[i * r : (i + 1) * r, j * r : (j + 1) * r].T,
            )


def straight_split(hi_ref, lo_ref, source, r):
    n = source.shape[0]
    for i in range(n // r):
        put_split(
            hi_ref, lo_ref, slice(i * r, (i + 1) * r), slice(None), source[i * r : (i + 1) * r, :]
        )


def level1_kernel(
    bs, scal, pattern, own, earlier, core_halves, out, dense, full, mh, ml, th, tl, xh, xl
):
    c, has1 = scal[2], scal[3]
    r = core_halves.shape[1] // 4
    third = (own.shape[0] - 2 * r - 8)
    first = c == 0
    base = 2 * r + 8
    own_half = jnp.where(first, own[base:, :], earlier[base:, :])
    core_half = jnp.where(first, core_halves[0:third, :], core_halves[third : 2 * third, :])
    flag = jnp.where(first, 1, has1)
    dense_turned(dense, scal, pattern, own_half, core_half, flag, r, bs)

    @pl.when(first)
    def _():
        straight_split(mh, ml, dense, r)
        transpose_split(th, tl, dense, r)

    @pl.when(jnp.logical_not(first))
    def _():
        straight_split(th, tl, dense, r)
        transpose_split(mh, ml, dense, r)

    x = jnp.where(first, earlier[0 : base, :], own[0 : base, :])

    def put(i, j, block):
        full[i * r : (i + 1) * r, j * r : (j + 1) * r] = block
        put_split(xh, xl, slice(i * r, (i + 1) * r), slice(j * r, (j + 1) * r), block)

    spread(x, r, put)
    carried = own[2 * r + 2 : 2 * r + 3, :] + row_times(
        earlier[2 * r + 1 : 2 * r + 2, :], full[...], r
    )
    e_new = earlier[2 * r + 2 : 2 * r + 3, :] + row_times(
        carried, mh[...].astype(F32) + ml[...].astype(F32), r
    )
    u = dot3(xh[...], xl[...], mh[...], ml[...])
    uh, ul = split(u)
    top = dot3(th[0 : 2 * r, :], tl[0 : 2 * r, :], uh, ul)
    low = dot3(th[2 * r :, :], tl[2 * r :, :], uh[:, 2 * r :], ul[:, 2 * r :])
    d = jnp.where(first, own[0 : base, :], earlier[0 : base, :])
    z11 = top[r : 2 * r, r : 2 * r]
    z33 = low[r : 2 * r, r : 2 * r]
    out[0:r, 0:r] = fold(top[0:r, 0:r], z11, r) + d[0:r, 0:r]
    out[0:r, r:] = top[0:r, r:] + d[0:r, r:]
    out[r : 2 * r, 0:r] = fold(low[0:r, 0:r], z33, r) + d[r : 2 * r, 0:r]
    out[r : 2 * r, r : 3 * r] = top[r : 2 * r, 2 * r :] + d[r : 2 * r, r : 3 * r]
    out[r : 2 * r, 3 * r :] = low[0:r, r : 2 * r] + d[r : 2 * r, 3 * r :]
    out[2 * r : 2 * r + 1, 0:r] = diagonal(z11, r) + d[2 * r : 2 * r + 1, 0:r]
    out[2 * r : 2 * r + 1, r : 2 * r] = diagonal(z33, r) + d[2 * r : 2 * r + 1, r : 2 * r]
    out[2 * r : 2 * r + 1, 2 * r :] = jnp.zeros((1, 2 * r), F32)
    out[2 * r + 1 : 2 * r + 2, :] = jnp.zeros((1, 4 * r), F32)
    out[2 * r + 2 : 2 * r + 3, :] = e_new
    out[2 * r + 3 : 2 * r + 8, :] = jnp.zeros((5, 4 * r), F32)


def dynamics_kernel(
    bs,
    scal,
    pattern,
    own_halves,
    core_halves,
    far_halves,
    far_core_halves,
    dyn_own,
    dyn_send,
    mh,
    ml,
    th,
    tl,
    vec,
    dense,
    a0h,
    a0l,
    a1h,
    a1l,
    a2h,
    a2l,
    a3h,
    a3l,
    product_ref,
):
    q, c = scal[0], scal[2]
    r = own_halves.shape[1] // 4
    third = (own_halves.shape[0] - 8) // 2
    first = c == 0
    sources = (
        (own_halves, core_halves, 0, 1),
        (own_halves, core_halves, 1, scal[3]),
        (far_halves, far_core_halves, 0, scal[4]),
        (far_halves, far_core_halves, 1, scal[5]),
    )
    targets = ((a0h, a0l), (a1h, a1l), (a2h, a2l), (a3h, a3l))
    b = [
        ref[2 * third + at : 2 * third + at + 1, :]
        for ref, at in ((own_halves, 0), (own_halves, 1), (far_halves, 0), (far_halves, 1))
    ]
    state = b[3]
    for at in (3, 2, 1, 0):
        mine, theirs, place, flag = sources[at]
        rows = slice(place * third, (place + 1) * third)
        dense_turned(dense, scal, pattern, mine[rows, :], theirs[rows, :], flag, r, bs)
        straight_split(targets[at][0], targets[at][1], dense, r)
        if at < 3:
            state = b[at] + row_times(state, dense[...], r)
        if at == 2:
            vec[0:1, :] = state
    vec[1:2, :] = state
    vec[2:8, :] = jnp.zeros((6, 4 * r), F32)

    @pl.when(first)
    def _():
        product_ref[...] = dot3(a1h[...], a1l[...], a0h[...], a0l[...])
        straight_split(mh, ml, product_ref, r)
        transpose_split(th, tl, product_ref, r)

    @pl.when(jnp.logical_not(first))
    def _():
        product_ref[...] = dot3(a3h[...], a3l[...], a2h[...], a2l[...])
        straight_split(th, tl, product_ref, r)
        transpose_split(mh, ml, product_ref, r)

    def wanted(ref):
        return jnp.concatenate([ref[:, 0:r], ref[:, 2 * r : 3 * r]], axis=1)

    t = dot3(a1h[...], a1l[...], wanted(a0h), wanted(a0l))
    t = dot3(a2h[...], a2l[...], *split(t))
    t = dot3(a3h[...], a3l[...], *split(t))
    for j in range(4):
        at = lanes(q ^ j, r)
        dyn_own[:, at] = t[j * r : (j + 1) * r, 0:r].T
        dyn_send[:, at] = t[j * r : (j + 1) * r, r : 2 * r].T


def level2_kernel(
    scal, own, earlier, mh, ml, th, tl, vec, keep, to_core, to_chip, to_far, full, xh, xl
):
    q, c = scal[0], scal[2]
    r = own.shape[1] // 4
    first = c == 0
    x = jnp.where(first, earlier[...], own[...])

    def put(i, j, block):
        full[i * r : (i + 1) * r, j * r : (j + 1) * r] = block
        put_split(xh, xl, slice(i * r, (i + 1) * r), slice(j * r, (j + 1) * r), block)

    spread(x, r, put)
    carried = own[2 * r + 2 : 2 * r + 3, :] + row_times(vec[0:1, :], full[...], r)
    e_new = earlier[2 * r + 2 : 2 * r + 3, :] + row_times(
        carried, mh[...].astype(F32) + ml[...].astype(F32), r
    )
    u = dot3(xh[...], xl[...], mh[...], ml[...])
    uh, ul = split(u)
    d = jnp.where(first, own[...], earlier[...])

    def keep_d(i, j, block):
        full[i * r : (i + 1) * r, j * r : (j + 1) * r] = block

    spread(d, r, keep_d)
    z = dot3(th[...], tl[...], uh, ul) + full[...]
    for i, ref in enumerate((keep, to_core, to_chip, to_far)):
        for j in range(4):
            ref[0:r, lanes(q ^ j, r)] = z[i * r : (i + 1) * r, j * r : (j + 1) * r]
        ref[r : r + 8, :] = jnp.zeros((8, 4 * r), F32)
        ref[r : r + 1, 0:r] = e_new[:, i * r : (i + 1) * r]
        ref[r : r + 1, r : 2 * r] = vec[1:2, i * r : (i + 1) * r]


def place_kernel(
    scal,
    keep,
    from_core,
    from_chip,
    from_far,
    dyn_own,
    dyn_recv,
    dyn_out,
    drift_out,
    cov_out,
    cost_out,
    eta_out,
):
    y, c = scal[1], scal[2]
    first = c == 0
    r = dyn_own.shape[0]
    dyn_out[y] = dyn_own[...]
    dyn_out[1 - y] = dyn_recv[...]
    cov_out[y] = jnp.where(first, keep[0:r, :], from_core[0:r, :])
    cov_out[1 - y] = jnp.where(first, from_chip[0:r, :], from_far[0:r, :])
    cost_out[y] = jnp.where(first, from_core[0:r, :], keep[0:r, :])
    cost_out[1 - y] = jnp.where(first, from_far[0:r, :], from_chip[0:r, :])
    drift_out[pl.ds(y, 1), :] = keep[r : r + 1, r : 2 * r]
    drift_out[pl.ds(1 - y, 1), :] = from_chip[r : r + 1, r : 2 * r]
    eta_out[pl.ds(y, 1), :] = jnp.where(first, from_core[r : r + 1, 0:r], keep[r : r + 1, 0:r])
    eta_out[pl.ds(1 - y, 1), :] = jnp.where(
        first, from_far[r : r + 1, 0:r], from_chip[r : r + 1, 0:r]
    )


def kernel(body, name, operands, shapes, scratch=(), scalars=1):
    smem = pl.BlockSpec(memory_space=pltpu.SMEM)
    vmem = pl.BlockSpec(memory_space=pltpu.VMEM)
    return pl.pallas_call(
        body,
        name=name,
        in_specs=[smem] * scalars + [vmem] * (len(operands) - scalars),
        out_specs=jax.tree.map(lambda _: vmem, shapes),
        out_shape=shapes,
        scratch_shapes=list(scratch),
    )(*operands)


def per_device_split(blocks, pattern, drift, cov, cost, eta):
    elements, r, n = cov.shape
    bs = blocks.shape[2] // 3
    tms, cols = lax.axis_size("tm"), lax.axis_size("col")
    position, q = lax.axis_index("tm"), lax.axis_index("col")
    third = 3 * bs // 2

    def swap(value, bit):
        return lax.ppermute(value, "col", [(i, i ^ bit) for i in range(cols)])

    def later(value, distance):
        return lax.ppermute(value, "tm", [(i, i + distance) for i in range(tms - distance)])

    def flag(x):
        return x.astype(jnp.int32)

    scal = jnp.stack(
        [
            q,
            q // 2,
            q % 2,
            flag(position >= 1),
            flag(position >= 2),
            flag(position >= 3),
        ]
    ).astype(jnp.int32)

    def shape(*dims):
        return jax.ShapeDtypeStruct(dims, F32)

    def half(*dims):
        return jax.ShapeDtypeStruct(dims, BF16)

    turned = jnp.swapaxes(blocks, 1, 2)
    given = (scal, cov, cost, turned, drift, eta)
    to_core, to_chip, to_far = kernel(
        send_kernel,
        "send",
        given,
        (shape(r + 8, 3 * r), shape(r + 8 + third, 2 * r), shape(r + 8, r)),
    )
    from_core, from_chip, from_far = swap(to_core, 1), swap(to_chip, 2), swap(to_far, 3)
    packed = kernel(
        pack_kernel,
        "pack",
        given + (from_core, from_chip, from_far),
        shape(2 * r + 8 + third, n),
    )
    earlier = later(packed, 1)
    base = 2 * r + 8
    halves = jnp.concatenate(
        [
            packed[base:],
            earlier[base:],
            packed[2 * r + 1 : 2 * r + 2],
            earlier[2 * r + 1 : 2 * r + 2],
            jnp.zeros((6, n), F32),
        ]
    )
    core_halves = swap(halves, 1)
    far_halves = later(halves, 2)
    square = lambda dtype: pltpu.VMEM((n, n), dtype)
    level1 = kernel(
        functools.partial(level1_kernel, bs),
        "level1",
        (scal, pattern, packed, earlier, core_halves),
        shape(base, n),
        [square(F32)] * 2 + [square(BF16)] * 6,
        scalars=2,
    )
    earlier1 = later(level1, 2)
    far_core_halves = swap(far_halves, 1)
    dyn_own, dyn_send, mh, ml, th, tl, vec = kernel(
        functools.partial(dynamics_kernel, bs),
        "dynamics",
        (scal, pattern, halves, core_halves, far_halves, far_core_halves),
        (shape(r, n), shape(r, n)) + (half(n, n),) * 4 + (shape(8, n),),
        [square(F32)] + [square(BF16)] * 8 + [square(F32)],
        scalars=2,
    )
    dyn_recv = swap(dyn_send, 2)
    keep, to_core, to_chip, to_far = kernel(
        level2_kernel,
        "level2",
        (scal, level1, earlier1, mh, ml, th, tl, vec),
        (shape(r + 8, n),) * 4,
        [square(F32)] + [square(BF16)] * 2,
    )
    from_core, from_chip, from_far = swap(to_core, 1), swap(to_chip, 2), swap(to_far, 3)
    return kernel(
        place_kernel,
        "place",
        (scal, keep, from_core, from_chip, from_far, dyn_own, dyn_recv),
        (
            shape(elements, r, n),
            shape(elements, r),
            shape(elements, r, n),
            shape(elements, r, n),
            shape(elements, r),
        ),
    )


def per_device(blocks, pattern, drift, cov, cost, eta):
    elements, r, n = cov.shape
    bs = blocks.shape[2] // 3
    fits = elements == 2 and lax.axis_size("col") == 4 and r % 128 == 0
    if fits and r % bs == 0 and (3 * bs) % 16 == 0:
        return per_device_split(blocks, pattern, drift, cov, cost, eta)
    return per_device_general(blocks, pattern, drift, cov, cost, eta)


def solution(mesh):
    return jax.shard_map(
        per_device,
        mesh=mesh,
        in_specs=(
            P("tm", "col", None),
            P(),
            P("tm", "col"),
            P("tm", "col", None),
            P("tm", "col", None),
            P("tm", "col"),
        ),
        out_specs=(
            P("tm", "col", None),
            P("tm", "col"),
            P("tm", "col", None),
            P("tm", "col", None),
            P("tm", "col"),
        ),
        check_vma=False,
    )
```

```python
import functools

import jax
import jax.numpy as jnp
from jax import lax
from jax.experimental import pallas as pl
from jax.experimental.pallas import tpu as pltpu
from jax.sharding import PartitionSpec as P

HIGH = lax.Precision.HIGHEST
F32 = jnp.float32
BF16 = jnp.bfloat16


def shifted(block, axis, distance):
    devices = range(lax.axis_size(axis))
    route = [(i - distance, i) for i in devices if i - distance in devices]
    return lax.ppermute(block, axis, route)


def product(form, left, right):
    return jnp.einsum(form, left, right, precision=HIGH)


def densify(row_blocks, row_ids, pattern, block_size):
    block_count = pattern.shape[0]
    row_block = row_ids // block_size
    chooser = (row_block[:, None] == jnp.arange(block_count, dtype=jnp.int32)[None, :]).astype(
        jnp.int32
    )
    columns = jnp.sum(chooser[:, :, None] * pattern[None, :, :], axis=1)
    matches = (
        columns[:, :, None] == jnp.arange(block_count, dtype=jnp.int32)[None, None, :]
    ).astype(jnp.float32)
    pieces = row_blocks.reshape(row_blocks.shape[:-1] + (3, 1, block_size))
    filled = jnp.sum(matches[:, :, :, None] * pieces, axis=-3)
    return filled.reshape(row_blocks.shape[:-1] + (block_count * block_size,))


def combine_rows(
    dyn_prev_full,
    dyn_own_full,
    dyn_own,
    drift_prev_full,
    drift_own,
    cov_prev,
    cov_own,
    cost_prev,
    cost_own,
    eta_prev,
    eta_own,
    first_row,
):
    height = dyn_own.shape[1]
    dyn_res = product("tij,tjk->tik", dyn_own, dyn_prev_full)
    drift_res = product("tij,tj->ti", dyn_own, drift_prev_full) + drift_own
    carried = eta_own + product("tij,tj->ti", cost_own, drift_prev_full)
    value_rows = product("tij,tjk->tik", cost_own, dyn_prev_full)
    prev_columns = lax.dynamic_slice_in_dim(dyn_prev_full, first_row, height, 2)
    cov_full, carried_full, value_full = (
        lax.all_gather(cov_prev, "col", axis=1, tiled=True),
        lax.all_gather(carried, "col", axis=1, tiled=True),
        lax.all_gather(value_rows, "col", axis=1, tiled=True),
    )
    cost_res = cost_prev + product("tki,tkj->tij", prev_columns, value_full)
    cov_res = (
        product("tik,tjk->tij", product("tij,tjk->tik", dyn_own, cov_full), dyn_own_full) + cov_own
    )
    eta_res = eta_prev + product("tki,tk->ti", prev_columns, carried_full)
    return (dyn_res, drift_res, cov_res, cost_res, eta_res)


def choose(flag, combined, kept):
    return tuple(jnp.where(flag, new, old) for new, old in zip(combined, kept))


def per_device_general(blocks, pattern, drift, cov, cost, eta):
    height = cov.shape[1]
    modes = cov.shape[2]
    block_size = blocks.shape[2] // 3
    first_row = lax.axis_index("col") * height
    own_ids = first_row + jnp.arange(height, dtype=jnp.int32)
    all_ids = jnp.arange(modes, dtype=jnp.int32)
    position = lax.axis_index("tm")
    dyn_own = densify(blocks, own_ids, pattern, block_size)
    received = shifted((blocks, drift, cov, cost, eta), "tm", 1)
    blocks_prev, blocks_own, drift_prev_full = (
        lax.all_gather(received[0], "col", axis=1, tiled=True),
        lax.all_gather(blocks, "col", axis=1, tiled=True),
        lax.all_gather(received[1], "col", axis=1, tiled=True),
    )
    merged = combine_rows(
        densify(blocks_prev, all_ids, pattern, block_size),
        densify(blocks_own, all_ids, pattern, block_size),
        dyn_own,
        drift_prev_full,
        drift,
        received[2],
        cov,
        received[3],
        cost,
        received[4],
        eta,
        first_row,
    )
    current = choose(position >= 1, merged, (dyn_own, drift, cov, cost, eta))
    received = shifted(current, "tm", 2)
    dyn_prev_full = lax.all_gather(received[0], "col", axis=1, tiled=True)
    dyn_own_full = lax.all_gather(current[0], "col", axis=1, tiled=True)
    drift_prev_full = lax.all_gather(received[1], "col", axis=1, tiled=True)
    merged = combine_rows(
        dyn_prev_full,
        dyn_own_full,
        current[0],
        drift_prev_full,
        current[1],
        received[2],
        current[2],
        received[3],
        current[3],
        received[4],
        current[4],
        first_row,
    )
    return choose(position >= 2, merged, current)


def split(x):
    hi = x.astype(BF16)
    lo = (x - hi.astype(F32)).astype(BF16)
    return hi, lo


def dot(a, b):
    return jnp.dot(a, b, preferred_element_type=F32)


def dot3(ah, al, bh, bl):
    return dot(ah, bh) + (dot(ah, bl) + dot(al, bh))


def triangle(r):
    rows = lax.broadcasted_iota(jnp.int32, (r, r), 0)
    cols = lax.broadcasted_iota(jnp.int32, (r, r), 1)
    return rows, cols


def fold(first, second, r):
    rows, cols = triangle(r)
    return jnp.where(rows >= cols, first, second)


def diagonal(block, r):
    rows, cols = triangle(r)
    return jnp.sum(jnp.where(rows == cols, block, 0.0), axis=0, keepdims=True)


def unfold(folded, second_diag, r):
    rows, cols = triangle(r)
    turned = folded.T
    first = jnp.where(rows >= cols, folded, turned)
    second = jnp.where(rows < cols, folded, turned)
    second = jnp.where(rows == cols, jnp.broadcast_to(second_diag, (r, r)), second)
    return first, second


UPPER = ((0, 1), (0, 2), (0, 3), (1, 2), (1, 3), (2, 3))


def spread(packed, r, put):
    panel0, panel1, diags = packed[0:r], packed[r : 2 * r], packed[2 * r : 2 * r + 1]
    k00, k11 = unfold(panel0[:, 0:r], diags[:, 0:r], r)
    k22, k33 = unfold(panel1[:, 0:r], diags[:, r : 2 * r], r)
    for i, block in enumerate((k00, k11, k22, k33)):
        put(i, i, block)
    for at, (i, j) in enumerate(UPPER):
        panel = panel0 if at < 3 else panel1
        block = panel[:, (at % 3 + 1) * r : (at % 3 + 2) * r]
        put(i, j, block)
        put(j, i, block.T)


def column(row, r):
    rows, cols = triangle(r)
    pieces = []
    for at in range(row.shape[1] // r):
        piece = jnp.broadcast_to(row[:, at * r : (at + 1) * r], (r, r))
        pieces.append(jnp.sum(jnp.where(rows == cols, piece, 0.0), axis=1, keepdims=True))
    return jnp.concatenate(pieces, axis=0)


def row_times(row, matrix, r):
    return jnp.sum(column(row, r) * matrix, axis=0, keepdims=True)


def lanes(index, r):
    return pl.ds(pl.multiple_of(index * r, r), r)


def send_kernel(scal, cov, cost, turned, drift, eta, to_core, to_chip, to_far):
    q, y, c = scal[0], scal[1], scal[2]
    r = cov.shape[1]
    third = turned.shape[1] // 2

    def kind(which, element, col_block):
        at = lanes(col_block, r)
        return jnp.where(which == 0, cov[element, :, at], cost[element, :, at])

    def vectors(element):
        return drift[pl.ds(element, 1), :], eta[pl.ds(element, 1), :]

    b, e = vectors(y)
    for j in range(1, 4):
        to_core[0:r, (j - 1) * r : j * r] = kind(1 - c, y, (q ^ 1) ^ j)
    to_core[r : r + 1, 0:r] = b
    to_core[r : r + 1, r : 2 * r] = e
    b, e = vectors(1 - y)
    for j in range(2, 4):
        to_chip[0:r, (j - 2) * r : (j - 1) * r] = kind(c, 1 - y, (q ^ 2) ^ j)
    to_chip[r : r + 1, 0:r] = b
    to_chip[r : r + 1, r : 2 * r] = e
    to_chip[r + 8 :, 0:r] = turned[1 - y, 0:third, :]
    to_chip[r + 8 :, r : 2 * r] = turned[1 - y, third:, :]
    to_far[0:r, :] = kind(1 - c, 1 - y, q)
    to_far[r : r + 1, :] = b
    to_far[r + 1 : r + 2, :] = e


def pack_kernel(scal, cov, cost, turned, drift, eta, from_core, from_chip, from_far, packed):
    q, y, c = scal[0], scal[1], scal[2]
    r = cov.shape[1]
    third = turned.shape[1] // 2

    def own(j):
        at = lanes(q ^ j, r)
        return jnp.where(c == 0, cov[y, :, at], cost[y, :, at])

    k11 = from_core[0:r, 0:r]
    k33 = from_far[0:r, :]
    packed[0:r, 0:r] = fold(own(0), k11, r)
    for j in range(1, 4):
        packed[0:r, j * r : (j + 1) * r] = own(j)
    packed[r : 2 * r, 0:r] = fold(from_chip[0:r, 0:r], k33, r)
    packed[r : 2 * r, r : 3 * r] = from_core[0:r, r : 3 * r]
    packed[r : 2 * r, 3 * r :] = from_chip[0:r, r : 2 * r]
    base = 2 * r
    packed[base : base + 8, :] = jnp.zeros((8, packed.shape[1]), F32)
    packed[base : base + 1, 0:r] = diagonal(k11, r)
    packed[base : base + 1, r : 2 * r] = diagonal(k33, r)
    parts_b = (
        drift[pl.ds(y, 1), :],
        from_core[r : r + 1, 0:r],
        from_chip[r : r + 1, 0:r],
        from_far[r : r + 1, :],
    )
    parts_e = (
        eta[pl.ds(y, 1), :],
        from_core[r : r + 1, r : 2 * r],
        from_chip[r : r + 1, r : 2 * r],
        from_far[r + 1 : r + 2, :],
    )
    for j in range(4):
        packed[base + 1 : base + 2, j * r : (j + 1) * r] = parts_b[j]
        packed[base + 2 : base + 3, j * r : (j + 1) * r] = parts_e[j]
    packed[base + 8 :, 0:r] = turned[y, 0:third, :]
    packed[base + 8 :, r : 2 * r] = turned[y, third:, :]
    packed[base + 8 :, 2 * r :] = from_chip[r + 8 :, :]


def dense_turned(out, scal, pattern, own_half, core_half, flag, r, bs):
    q = scal[0]
    n = out.shape[0]
    lane = lax.broadcasted_iota(jnp.int32, (bs, r), 1) // bs
    rows = lax.broadcasted_iota(jnp.int32, (bs, r), 0)
    cols = lax.broadcasted_iota(jnp.int32, (bs, r), 1)
    per = r // bs
    for j in range(4):
        half = own_half if j % 2 == 0 else core_half
        at = (j // 2) * 2 * r
        full = jnp.concatenate([half[:, at : at + r], half[:, at + r : at + 2 * r]], axis=0)
        wanted = []
        for k in range(3):
            want = jnp.zeros((bs, r), jnp.int32)
            for h in range(per):
                block = pattern[(q ^ j) * per + h, k] ^ (q * per)
                want = jnp.where(lane == h, block, want)
            wanted.append(jnp.where(flag == 1, want, -1))
        for block in range(n // bs):
            value = jnp.where(
                jnp.logical_and(rows + block * bs == cols + j * r, flag == 0), 1.0, 0.0
            )
            for k in range(3):
                piece = full[k * bs : (k + 1) * bs, :]
                value = value + jnp.where(wanted[k] == block, piece, 0.0)
            out[block * bs : (block + 1) * bs, j * r : (j + 1) * r] = value


def put_split(hi_ref, lo_ref, rows, cols, value):
    hi, lo = split(value)
    hi_ref[rows, cols] = hi
    lo_ref[rows, cols] = lo


def transpose_split(hi_ref, lo_ref, source, r):
    n = source.shape[0]
    for i in range(n // r):
        for j in range(n // r):
            put_split(
                hi_ref,
                lo_ref,
                slice(j * r, (j + 1) * r),
                slice(i * r, (i + 1) * r),
                source[i * r : (i + 1) * r, j * r : (j + 1) * r].T,
            )


def straight_split(hi_ref, lo_ref, source, r):
    n = source.shape[0]
    for i in range(n // r):
        put_split(
            hi_ref, lo_ref, slice(i * r, (i + 1) * r), slice(None), source[i * r : (i + 1) * r, :]
        )


def level1_kernel(
    bs, scal, pattern, own, earlier, core_halves, out, dense, full, mh, ml, th, tl, xh, xl
):
    c, has1 = scal[2], scal[3]
    r = core_halves.shape[1] // 4
    third = (own.shape[0] - 2 * r - 8)
    first = c == 0
    base = 2 * r + 8
    own_half = jnp.where(first, own[base:, :], earlier[base:, :])
    core_half = jnp.where(first, core_halves[0:third, :], core_halves[third : 2 * third, :])
    flag = jnp.where(first, 1, has1)
    dense_turned(dense, scal, pattern, own_half, core_half, flag, r, bs)

    @pl.when(first)
    def _():
        straight_split(mh, ml, dense, r)
        transpose_split(th, tl, dense, r)

    @pl.when(jnp.logical_not(first))
    def _():
        straight_split(th, tl, dense, r)
        transpose_split(mh, ml, dense, r)

    x = jnp.where(first, earlier[0 : base, :], own[0 : base, :])

    def put(i, j, block):
        full[i * r : (i + 1) * r, j * r : (j + 1) * r] = block
        put_split(xh, xl, slice(i * r, (i + 1) * r), slice(j * r, (j + 1) * r), block)

    spread(x, r, put)
    carried = own[2 * r + 2 : 2 * r + 3, :] + row_times(
        earlier[2 * r + 1 : 2 * r + 2, :], full[...], r
    )
    e_new = earlier[2 * r + 2 : 2 * r + 3, :] + row_times(
        carried, mh[...].astype(F32) + ml[...].astype(F32), r
    )
    u = dot3(xh[...], xl[...], mh[...], ml[...])
    uh, ul = split(u)
    top = dot3(th[0 : 2 * r, :], tl[0 : 2 * r, :], uh, ul)
    low = dot3(th[2 * r :, :], tl[2 * r :, :], uh[:, 2 * r :], ul[:, 2 * r :])
    d = jnp.where(first, own[0 : base, :], earlier[0 : base, :])
    z11 = top[r : 2 * r, r : 2 * r]
    z33 = low[r : 2 * r, r : 2 * r]
    out[0:r, 0:r] = fold(top[0:r, 0:r], z11, r) + d[0:r, 0:r]
    out[0:r, r:] = top[0:r, r:] + d[0:r, r:]
    out[r : 2 * r, 0:r] = fold(low[0:r, 0:r], z33, r) + d[r : 2 * r, 0:r]
    out[r : 2 * r, r : 3 * r] = top[r : 2 * r, 2 * r :] + d[r : 2 * r, r : 3 * r]
    out[r : 2 * r, 3 * r :] = low[0:r, r : 2 * r] + d[r : 2 * r, 3 * r :]
    out[2 * r : 2 * r + 1, 0:r] = diagonal(z11, r) + d[2 * r : 2 * r + 1, 0:r]
    out[2 * r : 2 * r + 1, r : 2 * r] = diagonal(z33, r) + d[2 * r : 2 * r + 1, r : 2 * r]
    out[2 * r : 2 * r + 1, 2 * r :] = jnp.zeros((1, 2 * r), F32)
    out[2 * r + 1 : 2 * r + 2, :] = jnp.zeros((1, 4 * r), F32)
    out[2 * r + 2 : 2 * r + 3, :] = e_new
    out[2 * r + 3 : 2 * r + 8, :] = jnp.zeros((5, 4 * r), F32)


def dynamics_kernel(
    bs,
    scal,
    pattern,
    own_halves,
    core_halves,
    far_halves,
    far_core_halves,
    dyn_own,
    dyn_send,
    mh,
    ml,
    th,
    tl,
    vec,
    dense,
    a0h,
    a0l,
    a1h,
    a1l,
    a2h,
    a2l,
    a3h,
    a3l,
    product_ref,
):
    q, c = scal[0], scal[2]
    r = own_halves.shape[1] // 4
    third = (own_halves.shape[0] - 8) // 2
    first = c == 0
    sources = (
        (own_halves, core_halves, 0, 1),
        (own_halves, core_halves, 1, scal[3]),
        (far_halves, far_core_halves, 0, scal[4]),
        (far_halves, far_core_halves, 1, scal[5]),
    )
    targets = ((a0h, a0l), (a1h, a1l), (a2h, a2l), (a3h, a3l))
    b = [
        ref[2 * third + at : 2 * third + at + 1, :]
        for ref, at in ((own_halves, 0), (own_halves, 1), (far_halves, 0), (far_halves, 1))
    ]
    state = b[3]
    for at in (3, 2, 1, 0):
        mine, theirs, place, flag = sources[at]
        rows = slice(place * third, (place + 1) * third)
        dense_turned(dense, scal, pattern, mine[rows, :], theirs[rows, :], flag, r, bs)
        straight_split(targets[at][0], targets[at][1], dense, r)
        if at < 3:
            state = b[at] + row_times(state, dense[...], r)
        if at == 2:
            vec[0:1, :] = state
    vec[1:2, :] = state
    vec[2:8, :] = jnp.zeros((6, 4 * r), F32)

    @pl.when(first)
    def _():
        product_ref[...] = dot3(a1h[...], a1l[...], a0h[...], a0l[...])
        straight_split(mh, ml, product_ref, r)
        transpose_split(th, tl, product_ref, r)

    @pl.when(jnp.logical_not(first))
    def _():
        product_ref[...] = dot3(a3h[...], a3l[...], a2h[...], a2l[...])
        straight_split(th, tl, product_ref, r)
        transpose_split(mh, ml, product_ref, r)

    def wanted(ref):
        return jnp.concatenate([ref[:, 0:r], ref[:, 2 * r : 3 * r]], axis=1)

    t = dot3(a1h[...], a1l[...], wanted(a0h), wanted(a0l))
    t = dot3(a2h[...], a2l[...], *split(t))
    t = dot3(a3h[...], a3l[...], *split(t))
    for j in range(4):
        at = lanes(q ^ j, r)
        dyn_own[:, at] = t[j * r : (j + 1) * r, 0:r].T
        dyn_send[:, at] = t[j * r : (j + 1) * r, r : 2 * r].T


def level2_kernel(
    scal, own, earlier, mh, ml, th, tl, vec, keep, to_core, to_chip, to_far, full, xh, xl
):
    q, c = scal[0], scal[2]
    r = own.shape[1] // 4
    first = c == 0
    x = jnp.where(first, earlier[...], own[...])

    def put(i, j, block):
        full[i * r : (i + 1) * r, j * r : (j + 1) * r] = block
        put_split(xh, xl, slice(i * r, (i + 1) * r), slice(j * r, (j + 1) * r), block)

    spread(x, r, put)
    carried = own[2 * r + 2 : 2 * r + 3, :] + row_times(vec[0:1, :], full[...], r)
    e_new = earlier[2 * r + 2 : 2 * r + 3, :] + row_times(
        carried, mh[...].astype(F32) + ml[...].astype(F32), r
    )
    u = dot3(xh[...], xl[...], mh[...], ml[...])
    uh, ul = split(u)
    d = jnp.where(first, own[...], earlier[...])

    def keep_d(i, j, block):
        full[i * r : (i + 1) * r, j * r : (j + 1) * r] = block

    spread(d, r, keep_d)
    z = dot3(th[...], tl[...], uh, ul) + full[...]
    for i, ref in enumerate((keep, to_core, to_chip, to_far)):
        for j in range(4):
            ref[0:r, lanes(q ^ j, r)] = z[i * r : (i + 1) * r, j * r : (j + 1) * r]
        ref[r : r + 8, :] = jnp.zeros((8, 4 * r), F32)
        ref[r : r + 1, 0:r] = e_new[:, i * r : (i + 1) * r]
        ref[r : r + 1, r : 2 * r] = vec[1:2, i * r : (i + 1) * r]


def place_kernel(
    scal,
    keep,
    from_core,
    from_chip,
    from_far,
    dyn_own,
    dyn_recv,
    dyn_out,
    drift_out,
    cov_out,
    cost_out,
    eta_out,
):
    y, c = scal[1], scal[2]
    first = c == 0
    r = dyn_own.shape[0]
    dyn_out[y] = dyn_own[...]
    dyn_out[1 - y] = dyn_recv[...]
    cov_out[y] = jnp.where(first, keep[0:r, :], from_core[0:r, :])
    cov_out[1 - y] = jnp.where(first, from_chip[0:r, :], from_far[0:r, :])
    cost_out[y] = jnp.where(first, from_core[0:r, :], keep[0:r, :])
    cost_out[1 - y] = jnp.where(first, from_far[0:r, :], from_chip[0:r, :])
    drift_out[pl.ds(y, 1), :] = keep[r : r + 1, r : 2 * r]
    drift_out[pl.ds(1 - y, 1), :] = from_chip[r : r + 1, r : 2 * r]
    eta_out[pl.ds(y, 1), :] = jnp.where(first, from_core[r : r + 1, 0:r], keep[r : r + 1, 0:r])
    eta_out[pl.ds(1 - y, 1), :] = jnp.where(
        first, from_far[r : r + 1, 0:r], from_chip[r : r + 1, 0:r]
    )


def kernel(body, name, operands, shapes, scratch=(), scalars=1, near=0, out_near=True):
    operands = [
        pltpu.with_memory_space_constraint(x, pltpu.VMEM) if i >= max(near, scalars) else x
        for i, x in enumerate(operands)
    ]
    if out_near:
        shapes = jax.tree.map(lambda s: pltpu.VMEM(s.shape, s.dtype), shapes)
    smem = pl.BlockSpec(memory_space=pltpu.SMEM)
    vmem = pl.BlockSpec(memory_space=pltpu.VMEM)
    return pl.pallas_call(
        body,
        name=name,
        in_specs=[smem] * scalars + [vmem] * (len(operands) - scalars),
        out_specs=jax.tree.map(lambda _: vmem, shapes),
        out_shape=shapes,
        scratch_shapes=list(scratch),
        compiler_params=pltpu.CompilerParams(vmem_limit_bytes=24 * 2**20),
    )(*operands)


def per_device_split(blocks, pattern, drift, cov, cost, eta):
    elements, r, n = cov.shape
    bs = blocks.shape[2] // 3
    tms, cols = lax.axis_size("tm"), lax.axis_size("col")
    position, q = lax.axis_index("tm"), lax.axis_index("col")
    third = 3 * bs // 2

    def swap(value, bit):
        return lax.ppermute(value, "col", [(i, i ^ bit) for i in range(cols)])

    def later(value, distance):
        return lax.ppermute(value, "tm", [(i, i + distance) for i in range(tms - distance)])

    def flag(x):
        return x.astype(jnp.int32)

    scal = jnp.stack(
        [
            q,
            q // 2,
            q % 2,
            flag(position >= 1),
            flag(position >= 2),
            flag(position >= 3),
        ]
    ).astype(jnp.int32)

    def shape(*dims):
        return jax.ShapeDtypeStruct(dims, F32)

    def half(*dims):
        return jax.ShapeDtypeStruct(dims, BF16)

    turned = jnp.swapaxes(blocks, 1, 2)
    given = (scal, cov, cost, turned, drift, eta)
    to_core, to_chip, to_far = kernel(
        send_kernel,
        "send",
        given,
        (shape(r + 8, 3 * r), shape(r + 8 + third, 2 * r), shape(r + 8, r)),
        near=len(given),
    )
    from_core, from_chip, from_far = swap(to_core, 1), swap(to_chip, 2), swap(to_far, 3)
    packed = kernel(
        pack_kernel,
        "pack",
        given + (from_core, from_chip, from_far),
        shape(2 * r + 8 + third, n),
        near=len(given),
    )
    earlier = later(packed, 1)
    base = 2 * r + 8
    halves = jnp.concatenate(
        [
            packed[base:],
            earlier[base:],
            packed[2 * r + 1 : 2 * r + 2],
            earlier[2 * r + 1 : 2 * r + 2],
            jnp.zeros((6, n), F32),
        ]
    )
    core_halves = swap(halves, 1)
    far_halves = later(halves, 2)
    square = lambda dtype: pltpu.VMEM((n, n), dtype)
    level1 = kernel(
        functools.partial(level1_kernel, bs),
        "level1",
        (scal, pattern, packed, earlier, core_halves),
        shape(base, n),
        [square(F32)] * 2 + [square(BF16)] * 6,
        scalars=2,
    )
    earlier1 = later(level1, 2)
    far_core_halves = swap(far_halves, 1)
    dyn_own, dyn_send, mh, ml, th, tl, vec = kernel(
        functools.partial(dynamics_kernel, bs),
        "dynamics",
        (scal, pattern, halves, core_halves, far_halves, far_core_halves),
        (shape(r, n), shape(r, n)) + (half(n, n),) * 4 + (shape(8, n),),
        [square(F32)] + [square(BF16)] * 8 + [square(F32)],
        scalars=2,
    )
    dyn_recv = swap(dyn_send, 2)
    keep, to_core, to_chip, to_far = kernel(
        level2_kernel,
        "level2",
        (scal, level1, earlier1, mh, ml, th, tl, vec),
        (shape(r + 8, n),) * 4,
        [square(F32)] + [square(BF16)] * 2,
    )
    from_core, from_chip, from_far = swap(to_core, 1), swap(to_chip, 2), swap(to_far, 3)
    return kernel(
        place_kernel,
        "place",
        (scal, keep, from_core, from_chip, from_far, dyn_own, dyn_recv),
        (
            shape(elements, r, n),
            shape(elements, r),
            shape(elements, r, n),
            shape(elements, r, n),
            shape(elements, r),
        ),
        out_near=False,
    )


def per_device(blocks, pattern, drift, cov, cost, eta):
    elements, r, n = cov.shape
    bs = blocks.shape[2] // 3
    fits = elements == 2 and lax.axis_size("col") == 4 and r % 128 == 0
    if fits and r % bs == 0 and (3 * bs) % 16 == 0:
        return per_device_split(blocks, pattern, drift, cov, cost, eta)
    return per_device_general(blocks, pattern, drift, cov, cost, eta)


def solution(mesh):
    return jax.shard_map(
        per_device,
        mesh=mesh,
        in_specs=(
            P("tm", "col", None),
            P(),
            P("tm", "col"),
            P("tm", "col", None),
            P("tm", "col", None),
            P("tm", "col"),
        ),
        out_specs=(
            P("tm", "col", None),
            P("tm", "col"),
            P("tm", "col", None),
            P("tm", "col", None),
            P("tm", "col"),
        ),
        check_vma=False,
    )
```

```python
import functools

import jax
import jax.numpy as jnp
from jax import lax
from jax.experimental import pallas as pl
from jax.experimental.pallas import tpu as pltpu
from jax.sharding import PartitionSpec as P


HIGH = lax.Precision.HIGHEST
F32 = jnp.float32
BF16 = jnp.bfloat16


def shifted(block, axis, distance):
    devices = range(lax.axis_size(axis))
    route = [(i - distance, i) for i in devices if i - distance in devices]
    return lax.ppermute(block, axis, route)


def product(form, left, right):
    return jnp.einsum(form, left, right, precision=HIGH)


def densify(row_blocks, row_ids, pattern, block_size):
    block_count = pattern.shape[0]
    row_block = row_ids // block_size
    chooser = (row_block[:, None] == jnp.arange(block_count, dtype=jnp.int32)[None, :]).astype(
        jnp.int32
    )
    columns = jnp.sum(chooser[:, :, None] * pattern[None, :, :], axis=1)
    matches = (
        columns[:, :, None] == jnp.arange(block_count, dtype=jnp.int32)[None, None, :]
    ).astype(jnp.float32)
    pieces = row_blocks.reshape(row_blocks.shape[:-1] + (3, 1, block_size))
    filled = jnp.sum(matches[:, :, :, None] * pieces, axis=-3)
    return filled.reshape(row_blocks.shape[:-1] + (block_count * block_size,))


def combine_rows(
    dyn_prev_full,
    dyn_own_full,
    dyn_own,
    drift_prev_full,
    drift_own,
    cov_prev,
    cov_own,
    cost_prev,
    cost_own,
    eta_prev,
    eta_own,
    first_row,
):
    height = dyn_own.shape[1]
    dyn_res = product("tij,tjk->tik", dyn_own, dyn_prev_full)
    drift_res = product("tij,tj->ti", dyn_own, drift_prev_full) + drift_own
    carried = eta_own + product("tij,tj->ti", cost_own, drift_prev_full)
    value_rows = product("tij,tjk->tik", cost_own, dyn_prev_full)
    prev_columns = lax.dynamic_slice_in_dim(dyn_prev_full, first_row, height, 2)
    cov_full, carried_full, value_full = (
        lax.all_gather(cov_prev, "col", axis=1, tiled=True),
        lax.all_gather(carried, "col", axis=1, tiled=True),
        lax.all_gather(value_rows, "col", axis=1, tiled=True),
    )
    cost_res = cost_prev + product("tki,tkj->tij", prev_columns, value_full)
    cov_res = (
        product("tik,tjk->tij", product("tij,tjk->tik", dyn_own, cov_full), dyn_own_full) + cov_own
    )
    eta_res = eta_prev + product("tki,tk->ti", prev_columns, carried_full)
    return (dyn_res, drift_res, cov_res, cost_res, eta_res)


def choose(flag, combined, kept):
    return tuple(jnp.where(flag, new, old) for new, old in zip(combined, kept))


def per_device_general(blocks, pattern, drift, cov, cost, eta):
    height = cov.shape[1]
    modes = cov.shape[2]
    block_size = blocks.shape[2] // 3
    first_row = lax.axis_index("col") * height
    own_ids = first_row + jnp.arange(height, dtype=jnp.int32)
    all_ids = jnp.arange(modes, dtype=jnp.int32)
    position = lax.axis_index("tm")
    dyn_own = densify(blocks, own_ids, pattern, block_size)
    received = shifted((blocks, drift, cov, cost, eta), "tm", 1)
    blocks_prev, blocks_own, drift_prev_full = (
        lax.all_gather(received[0], "col", axis=1, tiled=True),
        lax.all_gather(blocks, "col", axis=1, tiled=True),
        lax.all_gather(received[1], "col", axis=1, tiled=True),
    )
    merged = combine_rows(
        densify(blocks_prev, all_ids, pattern, block_size),
        densify(blocks_own, all_ids, pattern, block_size),
        dyn_own,
        drift_prev_full,
        drift,
        received[2],
        cov,
        received[3],
        cost,
        received[4],
        eta,
        first_row,
    )
    current = choose(position >= 1, merged, (dyn_own, drift, cov, cost, eta))
    received = shifted(current, "tm", 2)
    dyn_prev_full = lax.all_gather(received[0], "col", axis=1, tiled=True)
    dyn_own_full = lax.all_gather(current[0], "col", axis=1, tiled=True)
    drift_prev_full = lax.all_gather(received[1], "col", axis=1, tiled=True)
    merged = combine_rows(
        dyn_prev_full,
        dyn_own_full,
        current[0],
        drift_prev_full,
        current[1],
        received[2],
        current[2],
        received[3],
        current[3],
        received[4],
        current[4],
        first_row,
    )
    return choose(position >= 2, merged, current)


def split(x):
    hi = x.astype(BF16)
    lo = (x - hi.astype(F32)).astype(BF16)
    return hi, lo


def dot(a, b):
    return jnp.dot(a, b, preferred_element_type=F32)


def dot3(ah, al, bh, bl):
    return dot(ah, bh) + (dot(ah, bl) + dot(al, bh))


def triangle(r):
    rows = lax.broadcasted_iota(jnp.int32, (r, r), 0)
    cols = lax.broadcasted_iota(jnp.int32, (r, r), 1)
    return rows, cols


def fold(first, second, r):
    rows, cols = triangle(r)
    return jnp.where(rows >= cols, first, second)


def diagonal(block, r):
    rows, cols = triangle(r)
    return jnp.sum(jnp.where(rows == cols, block, 0.0), axis=0, keepdims=True)


def unfold(folded, second_diag, r):
    rows, cols = triangle(r)
    turned = folded.T
    first = jnp.where(rows >= cols, folded, turned)
    second = jnp.where(rows < cols, folded, turned)
    second = jnp.where(rows == cols, jnp.broadcast_to(second_diag, (r, r)), second)
    return first, second


UPPER = ((0, 1), (0, 2), (0, 3), (1, 2), (1, 3), (2, 3))


def spread(packed, r, put):
    panel0, panel1, diags = packed[0:r], packed[r : 2 * r], packed[2 * r : 2 * r + 1]
    k00, k11 = unfold(panel0[:, 0:r], diags[:, 0:r], r)
    k22, k33 = unfold(panel1[:, 0:r], diags[:, r : 2 * r], r)
    for i, block in enumerate((k00, k11, k22, k33)):
        put(i, i, block)
    for at, (i, j) in enumerate(UPPER):
        panel = panel0 if at < 3 else panel1
        block = panel[:, (at % 3 + 1) * r : (at % 3 + 2) * r]
        put(i, j, block)
        put(j, i, block.T)


def column(row, r):
    rows, cols = triangle(r)
    pieces = []
    for at in range(row.shape[1] // r):
        piece = jnp.broadcast_to(row[:, at * r : (at + 1) * r], (r, r))
        pieces.append(jnp.sum(jnp.where(rows == cols, piece, 0.0), axis=1, keepdims=True))
    return jnp.concatenate(pieces, axis=0)


def row_times(row, matrix, r):
    return jnp.sum(column(row, r) * matrix, axis=0, keepdims=True)


def lanes(index, r):
    return pl.ds(pl.multiple_of(index * r, r), r)


def send_kernel(scal, cov, cost, drift, eta, to_core, to_chip, to_far):
    q, y, c = scal[0], scal[1], scal[2]
    r = cov.shape[1]

    def kind(which, element, col_block):
        at = lanes(col_block, r)
        return jnp.where(which == 0, cov[element, :, at], cost[element, :, at])

    def vectors(element):
        return drift[pl.ds(element, 1), :], eta[pl.ds(element, 1), :]

    b, e = vectors(y)
    for j in range(1, 4):
        to_core[0:r, (j - 1) * r : j * r] = kind(1 - c, y, (q ^ 1) ^ j)
    to_core[r : r + 1, 0:r] = b
    to_core[r : r + 1, r : 2 * r] = e
    b, e = vectors(1 - y)
    for j in range(2, 4):
        to_chip[0:r, (j - 2) * r : (j - 1) * r] = kind(c, 1 - y, (q ^ 2) ^ j)
    to_chip[r : r + 1, 0:r] = b
    to_chip[r : r + 1, r : 2 * r] = e
    to_far[0:r, :] = kind(1 - c, 1 - y, q)
    to_far[r : r + 1, :] = b
    to_far[r + 1 : r + 2, :] = e


def pack_near_kernel(scal, cov, cost, from_core, packed):
    q, y, c = scal[0], scal[1], scal[2]
    r = cov.shape[1]

    def own(j):
        at = lanes(q ^ j, r)
        return jnp.where(c == 0, cov[y, :, at], cost[y, :, at])

    packed[:, 0:r] = fold(own(0), from_core[0:r, 0:r], r)
    for j in range(1, 4):
        packed[:, j * r : (j + 1) * r] = own(j)
    packed[:, 4 * r :] = from_core[0:r, r : 3 * r]


def pack_far_kernel(scal, drift, eta, from_core, from_chip, from_far, packed):
    y = scal[1]
    r = drift.shape[1]
    k33 = from_far[0:r, :]
    packed[0:r, 0:r] = fold(from_chip[0:r, 0:r], k33, r)
    packed[0:r, r:] = from_chip[0:r, r : 2 * r]
    packed[r : r + 1, 0:r] = diagonal(from_core[0:r, 0:r], r)
    packed[r : r + 1, r:] = diagonal(k33, r)
    b = (
        drift[pl.ds(y, 1), :],
        from_core[r : r + 1, 0:r],
        from_chip[r : r + 1, 0:r],
        from_far[r : r + 1, :],
    )
    e = (
        eta[pl.ds(y, 1), :],
        from_core[r : r + 1, r : 2 * r],
        from_chip[r : r + 1, r : 2 * r],
        from_far[r + 1 : r + 2, :],
    )
    for j in range(4):
        at = slice(j % 2 * r, (j % 2 + 1) * r)
        packed[r + 1 + j // 2 : r + 2 + j // 2, at] = b[j]
        packed[r + 3 + j // 2 : r + 4 + j // 2, at] = e[j]
    packed[r + 5 : r + 8, :] = jnp.zeros((3, 2 * r), F32)


def far_row(packed, r, at):
    return jnp.concatenate(
        [packed[r + at : r + at + 1, :], packed[r + at + 1 : r + at + 2, :]], axis=1
    )


def pick_kernel(scal, turned, before, out):
    y = scal[1]
    height = turned.shape[1]
    out[0:height, :] = turned[1 - y]
    out[height:, :] = before[1 - y]


def halves_kernel(scal, turned, before, other, out):
    y = scal[1]
    height = turned.shape[1]
    out[0:height, :] = turned[y]
    out[height : 2 * height, :] = other[0:height, :]
    out[2 * height : 3 * height, :] = before[y]
    out[3 * height :, :] = other[height:, :]


def dense_turned(put, scal, pattern, own_half, core_half, flag, n, r, bs):
    q = scal[0]
    lane = lax.broadcasted_iota(jnp.int32, (bs, r), 1) // bs
    rows = lax.broadcasted_iota(jnp.int32, (bs, r), 0)
    cols = lax.broadcasted_iota(jnp.int32, (bs, r), 1)
    per = r // bs
    height = 3 * bs
    for j in range(4):
        half = own_half if j % 2 == 0 else core_half
        full = half[(j // 2) * height : (j // 2 + 1) * height, :]
        wanted = []
        for k in range(3):
            want = jnp.zeros((bs, r), jnp.int32)
            for h in range(per):
                block = pattern[(q ^ j) * per + h, k] ^ (q * per)
                want = jnp.where(lane == h, block, want)
            wanted.append(jnp.where(flag == 1, want, -1))
        for block in range(n // bs):
            if j * r <= block * bs < (j + 1) * r:
                value = jnp.where(
                    jnp.logical_and(rows + block * bs == cols + j * r, flag == 0), 1.0, 0.0
                )
            else:
                value = jnp.zeros((bs, r), F32)
            for k in range(3):
                piece = full[k * bs : (k + 1) * bs, :]
                value = value + jnp.where(wanted[k] == block, piece, 0.0)
            put(slice(block * bs, (block + 1) * bs), slice(j * r, (j + 1) * r), value)


def put_split(hi_ref, lo_ref, rows, cols, value):
    hi, lo = split(value)
    hi_ref[rows, cols] = hi
    lo_ref[rows, cols] = lo


def transpose_split(hi_ref, lo_ref, source, r):
    n = source.shape[0]
    for i in range(n // r):
        for j in range(n // r):
            put_split(
                hi_ref,
                lo_ref,
                slice(j * r, (j + 1) * r),
                slice(i * r, (i + 1) * r),
                source[i * r : (i + 1) * r, j * r : (j + 1) * r].T,
            )


def straight_split(hi_ref, lo_ref, source, r):
    n = source.shape[0]
    for i in range(n // r):
        put_split(
            hi_ref, lo_ref, slice(i * r, (i + 1) * r), slice(None), source[i * r : (i + 1) * r, :]
        )


def prepare_kernel(
    bs, scal, pattern, halves, core_halves, mh, ml, th, tl, a0h, a0l, a1h, a1l, dense
):
    c, has1 = scal[2], scal[3]
    n = dense.shape[0]
    r = halves.shape[1]
    half = halves.shape[0] // 2
    first = c == 0
    for at, flag, hi, lo in ((0, 1, a0h, a0l), (1, has1, a1h, a1l)):
        rows = slice(at * half, (at + 1) * half)
        mine = first if at == 0 else jnp.logical_not(first)

        def put(row, col, value):
            put_split(hi, lo, row, col, value)
            dense[row, col] = value

        dense_turned(put, scal, pattern, halves[rows, :], core_halves[rows, :], flag, n, r, bs)

        @pl.when(mine)
        def _():
            if at == 0:
                straight_split(mh, ml, dense, r)
                transpose_split(th, tl, dense, r)
            else:
                straight_split(th, tl, dense, r)
                transpose_split(mh, ml, dense, r)


def level1_kernel(
    scal, own_near, own_far, near, far, mh, ml, th, tl, out, full, xh, xl
):
    c = scal[2]
    r = own_near.shape[0]
    first = c == 0
    xn = jnp.where(first, near[...], own_near[...])
    xf = jnp.where(first, far[...], own_far[...])
    x = jnp.concatenate(
        [
            xn[:, 0 : 4 * r],
            jnp.concatenate([xf[0:r, 0:r], xn[:, 4 * r :], xf[0:r, r:]], axis=1),
            jnp.concatenate([xf[r : r + 1, :], xf[r : r + 1, :]], axis=1),
        ],
        axis=0,
    )

    def put(i, j, block):
        full[i * r : (i + 1) * r, j * r : (j + 1) * r] = block
        put_split(xh, xl, slice(i * r, (i + 1) * r), slice(j * r, (j + 1) * r), block)

    spread(x, r, put)
    b_before, b_own = far_row(far, r, 1), far_row(own_far, r, 1)
    e_before, e_own = far_row(far, r, 3), far_row(own_far, r, 3)
    carried = jnp.where(first, b_before, e_own + row_times(b_before, full[...], r))
    vec = jnp.where(first, b_own, e_before) + row_times(
        carried, mh[...].astype(F32) + ml[...].astype(F32), r
    )
    u = dot3(xh[...], xl[...], mh[...], ml[...])
    uh, ul = split(u)
    top = dot3(th[0 : 2 * r, :], tl[0 : 2 * r, :], uh, ul)
    low = dot3(th[2 * r :, :], tl[2 * r :, :], uh[:, 2 * r :], ul[:, 2 * r :])
    dn = jnp.where(first, own_near[...], near[...])
    df = jnp.where(first, own_far[...], far[...])
    z11 = top[r : 2 * r, r : 2 * r]
    z33 = low[r : 2 * r, r : 2 * r]
    out[0:r, 0:r] = fold(top[0:r, 0:r], z11, r) + dn[:, 0:r]
    out[0:r, r:] = top[0:r, r:] + dn[:, r : 4 * r]
    out[r : 2 * r, 0:r] = fold(low[0:r, 0:r], z33, r) + df[0:r, 0:r]
    out[r : 2 * r, r : 3 * r] = top[r : 2 * r, 2 * r :] + dn[:, 4 * r :]
    out[r : 2 * r, 3 * r :] = low[0:r, r : 2 * r] + df[0:r, r:]
    base = 2 * r
    out[base : base + 1, 0:r] = diagonal(z11, r) + df[r : r + 1, 0:r]
    out[base : base + 1, r : 2 * r] = diagonal(z33, r) + df[r : r + 1, r:]
    out[base : base + 1, 2 * r :] = jnp.zeros((1, 2 * r), F32)
    out[base + 1 : base + 2, :] = b_own
    out[base + 2 : base + 3, :] = vec
    out[base + 3 : base + 4, :] = b_before
    out[base + 4 : base + 8, :] = jnp.zeros((4, 4 * r), F32)


def dynamics_kernel(
    bs,
    scal,
    pattern,
    halves,
    core_halves,
    a0h,
    a0l,
    a1h,
    a1l,
    dyn_own,
    dyn_send,
    mh,
    ml,
    th,
    tl,
    a2,
    a2h,
    a2l,
    a3h,
    a3l,
    product_ref,
):
    q, c = scal[0], scal[2]
    n = a0h.shape[0]
    r = halves.shape[1]
    half = halves.shape[0] // 2
    first = c == 0

    def put2(row, col, value):
        put_split(a2h, a2l, row, col, value)
        a2[row, col] = value

    def put3(row, col, value):
        put_split(a3h, a3l, row, col, value)

    for at, flag, put in ((0, scal[4], put2), (1, scal[5], put3)):
        rows = slice(at * half, (at + 1) * half)
        dense_turned(put, scal, pattern, halves[rows, :], core_halves[rows, :], flag, n, r, bs)

    def wanted(ref):
        return jnp.concatenate([ref[:, 0:r], ref[:, 2 * r : 3 * r]], axis=1)

    t = dot3(a1h[...], a1l[...], wanted(a0h), wanted(a0l))
    t = dot3(a2h[...], a2l[...], *split(t))
    t = dot3(a3h[...], a3l[...], *split(t))
    for j in range(4):
        at = lanes(q ^ j, r)
        dyn_own[:, at] = t[j * r : (j + 1) * r, 0:r].T
        dyn_send[:, at] = t[j * r : (j + 1) * r, r : 2 * r].T

    @pl.when(first)
    def _():
        product_ref[...] = dot3(a1h[...], a1l[...], a0h[...], a0l[...])
        straight_split(mh, ml, product_ref, r)
        transpose_split(th, tl, product_ref, r)

    @pl.when(jnp.logical_not(first))
    def _():
        product_ref[...] = dot3(a3h[...], a3l[...], a2h[...], a2l[...])
        straight_split(th, tl, product_ref, r)
        transpose_split(mh, ml, product_ref, r)


def level2_kernel(
    scal, own, earlier, mh, ml, th, tl, a2, keep, to_core, to_chip, to_far, full, xh, xl
):
    q, c = scal[0], scal[2]
    r = own.shape[1] // 4
    first = c == 0
    x = jnp.where(first, earlier[...], own[...])

    def put(i, j, block):
        full[i * r : (i + 1) * r, j * r : (j + 1) * r] = block
        put_split(xh, xl, slice(i * r, (i + 1) * r), slice(j * r, (j + 1) * r), block)

    spread(x, r, put)
    base = 2 * r
    d = jnp.where(first, own[...], earlier[...])
    b1 = earlier[base + 1 : base + 2, :] + row_times(
        earlier[base + 3 : base + 4, :], a2[...], r
    )
    carried = jnp.where(first, b1, own[base + 2 : base + 3, :] + row_times(b1, full[...], r))
    vec = d[base + 2 : base + 3, :] + row_times(
        carried, mh[...].astype(F32) + ml[...].astype(F32), r
    )
    u = dot3(xh[...], xl[...], mh[...], ml[...])
    uh, ul = split(u)

    def keep_d(i, j, block):
        full[i * r : (i + 1) * r, j * r : (j + 1) * r] = block

    spread(d, r, keep_d)
    z = dot3(th[...], tl[...], uh, ul) + full[...]
    for i, ref in enumerate((keep, to_core, to_chip, to_far)):
        for j in range(4):
            ref[0:r, lanes(q ^ j, r)] = z[i * r : (i + 1) * r, j * r : (j + 1) * r]
        ref[r : r + 8, :] = jnp.zeros((8, 4 * r), F32)
        ref[r : r + 1, 0:r] = vec[:, i * r : (i + 1) * r]


def place_kernel(
    scal,
    keep,
    from_core,
    from_chip,
    from_far,
    dyn_own,
    dyn_recv,
    dyn_out,
    drift_out,
    cov_out,
    cost_out,
    eta_out,
):
    y, c = scal[1], scal[2]
    first = c == 0
    r = dyn_own.shape[0]
    dyn_out[y] = dyn_own[...]
    dyn_out[1 - y] = dyn_recv[...]
    pairs = (
        (cov_out, drift_out, keep, from_core, from_chip, from_far),
        (cost_out, eta_out, from_core, keep, from_far, from_chip),
    )
    for matrix, vector, one, two, three, four in pairs:
        matrix[y] = jnp.where(first, one[0:r, :], two[0:r, :])
        matrix[1 - y] = jnp.where(first, three[0:r, :], four[0:r, :])
        at = slice(r, r + 1)
        vector[pl.ds(y, 1), :] = jnp.where(first, one[at, 0:r], two[at, 0:r])
        vector[pl.ds(1 - y, 1), :] = jnp.where(first, three[at, 0:r], four[at, 0:r])


def kernel(body, operands, shapes, scratch=(), scalars=1, near=0, out_near=True):
    operands = [
        pltpu.with_memory_space_constraint(x, pltpu.VMEM) if i >= max(near, scalars) else x
        for i, x in enumerate(operands)
    ]
    if out_near:
        shapes = jax.tree.map(lambda s: pltpu.VMEM(s.shape, s.dtype), shapes)
    smem = pl.BlockSpec(memory_space=pltpu.SMEM)
    vmem = pl.BlockSpec(memory_space=pltpu.VMEM)
    return pl.pallas_call(
        body,
        in_specs=[smem] * scalars + [vmem] * (len(operands) - scalars),
        out_specs=jax.tree.map(lambda _: vmem, shapes),
        out_shape=shapes,
        scratch_shapes=list(scratch),
        compiler_params=pltpu.CompilerParams(vmem_limit_bytes=24 * 2**20),
    )(*operands)


def per_device_split(blocks, pattern, drift, cov, cost, eta):
    elements, r, n = cov.shape
    bs = blocks.shape[2] // 3
    tms, cols = lax.axis_size("tm"), lax.axis_size("col")
    position, q = lax.axis_index("tm"), lax.axis_index("col")

    def swap(value, bit):
        return lax.ppermute(value, "col", [(i, i ^ bit) for i in range(cols)])

    def later(value, distance):
        return lax.ppermute(value, "tm", [(i, i + distance) for i in range(tms - distance)])

    def flag(x):
        return x.astype(jnp.int32)

    scal = jnp.stack(
        [
            q,
            q >> 1,
            q & 1,
            flag(position >= 1),
            flag(position >= 2),
            flag(position >= 3),
        ]
    ).astype(jnp.int32)

    def shape(*dims):
        return jax.ShapeDtypeStruct(dims, F32)

    def half(*dims):
        return jax.ShapeDtypeStruct(dims, BF16)

    def square(dtype):
        return pltpu.VMEM((n, n), dtype)

    turned = jnp.swapaxes(blocks, 1, 2)
    before = later(turned, 1)
    to_core, to_chip, to_far = kernel(
        send_kernel,
        (scal, cov, cost, drift, eta),
        (shape(r + 8, 3 * r), shape(r + 8, 2 * r), shape(r + 8, r)),
        near=5,
    )
    from_core = swap(to_core, 1)
    from_chip = swap(to_chip, 2)
    from_far = swap(to_far, 3)
    own_near = kernel(
        pack_near_kernel, (scal, cov, cost, from_core), shape(r, 6 * r), near=3
    )
    near = later(own_near, 1)
    own_far = kernel(
        pack_far_kernel,
        (scal, drift, eta, from_core, from_chip, from_far),
        shape(r + 8, 2 * r),
        near=3,
    )
    far = later(own_far, 1)
    picked = kernel(pick_kernel, (scal, turned, before), shape(6 * bs, r), near=2)
    other = swap(picked, 2)
    halves = kernel(
        halves_kernel, (scal, turned, before, other), shape(12 * bs, r), near=2
    )
    core_halves = swap(halves, 1)
    far_halves = later(halves, 2)
    factors = kernel(
        functools.partial(prepare_kernel, bs),
        (scal, pattern, halves, core_halves),
        (half(n, n),) * 8,
        [square(F32)],
        scalars=2,
    )
    m1, a01 = factors[:4], factors[4:]
    level1 = kernel(
        level1_kernel,
        (scal, own_near, own_far, near, far) + tuple(m1),
        shape(2 * r + 8, n),
        [square(F32)] + [square(BF16)] * 2,
    )
    earlier = later(level1, 2)
    far_core_halves = swap(far_halves, 1)
    dyn_own, dyn_send, *m2 = kernel(
        functools.partial(dynamics_kernel, bs),
        (scal, pattern, far_halves, far_core_halves) + tuple(a01),
        (shape(r, n), shape(r, n)) + (half(n, n),) * 4 + (shape(n, n),),
        [square(BF16)] * 4 + [square(F32)],
        scalars=2,
    )
    dyn_recv = swap(dyn_send, 2)
    keep, to_core, to_chip, to_far = kernel(
        level2_kernel,
        (scal, level1, earlier) + tuple(m2),
        (shape(r + 8, n),) * 4,
        [square(F32)] + [square(BF16)] * 2,
    )
    from_core = swap(to_core, 1)
    from_chip = swap(to_chip, 2)
    from_far = swap(to_far, 3)
    return kernel(
        place_kernel,
        (scal, keep, from_core, from_chip, from_far, dyn_own, dyn_recv),
        (
            shape(elements, r, n),
            shape(elements, r),
            shape(elements, r, n),
            shape(elements, r, n),
            shape(elements, r),
        ),
        out_near=False,
    )


def takes_split(elements, r, bs, cols):
    return elements == 2 and cols == 4 and r % 128 == 0 and r % bs == 0 and bs % 8 == 0


def per_device(blocks, pattern, drift, cov, cost, eta):
    elements, r, _ = cov.shape
    bs = blocks.shape[2] // 3
    if takes_split(elements, r, bs, lax.axis_size("col")):
        return per_device_split(blocks, pattern, drift, cov, cost, eta)
    return per_device_general(blocks, pattern, drift, cov, cost, eta)


def solution(mesh):
    return jax.shard_map(
        per_device,
        mesh=mesh,
        in_specs=(
            P("tm", "col", None),
            P(),
            P("tm", "col"),
            P("tm", "col", None),
            P("tm", "col", None),
            P("tm", "col"),
        ),
        out_specs=(
            P("tm", "col", None),
            P("tm", "col"),
            P("tm", "col", None),
            P("tm", "col", None),
            P("tm", "col"),
        ),
        check_vma=False,
    )
```

```python
import functools

import jax
import jax.numpy as jnp
from jax import lax
from jax.experimental import pallas as pl
from jax.experimental.pallas import tpu as pltpu
from jax.sharding import PartitionSpec as P


HIGH = lax.Precision.HIGHEST
F32 = jnp.float32
BF16 = jnp.bfloat16


def shifted(block, axis, distance):
    devices = range(lax.axis_size(axis))
    route = [(i - distance, i) for i in devices if i - distance in devices]
    return lax.ppermute(block, axis, route)


def product(form, left, right):
    return jnp.einsum(form, left, right, precision=HIGH)


def densify(row_blocks, row_ids, pattern, block_size):
    block_count = pattern.shape[0]
    row_block = row_ids // block_size
    chooser = (row_block[:, None] == jnp.arange(block_count, dtype=jnp.int32)[None, :]).astype(
        jnp.int32
    )
    columns = jnp.sum(chooser[:, :, None] * pattern[None, :, :], axis=1)
    matches = (
        columns[:, :, None] == jnp.arange(block_count, dtype=jnp.int32)[None, None, :]
    ).astype(jnp.float32)
    pieces = row_blocks.reshape(row_blocks.shape[:-1] + (3, 1, block_size))
    filled = jnp.sum(matches[:, :, :, None] * pieces, axis=-3)
    return filled.reshape(row_blocks.shape[:-1] + (block_count * block_size,))


def combine_rows(
    dyn_prev_full,
    dyn_own_full,
    dyn_own,
    drift_prev_full,
    drift_own,
    cov_prev,
    cov_own,
    cost_prev,
    cost_own,
    eta_prev,
    eta_own,
    first_row,
):
    height = dyn_own.shape[1]
    dyn_res = product("tij,tjk->tik", dyn_own, dyn_prev_full)
    drift_res = product("tij,tj->ti", dyn_own, drift_prev_full) + drift_own
    carried = eta_own + product("tij,tj->ti", cost_own, drift_prev_full)
    value_rows = product("tij,tjk->tik", cost_own, dyn_prev_full)
    prev_columns = lax.dynamic_slice_in_dim(dyn_prev_full, first_row, height, 2)
    cov_full, carried_full, value_full = (
        lax.all_gather(cov_prev, "col", axis=1, tiled=True),
        lax.all_gather(carried, "col", axis=1, tiled=True),
        lax.all_gather(value_rows, "col", axis=1, tiled=True),
    )
    cost_res = cost_prev + product("tki,tkj->tij", prev_columns, value_full)
    cov_res = (
        product("tik,tjk->tij", product("tij,tjk->tik", dyn_own, cov_full), dyn_own_full) + cov_own
    )
    eta_res = eta_prev + product("tki,tk->ti", prev_columns, carried_full)
    return (dyn_res, drift_res, cov_res, cost_res, eta_res)


def choose(flag, combined, kept):
    return tuple(jnp.where(flag, new, old) for new, old in zip(combined, kept))


def per_device_general(blocks, pattern, drift, cov, cost, eta):
    height = cov.shape[1]
    modes = cov.shape[2]
    block_size = blocks.shape[2] // 3
    first_row = lax.axis_index("col") * height
    own_ids = first_row + jnp.arange(height, dtype=jnp.int32)
    all_ids = jnp.arange(modes, dtype=jnp.int32)
    position = lax.axis_index("tm")
    dyn_own = densify(blocks, own_ids, pattern, block_size)
    received = shifted((blocks, drift, cov, cost, eta), "tm", 1)
    blocks_prev, blocks_own, drift_prev_full = (
        lax.all_gather(received[0], "col", axis=1, tiled=True),
        lax.all_gather(blocks, "col", axis=1, tiled=True),
        lax.all_gather(received[1], "col", axis=1, tiled=True),
    )
    merged = combine_rows(
        densify(blocks_prev, all_ids, pattern, block_size),
        densify(blocks_own, all_ids, pattern, block_size),
        dyn_own,
        drift_prev_full,
        drift,
        received[2],
        cov,
        received[3],
        cost,
        received[4],
        eta,
        first_row,
    )
    current = choose(position >= 1, merged, (dyn_own, drift, cov, cost, eta))
    received = shifted(current, "tm", 2)
    dyn_prev_full = lax.all_gather(received[0], "col", axis=1, tiled=True)
    dyn_own_full = lax.all_gather(current[0], "col", axis=1, tiled=True)
    drift_prev_full = lax.all_gather(received[1], "col", axis=1, tiled=True)
    merged = combine_rows(
        dyn_prev_full,
        dyn_own_full,
        current[0],
        drift_prev_full,
        current[1],
        received[2],
        current[2],
        received[3],
        current[3],
        received[4],
        current[4],
        first_row,
    )
    return choose(position >= 2, merged, current)


def split(x):
    hi = x.astype(BF16)
    lo = (x - hi.astype(F32)).astype(BF16)
    return hi, lo


def dot(a, b):
    return jnp.dot(a, b, preferred_element_type=F32)


def dot3(ah, al, bh, bl):
    return dot(ah, bh) + (dot(ah, bl) + dot(al, bh))


def triangle(r):
    rows = lax.broadcasted_iota(jnp.int32, (r, r), 0)
    cols = lax.broadcasted_iota(jnp.int32, (r, r), 1)
    return rows, cols


def fold(first, second, r):
    rows, cols = triangle(r)
    return jnp.where(rows >= cols, first, second)


def diagonal(block, r):
    rows, cols = triangle(r)
    return jnp.sum(jnp.where(rows == cols, block, 0.0), axis=0, keepdims=True)


def unfold(folded, second_diag, r):
    rows, cols = triangle(r)
    turned = folded.T
    first = jnp.where(rows >= cols, folded, turned)
    second = jnp.where(rows < cols, folded, turned)
    second = jnp.where(rows == cols, jnp.broadcast_to(second_diag, (r, r)), second)
    return first, second


UPPER = ((0, 1), (0, 2), (0, 3), (1, 2), (1, 3), (2, 3))


def spread(packed, r, put, rows=(0, 1, 2, 3)):
    panel0, panel1, diags = packed[0:r], packed[r : 2 * r], packed[2 * r : 2 * r + 1]
    for at, (panel, pair) in enumerate(((panel0, (0, 1)), (panel1, (2, 3)))):
        if pair[0] in rows or pair[1] in rows:
            blocks = unfold(panel[:, 0:r], diags[:, at * r : (at + 1) * r], r)
            for i, block in zip(pair, blocks):
                if i in rows:
                    put(i, i, block)
    for at, (i, j) in enumerate(UPPER):
        panel = panel0 if at < 3 else panel1
        block = panel[:, (at % 3 + 1) * r : (at % 3 + 2) * r]
        if i in rows:
            put(i, j, block)
        if j in rows:
            put(j, i, block.T)


def column(row, r):
    rows, cols = triangle(r)
    pieces = []
    for at in range(row.shape[1] // r):
        piece = jnp.broadcast_to(row[:, at * r : (at + 1) * r], (r, r))
        pieces.append(jnp.sum(jnp.where(rows == cols, piece, 0.0), axis=1, keepdims=True))
    return jnp.concatenate(pieces, axis=0)


def row_times(row, matrix, r):
    return jnp.sum(column(row, r) * matrix, axis=0, keepdims=True)


def lanes(index, r):
    return pl.ds(pl.multiple_of(index * r, r), r)


def copy_all(pairs, sems):
    copies = [
        pltpu.make_async_copy(source, target, sems.at[i]) for i, (source, target) in enumerate(pairs)
    ]
    for copy in copies:
        copy.start()
    for copy in copies:
        copy.wait()


def send_kernel(
    scal, cov, cost, drift, eta, to_core, to_chip, to_far, panel, vecs, b_in, e_in, sems
):
    q, y, c = scal[0], scal[1], scal[2]
    r = to_far.shape[1]

    def load(mine, theirs):
        pairs = []
        for j in range(2, 4):
            source = mine.at[1 - y, :, lanes((q ^ 2) ^ j, r)]
            pairs.append((source, to_chip.at[pl.ds(0, r), pl.ds((j - 2) * r, r)]))
        pairs.append((theirs.at[1 - y, :, lanes(q, r)], to_far.at[pl.ds(0, r), :]))
        for j in range(1, 4):
            source = theirs.at[y, :, lanes((q ^ 1) ^ j, r)]
            pairs.append((source, to_core.at[pl.ds(0, r), pl.ds((j - 1) * r, r)]))
        for j in range(4):
            pairs.append((mine.at[y, :, lanes(q ^ j, r)], panel.at[:, pl.ds(j * r, r)]))
        pairs.append((drift, b_in))
        pairs.append((eta, e_in))
        copy_all(pairs, sems)

    @pl.when(c == 0)
    def _():
        load(cov, cost)

    @pl.when(c == 1)
    def _():
        load(cost, cov)

    b, e = b_in[pl.ds(y, 1), :], e_in[pl.ds(y, 1), :]
    vecs[...] = jnp.zeros(vecs.shape, F32)
    vecs[0:1, :] = b
    vecs[1:2, :] = e
    to_core[r : r + 8, :] = jnp.zeros((8, 3 * r), F32)
    to_core[r : r + 1, 0:r] = b
    to_core[r : r + 1, r : 2 * r] = e
    b, e = b_in[pl.ds(1 - y, 1), :], e_in[pl.ds(1 - y, 1), :]
    to_chip[r : r + 8, :] = jnp.zeros((8, 2 * r), F32)
    to_chip[r : r + 1, 0:r] = b
    to_chip[r : r + 1, r : 2 * r] = e
    to_far[r : r + 8, :] = jnp.zeros((8, r), F32)
    to_far[r : r + 1, :] = b
    to_far[r + 1 : r + 2, :] = e


def pack_near_kernel(panel, from_core, packed):
    r = panel.shape[0]
    packed[:, 0:r] = fold(panel[:, 0:r], from_core[0:r, 0:r], r)
    packed[:, r : 4 * r] = panel[:, r:]
    packed[:, 4 * r :] = from_core[0:r, r : 3 * r]


def pack_far_kernel(vecs, from_core, from_chip, from_far, packed):
    r = vecs.shape[1]
    k33 = from_far[0:r, :]
    packed[0:r, 0:r] = fold(from_chip[0:r, 0:r], k33, r)
    packed[0:r, r:] = from_chip[0:r, r : 2 * r]
    packed[r : r + 1, 0:r] = diagonal(from_core[0:r, 0:r], r)
    packed[r : r + 1, r:] = diagonal(k33, r)
    b = (
        vecs[0:1, :],
        from_core[r : r + 1, 0:r],
        from_chip[r : r + 1, 0:r],
        from_far[r : r + 1, :],
    )
    e = (
        vecs[1:2, :],
        from_core[r : r + 1, r : 2 * r],
        from_chip[r : r + 1, r : 2 * r],
        from_far[r + 1 : r + 2, :],
    )
    for j in range(4):
        at = slice(j % 2 * r, (j % 2 + 1) * r)
        packed[r + 1 + j // 2 : r + 2 + j // 2, at] = b[j]
        packed[r + 3 + j // 2 : r + 4 + j // 2, at] = e[j]
    packed[r + 5 : r + 8, :] = jnp.zeros((3, 2 * r), F32)


def far_row(packed, r, at):
    return jnp.concatenate(
        [packed[r + at : r + at + 1, :], packed[r + at + 1 : r + at + 2, :]], axis=1
    )


def pick_kernel(scal, turned, before, out):
    y = scal[1]
    height = turned.shape[1]
    out[0:height, :] = turned[1 - y]
    out[height:, :] = before[1 - y]


def halves_kernel(scal, turned, before, other, out):
    y = scal[1]
    height = turned.shape[1]
    out[0:height, :] = turned[y]
    out[height : 2 * height, :] = other[0:height, :]
    out[2 * height : 3 * height, :] = before[y]
    out[3 * height :, :] = other[height:, :]


def dense_turned(put, scal, pattern, own_half, core_half, flag, n, r, bs):
    q = scal[0]
    lane = lax.broadcasted_iota(jnp.int32, (bs, r), 1) // bs
    rows = lax.broadcasted_iota(jnp.int32, (bs, r), 0)
    cols = lax.broadcasted_iota(jnp.int32, (bs, r), 1)
    per = r // bs
    height = 3 * bs
    for j in range(4):
        half = own_half if j % 2 == 0 else core_half
        full = half[(j // 2) * height : (j // 2 + 1) * height, :]
        wanted = []
        for k in range(3):
            want = jnp.zeros((bs, r), jnp.int32)
            for h in range(per):
                block = pattern[(q ^ j) * per + h, k] ^ (q * per)
                want = jnp.where(lane == h, block, want)
            wanted.append(jnp.where(flag == 1, want, -1))
        for block in range(n // bs):
            if j * r <= block * bs < (j + 1) * r:
                value = jnp.where(
                    jnp.logical_and(rows + block * bs == cols + j * r, flag == 0), 1.0, 0.0
                )
            else:
                value = jnp.zeros((bs, r), F32)
            for k in range(3):
                piece = full[k * bs : (k + 1) * bs, :]
                value = value + jnp.where(wanted[k] == block, piece, 0.0)
            put(slice(block * bs, (block + 1) * bs), slice(j * r, (j + 1) * r), value)


def put_split(hi_ref, lo_ref, rows, cols, value):
    hi, lo = split(value)
    hi_ref[rows, cols] = hi
    lo_ref[rows, cols] = lo


def transpose_split(hi_ref, lo_ref, source, r):
    n = source.shape[0]
    for i in range(n // r):
        for j in range(n // r):
            put_split(
                hi_ref,
                lo_ref,
                slice(j * r, (j + 1) * r),
                slice(i * r, (i + 1) * r),
                source[i * r : (i + 1) * r, j * r : (j + 1) * r].T,
            )


def straight_split(hi_ref, lo_ref, source, r):
    n = source.shape[0]
    for i in range(n // r):
        put_split(
            hi_ref, lo_ref, slice(i * r, (i + 1) * r), slice(None), source[i * r : (i + 1) * r, :]
        )


def prepare_kernel(bs, scal, pattern, halves, core_halves, mh, ml, th, tl, dense):
    c, has1 = scal[2], scal[3]
    n = dense.shape[0]
    r = halves.shape[1]
    half = halves.shape[0] // 2
    first = c == 0
    own_half = jnp.where(first, halves[0:half, :], halves[half:, :])
    core_half = jnp.where(first, core_halves[0:half, :], core_halves[half:, :])
    flag = jnp.where(first, 1, has1)

    def put(row, col, value):
        dense[row, col] = value

    dense_turned(put, scal, pattern, own_half, core_half, flag, n, r, bs)

    @pl.when(first)
    def _():
        straight_split(mh, ml, dense, r)
        transpose_split(th, tl, dense, r)

    @pl.when(jnp.logical_not(first))
    def _():
        straight_split(th, tl, dense, r)
        transpose_split(mh, ml, dense, r)


def level1_kernel(
    scal, own_near, own_far, near, far, mh, ml, th, tl, out, full, xh, xl
):
    c = scal[2]
    r = own_near.shape[0]
    first = c == 0
    xn = jnp.where(first, near[...], own_near[...])
    xf = jnp.where(first, far[...], own_far[...])
    x = jnp.concatenate(
        [
            xn[:, 0 : 4 * r],
            jnp.concatenate([xf[0:r, 0:r], xn[:, 4 * r :], xf[0:r, r:]], axis=1),
            jnp.concatenate([xf[r : r + 1, :], xf[r : r + 1, :]], axis=1),
        ],
        axis=0,
    )

    def put(i, j, block):
        full[i * r : (i + 1) * r, j * r : (j + 1) * r] = block
        put_split(xh, xl, slice(i * r, (i + 1) * r), slice(j * r, (j + 1) * r), block)

    spread(x, r, put)
    b_before, b_own = far_row(far, r, 1), far_row(own_far, r, 1)
    e_before, e_own = far_row(far, r, 3), far_row(own_far, r, 3)
    carried = jnp.where(first, b_before, e_own + row_times(b_before, full[...], r))
    vec = jnp.where(first, b_own, e_before) + row_times(
        carried, mh[...].astype(F32) + ml[...].astype(F32), r
    )
    u = dot3(xh[...], xl[...], mh[...], ml[...])
    uh, ul = split(u)
    top = dot3(th[0 : 2 * r, :], tl[0 : 2 * r, :], uh, ul)
    low = dot3(th[2 * r :, :], tl[2 * r :, :], uh[:, 2 * r :], ul[:, 2 * r :])
    dn = jnp.where(first, own_near[...], near[...])
    df = jnp.where(first, own_far[...], far[...])
    z11 = top[r : 2 * r, r : 2 * r]
    z33 = low[r : 2 * r, r : 2 * r]
    out[0:r, 0:r] = fold(top[0:r, 0:r], z11, r) + dn[:, 0:r]
    out[0:r, r:] = top[0:r, r:] + dn[:, r : 4 * r]
    out[r : 2 * r, 0:r] = fold(low[0:r, 0:r], z33, r) + df[0:r, 0:r]
    out[r : 2 * r, r : 3 * r] = top[r : 2 * r, 2 * r :] + dn[:, 4 * r :]
    out[r : 2 * r, 3 * r :] = low[0:r, r : 2 * r] + df[0:r, r:]
    base = 2 * r
    out[base : base + 1, 0:r] = diagonal(z11, r) + df[r : r + 1, 0:r]
    out[base : base + 1, r : 2 * r] = diagonal(z33, r) + df[r : r + 1, r:]
    out[base : base + 1, 2 * r :] = jnp.zeros((1, 2 * r), F32)
    out[base + 1 : base + 2, :] = b_own
    out[base + 2 : base + 3, :] = vec
    out[base + 3 : base + 4, :] = b_before
    out[base + 4 : base + 8, :] = jnp.zeros((4, 4 * r), F32)


def early_kernel(bs, scal, pattern, halves, core_halves, a0h, a0l, a1h, a1l, t):
    n = a0h.shape[0]
    r = halves.shape[1]
    half = halves.shape[0] // 2
    for at, flag, hi, lo in ((0, 1, a0h, a0l), (1, scal[3], a1h, a1l)):
        rows = slice(at * half, (at + 1) * half)
        put = functools.partial(put_split, hi, lo)
        dense_turned(put, scal, pattern, halves[rows, :], core_halves[rows, :], flag, n, r, bs)

    def wanted(ref):
        return jnp.concatenate([ref[:, 0:r], ref[:, 2 * r : 3 * r]], axis=1)

    t[...] = dot3(a1h[...], a1l[...], wanted(a0h), wanted(a0l))


def dynamics_kernel(
    bs,
    scal,
    pattern,
    halves,
    core_halves,
    a0h,
    a0l,
    a1h,
    a1l,
    t,
    dyn_own,
    dyn_send,
    mh,
    ml,
    th,
    tl,
    a2,
    a2h,
    a2l,
    a3h,
    a3l,
    product_ref,
):
    q, c = scal[0], scal[2]
    n = a0h.shape[0]
    r = halves.shape[1]
    half = halves.shape[0] // 2
    first = c == 0

    def put2(row, col, value):
        put_split(a2h, a2l, row, col, value)
        a2[row, col] = value

    def put3(row, col, value):
        put_split(a3h, a3l, row, col, value)

    for at, flag, put in ((0, scal[4], put2), (1, scal[5], put3)):
        rows = slice(at * half, (at + 1) * half)
        dense_turned(put, scal, pattern, halves[rows, :], core_halves[rows, :], flag, n, r, bs)
    rows = dot3(a2h[...], a2l[...], *split(t[...]))
    rows = dot3(a3h[...], a3l[...], *split(rows))
    for j in range(4):
        at = lanes(q ^ j, r)
        dyn_own[:, at] = rows[j * r : (j + 1) * r, 0:r].T
        dyn_send[:, at] = rows[j * r : (j + 1) * r, r : 2 * r].T

    @pl.when(first)
    def _():
        product_ref[...] = dot3(a1h[...], a1l[...], a0h[...], a0l[...])
        straight_split(mh, ml, product_ref, r)
        transpose_split(th, tl, product_ref, r)

    @pl.when(jnp.logical_not(first))
    def _():
        product_ref[...] = dot3(a3h[...], a3l[...], a2h[...], a2l[...])
        straight_split(th, tl, product_ref, r)
        transpose_split(mh, ml, product_ref, r)


def ahead_kernel(scal, own, mh, ml, th, tl, full, z, xh, xl):
    r = own.shape[1] // 4

    def put(i, j, block):
        full[i * r : (i + 1) * r, j * r : (j + 1) * r] = block

    spread(own, r, put)

    @pl.when(scal[2] == 1)
    def _():
        straight_split(xh, xl, full, r)
        u = dot3(xh[...], xl[...], mh[...], ml[...])
        z[...] = dot3(th[...], tl[...], *split(u))


def put_rows(ref, value, q, r):
    for j in range(4):
        ref[lanes(q ^ j, r), :] = value[:, j * r : (j + 1) * r]


def level2_kernel(
    scal,
    own,
    earlier,
    mh,
    ml,
    th,
    tl,
    a2,
    full,
    z,
    to_chip,
    to_far,
    uh,
    ul,
    vec,
    xh,
    xl,
    rest,
):
    q, c = scal[0], scal[2]
    r = own.shape[1] // 4
    n = 4 * r
    base = 2 * r
    b1 = earlier[base + 1 : base + 2, :] + row_times(earlier[base + 3 : base + 4, :], a2[...], r)

    @pl.when(c == 0)
    def _():
        def put(i, j, block):
            put_split(xh, xl, slice(i * r, (i + 1) * r), slice(j * r, (j + 1) * r), block)

        spread(earlier, r, put)
        hi, lo = split(dot3(xh[...], xl[...], mh[...], ml[...]))
        uh[...] = hi
        ul[...] = lo
        rest[...] = dot3(th[2 * r :, :], tl[2 * r :, :], hi, lo) + full[2 * r :, :]
        vec[0:1, :] = b1
        vec[1:2, :] = own[base + 2 : base + 3, :]

    @pl.when(c == 1)
    def _():
        def put(i, j, block):
            rows = slice((i - 2) * r, (i - 1) * r)
            cols = slice(j * r, (j + 1) * r)
            rest[rows, cols] = z[i * r : (i + 1) * r, cols] + block

        spread(earlier, r, put, rows=(2, 3))
        vec[0:1, :] = own[base + 2 : base + 3, :] + row_times(b1, full[...], r)
        vec[1:2, :] = earlier[base + 2 : base + 3, :]

    out = vec[1:2, :] + row_times(vec[0:1, :], mh[...].astype(F32) + ml[...].astype(F32), r)
    vec[0:1, :] = out
    for i, ref in ((2, to_chip), (3, to_far)):
        put_rows(ref, rest[(i - 2) * r : (i - 1) * r, :], q, r)
        ref[n : n + 8, :] = jnp.broadcast_to(out[:, i * r : (i + 1) * r], (8, r))


def rest_kernel(scal, earlier, th, tl, full, z, uh, ul, vec, keep, to_core, rest):
    q, c = scal[0], scal[2]
    r = earlier.shape[1] // 4
    n = 4 * r

    @pl.when(c == 0)
    def _():
        rest[...] = dot3(th[0 : 2 * r, :], tl[0 : 2 * r, :], uh[...], ul[...]) + full[0 : 2 * r, :]

    @pl.when(c == 1)
    def _():
        def put(i, j, block):
            rows = slice(i * r, (i + 1) * r)
            cols = slice(j * r, (j + 1) * r)
            rest[rows, cols] = z[rows, cols] + block

        spread(earlier, r, put, rows=(0, 1))

    for i, ref in ((0, keep), (1, to_core)):
        put_rows(ref, rest[i * r : (i + 1) * r, :], q, r)
        ref[n : n + 8, :] = jnp.broadcast_to(vec[0:1, i * r : (i + 1) * r], (8, r))


def panel_copies(panel, target, element, r):
    return [
        (panel.at[pl.ds(g * r, r), :], target.at[element, :, pl.ds(g * r, r)]) for g in range(4)
    ]


def fill_kernel(scal, keep, from_core, dyn_own, dyn_recv, dyn_out, cov_out, cost_out, sems):
    y, c = scal[1], scal[2]
    r = dyn_own.shape[0]
    dyn = [(dyn_own, dyn_out.at[y]), (dyn_recv, dyn_out.at[1 - y])]

    @pl.when(c == 0)
    def _():
        copy_all(
            dyn + panel_copies(keep, cov_out, y, r) + panel_copies(from_core, cost_out, y, r), sems
        )

    @pl.when(c == 1)
    def _():
        copy_all(
            dyn + panel_copies(from_core, cov_out, y, r) + panel_copies(keep, cost_out, y, r), sems
        )


def place_kernel(
    scal,
    cov_in,
    cost_in,
    keep,
    from_core,
    from_chip,
    from_far,
    cov_out,
    cost_out,
    drift_out,
    eta_out,
    sems,
):
    del cov_in, cost_in
    y, c = scal[1], scal[2]
    first = c == 0
    r = keep.shape[1]

    @pl.when(c == 0)
    def _():
        copy_all(
            panel_copies(from_chip, cov_out, 1 - y, r) + panel_copies(from_far, cost_out, 1 - y, r),
            sems,
        )

    @pl.when(c == 1)
    def _():
        copy_all(
            panel_copies(from_far, cov_out, 1 - y, r) + panel_copies(from_chip, cost_out, 1 - y, r),
            sems,
        )

    at = slice(4 * r, 4 * r + 1)
    for vector, one, two, three, four in (
        (drift_out, keep, from_core, from_chip, from_far),
        (eta_out, from_core, keep, from_far, from_chip),
    ):
        vector[pl.ds(y, 1), :] = jnp.where(first, one[at, :], two[at, :])
        vector[pl.ds(1 - y, 1), :] = jnp.where(first, three[at, :], four[at, :])


IN_SMEM, IN_HBM, IN_VMEM, IN_OUT = 0, 1, 2, 3


def kernel(body, operands, shapes, scratch=(), aliases=None):
    specs = {
        IN_SMEM: pl.BlockSpec(memory_space=pltpu.SMEM),
        IN_HBM: pl.BlockSpec(memory_space=pltpu.HBM),
        IN_VMEM: pl.BlockSpec(memory_space=pltpu.VMEM),
        IN_OUT: pl.BlockSpec(memory_space=pltpu.VMEM),
    }
    call = pl.pallas_call(
        body,
        in_specs=[specs[where] for where, _ in operands],
        out_specs=[specs[where] for where, _ in shapes],
        out_shape=[
            pltpu.VMEM(s.shape, s.dtype) if where == IN_VMEM else s for where, s in shapes
        ],
        scratch_shapes=list(scratch),
        input_output_aliases=aliases or {},
        compiler_params=pltpu.CompilerParams(vmem_limit_bytes=20 * 2**20),
    )
    kept = {IN_HBM: pltpu.HBM, IN_VMEM: pltpu.VMEM}
    return call(
        *(
            pltpu.with_memory_space_constraint(x, kept[where]) if where in kept else x
            for where, x in operands
        )
    )


def per_device_split(blocks, pattern, drift, cov, cost, eta):
    elements, r, n = cov.shape
    bs = blocks.shape[2] // 3
    tms, cols = lax.axis_size("tm"), lax.axis_size("col")
    position, q = lax.axis_index("tm"), lax.axis_index("col")

    def swap(value, bit):
        return lax.ppermute(value, "col", [(i, i ^ bit) for i in range(cols)])

    def later(value, distance):
        return lax.ppermute(value, "tm", [(i, i + distance) for i in range(tms - distance)])

    def flag(x):
        return x.astype(jnp.int32)

    scal = jnp.stack(
        [
            q,
            q >> 1,
            q & 1,
            flag(position >= 1),
            flag(position >= 2),
            flag(position >= 3),
        ]
    ).astype(jnp.int32)

    def smem(*arrays):
        return [(IN_SMEM, x) for x in arrays]

    def hbm(*arrays):
        return [(IN_HBM, x) for x in arrays]

    def vmem(*arrays):
        return [(IN_VMEM, x) for x in arrays]

    def shape(*dims):
        return jax.ShapeDtypeStruct(dims, F32)

    def half(*dims):
        return jax.ShapeDtypeStruct(dims, BF16)

    def square(dtype):
        return pltpu.VMEM((n, n), dtype)

    def sems(count):
        return pltpu.SemaphoreType.DMA((count,))

    turned = jnp.swapaxes(blocks, 1, 2)
    before = later(turned, 1)
    to_core, to_chip, to_far, panel, vecs = kernel(
        send_kernel,
        smem(scal) + hbm(cov, cost, drift, eta),
        vmem(shape(r + 8, 3 * r), shape(r + 8, 2 * r), shape(r + 8, r), shape(r, n), shape(8, r)),
        [pltpu.VMEM(drift.shape, F32), pltpu.VMEM(eta.shape, F32), sems(12)],
    )
    from_core = swap(to_core, 1)
    from_chip = swap(to_chip, 2)
    from_far = swap(to_far, 3)
    (own_near,) = kernel(pack_near_kernel, vmem(panel, from_core), vmem(shape(r, 6 * r)))
    near = later(own_near, 1)
    (own_far,) = kernel(
        pack_far_kernel, vmem(vecs, from_core, from_chip, from_far), vmem(shape(r + 8, 2 * r))
    )
    far = later(own_far, 1)
    (picked,) = kernel(pick_kernel, smem(scal) + vmem(turned, before), vmem(shape(6 * bs, r)))
    other = swap(picked, 2)
    (halves,) = kernel(
        halves_kernel, smem(scal) + vmem(turned, before, other), vmem(shape(12 * bs, r))
    )
    core_halves = swap(halves, 1)
    far_halves = later(halves, 2)
    m1 = kernel(
        functools.partial(prepare_kernel, bs),
        smem(scal, pattern) + vmem(halves, core_halves),
        vmem(*[half(n, n)] * 4),
        [square(F32)],
    )
    (level1,) = kernel(
        level1_kernel,
        smem(scal) + vmem(own_near, own_far, near, far, *m1),
        vmem(shape(2 * r + 8, n)),
        [square(F32)] + [square(BF16)] * 2,
    )
    earlier = later(level1, 2)
    a01 = kernel(
        functools.partial(early_kernel, bs),
        smem(scal, pattern) + vmem(halves, core_halves),
        vmem(*[half(n, n)] * 4, shape(n, 2 * r)),
    )
    far_core_halves = swap(far_halves, 1)
    dyn_own, dyn_send, *m2, a2 = kernel(
        functools.partial(dynamics_kernel, bs),
        smem(scal, pattern) + vmem(far_halves, far_core_halves, *a01),
        vmem(shape(r, n), shape(r, n), *[half(n, n)] * 4, shape(n, n)),
        [square(BF16)] * 4 + [square(F32)],
    )
    dyn_recv = swap(dyn_send, 2)
    full, z = kernel(
        ahead_kernel,
        smem(scal) + vmem(level1, *m2),
        vmem(shape(n, n), shape(n, n)),
        [square(BF16)] * 2,
    )
    to_chip, to_far, *u, vec = kernel(
        level2_kernel,
        smem(scal) + vmem(level1, earlier, *m2, a2, full, z),
        vmem(shape(n + 8, r), shape(n + 8, r), half(n, n), half(n, n), shape(8, n)),
        [square(BF16)] * 2 + [pltpu.VMEM((2 * r, n), F32)],
    )
    from_chip = swap(to_chip, 2)
    from_far = swap(to_far, 3)
    keep, to_core = kernel(
        rest_kernel,
        smem(scal) + vmem(earlier, *m2[2:], full, z, *u, vec),
        vmem(shape(n + 8, r), shape(n + 8, r)),
        [pltpu.VMEM((2 * r, n), F32)],
    )
    from_core = swap(to_core, 1)
    whole = shape(elements, r, n)
    dyn_out, cov_out, cost_out = kernel(
        fill_kernel,
        smem(scal) + vmem(keep, from_core, dyn_own, dyn_recv),
        hbm(whole, whole, whole),
        [sems(10)],
    )
    cov_out, cost_out, drift_out, eta_out = kernel(
        place_kernel,
        smem(scal)
        + hbm(cov_out, cost_out)
        + vmem(keep, from_core, from_chip, from_far),
        hbm(whole, whole) + [(IN_OUT, shape(elements, r))] * 2,
        [sems(8)],
        {1: 0, 2: 1},
    )
    return dyn_out, drift_out, cov_out, cost_out, eta_out


def takes_split(elements, r, bs, cols):
    return elements == 2 and cols == 4 and r % 128 == 0 and r % bs == 0 and bs % 8 == 0


def per_device(blocks, pattern, drift, cov, cost, eta):
    elements, r, _ = cov.shape
    bs = blocks.shape[2] // 3
    if takes_split(elements, r, bs, lax.axis_size("col")):
        return per_device_split(blocks, pattern, drift, cov, cost, eta)
    return per_device_general(blocks, pattern, drift, cov, cost, eta)


def solution(mesh):
    return jax.shard_map(
        per_device,
        mesh=mesh,
        in_specs=(
            P("tm", "col", None),
            P(),
            P("tm", "col"),
            P("tm", "col", None),
            P("tm", "col", None),
            P("tm", "col"),
        ),
        out_specs=(
            P("tm", "col", None),
            P("tm", "col"),
            P("tm", "col", None),
            P("tm", "col", None),
            P("tm", "col"),
        ),
        check_vma=False,
    )
```

```python
import functools

import jax
import jax.numpy as jnp
from jax import lax
from jax.experimental import pallas as pl
from jax.experimental.pallas import tpu as pltpu
from jax.sharding import PartitionSpec as P


HIGH = lax.Precision.HIGHEST
F32 = jnp.float32
BF16 = jnp.bfloat16


def shifted(block, axis, distance):
    devices = range(lax.axis_size(axis))
    route = [(i - distance, i) for i in devices if i - distance in devices]
    return lax.ppermute(block, axis, route)


def product(form, left, right):
    return jnp.einsum(form, left, right, precision=HIGH)


def densify(row_blocks, row_ids, pattern, block_size):
    block_count = pattern.shape[0]
    row_block = row_ids // block_size
    chooser = (row_block[:, None] == jnp.arange(block_count, dtype=jnp.int32)[None, :]).astype(
        jnp.int32
    )
    columns = jnp.sum(chooser[:, :, None] * pattern[None, :, :], axis=1)
    matches = (
        columns[:, :, None] == jnp.arange(block_count, dtype=jnp.int32)[None, None, :]
    ).astype(jnp.float32)
    pieces = row_blocks.reshape(row_blocks.shape[:-1] + (3, 1, block_size))
    filled = jnp.sum(matches[:, :, :, None] * pieces, axis=-3)
    return filled.reshape(row_blocks.shape[:-1] + (block_count * block_size,))


def combine_rows(
    dyn_prev_full,
    dyn_own_full,
    dyn_own,
    drift_prev_full,
    drift_own,
    cov_prev,
    cov_own,
    cost_prev,
    cost_own,
    eta_prev,
    eta_own,
    first_row,
):
    height = dyn_own.shape[1]
    dyn_res = product("tij,tjk->tik", dyn_own, dyn_prev_full)
    drift_res = product("tij,tj->ti", dyn_own, drift_prev_full) + drift_own
    carried = eta_own + product("tij,tj->ti", cost_own, drift_prev_full)
    value_rows = product("tij,tjk->tik", cost_own, dyn_prev_full)
    prev_columns = lax.dynamic_slice_in_dim(dyn_prev_full, first_row, height, 2)
    cov_full, carried_full, value_full = (
        lax.all_gather(cov_prev, "col", axis=1, tiled=True),
        lax.all_gather(carried, "col", axis=1, tiled=True),
        lax.all_gather(value_rows, "col", axis=1, tiled=True),
    )
    cost_res = cost_prev + product("tki,tkj->tij", prev_columns, value_full)
    cov_res = (
        product("tik,tjk->tij", product("tij,tjk->tik", dyn_own, cov_full), dyn_own_full) + cov_own
    )
    eta_res = eta_prev + product("tki,tk->ti", prev_columns, carried_full)
    return (dyn_res, drift_res, cov_res, cost_res, eta_res)


def choose(flag, combined, kept):
    return tuple(jnp.where(flag, new, old) for new, old in zip(combined, kept))


def per_device_general(blocks, pattern, drift, cov, cost, eta):
    height = cov.shape[1]
    modes = cov.shape[2]
    block_size = blocks.shape[2] // 3
    first_row = lax.axis_index("col") * height
    own_ids = first_row + jnp.arange(height, dtype=jnp.int32)
    all_ids = jnp.arange(modes, dtype=jnp.int32)
    position = lax.axis_index("tm")
    dyn_own = densify(blocks, own_ids, pattern, block_size)
    received = shifted((blocks, drift, cov, cost, eta), "tm", 1)
    blocks_prev, blocks_own, drift_prev_full = (
        lax.all_gather(received[0], "col", axis=1, tiled=True),
        lax.all_gather(blocks, "col", axis=1, tiled=True),
        lax.all_gather(received[1], "col", axis=1, tiled=True),
    )
    merged = combine_rows(
        densify(blocks_prev, all_ids, pattern, block_size),
        densify(blocks_own, all_ids, pattern, block_size),
        dyn_own,
        drift_prev_full,
        drift,
        received[2],
        cov,
        received[3],
        cost,
        received[4],
        eta,
        first_row,
    )
    current = choose(position >= 1, merged, (dyn_own, drift, cov, cost, eta))
    received = shifted(current, "tm", 2)
    dyn_prev_full = lax.all_gather(received[0], "col", axis=1, tiled=True)
    dyn_own_full = lax.all_gather(current[0], "col", axis=1, tiled=True)
    drift_prev_full = lax.all_gather(received[1], "col", axis=1, tiled=True)
    merged = combine_rows(
        dyn_prev_full,
        dyn_own_full,
        current[0],
        drift_prev_full,
        current[1],
        received[2],
        current[2],
        received[3],
        current[3],
        received[4],
        current[4],
        first_row,
    )
    return choose(position >= 2, merged, current)


def split(x):
    hi = x.astype(BF16)
    lo = (x - hi.astype(F32)).astype(BF16)
    return hi, lo


def dot(a, b):
    return jnp.dot(a, b, preferred_element_type=F32)


def dot3(ah, al, bh, bl):
    return dot(ah, bh) + (dot(ah, bl) + dot(al, bh))


def triangle(r):
    rows = lax.broadcasted_iota(jnp.int32, (r, r), 0)
    cols = lax.broadcasted_iota(jnp.int32, (r, r), 1)
    return rows, cols


def fold(first, second, r):
    rows, cols = triangle(r)
    return jnp.where(rows >= cols, first, second)


def diagonal(block, r):
    rows, cols = triangle(r)
    return jnp.sum(jnp.where(rows == cols, block, 0.0), axis=0, keepdims=True)


def unfold(folded, second_diag, r):
    rows, cols = triangle(r)
    turned = folded.T
    first = jnp.where(rows >= cols, folded, turned)
    second = jnp.where(rows < cols, folded, turned)
    second = jnp.where(rows == cols, jnp.broadcast_to(second_diag, (r, r)), second)
    return first, second


UPPER = ((0, 1), (0, 2), (0, 3), (1, 2), (1, 3), (2, 3))


def spread(packed, r, put, rows=(0, 1, 2, 3)):
    panel0, panel1, diags = packed[0:r], packed[r : 2 * r], packed[2 * r : 2 * r + 1]
    for at, (panel, pair) in enumerate(((panel0, (0, 1)), (panel1, (2, 3)))):
        if pair[0] in rows or pair[1] in rows:
            blocks = unfold(panel[:, 0:r], diags[:, at * r : (at + 1) * r], r)
            for i, block in zip(pair, blocks):
                if i in rows:
                    put(i, i, block)
    for at, (i, j) in enumerate(UPPER):
        panel = panel0 if at < 3 else panel1
        block = panel[:, (at % 3 + 1) * r : (at % 3 + 2) * r]
        if i in rows:
            put(i, j, block)
        if j in rows:
            put(j, i, block.T)


def column(row, r):
    rows, cols = triangle(r)
    pieces = []
    for at in range(row.shape[1] // r):
        piece = jnp.broadcast_to(row[:, at * r : (at + 1) * r], (r, r))
        pieces.append(jnp.sum(jnp.where(rows == cols, piece, 0.0), axis=1, keepdims=True))
    return jnp.concatenate(pieces, axis=0)


def row_times(row, matrix, r):
    return jnp.sum(column(row, r) * matrix, axis=0, keepdims=True)


def place_of():
    q = lax.axis_index("col")
    return q, q >> 1, q & 1


def has(distance):
    return (lax.axis_index("tm") >= distance).astype(jnp.int32)


def lanes(index, r):
    return pl.ds(pl.multiple_of(index * r, r), r)


def copy_all(pairs, sems):
    copies = [
        pltpu.make_async_copy(source, target, sems.at[i]) for i, (source, target) in enumerate(pairs)
    ]
    for copy in copies:
        copy.start()
    for copy in copies:
        copy.wait()


def send_kernel(
    cov, cost, drift, eta, to_core, to_chip, to_far, panel, vecs, b_in, e_in, sems
):
    q, y, c = place_of()
    r = to_far.shape[1]

    def load(mine, theirs):
        pairs = []
        for j in range(2, 4):
            source = mine.at[1 - y, :, lanes((q ^ 2) ^ j, r)]
            pairs.append((source, to_chip.at[pl.ds(0, r), pl.ds((j - 2) * r, r)]))
        pairs.append((theirs.at[1 - y, :, lanes(q, r)], to_far.at[pl.ds(0, r), :]))
        for j in range(1, 4):
            source = theirs.at[y, :, lanes((q ^ 1) ^ j, r)]
            pairs.append((source, to_core.at[pl.ds(0, r), pl.ds((j - 1) * r, r)]))
        for j in range(4):
            pairs.append((mine.at[y, :, lanes(q ^ j, r)], panel.at[:, pl.ds(j * r, r)]))
        pairs.append((drift, b_in))
        pairs.append((eta, e_in))
        copy_all(pairs, sems)

    @pl.when(c == 0)
    def _():
        load(cov, cost)

    @pl.when(c == 1)
    def _():
        load(cost, cov)

    b, e = b_in[pl.ds(y, 1), :], e_in[pl.ds(y, 1), :]
    vecs[...] = jnp.zeros(vecs.shape, F32)
    vecs[0:1, :] = b
    vecs[1:2, :] = e
    to_core[r : r + 8, :] = jnp.zeros((8, 3 * r), F32)
    to_core[r : r + 1, 0:r] = b
    to_core[r : r + 1, r : 2 * r] = e
    b, e = b_in[pl.ds(1 - y, 1), :], e_in[pl.ds(1 - y, 1), :]
    to_chip[r : r + 8, :] = jnp.zeros((8, 2 * r), F32)
    to_chip[r : r + 1, 0:r] = b
    to_chip[r : r + 1, r : 2 * r] = e
    to_far[r : r + 8, :] = jnp.zeros((8, r), F32)
    to_far[r : r + 1, :] = b
    to_far[r + 1 : r + 2, :] = e


def pack_near_kernel(panel, from_core, packed):
    r = panel.shape[0]
    packed[:, 0:r] = fold(panel[:, 0:r], from_core[0:r, 0:r], r)
    packed[:, r : 4 * r] = panel[:, r:]
    packed[:, 4 * r :] = from_core[0:r, r : 3 * r]


def pack_far_kernel(vecs, from_core, from_chip, from_far, packed):
    r = vecs.shape[1]
    k33 = from_far[0:r, :]
    packed[0:r, 0:r] = fold(from_chip[0:r, 0:r], k33, r)
    packed[0:r, r:] = from_chip[0:r, r : 2 * r]
    packed[r : r + 1, 0:r] = diagonal(from_core[0:r, 0:r], r)
    packed[r : r + 1, r:] = diagonal(k33, r)
    b = (
        vecs[0:1, :],
        from_core[r : r + 1, 0:r],
        from_chip[r : r + 1, 0:r],
        from_far[r : r + 1, :],
    )
    e = (
        vecs[1:2, :],
        from_core[r : r + 1, r : 2 * r],
        from_chip[r : r + 1, r : 2 * r],
        from_far[r + 1 : r + 2, :],
    )
    for j in range(4):
        at = slice(j % 2 * r, (j % 2 + 1) * r)
        packed[r + 1 + j // 2 : r + 2 + j // 2, at] = b[j]
        packed[r + 3 + j // 2 : r + 4 + j // 2, at] = e[j]
    packed[r + 5 : r + 8, :] = jnp.zeros((3, 2 * r), F32)


def far_row(packed, r, at):
    return jnp.concatenate(
        [packed[r + at : r + at + 1, :], packed[r + at + 1 : r + at + 2, :]], axis=1
    )


def pick_kernel(turned, before, out):
    y = place_of()[1]
    height = turned.shape[1]
    out[0:height, :] = turned[1 - y]
    out[height:, :] = before[1 - y]


def halves_kernel(turned, before, other, out):
    y = place_of()[1]
    height = turned.shape[1]
    out[0:height, :] = turned[y]
    out[height : 2 * height, :] = other[0:height, :]
    out[2 * height : 3 * height, :] = before[y]
    out[3 * height :, :] = other[height:, :]


def dense_turned(put, pattern, own_half, core_half, flag, n, r, bs):
    q = place_of()[0]
    lane = lax.broadcasted_iota(jnp.int32, (bs, r), 1) // bs
    rows = lax.broadcasted_iota(jnp.int32, (bs, r), 0)
    cols = lax.broadcasted_iota(jnp.int32, (bs, r), 1)
    per = r // bs
    height = 3 * bs
    for j in range(4):
        half = own_half if j % 2 == 0 else core_half
        full = half[(j // 2) * height : (j // 2 + 1) * height, :]
        wanted = []
        for k in range(3):
            want = jnp.zeros((bs, r), jnp.int32)
            for h in range(per):
                block = pattern[pl.ds((q ^ j) * per + h, 1), :][:, k : k + 1] ^ (q * per)
                want = jnp.where(lane == h, jnp.broadcast_to(block, (bs, r)), want)
            wanted.append(jnp.where(flag == 1, want, -1))
        for block in range(n // bs):
            if j * r <= block * bs < (j + 1) * r:
                value = jnp.where(
                    jnp.logical_and(rows + block * bs == cols + j * r, flag == 0), 1.0, 0.0
                )
            else:
                value = jnp.zeros((bs, r), F32)
            for k in range(3):
                piece = full[k * bs : (k + 1) * bs, :]
                value = value + jnp.where(wanted[k] == block, piece, 0.0)
            put(slice(block * bs, (block + 1) * bs), slice(j * r, (j + 1) * r), value)


def put_split(hi_ref, lo_ref, rows, cols, value):
    hi, lo = split(value)
    hi_ref[rows, cols] = hi
    lo_ref[rows, cols] = lo


def transpose_split(hi_ref, lo_ref, source, r):
    n = source.shape[0]
    for i in range(n // r):
        for j in range(n // r):
            put_split(
                hi_ref,
                lo_ref,
                slice(j * r, (j + 1) * r),
                slice(i * r, (i + 1) * r),
                source[i * r : (i + 1) * r, j * r : (j + 1) * r].T,
            )


def straight_split(hi_ref, lo_ref, source, r):
    n = source.shape[0]
    for i in range(n // r):
        put_split(
            hi_ref, lo_ref, slice(i * r, (i + 1) * r), slice(None), source[i * r : (i + 1) * r, :]
        )


def prepare_kernel(bs, pattern, halves, core_halves, mh, ml, th, tl, dense):
    c, has1 = place_of()[2], has(1)
    n = dense.shape[0]
    r = halves.shape[1]
    half = halves.shape[0] // 2
    first = c == 0
    own_half = jnp.where(first, halves[0:half, :], halves[half:, :])
    core_half = jnp.where(first, core_halves[0:half, :], core_halves[half:, :])
    flag = jnp.where(first, 1, has1)

    def put(row, col, value):
        dense[row, col] = value

    dense_turned(put, pattern, own_half, core_half, flag, n, r, bs)

    @pl.when(first)
    def _():
        straight_split(mh, ml, dense, r)
        transpose_split(th, tl, dense, r)

    @pl.when(jnp.logical_not(first))
    def _():
        straight_split(th, tl, dense, r)
        transpose_split(mh, ml, dense, r)


def level1_kernel(
    own_near, own_far, near, far, mh, ml, th, tl, out, full, xh, xl
):
    c = place_of()[2]
    r = own_near.shape[0]
    first = c == 0
    xn = jnp.where(first, near[...], own_near[...])
    xf = jnp.where(first, far[...], own_far[...])
    x = jnp.concatenate(
        [
            xn[:, 0 : 4 * r],
            jnp.concatenate([xf[0:r, 0:r], xn[:, 4 * r :], xf[0:r, r:]], axis=1),
            jnp.concatenate([xf[r : r + 1, :], xf[r : r + 1, :]], axis=1),
        ],
        axis=0,
    )

    def put(i, j, block):
        full[i * r : (i + 1) * r, j * r : (j + 1) * r] = block
        put_split(xh, xl, slice(i * r, (i + 1) * r), slice(j * r, (j + 1) * r), block)

    spread(x, r, put)
    b_before, b_own = far_row(far, r, 1), far_row(own_far, r, 1)
    e_before, e_own = far_row(far, r, 3), far_row(own_far, r, 3)
    carried = jnp.where(first, b_before, e_own + row_times(b_before, full[...], r))
    vec = jnp.where(first, b_own, e_before) + row_times(
        carried, mh[...].astype(F32) + ml[...].astype(F32), r
    )
    u = dot3(xh[...], xl[...], mh[...], ml[...])
    uh, ul = split(u)
    top = dot3(th[0 : 2 * r, :], tl[0 : 2 * r, :], uh, ul)
    low = dot3(th[2 * r :, :], tl[2 * r :, :], uh[:, 2 * r :], ul[:, 2 * r :])
    dn = jnp.where(first, own_near[...], near[...])
    df = jnp.where(first, own_far[...], far[...])
    z11 = top[r : 2 * r, r : 2 * r]
    z33 = low[r : 2 * r, r : 2 * r]
    out[0:r, 0:r] = fold(top[0:r, 0:r], z11, r) + dn[:, 0:r]
    out[0:r, r:] = top[0:r, r:] + dn[:, r : 4 * r]
    out[r : 2 * r, 0:r] = fold(low[0:r, 0:r], z33, r) + df[0:r, 0:r]
    out[r : 2 * r, r : 3 * r] = top[r : 2 * r, 2 * r :] + dn[:, 4 * r :]
    out[r : 2 * r, 3 * r :] = low[0:r, r : 2 * r] + df[0:r, r:]
    base = 2 * r
    out[base : base + 1, 0:r] = diagonal(z11, r) + df[r : r + 1, 0:r]
    out[base : base + 1, r : 2 * r] = diagonal(z33, r) + df[r : r + 1, r:]
    out[base : base + 1, 2 * r :] = jnp.zeros((1, 2 * r), F32)
    out[base + 1 : base + 2, :] = b_own
    out[base + 2 : base + 3, :] = vec
    out[base + 3 : base + 4, :] = b_before
    out[base + 4 : base + 8, :] = jnp.zeros((4, 4 * r), F32)


def early_kernel(bs, pattern, halves, core_halves, a0h, a0l, a1h, a1l, t):
    n = a0h.shape[0]
    r = halves.shape[1]
    half = halves.shape[0] // 2
    for at, flag, hi, lo in ((0, 1, a0h, a0l), (1, has(1), a1h, a1l)):
        rows = slice(at * half, (at + 1) * half)
        put = functools.partial(put_split, hi, lo)
        dense_turned(put, pattern, halves[rows, :], core_halves[rows, :], flag, n, r, bs)

    def wanted(ref):
        return jnp.concatenate([ref[:, 0:r], ref[:, 2 * r : 3 * r]], axis=1)

    t[...] = dot3(a1h[...], a1l[...], wanted(a0h), wanted(a0l))


def dynamics_kernel(
    bs,
    pattern,
    halves,
    core_halves,
    a0h,
    a0l,
    a1h,
    a1l,
    t,
    dyn_own,
    dyn_send,
    mh,
    ml,
    th,
    tl,
    a2,
    a2h,
    a2l,
    a3h,
    a3l,
    product_ref,
):
    q, _, c = place_of()
    n = a0h.shape[0]
    r = halves.shape[1]
    half = halves.shape[0] // 2
    first = c == 0

    def put2(row, col, value):
        put_split(a2h, a2l, row, col, value)
        a2[row, col] = value

    def put3(row, col, value):
        put_split(a3h, a3l, row, col, value)

    for at, flag, put in ((0, has(2), put2), (1, has(3), put3)):
        rows = slice(at * half, (at + 1) * half)
        dense_turned(put, pattern, halves[rows, :], core_halves[rows, :], flag, n, r, bs)
    rows = dot3(a2h[...], a2l[...], *split(t[...]))
    rows = dot3(a3h[...], a3l[...], *split(rows))
    for j in range(4):
        at = lanes(q ^ j, r)
        dyn_own[:, at] = rows[j * r : (j + 1) * r, 0:r].T
        dyn_send[:, at] = rows[j * r : (j + 1) * r, r : 2 * r].T

    @pl.when(first)
    def _():
        product_ref[...] = dot3(a1h[...], a1l[...], a0h[...], a0l[...])
        straight_split(mh, ml, product_ref, r)
        transpose_split(th, tl, product_ref, r)

    @pl.when(jnp.logical_not(first))
    def _():
        product_ref[...] = dot3(a3h[...], a3l[...], a2h[...], a2l[...])
        straight_split(th, tl, product_ref, r)
        transpose_split(mh, ml, product_ref, r)


def ahead_kernel(own, mh, ml, th, tl, full, z, xh, xl):
    r = own.shape[1] // 4

    def put(i, j, block):
        full[i * r : (i + 1) * r, j * r : (j + 1) * r] = block

    spread(own, r, put)

    @pl.when(place_of()[2] == 1)
    def _():
        straight_split(xh, xl, full, r)
        u = dot3(xh[...], xl[...], mh[...], ml[...])
        z[...] = dot3(th[...], tl[...], *split(u))


def put_rows(ref, value, q, r):
    for j in range(4):
        ref[lanes(q ^ j, r), :] = value[:, j * r : (j + 1) * r]


def level2_kernel(own, earlier, mh, ml, th, tl, full, z, to_chip, to_far, uh, ul, xh, xl, rest):
    q, _, c = place_of()
    r = own.shape[1] // 4

    @pl.when(c == 0)
    def _():
        def put(i, j, block):
            put_split(xh, xl, slice(i * r, (i + 1) * r), slice(j * r, (j + 1) * r), block)

        spread(earlier, r, put)
        hi, lo = split(dot3(xh[...], xl[...], mh[...], ml[...]))
        uh[...] = hi
        ul[...] = lo
        rest[...] = dot3(th[2 * r :, :], tl[2 * r :, :], hi, lo) + full[2 * r :, :]

    @pl.when(c == 1)
    def _():
        def put(i, j, block):
            rows = slice((i - 2) * r, (i - 1) * r)
            cols = slice(j * r, (j + 1) * r)
            rest[rows, cols] = z[i * r : (i + 1) * r, cols] + block

        spread(earlier, r, put, rows=(2, 3))

    put_rows(to_chip, rest[0:r, :], q, r)
    put_rows(to_far, rest[r : 2 * r, :], q, r)


def rest_kernel(
    own, earlier, mh, ml, th, tl, a2, full, z, uh, ul, keep, to_core, short, vec, rest
):
    q, _, c = place_of()
    r = own.shape[1] // 4
    base = 2 * r
    b1 = earlier[base + 1 : base + 2, :] + row_times(earlier[base + 3 : base + 4, :], a2[...], r)

    @pl.when(c == 0)
    def _():
        rest[...] = dot3(th[0 : 2 * r, :], tl[0 : 2 * r, :], uh[...], ul[...]) + full[0 : 2 * r, :]
        vec[0:1, :] = b1
        vec[1:2, :] = own[base + 2 : base + 3, :]

    @pl.when(c == 1)
    def _():
        def put(i, j, block):
            rows = slice(i * r, (i + 1) * r)
            cols = slice(j * r, (j + 1) * r)
            rest[rows, cols] = z[rows, cols] + block

        spread(earlier, r, put, rows=(0, 1))
        vec[0:1, :] = own[base + 2 : base + 3, :] + row_times(b1, full[...], r)
        vec[1:2, :] = earlier[base + 2 : base + 3, :]

    out = vec[1:2, :] + row_times(vec[0:1, :], mh[...].astype(F32) + ml[...].astype(F32), r)
    put_rows(keep, rest[0:r, :], q, r)
    put_rows(to_core, rest[r : 2 * r, :], q, r)
    for i in range(4):
        short[i : i + 1, :] = out[:, i * r : (i + 1) * r]
    short[4:8, :] = jnp.zeros((4, r), F32)


def panel_copies(panel, target, element, r):
    return [
        (panel.at[pl.ds(g * r, r), :], target.at[element, :, pl.ds(g * r, r)]) for g in range(4)
    ]


def fill_kernel(keep, from_core, dyn_own, dyn_recv, dyn_out, cov_out, cost_out, sems):
    _, y, c = place_of()
    r = dyn_own.shape[0]
    dyn = [(dyn_own, dyn_out.at[y]), (dyn_recv, dyn_out.at[1 - y])]

    @pl.when(c == 0)
    def _():
        copy_all(
            dyn + panel_copies(keep, cov_out, y, r) + panel_copies(from_core, cost_out, y, r), sems
        )

    @pl.when(c == 1)
    def _():
        copy_all(
            dyn + panel_copies(from_core, cov_out, y, r) + panel_copies(keep, cost_out, y, r), sems
        )


def place_chip_kernel(
    cov_in,
    cost_in,
    short,
    core_short,
    chip_short,
    far_short,
    panel,
    cov_out,
    cost_out,
    drift_out,
    eta_out,
    lines,
    sems,
):
    del cov_in, cost_in
    _, y, c = place_of()
    first = c == 0
    r = short.shape[1]
    for at, (one, two, three, four) in enumerate(
        (
            (short[0:1, :], core_short[1:2, :], chip_short[2:3, :], far_short[3:4, :]),
            (core_short[1:2, :], short[0:1, :], far_short[3:4, :], chip_short[2:3, :]),
        )
    ):
        lines[at, pl.ds(y, 1), :] = jnp.where(first, one, two)
        lines[at, pl.ds(1 - y, 1), :] = jnp.where(first, three, four)
    vectors = [(lines.at[0], drift_out), (lines.at[1], eta_out)]

    @pl.when(first)
    def _():
        copy_all(vectors + panel_copies(panel, cov_out, 1 - y, r), sems)

    @pl.when(c == 1)
    def _():
        copy_all(vectors + panel_copies(panel, cost_out, 1 - y, r), sems)


def place_far_kernel(cov_in, cost_in, panel, cov_out, cost_out, sems):
    del cov_in, cost_in
    _, y, c = place_of()
    r = panel.shape[1]

    @pl.when(c == 0)
    def _():
        copy_all(panel_copies(panel, cost_out, 1 - y, r), sems)

    @pl.when(c == 1)
    def _():
        copy_all(panel_copies(panel, cov_out, 1 - y, r), sems)


IN_HBM, IN_VMEM = 0, 1


def kernel(body, operands, shapes, scratch=(), aliases=None):
    specs = {
        IN_HBM: pl.BlockSpec(memory_space=pltpu.HBM),
        IN_VMEM: pl.BlockSpec(memory_space=pltpu.VMEM),
    }
    call = pl.pallas_call(
        body,
        in_specs=[specs[where] for where, _ in operands],
        out_specs=[specs[where] for where, _ in shapes],
        out_shape=[
            pltpu.VMEM(s.shape, s.dtype) if where == IN_VMEM else s for where, s in shapes
        ],
        scratch_shapes=list(scratch),
        input_output_aliases=aliases or {},
        compiler_params=pltpu.CompilerParams(vmem_limit_bytes=20 * 2**20),
    )
    kept = {IN_HBM: pltpu.HBM, IN_VMEM: pltpu.VMEM}
    return call(
        *(
            pltpu.with_memory_space_constraint(x, kept[where]) if where in kept else x
            for where, x in operands
        )
    )


def per_device_split(blocks, pattern, drift, cov, cost, eta):
    elements, r, n = cov.shape
    bs = blocks.shape[2] // 3
    tms, cols = lax.axis_size("tm"), lax.axis_size("col")

    def swap(value, bit):
        return lax.ppermute(value, "col", [(i, i ^ bit) for i in range(cols)])

    def later(value, distance):
        return lax.ppermute(value, "tm", [(i, i + distance) for i in range(tms - distance)])

    def hbm(*arrays):
        return [(IN_HBM, x) for x in arrays]

    def vmem(*arrays):
        return [(IN_VMEM, x) for x in arrays]

    def shape(*dims):
        return jax.ShapeDtypeStruct(dims, F32)

    def half(*dims):
        return jax.ShapeDtypeStruct(dims, BF16)

    def square(dtype):
        return pltpu.VMEM((n, n), dtype)

    def sems(count):
        return pltpu.SemaphoreType.DMA((count,))

    turned = jnp.swapaxes(blocks, 1, 2)
    before = later(turned, 1)
    to_core, to_chip, to_far, panel, vecs = kernel(
        send_kernel,
        hbm(cov, cost, drift, eta),
        vmem(shape(r + 8, 3 * r), shape(r + 8, 2 * r), shape(r + 8, r), shape(r, n), shape(8, r)),
        [pltpu.VMEM(drift.shape, F32), pltpu.VMEM(eta.shape, F32), sems(12)],
    )
    from_core = swap(to_core, 1)
    from_chip = swap(to_chip, 2)
    from_far = swap(to_far, 3)
    (own_near,) = kernel(pack_near_kernel, vmem(panel, from_core), vmem(shape(r, 6 * r)))
    near = later(own_near, 1)
    (own_far,) = kernel(
        pack_far_kernel, vmem(vecs, from_core, from_chip, from_far), vmem(shape(r + 8, 2 * r))
    )
    far = later(own_far, 1)
    (picked,) = kernel(pick_kernel, vmem(turned, before), vmem(shape(6 * bs, r)))
    other = swap(picked, 2)
    (halves,) = kernel(halves_kernel, vmem(turned, before, other), vmem(shape(12 * bs, r)))
    core_halves = swap(halves, 1)
    far_halves = later(halves, 2)
    m1 = kernel(
        functools.partial(prepare_kernel, bs),
        vmem(pattern, halves, core_halves),
        vmem(*[half(n, n)] * 4),
        [square(F32)],
    )
    (level1,) = kernel(
        level1_kernel,
        vmem(own_near, own_far, near, far, *m1),
        vmem(shape(2 * r + 8, n)),
        [square(F32)] + [square(BF16)] * 2,
    )
    earlier = later(level1, 2)
    a01 = kernel(
        functools.partial(early_kernel, bs),
        vmem(pattern, halves, core_halves),
        vmem(*[half(n, n)] * 4, shape(n, 2 * r)),
    )
    far_core_halves = swap(far_halves, 1)
    dyn_own, dyn_send, *m2, a2 = kernel(
        functools.partial(dynamics_kernel, bs),
        vmem(pattern, far_halves, far_core_halves, *a01),
        vmem(shape(r, n), shape(r, n), *[half(n, n)] * 4, shape(n, n)),
        [square(BF16)] * 4 + [square(F32)],
    )
    dyn_recv = swap(dyn_send, 2)
    full, z = kernel(
        ahead_kernel, vmem(level1, *m2), vmem(shape(n, n), shape(n, n)), [square(BF16)] * 2
    )
    to_chip, to_far, *u = kernel(
        level2_kernel,
        vmem(level1, earlier, *m2, full, z),
        vmem(shape(n, r), shape(n, r), half(n, n), half(n, n)),
        [square(BF16)] * 2 + [pltpu.VMEM((2 * r, n), F32)],
    )
    from_chip = swap(to_chip, 2)
    from_far = swap(to_far, 3)
    keep, to_core, short = kernel(
        rest_kernel,
        vmem(level1, earlier, *m2, a2, full, z, *u),
        vmem(shape(n, r), shape(n, r), shape(8, r)),
        [pltpu.VMEM((8, n), F32), pltpu.VMEM((2 * r, n), F32)],
    )
    from_core = swap(to_core, 1)
    shorts = (short, swap(short, 1), swap(short, 2), swap(short, 3))
    whole, line = shape(elements, r, n), shape(elements, r)
    dyn_out, cov_out, cost_out = kernel(
        fill_kernel, vmem(keep, from_core, dyn_own, dyn_recv), hbm(whole, whole, whole), [sems(10)]
    )
    cov_out, cost_out, drift_out, eta_out = kernel(
        place_chip_kernel,
        hbm(cov_out, cost_out) + vmem(*shorts, from_chip),
        hbm(whole, whole, line, line),
        [pltpu.VMEM((2, elements, r), F32), sems(6)],
        {0: 0, 1: 1},
    )
    cov_out, cost_out = kernel(
        place_far_kernel,
        hbm(cov_out, cost_out) + vmem(from_far),
        hbm(whole, whole),
        [sems(4)],
        {0: 0, 1: 1},
    )
    return dyn_out, drift_out, cov_out, cost_out, eta_out


def takes_split(elements, r, bs, cols):
    return elements == 2 and cols == 4 and r % 128 == 0 and r % bs == 0 and bs % 8 == 0


def per_device(blocks, pattern, drift, cov, cost, eta):
    elements, r, _ = cov.shape
    bs = blocks.shape[2] // 3
    if takes_split(elements, r, bs, lax.axis_size("col")):
        return per_device_split(blocks, pattern, drift, cov, cost, eta)
    return per_device_general(blocks, pattern, drift, cov, cost, eta)


def solution(mesh):
    return jax.shard_map(
        per_device,
        mesh=mesh,
        in_specs=(
            P("tm", "col", None),
            P(),
            P("tm", "col"),
            P("tm", "col", None),
            P("tm", "col", None),
            P("tm", "col"),
        ),
        out_specs=(
            P("tm", "col", None),
            P("tm", "col"),
            P("tm", "col", None),
            P("tm", "col", None),
            P("tm", "col"),
        ),
        check_vma=False,
    )
```

```python
import functools

import jax
import jax.numpy as jnp
from jax import lax
from jax.experimental import pallas as pl
from jax.experimental.pallas import tpu as pltpu
from jax.sharding import PartitionSpec as P


HIGH = lax.Precision.HIGHEST
F32 = jnp.float32
BF16 = jnp.bfloat16


def shifted(block, axis, distance):
    devices = range(lax.axis_size(axis))
    route = [(i - distance, i) for i in devices if i - distance in devices]
    return lax.ppermute(block, axis, route)


def product(form, left, right):
    return jnp.einsum(form, left, right, precision=HIGH)


def densify(row_blocks, row_ids, pattern, block_size):
    block_count = pattern.shape[0]
    row_block = row_ids // block_size
    chooser = (row_block[:, None] == jnp.arange(block_count, dtype=jnp.int32)[None, :]).astype(
        jnp.int32
    )
    columns = jnp.sum(chooser[:, :, None] * pattern[None, :, :], axis=1)
    matches = (
        columns[:, :, None] == jnp.arange(block_count, dtype=jnp.int32)[None, None, :]
    ).astype(jnp.float32)
    pieces = row_blocks.reshape(row_blocks.shape[:-1] + (3, 1, block_size))
    filled = jnp.sum(matches[:, :, :, None] * pieces, axis=-3)
    return filled.reshape(row_blocks.shape[:-1] + (block_count * block_size,))


def combine_rows(
    dyn_prev_full,
    dyn_own_full,
    dyn_own,
    drift_prev_full,
    drift_own,
    cov_prev,
    cov_own,
    cost_prev,
    cost_own,
    eta_prev,
    eta_own,
    first_row,
):
    height = dyn_own.shape[1]
    dyn_res = product("tij,tjk->tik", dyn_own, dyn_prev_full)
    drift_res = product("tij,tj->ti", dyn_own, drift_prev_full) + drift_own
    carried = eta_own + product("tij,tj->ti", cost_own, drift_prev_full)
    value_rows = product("tij,tjk->tik", cost_own, dyn_prev_full)
    prev_columns = lax.dynamic_slice_in_dim(dyn_prev_full, first_row, height, 2)
    cov_full, carried_full, value_full = (
        lax.all_gather(cov_prev, "col", axis=1, tiled=True),
        lax.all_gather(carried, "col", axis=1, tiled=True),
        lax.all_gather(value_rows, "col", axis=1, tiled=True),
    )
    cost_res = cost_prev + product("tki,tkj->tij", prev_columns, value_full)
    cov_res = (
        product("tik,tjk->tij", product("tij,tjk->tik", dyn_own, cov_full), dyn_own_full) + cov_own
    )
    eta_res = eta_prev + product("tki,tk->ti", prev_columns, carried_full)
    return (dyn_res, drift_res, cov_res, cost_res, eta_res)


def choose(flag, combined, kept):
    return tuple(jnp.where(flag, new, old) for new, old in zip(combined, kept))


def per_device_general(blocks, pattern, drift, cov, cost, eta):
    height = cov.shape[1]
    modes = cov.shape[2]
    block_size = blocks.shape[2] // 3
    first_row = lax.axis_index("col") * height
    own_ids = first_row + jnp.arange(height, dtype=jnp.int32)
    all_ids = jnp.arange(modes, dtype=jnp.int32)
    position = lax.axis_index("tm")
    dyn_own = densify(blocks, own_ids, pattern, block_size)
    received = shifted((blocks, drift, cov, cost, eta), "tm", 1)
    blocks_prev, blocks_own, drift_prev_full = (
        lax.all_gather(received[0], "col", axis=1, tiled=True),
        lax.all_gather(blocks, "col", axis=1, tiled=True),
        lax.all_gather(received[1], "col", axis=1, tiled=True),
    )
    merged = combine_rows(
        densify(blocks_prev, all_ids, pattern, block_size),
        densify(blocks_own, all_ids, pattern, block_size),
        dyn_own,
        drift_prev_full,
        drift,
        received[2],
        cov,
        received[3],
        cost,
        received[4],
        eta,
        first_row,
    )
    current = choose(position >= 1, merged, (dyn_own, drift, cov, cost, eta))
    received = shifted(current, "tm", 2)
    dyn_prev_full = lax.all_gather(received[0], "col", axis=1, tiled=True)
    dyn_own_full = lax.all_gather(current[0], "col", axis=1, tiled=True)
    drift_prev_full = lax.all_gather(received[1], "col", axis=1, tiled=True)
    merged = combine_rows(
        dyn_prev_full,
        dyn_own_full,
        current[0],
        drift_prev_full,
        current[1],
        received[2],
        current[2],
        received[3],
        current[3],
        received[4],
        current[4],
        first_row,
    )
    return choose(position >= 2, merged, current)


def split(x):
    hi = x.astype(BF16)
    lo = (x - hi.astype(F32)).astype(BF16)
    return hi, lo


def dot(a, b):
    return jnp.dot(a, b, preferred_element_type=F32)


def dot3(ah, al, bh, bl):
    return dot(ah, bh) + (dot(ah, bl) + dot(al, bh))


def triangle(r):
    rows = lax.broadcasted_iota(jnp.int32, (r, r), 0)
    cols = lax.broadcasted_iota(jnp.int32, (r, r), 1)
    return rows, cols


def fold(first, second, r):
    rows, cols = triangle(r)
    return jnp.where(rows >= cols, first, second)


def diagonal(block, r):
    rows, cols = triangle(r)
    return jnp.sum(jnp.where(rows == cols, block, 0.0), axis=0, keepdims=True)


def unfold(folded, second_diag, r):
    rows, cols = triangle(r)
    turned = folded.T
    first = jnp.where(rows >= cols, folded, turned)
    second = jnp.where(rows < cols, folded, turned)
    second = jnp.where(rows == cols, jnp.broadcast_to(second_diag, (r, r)), second)
    return first, second


UPPER = ((0, 1), (0, 2), (0, 3), (1, 2), (1, 3), (2, 3))


def spread(packed, r, put, rows=(0, 1, 2, 3)):
    panel0, panel1, diags = packed[0:r], packed[r : 2 * r], packed[2 * r : 2 * r + 1]
    for at, (panel, pair) in enumerate(((panel0, (0, 1)), (panel1, (2, 3)))):
        if pair[0] in rows or pair[1] in rows:
            blocks = unfold(panel[:, 0:r], diags[:, at * r : (at + 1) * r], r)
            for i, block in zip(pair, blocks):
                if i in rows:
                    put(i, i, block)
    for at, (i, j) in enumerate(UPPER):
        panel = panel0 if at < 3 else panel1
        block = panel[:, (at % 3 + 1) * r : (at % 3 + 2) * r]
        if i in rows:
            put(i, j, block)
        if j in rows:
            put(j, i, block.T)


def column(row, r):
    rows, cols = triangle(r)
    pieces = []
    for at in range(row.shape[1] // r):
        piece = jnp.broadcast_to(row[:, at * r : (at + 1) * r], (r, r))
        pieces.append(jnp.sum(jnp.where(rows == cols, piece, 0.0), axis=1, keepdims=True))
    return jnp.concatenate(pieces, axis=0)


def row_times(row, matrix, r):
    return jnp.sum(column(row, r) * matrix, axis=0, keepdims=True)


def place_of():
    q = lax.axis_index("col")
    return q, q >> 1, q & 1


def has(distance):
    return (lax.axis_index("tm") >= distance).astype(jnp.int32)


def lanes(index, r):
    return pl.ds(pl.multiple_of(index * r, r), r)


def copy_all(pairs, sems):
    copies = [
        pltpu.make_async_copy(source, target, sems.at[i]) for i, (source, target) in enumerate(pairs)
    ]
    for copy in copies:
        copy.start()
    for copy in copies:
        copy.wait()


def send_kernel(
    cov, cost, drift, eta, to_core, to_chip, to_far, panel, vecs, b_in, e_in, sems
):
    q, y, c = place_of()
    r = to_far.shape[1]

    def load(mine, theirs):
        pairs = []
        for j in range(2, 4):
            source = mine.at[1 - y, :, lanes((q ^ 2) ^ j, r)]
            pairs.append((source, to_chip.at[pl.ds(0, r), pl.ds((j - 2) * r, r)]))
        pairs.append((theirs.at[1 - y, :, lanes(q, r)], to_far.at[pl.ds(0, r), :]))
        for j in range(1, 4):
            source = theirs.at[y, :, lanes((q ^ 1) ^ j, r)]
            pairs.append((source, to_core.at[pl.ds(0, r), pl.ds((j - 1) * r, r)]))
        for j in range(4):
            pairs.append((mine.at[y, :, lanes(q ^ j, r)], panel.at[:, pl.ds(j * r, r)]))
        pairs.append((drift, b_in))
        pairs.append((eta, e_in))
        copy_all(pairs, sems)

    @pl.when(c == 0)
    def _():
        load(cov, cost)

    @pl.when(c == 1)
    def _():
        load(cost, cov)

    b, e = b_in[pl.ds(y, 1), :], e_in[pl.ds(y, 1), :]
    vecs[...] = jnp.zeros(vecs.shape, F32)
    vecs[0:1, :] = b
    vecs[1:2, :] = e
    to_core[r : r + 8, :] = jnp.zeros((8, 3 * r), F32)
    to_core[r : r + 1, 0:r] = b
    to_core[r : r + 1, r : 2 * r] = e
    b, e = b_in[pl.ds(1 - y, 1), :], e_in[pl.ds(1 - y, 1), :]
    to_chip[r : r + 8, :] = jnp.zeros((8, 2 * r), F32)
    to_chip[r : r + 1, 0:r] = b
    to_chip[r : r + 1, r : 2 * r] = e
    to_far[r : r + 8, :] = jnp.zeros((8, r), F32)
    to_far[r : r + 1, :] = b
    to_far[r + 1 : r + 2, :] = e


def pack_near_kernel(panel, from_core, packed):
    r = panel.shape[0]
    packed[:, 0:r] = fold(panel[:, 0:r], from_core[0:r, 0:r], r)
    packed[:, r : 4 * r] = panel[:, r:]
    packed[:, 4 * r :] = from_core[0:r, r : 3 * r]


def pack_far_kernel(vecs, from_core, from_chip, from_far, packed):
    r = vecs.shape[1]
    k33 = from_far[0:r, :]
    packed[0:r, 0:r] = fold(from_chip[0:r, 0:r], k33, r)
    packed[0:r, r:] = from_chip[0:r, r : 2 * r]
    packed[r : r + 1, 0:r] = diagonal(from_core[0:r, 0:r], r)
    packed[r : r + 1, r:] = diagonal(k33, r)
    b = (
        vecs[0:1, :],
        from_core[r : r + 1, 0:r],
        from_chip[r : r + 1, 0:r],
        from_far[r : r + 1, :],
    )
    e = (
        vecs[1:2, :],
        from_core[r : r + 1, r : 2 * r],
        from_chip[r : r + 1, r : 2 * r],
        from_far[r + 1 : r + 2, :],
    )
    for j in range(4):
        at = slice(j % 2 * r, (j % 2 + 1) * r)
        packed[r + 1 + j // 2 : r + 2 + j // 2, at] = b[j]
        packed[r + 3 + j // 2 : r + 4 + j // 2, at] = e[j]
    packed[r + 5 : r + 8, :] = jnp.zeros((3, 2 * r), F32)


def far_row(packed, r, at):
    return jnp.concatenate(
        [packed[r + at : r + at + 1, :], packed[r + at + 1 : r + at + 2, :]], axis=1
    )


def pick_kernel(turned, before, out):
    y = place_of()[1]
    height = turned.shape[1]
    out[0:height, :] = turned[1 - y]
    out[height:, :] = before[1 - y]


def halves_kernel(turned, before, other, out):
    y = place_of()[1]
    height = turned.shape[1]
    out[0:height, :] = turned[y]
    out[height : 2 * height, :] = other[0:height, :]
    out[2 * height : 3 * height, :] = before[y]
    out[3 * height :, :] = other[height:, :]


def dense_turned(put, pattern, own_half, core_half, flag, n, r, bs):
    q = place_of()[0]
    lane = lax.broadcasted_iota(jnp.int32, (bs, r), 1) // bs
    rows = lax.broadcasted_iota(jnp.int32, (bs, r), 0)
    cols = lax.broadcasted_iota(jnp.int32, (bs, r), 1)
    per = r // bs
    height = 3 * bs
    for j in range(4):
        half = own_half if j % 2 == 0 else core_half
        full = half[(j // 2) * height : (j // 2 + 1) * height, :]
        wanted = []
        for k in range(3):
            want = jnp.zeros((bs, r), jnp.int32)
            for h in range(per):
                block = pattern[pl.ds((q ^ j) * per + h, 1), :][:, k : k + 1] ^ (q * per)
                want = jnp.where(lane == h, jnp.broadcast_to(block, (bs, r)), want)
            wanted.append(jnp.where(flag == 1, want, -1))
        for block in range(n // bs):
            if j * r <= block * bs < (j + 1) * r:
                value = jnp.where(
                    jnp.logical_and(rows + block * bs == cols + j * r, flag == 0), 1.0, 0.0
                )
            else:
                value = jnp.zeros((bs, r), F32)
            for k in range(3):
                piece = full[k * bs : (k + 1) * bs, :]
                value = value + jnp.where(wanted[k] == block, piece, 0.0)
            put(slice(block * bs, (block + 1) * bs), slice(j * r, (j + 1) * r), value)


def put_split(hi_ref, lo_ref, rows, cols, value):
    hi, lo = split(value)
    hi_ref[rows, cols] = hi
    lo_ref[rows, cols] = lo


def transpose_split(hi_ref, lo_ref, source, r):
    n = source.shape[0]
    for i in range(n // r):
        for j in range(n // r):
            put_split(
                hi_ref,
                lo_ref,
                slice(j * r, (j + 1) * r),
                slice(i * r, (i + 1) * r),
                source[i * r : (i + 1) * r, j * r : (j + 1) * r].T,
            )


def straight_split(hi_ref, lo_ref, source, r):
    n = source.shape[0]
    for i in range(n // r):
        put_split(
            hi_ref, lo_ref, slice(i * r, (i + 1) * r), slice(None), source[i * r : (i + 1) * r, :]
        )


def prepare_kernel(bs, pattern, halves, core_halves, mh, ml, th, tl, dense):
    c, has1 = place_of()[2], has(1)
    n = dense.shape[0]
    r = halves.shape[1]
    half = halves.shape[0] // 2
    first = c == 0
    own_half = jnp.where(first, halves[0:half, :], halves[half:, :])
    core_half = jnp.where(first, core_halves[0:half, :], core_halves[half:, :])
    flag = jnp.where(first, 1, has1)

    def put(row, col, value):
        dense[row, col] = value

    dense_turned(put, pattern, own_half, core_half, flag, n, r, bs)

    @pl.when(first)
    def _():
        straight_split(mh, ml, dense, r)
        transpose_split(th, tl, dense, r)

    @pl.when(jnp.logical_not(first))
    def _():
        straight_split(th, tl, dense, r)
        transpose_split(mh, ml, dense, r)


def level1_kernel(
    own_near, own_far, near, far, mh, ml, th, tl, out, full, xh, xl
):
    c = place_of()[2]
    r = own_near.shape[0]
    first = c == 0
    xn = jnp.where(first, near[...], own_near[...])
    xf = jnp.where(first, far[...], own_far[...])
    x = jnp.concatenate(
        [
            xn[:, 0 : 4 * r],
            jnp.concatenate([xf[0:r, 0:r], xn[:, 4 * r :], xf[0:r, r:]], axis=1),
            jnp.concatenate([xf[r : r + 1, :], xf[r : r + 1, :]], axis=1),
        ],
        axis=0,
    )

    def put(i, j, block):
        full[i * r : (i + 1) * r, j * r : (j + 1) * r] = block
        put_split(xh, xl, slice(i * r, (i + 1) * r), slice(j * r, (j + 1) * r), block)

    spread(x, r, put)
    b_before, b_own = far_row(far, r, 1), far_row(own_far, r, 1)
    e_before, e_own = far_row(far, r, 3), far_row(own_far, r, 3)
    carried = jnp.where(first, b_before, e_own + row_times(b_before, full[...], r))
    vec = jnp.where(first, b_own, e_before) + row_times(
        carried, mh[...].astype(F32) + ml[...].astype(F32), r
    )
    u = dot3(xh[...], xl[...], mh[...], ml[...])
    uh, ul = split(u)
    top = dot3(th[0 : 2 * r, :], tl[0 : 2 * r, :], uh, ul)
    low = dot3(th[2 * r :, :], tl[2 * r :, :], uh[:, 2 * r :], ul[:, 2 * r :])
    dn = jnp.where(first, own_near[...], near[...])
    df = jnp.where(first, own_far[...], far[...])
    z11 = top[r : 2 * r, r : 2 * r]
    z33 = low[r : 2 * r, r : 2 * r]
    out[0:r, 0:r] = fold(top[0:r, 0:r], z11, r) + dn[:, 0:r]
    out[0:r, r:] = top[0:r, r:] + dn[:, r : 4 * r]
    out[r : 2 * r, 0:r] = fold(low[0:r, 0:r], z33, r) + df[0:r, 0:r]
    out[r : 2 * r, r : 3 * r] = top[r : 2 * r, 2 * r :] + dn[:, 4 * r :]
    out[r : 2 * r, 3 * r :] = low[0:r, r : 2 * r] + df[0:r, r:]
    base = 2 * r
    out[base : base + 1, 0:r] = diagonal(z11, r) + df[r : r + 1, 0:r]
    out[base : base + 1, r : 2 * r] = diagonal(z33, r) + df[r : r + 1, r:]
    out[base : base + 1, 2 * r :] = jnp.zeros((1, 2 * r), F32)
    out[base + 1 : base + 2, :] = b_own
    out[base + 2 : base + 3, :] = vec
    out[base + 3 : base + 4, :] = b_before
    out[base + 4 : base + 8, :] = jnp.zeros((4, 4 * r), F32)


def early_kernel(bs, pattern, halves, core_halves, a0h, a0l, a1h, a1l, t):
    n = a0h.shape[0]
    r = halves.shape[1]
    half = halves.shape[0] // 2
    for at, flag, hi, lo in ((0, 1, a0h, a0l), (1, has(1), a1h, a1l)):
        rows = slice(at * half, (at + 1) * half)
        put = functools.partial(put_split, hi, lo)
        dense_turned(put, pattern, halves[rows, :], core_halves[rows, :], flag, n, r, bs)

    def wanted(ref):
        return jnp.concatenate([ref[:, 0:r], ref[:, 2 * r : 3 * r]], axis=1)

    t[...] = dot3(a1h[...], a1l[...], wanted(a0h), wanted(a0l))


def rows_kernel(
    bs, pattern, halves, core_halves, t, dyn_own, dyn_send, a2, a2h, a2l, a3h, a3l
):
    q, _, _ = place_of()
    n = a2.shape[0]
    r = halves.shape[1]
    half = halves.shape[0] // 2

    def put2(row, col, value):
        put_split(a2h, a2l, row, col, value)
        a2[row, col] = value

    def put3(row, col, value):
        put_split(a3h, a3l, row, col, value)

    for at, flag, put in ((0, has(2), put2), (1, has(3), put3)):
        rows = slice(at * half, (at + 1) * half)
        dense_turned(put, pattern, halves[rows, :], core_halves[rows, :], flag, n, r, bs)
    rows = dot3(a2h[...], a2l[...], *split(t[...]))
    rows = dot3(a3h[...], a3l[...], *split(rows))
    for j in range(4):
        at = lanes(q ^ j, r)
        dyn_own[:, at] = rows[j * r : (j + 1) * r, 0:r].T
        dyn_send[:, at] = rows[j * r : (j + 1) * r, r : 2 * r].T


def product_kernel(
    a0h, a0l, a1h, a1l, a2h, a2l, a3h, a3l, mh, ml, th, tl, product_ref
):
    first = place_of()[2] == 0
    r = a0h.shape[0] // 4

    @pl.when(first)
    def _():
        product_ref[...] = dot3(a1h[...], a1l[...], a0h[...], a0l[...])
        straight_split(mh, ml, product_ref, r)
        transpose_split(th, tl, product_ref, r)

    @pl.when(jnp.logical_not(first))
    def _():
        product_ref[...] = dot3(a3h[...], a3l[...], a2h[...], a2l[...])
        straight_split(th, tl, product_ref, r)
        transpose_split(mh, ml, product_ref, r)


def ahead_kernel(own, mh, ml, th, tl, full, z, xh, xl):
    r = own.shape[1] // 4

    def put(i, j, block):
        full[i * r : (i + 1) * r, j * r : (j + 1) * r] = block

    spread(own, r, put)

    @pl.when(place_of()[2] == 1)
    def _():
        straight_split(xh, xl, full, r)
        u = dot3(xh[...], xl[...], mh[...], ml[...])
        z[...] = dot3(th[...], tl[...], *split(u))


def put_rows(ref, value, q, r):
    for j in range(4):
        ref[lanes(q ^ j, r), :] = value[:, j * r : (j + 1) * r]


def level2_kernel(own, earlier, mh, ml, th, tl, full, z, to_chip, to_far, uh, ul, xh, xl, rest):
    q, _, c = place_of()
    r = own.shape[1] // 4

    @pl.when(c == 0)
    def _():
        def put(i, j, block):
            put_split(xh, xl, slice(i * r, (i + 1) * r), slice(j * r, (j + 1) * r), block)

        spread(earlier, r, put)
        hi, lo = split(dot3(xh[...], xl[...], mh[...], ml[...]))
        uh[...] = hi
        ul[...] = lo
        rest[...] = dot3(th[2 * r :, :], tl[2 * r :, :], hi, lo) + full[2 * r :, :]

    @pl.when(c == 1)
    def _():
        def put(i, j, block):
            rows = slice((i - 2) * r, (i - 1) * r)
            cols = slice(j * r, (j + 1) * r)
            rest[rows, cols] = z[i * r : (i + 1) * r, cols] + block

        spread(earlier, r, put, rows=(2, 3))

    put_rows(to_chip, rest[0:r, :], q, r)
    put_rows(to_far, rest[r : 2 * r, :], q, r)


def rest_kernel(
    own, earlier, mh, ml, th, tl, a2, full, z, uh, ul, keep, to_core, short, vec, rest
):
    q, _, c = place_of()
    r = own.shape[1] // 4
    base = 2 * r
    b1 = earlier[base + 1 : base + 2, :] + row_times(earlier[base + 3 : base + 4, :], a2[...], r)

    @pl.when(c == 0)
    def _():
        rest[...] = dot3(th[0 : 2 * r, :], tl[0 : 2 * r, :], uh[...], ul[...]) + full[0 : 2 * r, :]
        vec[0:1, :] = b1
        vec[1:2, :] = own[base + 2 : base + 3, :]

    @pl.when(c == 1)
    def _():
        def put(i, j, block):
            rows = slice(i * r, (i + 1) * r)
            cols = slice(j * r, (j + 1) * r)
            rest[rows, cols] = z[rows, cols] + block

        spread(earlier, r, put, rows=(0, 1))
        vec[0:1, :] = own[base + 2 : base + 3, :] + row_times(b1, full[...], r)
        vec[1:2, :] = earlier[base + 2 : base + 3, :]

    out = vec[1:2, :] + row_times(vec[0:1, :], mh[...].astype(F32) + ml[...].astype(F32), r)
    put_rows(keep, rest[0:r, :], q, r)
    put_rows(to_core, rest[r : 2 * r, :], q, r)
    for i in range(4):
        short[i : i + 1, :] = out[:, i * r : (i + 1) * r]
    short[4:8, :] = jnp.zeros((4, r), F32)


def panel_copies(panel, target, element, r):
    return [
        (panel.at[pl.ds(g * r, r), :], target.at[element, :, pl.ds(g * r, r)]) for g in range(4)
    ]


def fill_kernel(keep, from_core, dyn_own, dyn_recv, dyn_out, cov_out, cost_out, sems):
    _, y, c = place_of()
    r = dyn_own.shape[0]
    dyn = [(dyn_own, dyn_out.at[y]), (dyn_recv, dyn_out.at[1 - y])]

    @pl.when(c == 0)
    def _():
        copy_all(
            dyn + panel_copies(keep, cov_out, y, r) + panel_copies(from_core, cost_out, y, r), sems
        )

    @pl.when(c == 1)
    def _():
        copy_all(
            dyn + panel_copies(from_core, cov_out, y, r) + panel_copies(keep, cost_out, y, r), sems
        )


def place_chip_kernel(cov_in, cost_in, panel, cov_out, cost_out, sems):
    del cov_in, cost_in
    _, y, c = place_of()
    r = panel.shape[1]

    @pl.when(c == 0)
    def _():
        copy_all(panel_copies(panel, cov_out, 1 - y, r), sems)

    @pl.when(c == 1)
    def _():
        copy_all(panel_copies(panel, cost_out, 1 - y, r), sems)


def place_far_kernel(
    cov_in,
    cost_in,
    short,
    core_short,
    chip_short,
    far_short,
    panel,
    cov_out,
    cost_out,
    drift_out,
    eta_out,
    lines,
    sems,
):
    del cov_in, cost_in
    _, y, c = place_of()
    first = c == 0
    r = short.shape[1]
    for at, (one, two, three, four) in enumerate(
        (
            (short[0:1, :], core_short[1:2, :], chip_short[2:3, :], far_short[3:4, :]),
            (core_short[1:2, :], short[0:1, :], far_short[3:4, :], chip_short[2:3, :]),
        )
    ):
        lines[at, pl.ds(y, 1), :] = jnp.where(first, one, two)
        lines[at, pl.ds(1 - y, 1), :] = jnp.where(first, three, four)
    vectors = [(lines.at[0], drift_out), (lines.at[1], eta_out)]

    @pl.when(first)
    def _():
        copy_all(vectors + panel_copies(panel, cost_out, 1 - y, r), sems)

    @pl.when(c == 1)
    def _():
        copy_all(vectors + panel_copies(panel, cov_out, 1 - y, r), sems)


IN_HBM, IN_VMEM = 0, 1


def kernel(body, operands, shapes, scratch=(), aliases=None):
    specs = {
        IN_HBM: pl.BlockSpec(memory_space=pltpu.HBM),
        IN_VMEM: pl.BlockSpec(memory_space=pltpu.VMEM),
    }
    call = pl.pallas_call(
        body,
        in_specs=[specs[where] for where, _ in operands],
        out_specs=[specs[where] for where, _ in shapes],
        out_shape=[
            pltpu.VMEM(s.shape, s.dtype) if where == IN_VMEM else s for where, s in shapes
        ],
        scratch_shapes=list(scratch),
        input_output_aliases=aliases or {},
        compiler_params=pltpu.CompilerParams(vmem_limit_bytes=20 * 2**20),
    )
    kept = {IN_HBM: pltpu.HBM, IN_VMEM: pltpu.VMEM}
    return call(
        *(
            pltpu.with_memory_space_constraint(x, kept[where]) if where in kept else x
            for where, x in operands
        )
    )


def per_device_split(blocks, pattern, drift, cov, cost, eta):
    elements, r, n = cov.shape
    bs = blocks.shape[2] // 3
    tms, cols = lax.axis_size("tm"), lax.axis_size("col")

    def swap(value, bit):
        return lax.ppermute(value, "col", [(i, i ^ bit) for i in range(cols)])

    def later(value, distance):
        return lax.ppermute(value, "tm", [(i, i + distance) for i in range(tms - distance)])

    def hbm(*arrays):
        return [(IN_HBM, x) for x in arrays]

    def vmem(*arrays):
        return [(IN_VMEM, x) for x in arrays]

    def shape(*dims):
        return jax.ShapeDtypeStruct(dims, F32)

    def half(*dims):
        return jax.ShapeDtypeStruct(dims, BF16)

    def square(dtype):
        return pltpu.VMEM((n, n), dtype)

    def sems(count):
        return pltpu.SemaphoreType.DMA((count,))

    turned = jnp.swapaxes(blocks, 1, 2)
    before = later(turned, 1)
    to_core, to_chip, to_far, panel, vecs = kernel(
        send_kernel,
        hbm(cov, cost, drift, eta),
        vmem(shape(r + 8, 3 * r), shape(r + 8, 2 * r), shape(r + 8, r), shape(r, n), shape(8, r)),
        [pltpu.VMEM(drift.shape, F32), pltpu.VMEM(eta.shape, F32), sems(12)],
    )
    from_core = swap(to_core, 1)
    from_chip = swap(to_chip, 2)
    from_far = swap(to_far, 3)
    (own_near,) = kernel(pack_near_kernel, vmem(panel, from_core), vmem(shape(r, 6 * r)))
    near = later(own_near, 1)
    (own_far,) = kernel(
        pack_far_kernel, vmem(vecs, from_core, from_chip, from_far), vmem(shape(r + 8, 2 * r))
    )
    far = later(own_far, 1)
    (picked,) = kernel(pick_kernel, vmem(turned, before), vmem(shape(6 * bs, r)))
    other = swap(picked, 2)
    (halves,) = kernel(halves_kernel, vmem(turned, before, other), vmem(shape(12 * bs, r)))
    core_halves = swap(halves, 1)
    far_halves = later(halves, 2)
    m1 = kernel(
        functools.partial(prepare_kernel, bs),
        vmem(pattern, halves, core_halves),
        vmem(*[half(n, n)] * 4),
        [square(F32)],
    )
    (level1,) = kernel(
        level1_kernel,
        vmem(own_near, own_far, near, far, *m1),
        vmem(shape(2 * r + 8, n)),
        [square(F32)] + [square(BF16)] * 2,
    )
    earlier = later(level1, 2)
    *a01, t = kernel(
        functools.partial(early_kernel, bs),
        vmem(pattern, halves, core_halves),
        vmem(*[half(n, n)] * 4, shape(n, 2 * r)),
    )
    far_core_halves = swap(far_halves, 1)
    dyn_own, dyn_send, a2, *a23 = kernel(
        functools.partial(rows_kernel, bs),
        vmem(pattern, far_halves, far_core_halves, t),
        vmem(shape(r, n), shape(r, n), shape(n, n), *[half(n, n)] * 4),
    )
    dyn_recv = swap(dyn_send, 2)
    m2 = kernel(product_kernel, vmem(*a01, *a23), vmem(*[half(n, n)] * 4), [square(F32)])
    full, z = kernel(
        ahead_kernel, vmem(level1, *m2), vmem(shape(n, n), shape(n, n)), [square(BF16)] * 2
    )
    to_chip, to_far, *u = kernel(
        level2_kernel,
        vmem(level1, earlier, *m2, full, z),
        vmem(shape(n, r), shape(n, r), half(n, n), half(n, n)),
        [square(BF16)] * 2 + [pltpu.VMEM((2 * r, n), F32)],
    )
    from_chip = swap(to_chip, 2)
    from_far = swap(to_far, 3)
    keep, to_core, short = kernel(
        rest_kernel,
        vmem(level1, earlier, *m2, a2, full, z, *u),
        vmem(shape(n, r), shape(n, r), shape(8, r)),
        [pltpu.VMEM((8, n), F32), pltpu.VMEM((2 * r, n), F32)],
    )
    from_core = swap(to_core, 1)
    shorts = (short, swap(short, 1), swap(short, 2), swap(short, 3))
    whole, line = shape(elements, r, n), shape(elements, r)
    dyn_out, cov_out, cost_out = kernel(
        fill_kernel, vmem(keep, from_core, dyn_own, dyn_recv), hbm(whole, whole, whole), [sems(10)]
    )
    cov_out, cost_out = kernel(
        place_chip_kernel,
        hbm(cov_out, cost_out) + vmem(from_chip),
        hbm(whole, whole),
        [sems(4)],
        {0: 0, 1: 1},
    )
    cov_out, cost_out, drift_out, eta_out = kernel(
        place_far_kernel,
        hbm(cov_out, cost_out) + vmem(*shorts, from_far),
        hbm(whole, whole, line, line),
        [pltpu.VMEM((2, elements, r), F32), sems(6)],
        {0: 0, 1: 1},
    )
    return dyn_out, drift_out, cov_out, cost_out, eta_out


def takes_split(elements, r, bs, cols):
    return elements == 2 and cols == 4 and r % 128 == 0 and r % bs == 0 and bs % 8 == 0


def per_device(blocks, pattern, drift, cov, cost, eta):
    elements, r, _ = cov.shape
    bs = blocks.shape[2] // 3
    if takes_split(elements, r, bs, lax.axis_size("col")):
        return per_device_split(blocks, pattern, drift, cov, cost, eta)
    return per_device_general(blocks, pattern, drift, cov, cost, eta)


def solution(mesh):
    return jax.shard_map(
        per_device,
        mesh=mesh,
        in_specs=(
            P("tm", "col", None),
            P(),
            P("tm", "col"),
            P("tm", "col", None),
            P("tm", "col", None),
            P("tm", "col"),
        ),
        out_specs=(
            P("tm", "col", None),
            P("tm", "col"),
            P("tm", "col", None),
            P("tm", "col", None),
            P("tm", "col"),
        ),
        check_vma=False,
    )
```

```python
import functools

import jax
import jax.numpy as jnp
from jax import lax
from jax.experimental import pallas as pl
from jax.experimental.pallas import tpu as pltpu
from jax.sharding import PartitionSpec as P


HIGH = lax.Precision.HIGHEST
F32 = jnp.float32
BF16 = jnp.bfloat16


def shifted(block, axis, distance):
    devices = range(lax.axis_size(axis))
    route = [(i - distance, i) for i in devices if i - distance in devices]
    return lax.ppermute(block, axis, route)


def product(form, left, right):
    return jnp.einsum(form, left, right, precision=HIGH)


def densify(row_blocks, row_ids, pattern, block_size):
    block_count = pattern.shape[0]
    row_block = row_ids // block_size
    chooser = (row_block[:, None] == jnp.arange(block_count, dtype=jnp.int32)[None, :]).astype(
        jnp.int32
    )
    columns = jnp.sum(chooser[:, :, None] * pattern[None, :, :], axis=1)
    matches = (
        columns[:, :, None] == jnp.arange(block_count, dtype=jnp.int32)[None, None, :]
    ).astype(jnp.float32)
    pieces = row_blocks.reshape(row_blocks.shape[:-1] + (3, 1, block_size))
    filled = jnp.sum(matches[:, :, :, None] * pieces, axis=-3)
    return filled.reshape(row_blocks.shape[:-1] + (block_count * block_size,))


def combine_rows(
    dyn_prev_full,
    dyn_own_full,
    dyn_own,
    drift_prev_full,
    drift_own,
    cov_prev,
    cov_own,
    cost_prev,
    cost_own,
    eta_prev,
    eta_own,
    first_row,
):
    height = dyn_own.shape[1]
    dyn_res = product("tij,tjk->tik", dyn_own, dyn_prev_full)
    drift_res = product("tij,tj->ti", dyn_own, drift_prev_full) + drift_own
    carried = eta_own + product("tij,tj->ti", cost_own, drift_prev_full)
    value_rows = product("tij,tjk->tik", cost_own, dyn_prev_full)
    prev_columns = lax.dynamic_slice_in_dim(dyn_prev_full, first_row, height, 2)
    cov_full, carried_full, value_full = (
        lax.all_gather(cov_prev, "col", axis=1, tiled=True),
        lax.all_gather(carried, "col", axis=1, tiled=True),
        lax.all_gather(value_rows, "col", axis=1, tiled=True),
    )
    cost_res = cost_prev + product("tki,tkj->tij", prev_columns, value_full)
    cov_res = (
        product("tik,tjk->tij", product("tij,tjk->tik", dyn_own, cov_full), dyn_own_full) + cov_own
    )
    eta_res = eta_prev + product("tki,tk->ti", prev_columns, carried_full)
    return (dyn_res, drift_res, cov_res, cost_res, eta_res)


def choose(flag, combined, kept):
    return tuple(jnp.where(flag, new, old) for new, old in zip(combined, kept))


def per_device_general(blocks, pattern, drift, cov, cost, eta):
    height = cov.shape[1]
    modes = cov.shape[2]
    block_size = blocks.shape[2] // 3
    first_row = lax.axis_index("col") * height
    own_ids = first_row + jnp.arange(height, dtype=jnp.int32)
    all_ids = jnp.arange(modes, dtype=jnp.int32)
    position = lax.axis_index("tm")
    dyn_own = densify(blocks, own_ids, pattern, block_size)
    received = shifted((blocks, drift, cov, cost, eta), "tm", 1)
    blocks_prev, blocks_own, drift_prev_full = (
        lax.all_gather(received[0], "col", axis=1, tiled=True),
        lax.all_gather(blocks, "col", axis=1, tiled=True),
        lax.all_gather(received[1], "col", axis=1, tiled=True),
    )
    merged = combine_rows(
        densify(blocks_prev, all_ids, pattern, block_size),
        densify(blocks_own, all_ids, pattern, block_size),
        dyn_own,
        drift_prev_full,
        drift,
        received[2],
        cov,
        received[3],
        cost,
        received[4],
        eta,
        first_row,
    )
    current = choose(position >= 1, merged, (dyn_own, drift, cov, cost, eta))
    received = shifted(current, "tm", 2)
    dyn_prev_full = lax.all_gather(received[0], "col", axis=1, tiled=True)
    dyn_own_full = lax.all_gather(current[0], "col", axis=1, tiled=True)
    drift_prev_full = lax.all_gather(received[1], "col", axis=1, tiled=True)
    merged = combine_rows(
        dyn_prev_full,
        dyn_own_full,
        current[0],
        drift_prev_full,
        current[1],
        received[2],
        current[2],
        received[3],
        current[3],
        received[4],
        current[4],
        first_row,
    )
    return choose(position >= 2, merged, current)


def split(x):
    hi = x.astype(BF16)
    lo = (x - hi.astype(F32)).astype(BF16)
    return hi, lo


def dot(a, b):
    return jnp.dot(a, b, preferred_element_type=F32)


def dot3(ah, al, bh, bl):
    return dot(ah, bh) + (dot(ah, bl) + dot(al, bh))


def triangle(r):
    rows = lax.broadcasted_iota(jnp.int32, (r, r), 0)
    cols = lax.broadcasted_iota(jnp.int32, (r, r), 1)
    return rows, cols


def fold(first, second, r):
    rows, cols = triangle(r)
    return jnp.where(rows >= cols, first, second)


def diagonal(block, r):
    rows, cols = triangle(r)
    return jnp.sum(jnp.where(rows == cols, block, 0.0), axis=0, keepdims=True)


def unfold(folded, second_diag, r):
    rows, cols = triangle(r)
    turned = folded.T
    first = jnp.where(rows >= cols, folded, turned)
    second = jnp.where(rows < cols, folded, turned)
    second = jnp.where(rows == cols, jnp.broadcast_to(second_diag, (r, r)), second)
    return first, second


UPPER = ((0, 1), (0, 2), (0, 3), (1, 2), (1, 3), (2, 3))


def spread(packed, r, put, rows=(0, 1, 2, 3)):
    panel0, panel1, diags = packed[0:r], packed[r : 2 * r], packed[2 * r : 2 * r + 1]
    for at, (panel, pair) in enumerate(((panel0, (0, 1)), (panel1, (2, 3)))):
        if pair[0] in rows or pair[1] in rows:
            blocks = unfold(panel[:, 0:r], diags[:, at * r : (at + 1) * r], r)
            for i, block in zip(pair, blocks):
                if i in rows:
                    put(i, i, block)
    for at, (i, j) in enumerate(UPPER):
        panel = panel0 if at < 3 else panel1
        block = panel[:, (at % 3 + 1) * r : (at % 3 + 2) * r]
        if i in rows:
            put(i, j, block)
        if j in rows:
            put(j, i, block.T)


def column(row, r):
    rows, cols = triangle(r)
    pieces = []
    for at in range(row.shape[1] // r):
        piece = jnp.broadcast_to(row[:, at * r : (at + 1) * r], (r, r))
        pieces.append(jnp.sum(jnp.where(rows == cols, piece, 0.0), axis=1, keepdims=True))
    return jnp.concatenate(pieces, axis=0)


def row_times(row, matrix, r):
    return jnp.sum(column(row, r) * matrix, axis=0, keepdims=True)


def place_of():
    q = lax.axis_index("col")
    return q, q >> 1, q & 1


def has(distance):
    return (lax.axis_index("tm") >= distance).astype(jnp.int32)


def lanes(index, r):
    return pl.ds(pl.multiple_of(index * r, r), r)


def copy_all(pairs, sems):
    copies = [
        pltpu.make_async_copy(source, target, sems.at[i]) for i, (source, target) in enumerate(pairs)
    ]
    for copy in copies:
        copy.start()
    for copy in copies:
        copy.wait()


def send_kernel(
    cov, cost, drift, eta, to_core, to_chip, to_far, panel, vecs, b_in, e_in, sems
):
    q, y, c = place_of()
    r = to_far.shape[1]

    def load(mine, theirs):
        pairs = []
        for j in range(2, 4):
            source = mine.at[1 - y, :, lanes((q ^ 2) ^ j, r)]
            pairs.append((source, to_chip.at[pl.ds(0, r), pl.ds((j - 2) * r, r)]))
        pairs.append((theirs.at[1 - y, :, lanes(q, r)], to_far.at[pl.ds(0, r), :]))
        for j in range(1, 4):
            source = theirs.at[y, :, lanes((q ^ 1) ^ j, r)]
            pairs.append((source, to_core.at[pl.ds(0, r), pl.ds((j - 1) * r, r)]))
        for j in range(4):
            pairs.append((mine.at[y, :, lanes(q ^ j, r)], panel.at[:, pl.ds(j * r, r)]))
        pairs.append((drift, b_in))
        pairs.append((eta, e_in))
        copy_all(pairs, sems)

    @pl.when(c == 0)
    def _():
        load(cov, cost)

    @pl.when(c == 1)
    def _():
        load(cost, cov)

    b, e = b_in[pl.ds(y, 1), :], e_in[pl.ds(y, 1), :]
    vecs[...] = jnp.zeros(vecs.shape, F32)
    vecs[0:1, :] = b
    vecs[1:2, :] = e
    to_core[r : r + 8, :] = jnp.zeros((8, 3 * r), F32)
    to_core[r : r + 1, 0:r] = b
    to_core[r : r + 1, r : 2 * r] = e
    b, e = b_in[pl.ds(1 - y, 1), :], e_in[pl.ds(1 - y, 1), :]
    to_chip[r : r + 8, :] = jnp.zeros((8, 2 * r), F32)
    to_chip[r : r + 1, 0:r] = b
    to_chip[r : r + 1, r : 2 * r] = e
    to_far[r : r + 8, :] = jnp.zeros((8, r), F32)
    to_far[r : r + 1, :] = b
    to_far[r + 1 : r + 2, :] = e


def pack_near_kernel(panel, from_core, packed):
    r = panel.shape[0]
    packed[:, 0:r] = fold(panel[:, 0:r], from_core[0:r, 0:r], r)
    packed[:, r : 4 * r] = panel[:, r:]
    packed[:, 4 * r :] = from_core[0:r, r : 3 * r]


def pack_far_kernel(vecs, from_core, from_chip, from_far, packed):
    r = vecs.shape[1]
    k33 = from_far[0:r, :]
    packed[0:r, 0:r] = fold(from_chip[0:r, 0:r], k33, r)
    packed[0:r, r:] = from_chip[0:r, r : 2 * r]
    packed[r : r + 1, 0:r] = diagonal(from_core[0:r, 0:r], r)
    packed[r : r + 1, r:] = diagonal(k33, r)
    b = (
        vecs[0:1, :],
        from_core[r : r + 1, 0:r],
        from_chip[r : r + 1, 0:r],
        from_far[r : r + 1, :],
    )
    e = (
        vecs[1:2, :],
        from_core[r : r + 1, r : 2 * r],
        from_chip[r : r + 1, r : 2 * r],
        from_far[r + 1 : r + 2, :],
    )
    for j in range(4):
        at = slice(j % 2 * r, (j % 2 + 1) * r)
        packed[r + 1 + j // 2 : r + 2 + j // 2, at] = b[j]
        packed[r + 3 + j // 2 : r + 4 + j // 2, at] = e[j]
    packed[r + 5 : r + 8, :] = jnp.zeros((3, 2 * r), F32)


def far_row(packed, r, at):
    return jnp.concatenate(
        [packed[r + at : r + at + 1, :], packed[r + at + 1 : r + at + 2, :]], axis=1
    )


def pick_kernel(turned, before, out):
    y = place_of()[1]
    height = turned.shape[1]
    out[0:height, :] = turned[1 - y]
    out[height:, :] = before[1 - y]


def halves_kernel(turned, before, other, out):
    y = place_of()[1]
    height = turned.shape[1]
    out[0:height, :] = turned[y]
    out[height : 2 * height, :] = other[0:height, :]
    out[2 * height : 3 * height, :] = before[y]
    out[3 * height :, :] = other[height:, :]


def dense_turned(put, pattern, own_half, core_half, flag, n, r, bs):
    q = place_of()[0]
    lane = lax.broadcasted_iota(jnp.int32, (bs, r), 1) // bs
    rows = lax.broadcasted_iota(jnp.int32, (bs, r), 0)
    cols = lax.broadcasted_iota(jnp.int32, (bs, r), 1)
    per = r // bs
    height = 3 * bs
    for j in range(4):
        half = own_half if j % 2 == 0 else core_half
        full = half[(j // 2) * height : (j // 2 + 1) * height, :]
        wanted = []
        for k in range(3):
            want = jnp.zeros((bs, r), jnp.int32)
            for h in range(per):
                block = pattern[pl.ds((q ^ j) * per + h, 1), :][:, k : k + 1] ^ (q * per)
                want = jnp.where(lane == h, jnp.broadcast_to(block, (bs, r)), want)
            wanted.append(jnp.where(flag == 1, want, -1))
        for block in range(n // bs):
            if j * r <= block * bs < (j + 1) * r:
                value = jnp.where(
                    jnp.logical_and(rows + block * bs == cols + j * r, flag == 0), 1.0, 0.0
                )
            else:
                value = jnp.zeros((bs, r), F32)
            for k in range(3):
                piece = full[k * bs : (k + 1) * bs, :]
                value = value + jnp.where(wanted[k] == block, piece, 0.0)
            put(slice(block * bs, (block + 1) * bs), slice(j * r, (j + 1) * r), value)


def put_split(hi_ref, lo_ref, rows, cols, value):
    hi, lo = split(value)
    hi_ref[rows, cols] = hi
    lo_ref[rows, cols] = lo


def transpose_split(hi_ref, lo_ref, source, r):
    n = source.shape[0]
    for i in range(n // r):
        for j in range(n // r):
            put_split(
                hi_ref,
                lo_ref,
                slice(j * r, (j + 1) * r),
                slice(i * r, (i + 1) * r),
                source[i * r : (i + 1) * r, j * r : (j + 1) * r].T,
            )


def straight_split(hi_ref, lo_ref, source, r):
    n = source.shape[0]
    for i in range(n // r):
        put_split(
            hi_ref, lo_ref, slice(i * r, (i + 1) * r), slice(None), source[i * r : (i + 1) * r, :]
        )


def prepare_kernel(bs, pattern, halves, core_halves, mh, ml, th, tl, dense):
    c, has1 = place_of()[2], has(1)
    n = dense.shape[0]
    r = halves.shape[1]
    half = halves.shape[0] // 2
    first = c == 0
    own_half = jnp.where(first, halves[0:half, :], halves[half:, :])
    core_half = jnp.where(first, core_halves[0:half, :], core_halves[half:, :])
    flag = jnp.where(first, 1, has1)

    def put(row, col, value):
        dense[row, col] = value

    dense_turned(put, pattern, own_half, core_half, flag, n, r, bs)

    @pl.when(first)
    def _():
        straight_split(mh, ml, dense, r)
        transpose_split(th, tl, dense, r)

    @pl.when(jnp.logical_not(first))
    def _():
        straight_split(th, tl, dense, r)
        transpose_split(mh, ml, dense, r)


def level1_kernel(
    own_near, own_far, near, far, mh, ml, th, tl, out, full, xh, xl
):
    c = place_of()[2]
    r = own_near.shape[0]
    first = c == 0
    xn = jnp.where(first, near[...], own_near[...])
    xf = jnp.where(first, far[...], own_far[...])
    x = jnp.concatenate(
        [
            xn[:, 0 : 4 * r],
            jnp.concatenate([xf[0:r, 0:r], xn[:, 4 * r :], xf[0:r, r:]], axis=1),
            jnp.concatenate([xf[r : r + 1, :], xf[r : r + 1, :]], axis=1),
        ],
        axis=0,
    )

    def put(i, j, block):
        full[i * r : (i + 1) * r, j * r : (j + 1) * r] = block
        put_split(xh, xl, slice(i * r, (i + 1) * r), slice(j * r, (j + 1) * r), block)

    spread(x, r, put)
    b_before, b_own = far_row(far, r, 1), far_row(own_far, r, 1)
    e_before, e_own = far_row(far, r, 3), far_row(own_far, r, 3)
    carried = jnp.where(first, b_before, e_own + row_times(b_before, full[...], r))
    vec = jnp.where(first, b_own, e_before) + row_times(
        carried, mh[...].astype(F32) + ml[...].astype(F32), r
    )
    u = dot3(xh[...], xl[...], mh[...], ml[...])
    uh, ul = split(u)
    top = dot3(th[0 : 2 * r, :], tl[0 : 2 * r, :], uh, ul)
    low = dot3(th[2 * r :, :], tl[2 * r :, :], uh[:, 2 * r :], ul[:, 2 * r :])
    dn = jnp.where(first, own_near[...], near[...])
    df = jnp.where(first, own_far[...], far[...])
    z11 = top[r : 2 * r, r : 2 * r]
    z33 = low[r : 2 * r, r : 2 * r]
    out[0:r, 0:r] = fold(top[0:r, 0:r], z11, r) + dn[:, 0:r]
    out[0:r, r:] = top[0:r, r:] + dn[:, r : 4 * r]
    out[r : 2 * r, 0:r] = fold(low[0:r, 0:r], z33, r) + df[0:r, 0:r]
    out[r : 2 * r, r : 3 * r] = top[r : 2 * r, 2 * r :] + dn[:, 4 * r :]
    out[r : 2 * r, 3 * r :] = low[0:r, r : 2 * r] + df[0:r, r:]
    base = 2 * r
    out[base : base + 1, 0:r] = diagonal(z11, r) + df[r : r + 1, 0:r]
    out[base : base + 1, r : 2 * r] = diagonal(z33, r) + df[r : r + 1, r:]
    out[base : base + 1, 2 * r :] = jnp.zeros((1, 2 * r), F32)
    out[base + 1 : base + 2, :] = b_own
    out[base + 2 : base + 3, :] = vec
    out[base + 3 : base + 4, :] = b_before
    out[base + 4 : base + 8, :] = jnp.zeros((4, 4 * r), F32)


def early_kernel(bs, pattern, halves, core_halves, a0h, a0l, a1h, a1l, t):
    n = a0h.shape[0]
    r = halves.shape[1]
    half = halves.shape[0] // 2
    for at, flag, hi, lo in ((0, 1, a0h, a0l), (1, has(1), a1h, a1l)):
        rows = slice(at * half, (at + 1) * half)
        put = functools.partial(put_split, hi, lo)
        dense_turned(put, pattern, halves[rows, :], core_halves[rows, :], flag, n, r, bs)

    def wanted(ref):
        return jnp.concatenate([ref[:, 0:r], ref[:, 2 * r : 3 * r]], axis=1)

    t[...] = dot3(a1h[...], a1l[...], wanted(a0h), wanted(a0l))


def rows_kernel(
    bs, pattern, halves, core_halves, t, dyn_own, dyn_send, a2, a2h, a2l, a3h, a3l
):
    q, _, _ = place_of()
    n = a2.shape[0]
    r = halves.shape[1]
    half = halves.shape[0] // 2

    def put2(row, col, value):
        put_split(a2h, a2l, row, col, value)
        a2[row, col] = value

    def put3(row, col, value):
        put_split(a3h, a3l, row, col, value)

    for at, flag, put in ((0, has(2), put2), (1, has(3), put3)):
        rows = slice(at * half, (at + 1) * half)
        dense_turned(put, pattern, halves[rows, :], core_halves[rows, :], flag, n, r, bs)
    rows = dot3(a2h[...], a2l[...], *split(t[...]))
    rows = dot3(a3h[...], a3l[...], *split(rows))
    for j in range(4):
        at = lanes(q ^ j, r)
        dyn_own[:, at] = rows[j * r : (j + 1) * r, 0:r].T
        dyn_send[:, at] = rows[j * r : (j + 1) * r, r : 2 * r].T


def product_kernel(
    a0h, a0l, a1h, a1l, a2h, a2l, a3h, a3l, mh, ml, th, tl, product_ref
):
    first = place_of()[2] == 0
    r = a0h.shape[0] // 4

    @pl.when(first)
    def _():
        product_ref[...] = dot3(a1h[...], a1l[...], a0h[...], a0l[...])
        straight_split(mh, ml, product_ref, r)
        transpose_split(th, tl, product_ref, r)

    @pl.when(jnp.logical_not(first))
    def _():
        product_ref[...] = dot3(a3h[...], a3l[...], a2h[...], a2l[...])
        straight_split(th, tl, product_ref, r)
        transpose_split(mh, ml, product_ref, r)


def ahead_kernel(own, mh, ml, th, tl, full, z, xh, xl):
    r = own.shape[1] // 4

    def put(i, j, block):
        full[i * r : (i + 1) * r, j * r : (j + 1) * r] = block

    spread(own, r, put)

    @pl.when(place_of()[2] == 1)
    def _():
        straight_split(xh, xl, full, r)
        u = dot3(xh[...], xl[...], mh[...], ml[...])
        z[...] = dot3(th[...], tl[...], *split(u))


def put_rows(ref, value, q, r):
    for j in range(4):
        ref[lanes(q ^ j, r), :] = value[:, j * r : (j + 1) * r]


CROSSING = ((2, 0), (2, 1), (2, 3))


def level2_kernel(own, earlier, mh, ml, th, tl, full, z, to_chip, uh, ul, xh, xl, rest):
    c = place_of()[2]
    r = own.shape[1] // 4
    two, three = slice(2 * r, 3 * r), slice(3 * r, 4 * r)

    @pl.when(c == 0)
    def _():
        def put(i, j, block):
            put_split(xh, xl, slice(i * r, (i + 1) * r), slice(j * r, (j + 1) * r), block)

        spread(earlier, r, put)
        hi, lo = split(dot3(xh[...], xl[...], mh[...], ml[...]))
        uh[...] = hi
        ul[...] = lo
        rest[:, 2 * r :] = dot3(th[2 * r :, :], tl[2 * r :, :], hi[:, 2 * r :], lo[:, 2 * r :])
        rest[0:r, 0 : 2 * r] = dot3(th[two, :], tl[two, :], hi[:, 0 : 2 * r], lo[:, 0 : 2 * r])
        rest[:, 2 * r :] = rest[:, 2 * r :] + full[2 * r :, 2 * r :]
        rest[0:r, 0 : 2 * r] = rest[0:r, 0 : 2 * r] + full[two, 0 : 2 * r]

    @pl.when(c == 1)
    def _():
        def put(i, j, block):
            if (i, j) in CROSSING or i == j:
                rows = slice((i - 2) * r, (i - 1) * r)
                cols = slice(j * r, (j + 1) * r)
                rest[rows, cols] = z[i * r : (i + 1) * r, cols] + block

        spread(earlier, r, put, rows=(2, 3))

    z33 = rest[r : 2 * r, three]
    to_chip[0:r, :] = fold(rest[0:r, two], z33, r)
    for at, (_, j) in enumerate(CROSSING):
        to_chip[(at + 1) * r : (at + 2) * r, :] = rest[0:r, j * r : (j + 1) * r]
    to_chip[4 * r :, :] = jnp.broadcast_to(diagonal(z33, r), (8, r))


def far_rows_kernel(
    own, earlier, mh, ml, th, tl, a2, full, z, uh, ul, to_far, short, vec, rest
):
    c = place_of()[2]
    r = own.shape[1] // 4
    base = 2 * r
    three = slice(3 * r, 4 * r)
    b1 = earlier[base + 1 : base + 2, :] + row_times(earlier[base + 3 : base + 4, :], a2[...], r)

    @pl.when(c == 0)
    def _():
        value = dot3(th[three, :], tl[three, :], uh[:, 0 : 2 * r], ul[:, 0 : 2 * r])
        rest[...] = value + full[three, 0 : 2 * r]
        vec[0:1, :] = b1
        vec[1:2, :] = own[base + 2 : base + 3, :]

    @pl.when(c == 1)
    def _():
        def put(i, j, block):
            if j < 2:
                cols = slice(j * r, (j + 1) * r)
                rest[:, cols] = z[three, cols] + block

        spread(earlier, r, put, rows=(3,))
        vec[0:1, :] = own[base + 2 : base + 3, :] + row_times(b1, full[...], r)
        vec[1:2, :] = earlier[base + 2 : base + 3, :]

    to_far[0:r, :] = rest[:, 0:r]
    to_far[r : 2 * r, :] = rest[:, r : 2 * r]
    out = vec[1:2, :] + row_times(vec[0:1, :], mh[...].astype(F32) + ml[...].astype(F32), r)
    for i in range(4):
        short[i : i + 1, :] = out[:, i * r : (i + 1) * r]
    short[4:8, :] = jnp.zeros((4, r), F32)


def rest_kernel(earlier, th, tl, full, z, uh, ul, keep, to_core, rest):
    q, _, c = place_of()
    r = earlier.shape[1] // 4

    @pl.when(c == 0)
    def _():
        rest[...] = dot3(th[0 : 2 * r, :], tl[0 : 2 * r, :], uh[...], ul[...]) + full[0 : 2 * r, :]

    @pl.when(c == 1)
    def _():
        def put(i, j, block):
            rows = slice(i * r, (i + 1) * r)
            cols = slice(j * r, (j + 1) * r)
            rest[rows, cols] = z[rows, cols] + block

        spread(earlier, r, put, rows=(0, 1))

    put_rows(keep, rest[0:r, :], q, r)
    put_rows(to_core, rest[r : 2 * r, :], q, r)


def turn_kernel(from_chip, diagonal_block, mirrored):
    r = diagonal_block.shape[0]
    first, second = unfold(from_chip[0:r, :], from_chip[4 * r : 4 * r + 1, :], r)
    diagonal_block[...] = first
    mirrored[0:r, :] = from_chip[3 * r : 4 * r, :].T
    mirrored[r : 2 * r, :] = second


def panel_copies(panel, target, element, r):
    return [
        (panel.at[pl.ds(g * r, r), :], target.at[element, :, pl.ds(g * r, r)]) for g in range(4)
    ]


def fill_kernel(keep, from_core, dyn_own, dyn_recv, dyn_out, cov_out, cost_out, sems):
    _, y, c = place_of()
    r = dyn_own.shape[0]
    dyn = [(dyn_own, dyn_out.at[y]), (dyn_recv, dyn_out.at[1 - y])]

    @pl.when(c == 0)
    def _():
        copy_all(
            dyn + panel_copies(keep, cov_out, y, r) + panel_copies(from_core, cost_out, y, r), sems
        )

    @pl.when(c == 1)
    def _():
        copy_all(
            dyn + panel_copies(from_core, cov_out, y, r) + panel_copies(keep, cost_out, y, r), sems
        )


def block_copies(blocks, target, element, r):
    return [(source, target.at[element, :, lanes(at, r)]) for source, at in blocks]


def place_chip_kernel(cov_in, cost_in, diagonal_block, panel, cov_out, cost_out, sems):
    del cov_in, cost_in
    q, y, c = place_of()
    r = panel.shape[1]
    blocks = [(diagonal_block, q)] + [
        (panel.at[pl.ds(at * r, r), :], q ^ bit) for at, bit in ((1, 2), (2, 3), (3, 1))
    ]

    @pl.when(c == 0)
    def _():
        copy_all(block_copies(blocks, cov_out, 1 - y, r), sems)

    @pl.when(c == 1)
    def _():
        copy_all(block_copies(blocks, cost_out, 1 - y, r), sems)


def place_far_kernel(
    cov_in,
    cost_in,
    short,
    core_short,
    chip_short,
    far_short,
    mirrored,
    panel,
    cov_out,
    cost_out,
    drift_out,
    eta_out,
    lines,
    sems,
):
    del cov_in, cost_in
    q, y, c = place_of()
    first = c == 0
    r = short.shape[1]
    for at, (one, two, three, four) in enumerate(
        (
            (short[0:1, :], core_short[1:2, :], chip_short[2:3, :], far_short[3:4, :]),
            (core_short[1:2, :], short[0:1, :], far_short[3:4, :], chip_short[2:3, :]),
        )
    ):
        lines[at, pl.ds(y, 1), :] = jnp.where(first, one, two)
        lines[at, pl.ds(1 - y, 1), :] = jnp.where(first, three, four)
    vectors = [(lines.at[0], drift_out), (lines.at[1], eta_out)]
    near, far = pl.ds(0, r), pl.ds(r, r)
    blocks = [
        (panel.at[near, :], q ^ 3),
        (panel.at[far, :], q ^ 2),
        (mirrored.at[near, :], q ^ 1),
        (mirrored.at[far, :], q),
    ]

    @pl.when(first)
    def _():
        copy_all(vectors + block_copies(blocks, cost_out, 1 - y, r), sems)

    @pl.when(c == 1)
    def _():
        copy_all(vectors + block_copies(blocks, cov_out, 1 - y, r), sems)


IN_HBM, IN_VMEM = 0, 1


def kernel(body, operands, shapes, scratch=(), aliases=None):
    specs = {
        IN_HBM: pl.BlockSpec(memory_space=pltpu.HBM),
        IN_VMEM: pl.BlockSpec(memory_space=pltpu.VMEM),
    }
    call = pl.pallas_call(
        body,
        in_specs=[specs[where] for where, _ in operands],
        out_specs=[specs[where] for where, _ in shapes],
        out_shape=[
            pltpu.VMEM(s.shape, s.dtype) if where == IN_VMEM else s for where, s in shapes
        ],
        scratch_shapes=list(scratch),
        input_output_aliases=aliases or {},
        compiler_params=pltpu.CompilerParams(vmem_limit_bytes=20 * 2**20),
    )
    kept = {IN_HBM: pltpu.HBM, IN_VMEM: pltpu.VMEM}
    return call(
        *(
            pltpu.with_memory_space_constraint(x, kept[where]) if where in kept else x
            for where, x in operands
        )
    )


def per_device_split(blocks, pattern, drift, cov, cost, eta):
    elements, r, n = cov.shape
    bs = blocks.shape[2] // 3
    tms, cols = lax.axis_size("tm"), lax.axis_size("col")

    def swap(value, bit):
        return lax.ppermute(value, "col", [(i, i ^ bit) for i in range(cols)])

    def later(value, distance):
        return lax.ppermute(value, "tm", [(i, i + distance) for i in range(tms - distance)])

    def hbm(*arrays):
        return [(IN_HBM, x) for x in arrays]

    def vmem(*arrays):
        return [(IN_VMEM, x) for x in arrays]

    def shape(*dims):
        return jax.ShapeDtypeStruct(dims, F32)

    def half(*dims):
        return jax.ShapeDtypeStruct(dims, BF16)

    def square(dtype):
        return pltpu.VMEM((n, n), dtype)

    def sems(count):
        return pltpu.SemaphoreType.DMA((count,))

    turned = jnp.swapaxes(blocks, 1, 2)
    before = later(turned, 1)
    to_core, to_chip, to_far, panel, vecs = kernel(
        send_kernel,
        hbm(cov, cost, drift, eta),
        vmem(shape(r + 8, 3 * r), shape(r + 8, 2 * r), shape(r + 8, r), shape(r, n), shape(8, r)),
        [pltpu.VMEM(drift.shape, F32), pltpu.VMEM(eta.shape, F32), sems(12)],
    )
    from_core = swap(to_core, 1)
    from_chip = swap(to_chip, 2)
    from_far = swap(to_far, 3)
    (own_near,) = kernel(pack_near_kernel, vmem(panel, from_core), vmem(shape(r, 6 * r)))
    near = later(own_near, 1)
    (own_far,) = kernel(
        pack_far_kernel, vmem(vecs, from_core, from_chip, from_far), vmem(shape(r + 8, 2 * r))
    )
    far = later(own_far, 1)
    (picked,) = kernel(pick_kernel, vmem(turned, before), vmem(shape(6 * bs, r)))
    other = swap(picked, 2)
    (halves,) = kernel(halves_kernel, vmem(turned, before, other), vmem(shape(12 * bs, r)))
    core_halves = swap(halves, 1)
    far_halves = later(halves, 2)
    m1 = kernel(
        functools.partial(prepare_kernel, bs),
        vmem(pattern, halves, core_halves),
        vmem(*[half(n, n)] * 4),
        [square(F32)],
    )
    (level1,) = kernel(
        level1_kernel,
        vmem(own_near, own_far, near, far, *m1),
        vmem(shape(2 * r + 8, n)),
        [square(F32)] + [square(BF16)] * 2,
    )
    earlier = later(level1, 2)
    *a01, t = kernel(
        functools.partial(early_kernel, bs),
        vmem(pattern, halves, core_halves),
        vmem(*[half(n, n)] * 4, shape(n, 2 * r)),
    )
    far_core_halves = swap(far_halves, 1)
    dyn_own, dyn_send, a2, *a23 = kernel(
        functools.partial(rows_kernel, bs),
        vmem(pattern, far_halves, far_core_halves, t),
        vmem(shape(r, n), shape(r, n), shape(n, n), *[half(n, n)] * 4),
    )
    dyn_recv = swap(dyn_send, 2)
    m2 = kernel(product_kernel, vmem(*a01, *a23), vmem(*[half(n, n)] * 4), [square(F32)])
    full, z = kernel(
        ahead_kernel, vmem(level1, *m2), vmem(shape(n, n), shape(n, n)), [square(BF16)] * 2
    )
    to_chip, *u = kernel(
        level2_kernel,
        vmem(level1, earlier, *m2, full, z),
        vmem(shape(n + 8, r), half(n, n), half(n, n)),
        [square(BF16)] * 2 + [pltpu.VMEM((2 * r, n), F32)],
    )
    from_chip = swap(to_chip, 2)
    to_far, short = kernel(
        far_rows_kernel,
        vmem(level1, earlier, *m2, a2, full, z, *u),
        vmem(shape(2 * r, r), shape(8, r)),
        [pltpu.VMEM((8, n), F32), pltpu.VMEM((r, 2 * r), F32)],
    )
    chip_short, far_short = swap(short, 2), swap(short, 3)
    from_far = swap(to_far, 3)
    keep, to_core = kernel(
        rest_kernel,
        vmem(earlier, *m2[2:], full, z, *u),
        vmem(shape(n, r), shape(n, r)),
        [pltpu.VMEM((2 * r, n), F32)],
    )
    from_core = swap(to_core, 1)
    shorts = (short, swap(short, 1), chip_short, far_short)
    diagonal_block, mirrored = kernel(
        turn_kernel, vmem(from_chip), vmem(shape(r, r), shape(2 * r, r))
    )
    mirrored = swap(mirrored, 1)
    whole, line = shape(elements, r, n), shape(elements, r)
    dyn_out, cov_out, cost_out = kernel(
        fill_kernel, vmem(keep, from_core, dyn_own, dyn_recv), hbm(whole, whole, whole), [sems(10)]
    )
    cov_out, cost_out = kernel(
        place_chip_kernel,
        hbm(cov_out, cost_out) + vmem(diagonal_block, from_chip),
        hbm(whole, whole),
        [sems(4)],
        {0: 0, 1: 1},
    )
    cov_out, cost_out, drift_out, eta_out = kernel(
        place_far_kernel,
        hbm(cov_out, cost_out) + vmem(*shorts, mirrored, from_far),
        hbm(whole, whole, line, line),
        [pltpu.VMEM((2, elements, r), F32), sems(6)],
        {0: 0, 1: 1},
    )
    return dyn_out, drift_out, cov_out, cost_out, eta_out


def takes_split(elements, r, bs, cols):
    return elements == 2 and cols == 4 and r % 128 == 0 and r % bs == 0 and bs % 8 == 0


def per_device(blocks, pattern, drift, cov, cost, eta):
    elements, r, _ = cov.shape
    bs = blocks.shape[2] // 3
    if takes_split(elements, r, bs, lax.axis_size("col")):
        return per_device_split(blocks, pattern, drift, cov, cost, eta)
    return per_device_general(blocks, pattern, drift, cov, cost, eta)


def solution(mesh):
    return jax.shard_map(
        per_device,
        mesh=mesh,
        in_specs=(
            P("tm", "col", None),
            P(),
            P("tm", "col"),
            P("tm", "col", None),
            P("tm", "col", None),
            P("tm", "col"),
        ),
        out_specs=(
            P("tm", "col", None),
            P("tm", "col"),
            P("tm", "col", None),
            P("tm", "col", None),
            P("tm", "col"),
        ),
        check_vma=False,
    )
```

```python
import functools

import jax
import jax.numpy as jnp
from jax import lax
from jax.experimental import pallas as pl
from jax.experimental.pallas import tpu as pltpu
from jax.sharding import PartitionSpec as P


HIGH = lax.Precision.HIGHEST
F32 = jnp.float32
BF16 = jnp.bfloat16


def shifted(block, axis, distance):
    devices = range(lax.axis_size(axis))
    route = [(i - distance, i) for i in devices if i - distance in devices]
    return lax.ppermute(block, axis, route)


def product(form, left, right):
    return jnp.einsum(form, left, right, precision=HIGH)


def densify(row_blocks, row_ids, pattern, block_size):
    block_count = pattern.shape[0]
    row_block = row_ids // block_size
    chooser = (row_block[:, None] == jnp.arange(block_count, dtype=jnp.int32)[None, :]).astype(
        jnp.int32
    )
    columns = jnp.sum(chooser[:, :, None] * pattern[None, :, :], axis=1)
    matches = (
        columns[:, :, None] == jnp.arange(block_count, dtype=jnp.int32)[None, None, :]
    ).astype(jnp.float32)
    pieces = row_blocks.reshape(row_blocks.shape[:-1] + (3, 1, block_size))
    filled = jnp.sum(matches[:, :, :, None] * pieces, axis=-3)
    return filled.reshape(row_blocks.shape[:-1] + (block_count * block_size,))


def combine_rows(
    dyn_prev_full,
    dyn_own_full,
    dyn_own,
    drift_prev_full,
    drift_own,
    cov_prev,
    cov_own,
    cost_prev,
    cost_own,
    eta_prev,
    eta_own,
    first_row,
):
    height = dyn_own.shape[1]
    dyn_res = product("tij,tjk->tik", dyn_own, dyn_prev_full)
    drift_res = product("tij,tj->ti", dyn_own, drift_prev_full) + drift_own
    carried = eta_own + product("tij,tj->ti", cost_own, drift_prev_full)
    value_rows = product("tij,tjk->tik", cost_own, dyn_prev_full)
    prev_columns = lax.dynamic_slice_in_dim(dyn_prev_full, first_row, height, 2)
    cov_full, carried_full, value_full = (
        lax.all_gather(cov_prev, "col", axis=1, tiled=True),
        lax.all_gather(carried, "col", axis=1, tiled=True),
        lax.all_gather(value_rows, "col", axis=1, tiled=True),
    )
    cost_res = cost_prev + product("tki,tkj->tij", prev_columns, value_full)
    cov_res = (
        product("tik,tjk->tij", product("tij,tjk->tik", dyn_own, cov_full), dyn_own_full) + cov_own
    )
    eta_res = eta_prev + product("tki,tk->ti", prev_columns, carried_full)
    return (dyn_res, drift_res, cov_res, cost_res, eta_res)


def choose(flag, combined, kept):
    return tuple(jnp.where(flag, new, old) for new, old in zip(combined, kept))


def per_device_general(blocks, pattern, drift, cov, cost, eta):
    height = cov.shape[1]
    modes = cov.shape[2]
    block_size = blocks.shape[2] // 3
    first_row = lax.axis_index("col") * height
    own_ids = first_row + jnp.arange(height, dtype=jnp.int32)
    all_ids = jnp.arange(modes, dtype=jnp.int32)
    position = lax.axis_index("tm")
    dyn_own = densify(blocks, own_ids, pattern, block_size)
    received = shifted((blocks, drift, cov, cost, eta), "tm", 1)
    blocks_prev, blocks_own, drift_prev_full = (
        lax.all_gather(received[0], "col", axis=1, tiled=True),
        lax.all_gather(blocks, "col", axis=1, tiled=True),
        lax.all_gather(received[1], "col", axis=1, tiled=True),
    )
    merged = combine_rows(
        densify(blocks_prev, all_ids, pattern, block_size),
        densify(blocks_own, all_ids, pattern, block_size),
        dyn_own,
        drift_prev_full,
        drift,
        received[2],
        cov,
        received[3],
        cost,
        received[4],
        eta,
        first_row,
    )
    current = choose(position >= 1, merged, (dyn_own, drift, cov, cost, eta))
    received = shifted(current, "tm", 2)
    dyn_prev_full = lax.all_gather(received[0], "col", axis=1, tiled=True)
    dyn_own_full = lax.all_gather(current[0], "col", axis=1, tiled=True)
    drift_prev_full = lax.all_gather(received[1], "col", axis=1, tiled=True)
    merged = combine_rows(
        dyn_prev_full,
        dyn_own_full,
        current[0],
        drift_prev_full,
        current[1],
        received[2],
        current[2],
        received[3],
        current[3],
        received[4],
        current[4],
        first_row,
    )
    return choose(position >= 2, merged, current)


def split(x):
    hi = x.astype(BF16)
    lo = (x - hi.astype(F32)).astype(BF16)
    return hi, lo


def dot(a, b):
    return jnp.dot(a, b, preferred_element_type=F32)


def dot3(ah, al, bh, bl):
    return dot(ah, bh) + (dot(ah, bl) + dot(al, bh))


def triangle(r):
    rows = lax.broadcasted_iota(jnp.int32, (r, r), 0)
    cols = lax.broadcasted_iota(jnp.int32, (r, r), 1)
    return rows, cols


def fold(first, second, r):
    rows, cols = triangle(r)
    return jnp.where(rows >= cols, first, second)


def diagonal(block, r):
    rows, cols = triangle(r)
    return jnp.sum(jnp.where(rows == cols, block, 0.0), axis=0, keepdims=True)


def unfold(folded, second_diag, r):
    rows, cols = triangle(r)
    turned = folded.T
    first = jnp.where(rows >= cols, folded, turned)
    second = jnp.where(rows < cols, folded, turned)
    second = jnp.where(rows == cols, jnp.broadcast_to(second_diag, (r, r)), second)
    return first, second


UPPER = ((0, 1), (0, 2), (0, 3), (1, 2), (1, 3), (2, 3))


def spread(packed, r, put, rows=(0, 1, 2, 3)):
    panel0, panel1, diags = packed[0:r], packed[r : 2 * r], packed[2 * r : 2 * r + 1]
    for at, (panel, pair) in enumerate(((panel0, (0, 1)), (panel1, (2, 3)))):
        if pair[0] in rows or pair[1] in rows:
            blocks = unfold(panel[:, 0:r], diags[:, at * r : (at + 1) * r], r)
            for i, block in zip(pair, blocks):
                if i in rows:
                    put(i, i, block)
    for at, (i, j) in enumerate(UPPER):
        panel = panel0 if at < 3 else panel1
        block = panel[:, (at % 3 + 1) * r : (at % 3 + 2) * r]
        if i in rows:
            put(i, j, block)
        if j in rows:
            put(j, i, block.T)


def column(row, r):
    rows, cols = triangle(r)
    pieces = []
    for at in range(row.shape[1] // r):
        piece = jnp.broadcast_to(row[:, at * r : (at + 1) * r], (r, r))
        pieces.append(jnp.sum(jnp.where(rows == cols, piece, 0.0), axis=1, keepdims=True))
    return jnp.concatenate(pieces, axis=0)


def row_times(row, matrix, r):
    return jnp.sum(column(row, r) * matrix, axis=0, keepdims=True)


def place_of():
    q = lax.axis_index("col")
    return q, q >> 1, q & 1


def has(distance):
    return (lax.axis_index("tm") >= distance).astype(jnp.int32)


def lanes(index, r):
    return pl.ds(pl.multiple_of(index * r, r), r)


def copy_all(pairs, sems):
    copies = [
        pltpu.make_async_copy(source, target, sems.at[i]) for i, (source, target) in enumerate(pairs)
    ]
    for copy in copies:
        copy.start()
    for copy in copies:
        copy.wait()


def send_kernel(
    cov, cost, drift, eta, to_core, to_chip, to_far, panel, vecs, b_in, e_in, sems
):
    q, y, c = place_of()
    r = to_far.shape[1]

    def load(mine, theirs):
        pairs = []
        for j in range(2, 4):
            source = mine.at[1 - y, :, lanes((q ^ 2) ^ j, r)]
            pairs.append((source, to_chip.at[pl.ds(0, r), pl.ds((j - 2) * r, r)]))
        pairs.append((theirs.at[1 - y, :, lanes(q, r)], to_far.at[pl.ds(0, r), :]))
        for j in range(1, 4):
            source = theirs.at[y, :, lanes((q ^ 1) ^ j, r)]
            pairs.append((source, to_core.at[pl.ds(0, r), pl.ds((j - 1) * r, r)]))
        for j in range(4):
            pairs.append((mine.at[y, :, lanes(q ^ j, r)], panel.at[:, pl.ds(j * r, r)]))
        pairs.append((drift, b_in))
        pairs.append((eta, e_in))
        copy_all(pairs, sems)

    @pl.when(c == 0)
    def _():
        load(cov, cost)

    @pl.when(c == 1)
    def _():
        load(cost, cov)

    b, e = b_in[pl.ds(y, 1), :], e_in[pl.ds(y, 1), :]
    vecs[...] = jnp.zeros(vecs.shape, F32)
    vecs[0:1, :] = b
    vecs[1:2, :] = e
    to_core[r : r + 8, :] = jnp.zeros((8, 3 * r), F32)
    to_core[r : r + 1, 0:r] = b
    to_core[r : r + 1, r : 2 * r] = e
    b, e = b_in[pl.ds(1 - y, 1), :], e_in[pl.ds(1 - y, 1), :]
    to_chip[r : r + 8, :] = jnp.zeros((8, 2 * r), F32)
    to_chip[r : r + 1, 0:r] = b
    to_chip[r : r + 1, r : 2 * r] = e
    to_far[r : r + 8, :] = jnp.zeros((8, r), F32)
    to_far[r : r + 1, :] = b
    to_far[r + 1 : r + 2, :] = e


def pack_near_kernel(panel, from_core, packed):
    r = panel.shape[0]
    packed[:, 0:r] = fold(panel[:, 0:r], from_core[0:r, 0:r], r)
    packed[:, r : 4 * r] = panel[:, r:]
    packed[:, 4 * r :] = from_core[0:r, r : 3 * r]


def pack_far_kernel(vecs, from_core, from_chip, from_far, packed):
    r = vecs.shape[1]
    k33 = from_far[0:r, :]
    packed[0:r, 0:r] = fold(from_chip[0:r, 0:r], k33, r)
    packed[0:r, r:] = from_chip[0:r, r : 2 * r]
    packed[r : r + 1, 0:r] = diagonal(from_core[0:r, 0:r], r)
    packed[r : r + 1, r:] = diagonal(k33, r)
    b = (
        vecs[0:1, :],
        from_core[r : r + 1, 0:r],
        from_chip[r : r + 1, 0:r],
        from_far[r : r + 1, :],
    )
    e = (
        vecs[1:2, :],
        from_core[r : r + 1, r : 2 * r],
        from_chip[r : r + 1, r : 2 * r],
        from_far[r + 1 : r + 2, :],
    )
    for j in range(4):
        at = slice(j % 2 * r, (j % 2 + 1) * r)
        packed[r + 1 + j // 2 : r + 2 + j // 2, at] = b[j]
        packed[r + 3 + j // 2 : r + 4 + j // 2, at] = e[j]
    packed[r + 5 : r + 8, :] = jnp.zeros((3, 2 * r), F32)


def far_row(packed, r, at):
    return jnp.concatenate(
        [packed[r + at : r + at + 1, :], packed[r + at + 1 : r + at + 2, :]], axis=1
    )


def pick_kernel(turned, before, out):
    y = place_of()[1]
    height = turned.shape[1]
    out[0:height, :] = turned[1 - y]
    out[height:, :] = before[1 - y]


def halves_kernel(turned, before, other, out):
    y = place_of()[1]
    height = turned.shape[1]
    out[0:height, :] = turned[y]
    out[height : 2 * height, :] = other[0:height, :]
    out[2 * height : 3 * height, :] = before[y]
    out[3 * height :, :] = other[height:, :]


def dense_turned(put, pattern, own_half, core_half, flag, n, r, bs):
    q = place_of()[0]
    lane = lax.broadcasted_iota(jnp.int32, (bs, r), 1) // bs
    rows = lax.broadcasted_iota(jnp.int32, (bs, r), 0)
    cols = lax.broadcasted_iota(jnp.int32, (bs, r), 1)
    per = r // bs
    height = 3 * bs
    for j in range(4):
        half = own_half if j % 2 == 0 else core_half
        full = half[(j // 2) * height : (j // 2 + 1) * height, :]
        wanted = []
        for k in range(3):
            want = jnp.zeros((bs, r), jnp.int32)
            for h in range(per):
                block = pattern[pl.ds((q ^ j) * per + h, 1), :][:, k : k + 1] ^ (q * per)
                want = jnp.where(lane == h, jnp.broadcast_to(block, (bs, r)), want)
            wanted.append(jnp.where(flag == 1, want, -1))
        for block in range(n // bs):
            if j * r <= block * bs < (j + 1) * r:
                value = jnp.where(
                    jnp.logical_and(rows + block * bs == cols + j * r, flag == 0), 1.0, 0.0
                )
            else:
                value = jnp.zeros((bs, r), F32)
            for k in range(3):
                piece = full[k * bs : (k + 1) * bs, :]
                value = value + jnp.where(wanted[k] == block, piece, 0.0)
            put(slice(block * bs, (block + 1) * bs), slice(j * r, (j + 1) * r), value)


def put_split(hi_ref, lo_ref, rows, cols, value):
    hi, lo = split(value)
    hi_ref[rows, cols] = hi
    lo_ref[rows, cols] = lo


def transpose_split(hi_ref, lo_ref, source, r):
    n = source.shape[0]
    for i in range(n // r):
        for j in range(n // r):
            put_split(
                hi_ref,
                lo_ref,
                slice(j * r, (j + 1) * r),
                slice(i * r, (i + 1) * r),
                source[i * r : (i + 1) * r, j * r : (j + 1) * r].T,
            )


def straight_split(hi_ref, lo_ref, source, r):
    n = source.shape[0]
    for i in range(n // r):
        put_split(
            hi_ref, lo_ref, slice(i * r, (i + 1) * r), slice(None), source[i * r : (i + 1) * r, :]
        )


def prepare_kernel(bs, pattern, halves, core_halves, mh, ml, th, tl, dense):
    c, has1 = place_of()[2], has(1)
    n = dense.shape[0]
    r = halves.shape[1]
    half = halves.shape[0] // 2
    first = c == 0
    own_half = jnp.where(first, halves[0:half, :], halves[half:, :])
    core_half = jnp.where(first, core_halves[0:half, :], core_halves[half:, :])
    flag = jnp.where(first, 1, has1)

    def put(row, col, value):
        dense[row, col] = value

    dense_turned(put, pattern, own_half, core_half, flag, n, r, bs)

    @pl.when(first)
    def _():
        straight_split(mh, ml, dense, r)
        transpose_split(th, tl, dense, r)

    @pl.when(jnp.logical_not(first))
    def _():
        straight_split(th, tl, dense, r)
        transpose_split(mh, ml, dense, r)


def level1_kernel(
    own_near, own_far, near, far, mh, ml, th, tl, out, full, xh, xl
):
    c = place_of()[2]
    r = own_near.shape[0]
    first = c == 0
    xn = jnp.where(first, near[...], own_near[...])
    xf = jnp.where(first, far[...], own_far[...])
    x = jnp.concatenate(
        [
            xn[:, 0 : 4 * r],
            jnp.concatenate([xf[0:r, 0:r], xn[:, 4 * r :], xf[0:r, r:]], axis=1),
            jnp.concatenate([xf[r : r + 1, :], xf[r : r + 1, :]], axis=1),
        ],
        axis=0,
    )

    def put(i, j, block):
        full[i * r : (i + 1) * r, j * r : (j + 1) * r] = block
        put_split(xh, xl, slice(i * r, (i + 1) * r), slice(j * r, (j + 1) * r), block)

    spread(x, r, put)
    b_before, b_own = far_row(far, r, 1), far_row(own_far, r, 1)
    e_before, e_own = far_row(far, r, 3), far_row(own_far, r, 3)
    carried = jnp.where(first, b_before, e_own + row_times(b_before, full[...], r))
    vec = jnp.where(first, b_own, e_before) + row_times(
        carried, mh[...].astype(F32) + ml[...].astype(F32), r
    )
    u = dot3(xh[...], xl[...], mh[...], ml[...])
    uh, ul = split(u)
    top = dot3(th[0 : 2 * r, :], tl[0 : 2 * r, :], uh, ul)
    low = dot3(th[2 * r :, :], tl[2 * r :, :], uh[:, 2 * r :], ul[:, 2 * r :])
    dn = jnp.where(first, own_near[...], near[...])
    df = jnp.where(first, own_far[...], far[...])
    z11 = top[r : 2 * r, r : 2 * r]
    z33 = low[r : 2 * r, r : 2 * r]
    out[0:r, 0:r] = fold(top[0:r, 0:r], z11, r) + dn[:, 0:r]
    out[0:r, r:] = top[0:r, r:] + dn[:, r : 4 * r]
    out[r : 2 * r, 0:r] = fold(low[0:r, 0:r], z33, r) + df[0:r, 0:r]
    out[r : 2 * r, r : 3 * r] = top[r : 2 * r, 2 * r :] + dn[:, 4 * r :]
    out[r : 2 * r, 3 * r :] = low[0:r, r : 2 * r] + df[0:r, r:]
    base = 2 * r
    out[base : base + 1, 0:r] = diagonal(z11, r) + df[r : r + 1, 0:r]
    out[base : base + 1, r : 2 * r] = diagonal(z33, r) + df[r : r + 1, r:]
    out[base : base + 1, 2 * r :] = jnp.zeros((1, 2 * r), F32)
    out[base + 1 : base + 2, :] = b_own
    out[base + 2 : base + 3, :] = vec
    out[base + 3 : base + 4, :] = b_before
    out[base + 4 : base + 8, :] = jnp.zeros((4, 4 * r), F32)


def early_kernel(bs, pattern, halves, core_halves, a0h, a0l, a1h, a1l, t):
    n = a0h.shape[0]
    r = halves.shape[1]
    half = halves.shape[0] // 2
    for at, flag, hi, lo in ((0, 1, a0h, a0l), (1, has(1), a1h, a1l)):
        rows = slice(at * half, (at + 1) * half)
        put = functools.partial(put_split, hi, lo)
        dense_turned(put, pattern, halves[rows, :], core_halves[rows, :], flag, n, r, bs)

    def wanted(ref):
        return jnp.concatenate([ref[:, 0:r], ref[:, 2 * r : 3 * r]], axis=1)

    t[...] = dot3(a1h[...], a1l[...], wanted(a0h), wanted(a0l))


def rows_kernel(
    bs, pattern, halves, core_halves, t, dyn_own, dyn_send, a2, a2h, a2l, a3h, a3l
):
    q, _, _ = place_of()
    n = a2.shape[0]
    r = halves.shape[1]
    half = halves.shape[0] // 2

    def put2(row, col, value):
        put_split(a2h, a2l, row, col, value)
        a2[row, col] = value

    def put3(row, col, value):
        put_split(a3h, a3l, row, col, value)

    for at, flag, put in ((0, has(2), put2), (1, has(3), put3)):
        rows = slice(at * half, (at + 1) * half)
        dense_turned(put, pattern, halves[rows, :], core_halves[rows, :], flag, n, r, bs)
    rows = dot3(a2h[...], a2l[...], *split(t[...]))
    rows = dot3(a3h[...], a3l[...], *split(rows))
    for j in range(4):
        at = lanes(q ^ j, r)
        dyn_own[:, at] = rows[j * r : (j + 1) * r, 0:r].T
        dyn_send[:, at] = rows[j * r : (j + 1) * r, r : 2 * r].T


def product_kernel(
    a0h, a0l, a1h, a1l, a2h, a2l, a3h, a3l, mh, ml, th, tl, product_ref
):
    first = place_of()[2] == 0
    r = a0h.shape[0] // 4

    @pl.when(first)
    def _():
        product_ref[...] = dot3(a1h[...], a1l[...], a0h[...], a0l[...])
        straight_split(mh, ml, product_ref, r)
        transpose_split(th, tl, product_ref, r)

    @pl.when(jnp.logical_not(first))
    def _():
        product_ref[...] = dot3(a3h[...], a3l[...], a2h[...], a2l[...])
        straight_split(th, tl, product_ref, r)
        transpose_split(mh, ml, product_ref, r)


def ahead_kernel(own, mh, ml, th, tl, full, z, xh, xl):
    r = own.shape[1] // 4

    def put(i, j, block):
        full[i * r : (i + 1) * r, j * r : (j + 1) * r] = block

    spread(own, r, put)

    @pl.when(place_of()[2] == 1)
    def _():
        straight_split(xh, xl, full, r)
        u = dot3(xh[...], xl[...], mh[...], ml[...])
        z[...] = dot3(th[...], tl[...], *split(u))


def put_rows(ref, value, q, r):
    for j in range(4):
        ref[lanes(q ^ j, r), :] = value[:, j * r : (j + 1) * r]


CROSSING = ((2, 0), (2, 1), (2, 3))


def level2_kernel(own, earlier, mh, ml, th, tl, full, z, to_chip, uh, ul, xh, xl, rest):
    c = place_of()[2]
    r = own.shape[1] // 4
    two, three = slice(2 * r, 3 * r), slice(3 * r, 4 * r)

    @pl.when(c == 0)
    def _():
        def put(i, j, block):
            put_split(xh, xl, slice(i * r, (i + 1) * r), slice(j * r, (j + 1) * r), block)

        spread(earlier, r, put)
        hi, lo = split(dot3(xh[...], xl[...], mh[...], ml[...]))
        uh[...] = hi
        ul[...] = lo
        rest[:, 2 * r :] = dot3(th[2 * r :, :], tl[2 * r :, :], hi[:, 2 * r :], lo[:, 2 * r :])
        rest[0:r, 0 : 2 * r] = dot3(th[two, :], tl[two, :], hi[:, 0 : 2 * r], lo[:, 0 : 2 * r])
        rest[:, 2 * r :] = rest[:, 2 * r :] + full[2 * r :, 2 * r :]
        rest[0:r, 0 : 2 * r] = rest[0:r, 0 : 2 * r] + full[two, 0 : 2 * r]

    @pl.when(c == 1)
    def _():
        def put(i, j, block):
            if (i, j) in CROSSING or i == j:
                rows = slice((i - 2) * r, (i - 1) * r)
                cols = slice(j * r, (j + 1) * r)
                rest[rows, cols] = z[i * r : (i + 1) * r, cols] + block

        spread(earlier, r, put, rows=(2, 3))

    z33 = rest[r : 2 * r, three]
    to_chip[0:r, :] = fold(rest[0:r, two], z33, r)
    for at, (_, j) in enumerate(CROSSING):
        to_chip[(at + 1) * r : (at + 2) * r, :] = rest[0:r, j * r : (j + 1) * r]
    to_chip[4 * r :, :] = jnp.broadcast_to(diagonal(z33, r), (8, r))


def far_rows_kernel(
    own, earlier, mh, ml, th, tl, a2, full, z, uh, ul, to_far, short, vec, rest
):
    c = place_of()[2]
    r = own.shape[1] // 4
    base = 2 * r
    three = slice(3 * r, 4 * r)
    b1 = earlier[base + 1 : base + 2, :] + row_times(earlier[base + 3 : base + 4, :], a2[...], r)

    @pl.when(c == 0)
    def _():
        value = dot3(th[three, :], tl[three, :], uh[:, 0 : 2 * r], ul[:, 0 : 2 * r])
        rest[...] = value + full[three, 0 : 2 * r]
        vec[0:1, :] = b1
        vec[1:2, :] = own[base + 2 : base + 3, :]

    @pl.when(c == 1)
    def _():
        def put(i, j, block):
            if j < 2:
                cols = slice(j * r, (j + 1) * r)
                rest[:, cols] = z[three, cols] + block

        spread(earlier, r, put, rows=(3,))
        vec[0:1, :] = own[base + 2 : base + 3, :] + row_times(b1, full[...], r)
        vec[1:2, :] = earlier[base + 2 : base + 3, :]

    to_far[0:r, :] = rest[:, 0:r]
    to_far[r : 2 * r, :] = rest[:, r : 2 * r]
    out = vec[1:2, :] + row_times(vec[0:1, :], mh[...].astype(F32) + ml[...].astype(F32), r)
    to_far[2 * r :, :] = jnp.broadcast_to(out[:, 3 * r :], (8, r))
    for i in range(4):
        short[i : i + 1, :] = out[:, i * r : (i + 1) * r]
    short[4:8, :] = jnp.zeros((4, r), F32)


def rest_kernel(earlier, th, tl, full, z, uh, ul, short, keep, to_core, rest):
    q, _, c = place_of()
    r = earlier.shape[1] // 4

    @pl.when(c == 0)
    def _():
        rest[...] = dot3(th[0 : 2 * r, :], tl[0 : 2 * r, :], uh[...], ul[...]) + full[0 : 2 * r, :]

    @pl.when(c == 1)
    def _():
        def put(i, j, block):
            rows = slice(i * r, (i + 1) * r)
            cols = slice(j * r, (j + 1) * r)
            rest[rows, cols] = z[rows, cols] + block

        spread(earlier, r, put, rows=(0, 1))

    put_rows(keep, rest[0:r, :], q, r)
    put_rows(to_core, rest[r : 2 * r, :], q, r)
    to_core[4 * r :, :] = jnp.broadcast_to(short[1:2, :], (8, r))


def turn_kernel(from_chip, diagonal_block, mirrored):
    r = diagonal_block.shape[0]
    first, second = unfold(from_chip[0:r, :], from_chip[4 * r : 4 * r + 1, :], r)
    diagonal_block[...] = first
    mirrored[0:r, :] = from_chip[3 * r : 4 * r, :].T
    mirrored[r : 2 * r, :] = second


def panel_copies(panel, target, element, r):
    return [
        (panel.at[pl.ds(g * r, r), :], target.at[element, :, pl.ds(g * r, r)]) for g in range(4)
    ]


def block_copies(blocks, target, element, r):
    return [(source, target.at[element, :, lanes(at, r)]) for source, at in blocks]


def fill_kernel(
    keep,
    from_core,
    dyn_own,
    dyn_recv,
    diagonal_block,
    from_chip,
    dyn_out,
    cov_out,
    cost_out,
    sems,
):
    q, y, c = place_of()
    r = dyn_own.shape[0]
    dyn = [(dyn_own, dyn_out.at[y]), (dyn_recv, dyn_out.at[1 - y])]
    blocks = [(diagonal_block, q)] + [
        (from_chip.at[pl.ds(at * r, r), :], q ^ bit) for at, bit in ((1, 2), (2, 3), (3, 1))
    ]

    def write(mine, other):
        copy_all(
            dyn
            + panel_copies(keep, mine, y, r)
            + panel_copies(from_core, other, y, r)
            + block_copies(blocks, mine, 1 - y, r),
            sems,
        )

    @pl.when(c == 0)
    def _():
        write(cov_out, cost_out)

    @pl.when(c == 1)
    def _():
        write(cost_out, cov_out)


def place_kernel(
    cov_in,
    cost_in,
    short,
    chip_short,
    from_core,
    mirrored,
    panel,
    cov_out,
    cost_out,
    drift_out,
    eta_out,
    lines,
    sems,
):
    del cov_in, cost_in
    q, y, c = place_of()
    first = c == 0
    r = short.shape[1]
    mine, other = short[0:1, :], from_core[4 * r : 4 * r + 1, :]
    chip, far = chip_short[2:3, :], panel[2 * r : 2 * r + 1, :]
    for at, (one, two, three, four) in enumerate(
        ((mine, other, chip, far), (other, mine, far, chip))
    ):
        lines[at, pl.ds(y, 1), :] = jnp.where(first, one, two)
        lines[at, pl.ds(1 - y, 1), :] = jnp.where(first, three, four)
    vectors = [(lines.at[0], drift_out), (lines.at[1], eta_out)]
    near, far = pl.ds(0, r), pl.ds(r, r)
    blocks = [
        (panel.at[near, :], q ^ 3),
        (panel.at[far, :], q ^ 2),
        (mirrored.at[near, :], q ^ 1),
        (mirrored.at[far, :], q),
    ]

    @pl.when(first)
    def _():
        copy_all(vectors + block_copies(blocks, cost_out, 1 - y, r), sems)

    @pl.when(c == 1)
    def _():
        copy_all(vectors + block_copies(blocks, cov_out, 1 - y, r), sems)


IN_HBM, IN_VMEM = 0, 1


def kernel(body, operands, shapes, scratch=(), aliases=None):
    specs = {
        IN_HBM: pl.BlockSpec(memory_space=pltpu.HBM),
        IN_VMEM: pl.BlockSpec(memory_space=pltpu.VMEM),
    }
    call = pl.pallas_call(
        body,
        in_specs=[specs[where] for where, _ in operands],
        out_specs=[specs[where] for where, _ in shapes],
        out_shape=[
            pltpu.VMEM(s.shape, s.dtype) if where == IN_VMEM else s for where, s in shapes
        ],
        scratch_shapes=list(scratch),
        input_output_aliases=aliases or {},
        compiler_params=pltpu.CompilerParams(vmem_limit_bytes=20 * 2**20),
    )
    kept = {IN_HBM: pltpu.HBM, IN_VMEM: pltpu.VMEM}
    return call(
        *(
            pltpu.with_memory_space_constraint(x, kept[where]) if where in kept else x
            for where, x in operands
        )
    )


def per_device_split(blocks, pattern, drift, cov, cost, eta):
    elements, r, n = cov.shape
    bs = blocks.shape[2] // 3
    tms, cols = lax.axis_size("tm"), lax.axis_size("col")

    def swap(value, bit):
        return lax.ppermute(value, "col", [(i, i ^ bit) for i in range(cols)])

    def later(value, distance):
        return lax.ppermute(value, "tm", [(i, i + distance) for i in range(tms - distance)])

    def hbm(*arrays):
        return [(IN_HBM, x) for x in arrays]

    def vmem(*arrays):
        return [(IN_VMEM, x) for x in arrays]

    def shape(*dims):
        return jax.ShapeDtypeStruct(dims, F32)

    def half(*dims):
        return jax.ShapeDtypeStruct(dims, BF16)

    def square(dtype):
        return pltpu.VMEM((n, n), dtype)

    def sems(count):
        return pltpu.SemaphoreType.DMA((count,))

    turned = jnp.swapaxes(blocks, 1, 2)
    before = later(turned, 1)
    to_core, to_chip, to_far, panel, vecs = kernel(
        send_kernel,
        hbm(cov, cost, drift, eta),
        vmem(shape(r + 8, 3 * r), shape(r + 8, 2 * r), shape(r + 8, r), shape(r, n), shape(8, r)),
        [pltpu.VMEM(drift.shape, F32), pltpu.VMEM(eta.shape, F32), sems(12)],
    )
    from_core = swap(to_core, 1)
    from_chip = swap(to_chip, 2)
    from_far = swap(to_far, 3)
    (own_near,) = kernel(pack_near_kernel, vmem(panel, from_core), vmem(shape(r, 6 * r)))
    near = later(own_near, 1)
    (own_far,) = kernel(
        pack_far_kernel, vmem(vecs, from_core, from_chip, from_far), vmem(shape(r + 8, 2 * r))
    )
    far = later(own_far, 1)
    (picked,) = kernel(pick_kernel, vmem(turned, before), vmem(shape(6 * bs, r)))
    other = swap(picked, 2)
    (halves,) = kernel(halves_kernel, vmem(turned, before, other), vmem(shape(12 * bs, r)))
    core_halves = swap(halves, 1)
    far_halves = later(halves, 2)
    m1 = kernel(
        functools.partial(prepare_kernel, bs),
        vmem(pattern, halves, core_halves),
        vmem(*[half(n, n)] * 4),
        [square(F32)],
    )
    (level1,) = kernel(
        level1_kernel,
        vmem(own_near, own_far, near, far, *m1),
        vmem(shape(2 * r + 8, n)),
        [square(F32)] + [square(BF16)] * 2,
    )
    earlier = later(level1, 2)
    *a01, t = kernel(
        functools.partial(early_kernel, bs),
        vmem(pattern, halves, core_halves),
        vmem(*[half(n, n)] * 4, shape(n, 2 * r)),
    )
    far_core_halves = swap(far_halves, 1)
    dyn_own, dyn_send, a2, *a23 = kernel(
        functools.partial(rows_kernel, bs),
        vmem(pattern, far_halves, far_core_halves, t),
        vmem(shape(r, n), shape(r, n), shape(n, n), *[half(n, n)] * 4),
    )
    dyn_recv = swap(dyn_send, 2)
    m2 = kernel(product_kernel, vmem(*a01, *a23), vmem(*[half(n, n)] * 4), [square(F32)])
    full, z = kernel(
        ahead_kernel, vmem(level1, *m2), vmem(shape(n, n), shape(n, n)), [square(BF16)] * 2
    )
    to_chip, *u = kernel(
        level2_kernel,
        vmem(level1, earlier, *m2, full, z),
        vmem(shape(n + 8, r), half(n, n), half(n, n)),
        [square(BF16)] * 2 + [pltpu.VMEM((2 * r, n), F32)],
    )
    from_chip = swap(to_chip, 2)
    to_far, short = kernel(
        far_rows_kernel,
        vmem(level1, earlier, *m2, a2, full, z, *u),
        vmem(shape(2 * r + 8, r), shape(8, r)),
        [pltpu.VMEM((8, n), F32), pltpu.VMEM((r, 2 * r), F32)],
    )
    chip_short = swap(short, 2)
    from_far = swap(to_far, 3)
    keep, to_core = kernel(
        rest_kernel,
        vmem(earlier, *m2[2:], full, z, *u, short),
        vmem(shape(n, r), shape(n + 8, r)),
        [pltpu.VMEM((2 * r, n), F32)],
    )
    from_core = swap(to_core, 1)
    diagonal_block, mirrored = kernel(
        turn_kernel, vmem(from_chip), vmem(shape(r, r), shape(2 * r, r))
    )
    mirrored = swap(mirrored, 1)
    whole, line = shape(elements, r, n), shape(elements, r)
    dyn_out, cov_out, cost_out = kernel(
        fill_kernel,
        vmem(keep, from_core, dyn_own, dyn_recv, diagonal_block, from_chip),
        hbm(whole, whole, whole),
        [sems(14)],
    )
    cov_out, cost_out, drift_out, eta_out = kernel(
        place_kernel,
        hbm(cov_out, cost_out) + vmem(short, chip_short, from_core, mirrored, from_far),
        hbm(whole, whole, line, line),
        [pltpu.VMEM((2, elements, r), F32), sems(6)],
        {0: 0, 1: 1},
    )
    return dyn_out, drift_out, cov_out, cost_out, eta_out


def takes_split(elements, r, bs, cols):
    return elements == 2 and cols == 4 and r % 128 == 0 and r % bs == 0 and bs % 8 == 0


def per_device(blocks, pattern, drift, cov, cost, eta):
    elements, r, _ = cov.shape
    bs = blocks.shape[2] // 3
    if takes_split(elements, r, bs, lax.axis_size("col")):
        return per_device_split(blocks, pattern, drift, cov, cost, eta)
    return per_device_general(blocks, pattern, drift, cov, cost, eta)


def solution(mesh):
    return jax.shard_map(
        per_device,
        mesh=mesh,
        in_specs=(
            P("tm", "col", None),
            P(),
            P("tm", "col"),
            P("tm", "col", None),
            P("tm", "col", None),
            P("tm", "col"),
        ),
        out_specs=(
            P("tm", "col", None),
            P("tm", "col"),
            P("tm", "col", None),
            P("tm", "col", None),
            P("tm", "col"),
        ),
        check_vma=False,
    )
```

```python
import functools

import jax
import jax.numpy as jnp
from jax import lax
from jax.experimental import pallas as pl
from jax.experimental.pallas import tpu as pltpu
from jax.sharding import PartitionSpec as P


HIGH = lax.Precision.HIGHEST
F32 = jnp.float32
BF16 = jnp.bfloat16


def shifted(block, axis, distance):
    devices = range(lax.axis_size(axis))
    route = [(i - distance, i) for i in devices if i - distance in devices]
    return lax.ppermute(block, axis, route)


def product(form, left, right):
    return jnp.einsum(form, left, right, precision=HIGH)


def densify(row_blocks, row_ids, pattern, block_size):
    block_count = pattern.shape[0]
    row_block = row_ids // block_size
    chooser = (row_block[:, None] == jnp.arange(block_count, dtype=jnp.int32)[None, :]).astype(
        jnp.int32
    )
    columns = jnp.sum(chooser[:, :, None] * pattern[None, :, :], axis=1)
    matches = (
        columns[:, :, None] == jnp.arange(block_count, dtype=jnp.int32)[None, None, :]
    ).astype(jnp.float32)
    pieces = row_blocks.reshape(row_blocks.shape[:-1] + (3, 1, block_size))
    filled = jnp.sum(matches[:, :, :, None] * pieces, axis=-3)
    return filled.reshape(row_blocks.shape[:-1] + (block_count * block_size,))


def combine_rows(
    dyn_prev_full,
    dyn_own_full,
    dyn_own,
    drift_prev_full,
    drift_own,
    cov_prev,
    cov_own,
    cost_prev,
    cost_own,
    eta_prev,
    eta_own,
    first_row,
):
    height = dyn_own.shape[1]
    dyn_res = product("tij,tjk->tik", dyn_own, dyn_prev_full)
    drift_res = product("tij,tj->ti", dyn_own, drift_prev_full) + drift_own
    carried = eta_own + product("tij,tj->ti", cost_own, drift_prev_full)
    value_rows = product("tij,tjk->tik", cost_own, dyn_prev_full)
    prev_columns = lax.dynamic_slice_in_dim(dyn_prev_full, first_row, height, 2)
    cov_full, carried_full, value_full = (
        lax.all_gather(cov_prev, "col", axis=1, tiled=True),
        lax.all_gather(carried, "col", axis=1, tiled=True),
        lax.all_gather(value_rows, "col", axis=1, tiled=True),
    )
    cost_res = cost_prev + product("tki,tkj->tij", prev_columns, value_full)
    cov_res = (
        product("tik,tjk->tij", product("tij,tjk->tik", dyn_own, cov_full), dyn_own_full) + cov_own
    )
    eta_res = eta_prev + product("tki,tk->ti", prev_columns, carried_full)
    return (dyn_res, drift_res, cov_res, cost_res, eta_res)


def choose(flag, combined, kept):
    return tuple(jnp.where(flag, new, old) for new, old in zip(combined, kept))


def per_device_general(blocks, pattern, drift, cov, cost, eta):
    height = cov.shape[1]
    modes = cov.shape[2]
    block_size = blocks.shape[2] // 3
    first_row = lax.axis_index("col") * height
    own_ids = first_row + jnp.arange(height, dtype=jnp.int32)
    all_ids = jnp.arange(modes, dtype=jnp.int32)
    position = lax.axis_index("tm")
    dyn_own = densify(blocks, own_ids, pattern, block_size)
    received = shifted((blocks, drift, cov, cost, eta), "tm", 1)
    blocks_prev, blocks_own, drift_prev_full = (
        lax.all_gather(received[0], "col", axis=1, tiled=True),
        lax.all_gather(blocks, "col", axis=1, tiled=True),
        lax.all_gather(received[1], "col", axis=1, tiled=True),
    )
    merged = combine_rows(
        densify(blocks_prev, all_ids, pattern, block_size),
        densify(blocks_own, all_ids, pattern, block_size),
        dyn_own,
        drift_prev_full,
        drift,
        received[2],
        cov,
        received[3],
        cost,
        received[4],
        eta,
        first_row,
    )
    current = choose(position >= 1, merged, (dyn_own, drift, cov, cost, eta))
    received = shifted(current, "tm", 2)
    dyn_prev_full = lax.all_gather(received[0], "col", axis=1, tiled=True)
    dyn_own_full = lax.all_gather(current[0], "col", axis=1, tiled=True)
    drift_prev_full = lax.all_gather(received[1], "col", axis=1, tiled=True)
    merged = combine_rows(
        dyn_prev_full,
        dyn_own_full,
        current[0],
        drift_prev_full,
        current[1],
        received[2],
        current[2],
        received[3],
        current[3],
        received[4],
        current[4],
        first_row,
    )
    return choose(position >= 2, merged, current)


def split(x):
    hi = x.astype(BF16)
    lo = (x - hi.astype(F32)).astype(BF16)
    return hi, lo


def dot(a, b):
    return jnp.dot(a, b, preferred_element_type=F32)


def dot3(ah, al, bh, bl):
    return dot(ah, bh) + (dot(ah, bl) + dot(al, bh))


def triangle(r):
    rows = lax.broadcasted_iota(jnp.int32, (r, r), 0)
    cols = lax.broadcasted_iota(jnp.int32, (r, r), 1)
    return rows, cols


def fold(first, second, r):
    rows, cols = triangle(r)
    return jnp.where(rows >= cols, first, second)


def diagonal(block, r):
    rows, cols = triangle(r)
    return jnp.sum(jnp.where(rows == cols, block, 0.0), axis=0, keepdims=True)


def unfold(folded, second_diag, r):
    rows, cols = triangle(r)
    turned = folded.T
    first = jnp.where(rows >= cols, folded, turned)
    second = jnp.where(rows < cols, folded, turned)
    second = jnp.where(rows == cols, jnp.broadcast_to(second_diag, (r, r)), second)
    return first, second


UPPER = ((0, 1), (0, 2), (0, 3), (1, 2), (1, 3), (2, 3))


def spread(packed, r, put, rows=(0, 1, 2, 3)):
    panel0, panel1, diags = packed[0:r], packed[r : 2 * r], packed[2 * r : 2 * r + 1]
    for at, (panel, pair) in enumerate(((panel0, (0, 1)), (panel1, (2, 3)))):
        if pair[0] in rows or pair[1] in rows:
            blocks = unfold(panel[:, 0:r], diags[:, at * r : (at + 1) * r], r)
            for i, block in zip(pair, blocks):
                if i in rows:
                    put(i, i, block)
    for at, (i, j) in enumerate(UPPER):
        panel = panel0 if at < 3 else panel1
        block = panel[:, (at % 3 + 1) * r : (at % 3 + 2) * r]
        if i in rows:
            put(i, j, block)
        if j in rows:
            put(j, i, block.T)


def column(row, r):
    rows, cols = triangle(r)
    pieces = []
    for at in range(row.shape[1] // r):
        piece = jnp.broadcast_to(row[:, at * r : (at + 1) * r], (r, r))
        pieces.append(jnp.sum(jnp.where(rows == cols, piece, 0.0), axis=1, keepdims=True))
    return jnp.concatenate(pieces, axis=0)


def row_times(row, matrix, r):
    return jnp.sum(column(row, r) * matrix, axis=0, keepdims=True)


def place_of():
    q = lax.axis_index("col")
    return q, q >> 1, q & 1


def has(distance):
    return (lax.axis_index("tm") >= distance).astype(jnp.int32)


def lanes(index, r):
    return pl.ds(pl.multiple_of(index * r, r), r)


def copy_all(pairs, sems):
    copies = [
        pltpu.make_async_copy(source, target, sems.at[i]) for i, (source, target) in enumerate(pairs)
    ]
    for copy in copies:
        copy.start()
    for copy in copies:
        copy.wait()


def send_kernel(
    cov, cost, drift, eta, to_core, to_chip, to_far, panel, vecs, b_in, e_in, sems
):
    q, y, c = place_of()
    r = to_far.shape[1]

    def load(mine, theirs):
        pairs = []
        for j in range(2, 4):
            source = mine.at[1 - y, :, lanes((q ^ 2) ^ j, r)]
            pairs.append((source, to_chip.at[pl.ds(0, r), pl.ds((j - 2) * r, r)]))
        pairs.append((theirs.at[1 - y, :, lanes(q, r)], to_far.at[pl.ds(0, r), :]))
        for j in range(1, 4):
            source = theirs.at[y, :, lanes((q ^ 1) ^ j, r)]
            pairs.append((source, to_core.at[pl.ds(0, r), pl.ds((j - 1) * r, r)]))
        for j in range(4):
            pairs.append((mine.at[y, :, lanes(q ^ j, r)], panel.at[:, pl.ds(j * r, r)]))
        pairs.append((drift, b_in))
        pairs.append((eta, e_in))
        copy_all(pairs, sems)

    @pl.when(c == 0)
    def _():
        load(cov, cost)

    @pl.when(c == 1)
    def _():
        load(cost, cov)

    b, e = b_in[pl.ds(y, 1), :], e_in[pl.ds(y, 1), :]
    vecs[...] = jnp.zeros(vecs.shape, F32)
    vecs[0:1, :] = b
    vecs[1:2, :] = e
    to_core[r : r + 8, :] = jnp.zeros((8, 3 * r), F32)
    to_core[r : r + 1, 0:r] = b
    to_core[r : r + 1, r : 2 * r] = e
    b, e = b_in[pl.ds(1 - y, 1), :], e_in[pl.ds(1 - y, 1), :]
    to_chip[r : r + 8, :] = jnp.zeros((8, 2 * r), F32)
    to_chip[r : r + 1, 0:r] = b
    to_chip[r : r + 1, r : 2 * r] = e
    to_far[r : r + 8, :] = jnp.zeros((8, r), F32)
    to_far[r : r + 1, :] = b
    to_far[r + 1 : r + 2, :] = e


def pack_near_kernel(panel, from_core, packed):
    r = panel.shape[0]
    packed[:, 0:r] = fold(panel[:, 0:r], from_core[0:r, 0:r], r)
    packed[:, r : 4 * r] = panel[:, r:]
    packed[:, 4 * r :] = from_core[0:r, r : 3 * r]


def pack_far_kernel(vecs, from_core, from_chip, from_far, packed):
    r = vecs.shape[1]
    k33 = from_far[0:r, :]
    packed[0:r, 0:r] = fold(from_chip[0:r, 0:r], k33, r)
    packed[0:r, r:] = from_chip[0:r, r : 2 * r]
    packed[r : r + 1, 0:r] = diagonal(from_core[0:r, 0:r], r)
    packed[r : r + 1, r:] = diagonal(k33, r)
    b = (
        vecs[0:1, :],
        from_core[r : r + 1, 0:r],
        from_chip[r : r + 1, 0:r],
        from_far[r : r + 1, :],
    )
    e = (
        vecs[1:2, :],
        from_core[r : r + 1, r : 2 * r],
        from_chip[r : r + 1, r : 2 * r],
        from_far[r + 1 : r + 2, :],
    )
    for j in range(4):
        at = slice(j % 2 * r, (j % 2 + 1) * r)
        packed[r + 1 + j // 2 : r + 2 + j // 2, at] = b[j]
        packed[r + 3 + j // 2 : r + 4 + j // 2, at] = e[j]
    packed[r + 5 : r + 8, :] = jnp.zeros((3, 2 * r), F32)


def far_row(packed, r, at):
    return jnp.concatenate(
        [packed[r + at : r + at + 1, :], packed[r + at + 1 : r + at + 2, :]], axis=1
    )


def pick_kernel(turned, before, out):
    y = place_of()[1]
    height = turned.shape[1]
    out[0:height, :] = turned[1 - y]
    out[height:, :] = before[1 - y]


def halves_kernel(turned, before, other, out):
    y = place_of()[1]
    height = turned.shape[1]
    out[0:height, :] = turned[y]
    out[height : 2 * height, :] = other[0:height, :]
    out[2 * height : 3 * height, :] = before[y]
    out[3 * height :, :] = other[height:, :]


def dense_turned(put, pattern, own_half, core_half, flag, n, r, bs):
    q = place_of()[0]
    lane = lax.broadcasted_iota(jnp.int32, (bs, r), 1) // bs
    rows = lax.broadcasted_iota(jnp.int32, (bs, r), 0)
    cols = lax.broadcasted_iota(jnp.int32, (bs, r), 1)
    per = r // bs
    height = 3 * bs
    for j in range(4):
        half = own_half if j % 2 == 0 else core_half
        full = half[(j // 2) * height : (j // 2 + 1) * height, :]
        wanted = []
        for k in range(3):
            want = jnp.zeros((bs, r), jnp.int32)
            for h in range(per):
                block = pattern[pl.ds((q ^ j) * per + h, 1), :][:, k : k + 1] ^ (q * per)
                want = jnp.where(lane == h, jnp.broadcast_to(block, (bs, r)), want)
            wanted.append(jnp.where(flag == 1, want, -1))
        for block in range(n // bs):
            if j * r <= block * bs < (j + 1) * r:
                value = jnp.where(
                    jnp.logical_and(rows + block * bs == cols + j * r, flag == 0), 1.0, 0.0
                )
            else:
                value = jnp.zeros((bs, r), F32)
            for k in range(3):
                piece = full[k * bs : (k + 1) * bs, :]
                value = value + jnp.where(wanted[k] == block, piece, 0.0)
            put(slice(block * bs, (block + 1) * bs), slice(j * r, (j + 1) * r), value)


def put_split(hi_ref, lo_ref, rows, cols, value):
    hi, lo = split(value)
    hi_ref[rows, cols] = hi
    lo_ref[rows, cols] = lo


def transpose_split(hi_ref, lo_ref, source, r):
    n = source.shape[0]
    for i in range(n // r):
        for j in range(n // r):
            put_split(
                hi_ref,
                lo_ref,
                slice(j * r, (j + 1) * r),
                slice(i * r, (i + 1) * r),
                source[i * r : (i + 1) * r, j * r : (j + 1) * r].T,
            )


def straight_split(hi_ref, lo_ref, source, r):
    n = source.shape[0]
    for i in range(n // r):
        put_split(
            hi_ref, lo_ref, slice(i * r, (i + 1) * r), slice(None), source[i * r : (i + 1) * r, :]
        )


def prepare_kernel(bs, pattern, halves, core_halves, mh, ml, th, tl, dense):
    c, has1 = place_of()[2], has(1)
    n = dense.shape[0]
    r = halves.shape[1]
    half = halves.shape[0] // 2
    first = c == 0
    own_half = jnp.where(first, halves[0:half, :], halves[half:, :])
    core_half = jnp.where(first, core_halves[0:half, :], core_halves[half:, :])
    flag = jnp.where(first, 1, has1)

    def put(row, col, value):
        dense[row, col] = value

    dense_turned(put, pattern, own_half, core_half, flag, n, r, bs)

    @pl.when(first)
    def _():
        straight_split(mh, ml, dense, r)
        transpose_split(th, tl, dense, r)

    @pl.when(jnp.logical_not(first))
    def _():
        straight_split(th, tl, dense, r)
        transpose_split(mh, ml, dense, r)


def level1_kernel(own_near, own_far, near, far, mh, ml, th, tl, out, xh, xl, sh, sl):
    c = place_of()[2]
    r = own_near.shape[0]
    n = 4 * r
    extra = slice(n, n + 16)
    first = c == 0
    xn = jnp.where(first, near[...], own_near[...])
    xf = jnp.where(first, far[...], own_far[...])
    x = jnp.concatenate(
        [
            xn[:, 0 : 4 * r],
            jnp.concatenate([xf[0:r, 0:r], xn[:, 4 * r :], xf[0:r, r:]], axis=1),
            jnp.concatenate([xf[r : r + 1, :], xf[r : r + 1, :]], axis=1),
        ],
        axis=0,
    )

    def put(i, j, block):
        put_split(xh, xl, slice(i * r, (i + 1) * r), slice(j * r, (j + 1) * r), block)

    spread(x, r, put)
    b_before, b_own = far_row(far, r, 1), far_row(own_far, r, 1)
    e_before, e_own = far_row(far, r, 3), far_row(own_far, r, 3)
    row = jnp.broadcast_to(jnp.where(first, b_before, e_own), (16, n))
    put_split(xh, xl, extra, slice(None), row)
    u = dot3(xh[...], xl[...], mh[...], ml[...])
    uh, ul = split(u[0:n, :])
    sh[0 : 2 * r, :] = th[0 : 2 * r, :]
    sl[0 : 2 * r, :] = tl[0 : 2 * r, :]
    row = jnp.broadcast_to(jnp.where(first, 0.0, b_before), (16, n))
    put_split(sh, sl, slice(2 * r, 2 * r + 16), slice(None), row)
    top = dot3(sh[...], sl[...], uh, ul)
    low = dot3(th[2 * r :, :], tl[2 * r :, :], uh[:, 2 * r :], ul[:, 2 * r :])
    vec = jnp.where(first, b_own, e_before) + u[n : n + 1, :] + top[2 * r : 2 * r + 1, :]
    dn = jnp.where(first, own_near[...], near[...])
    df = jnp.where(first, own_far[...], far[...])
    z11 = top[r : 2 * r, r : 2 * r]
    z33 = low[r : 2 * r, r : 2 * r]
    out[0:r, 0:r] = fold(top[0:r, 0:r], z11, r) + dn[:, 0:r]
    out[0:r, r:] = top[0:r, r:] + dn[:, r : 4 * r]
    out[r : 2 * r, 0:r] = fold(low[0:r, 0:r], z33, r) + df[0:r, 0:r]
    out[r : 2 * r, r : 3 * r] = top[r : 2 * r, 2 * r :] + dn[:, 4 * r :]
    out[r : 2 * r, 3 * r :] = low[0:r, r : 2 * r] + df[0:r, r:]
    base = 2 * r
    out[base : base + 1, 0:r] = diagonal(z11, r) + df[r : r + 1, 0:r]
    out[base : base + 1, r : 2 * r] = diagonal(z33, r) + df[r : r + 1, r:]
    out[base : base + 1, 2 * r :] = jnp.zeros((1, 2 * r), F32)
    out[base + 1 : base + 2, :] = b_own
    out[base + 2 : base + 3, :] = vec
    out[base + 3 : base + 4, :] = b_before
    out[base + 4 : base + 8, :] = jnp.zeros((4, 4 * r), F32)


def early_kernel(bs, pattern, halves, core_halves, a0h, a0l, a1h, a1l, t):
    n = a0h.shape[0]
    r = halves.shape[1]
    half = halves.shape[0] // 2
    for at, flag, hi, lo in ((0, 1, a0h, a0l), (1, has(1), a1h, a1l)):
        rows = slice(at * half, (at + 1) * half)
        put = functools.partial(put_split, hi, lo)
        dense_turned(put, pattern, halves[rows, :], core_halves[rows, :], flag, n, r, bs)

    def wanted(ref):
        return jnp.concatenate([ref[:, 0:r], ref[:, 2 * r : 3 * r]], axis=1)

    t[...] = dot3(a1h[...], a1l[...], wanted(a0h), wanted(a0l))


def rows_kernel(
    bs, pattern, halves, core_halves, t, dyn_own, dyn_send, a2, a2h, a2l, a3h, a3l
):
    q, _, _ = place_of()
    n = a2.shape[0]
    r = halves.shape[1]
    half = halves.shape[0] // 2

    def put2(row, col, value):
        put_split(a2h, a2l, row, col, value)
        a2[row, col] = value

    def put3(row, col, value):
        put_split(a3h, a3l, row, col, value)

    for at, flag, put in ((0, has(2), put2), (1, has(3), put3)):
        rows = slice(at * half, (at + 1) * half)
        dense_turned(put, pattern, halves[rows, :], core_halves[rows, :], flag, n, r, bs)
    rows = dot3(a2h[...], a2l[...], *split(t[...]))
    rows = dot3(a3h[...], a3l[...], *split(rows))
    for j in range(4):
        at = lanes(q ^ j, r)
        dyn_own[:, at] = rows[j * r : (j + 1) * r, 0:r].T
        dyn_send[:, at] = rows[j * r : (j + 1) * r, r : 2 * r].T


def product_kernel(
    a0h, a0l, a1h, a1l, a2h, a2l, a3h, a3l, mh, ml, th, tl, product_ref
):
    first = place_of()[2] == 0
    r = a0h.shape[0] // 4

    @pl.when(first)
    def _():
        product_ref[...] = dot3(a1h[...], a1l[...], a0h[...], a0l[...])
        straight_split(mh, ml, product_ref, r)
        transpose_split(th, tl, product_ref, r)

    @pl.when(jnp.logical_not(first))
    def _():
        product_ref[...] = dot3(a3h[...], a3l[...], a2h[...], a2l[...])
        straight_split(th, tl, product_ref, r)
        transpose_split(mh, ml, product_ref, r)


def ahead_kernel(own, mh, ml, th, tl, full, z, xh, xl):
    r = own.shape[1] // 4

    def put(i, j, block):
        full[i * r : (i + 1) * r, j * r : (j + 1) * r] = block

    spread(own, r, put)

    @pl.when(place_of()[2] == 1)
    def _():
        straight_split(xh, xl, full, r)
        u = dot3(xh[...], xl[...], mh[...], ml[...])
        z[...] = dot3(th[...], tl[...], *split(u))


def put_rows(ref, value, q, r):
    for j in range(4):
        ref[lanes(q ^ j, r), :] = value[:, j * r : (j + 1) * r]


CROSSING = ((2, 0), (2, 1), (2, 3))


def level2_kernel(own, earlier, mh, ml, th, tl, full, z, to_chip, uh, ul, xh, xl, rest):
    c = place_of()[2]
    r = own.shape[1] // 4
    two, three = slice(2 * r, 3 * r), slice(3 * r, 4 * r)

    @pl.when(c == 0)
    def _():
        def put(i, j, block):
            put_split(xh, xl, slice(i * r, (i + 1) * r), slice(j * r, (j + 1) * r), block)

        spread(earlier, r, put)
        hi, lo = split(dot3(xh[...], xl[...], mh[...], ml[...]))
        uh[...] = hi
        ul[...] = lo
        rest[:, 2 * r :] = dot3(th[2 * r :, :], tl[2 * r :, :], hi[:, 2 * r :], lo[:, 2 * r :])
        rest[0:r, 0 : 2 * r] = dot3(th[two, :], tl[two, :], hi[:, 0 : 2 * r], lo[:, 0 : 2 * r])
        rest[:, 2 * r :] = rest[:, 2 * r :] + full[2 * r :, 2 * r :]
        rest[0:r, 0 : 2 * r] = rest[0:r, 0 : 2 * r] + full[two, 0 : 2 * r]

    @pl.when(c == 1)
    def _():
        def put(i, j, block):
            if (i, j) in CROSSING or i == j:
                rows = slice((i - 2) * r, (i - 1) * r)
                cols = slice(j * r, (j + 1) * r)
                rest[rows, cols] = z[i * r : (i + 1) * r, cols] + block

        spread(earlier, r, put, rows=(2, 3))

    z33 = rest[r : 2 * r, three]
    to_chip[0:r, :] = fold(rest[0:r, two], z33, r)
    for at, (_, j) in enumerate(CROSSING):
        to_chip[(at + 1) * r : (at + 2) * r, :] = rest[0:r, j * r : (j + 1) * r]
    to_chip[4 * r :, :] = jnp.broadcast_to(diagonal(z33, r), (8, r))


def far_rows_kernel(
    own, earlier, mh, ml, th, tl, a2, full, z, uh, ul, to_far, short, vec, rest
):
    c = place_of()[2]
    r = own.shape[1] // 4
    base = 2 * r
    three = slice(3 * r, 4 * r)
    b1 = earlier[base + 1 : base + 2, :] + row_times(earlier[base + 3 : base + 4, :], a2[...], r)

    @pl.when(c == 0)
    def _():
        value = dot3(th[three, :], tl[three, :], uh[:, 0 : 2 * r], ul[:, 0 : 2 * r])
        rest[...] = value + full[three, 0 : 2 * r]
        vec[0:1, :] = b1
        vec[1:2, :] = own[base + 2 : base + 3, :]

    @pl.when(c == 1)
    def _():
        def put(i, j, block):
            if j < 2:
                cols = slice(j * r, (j + 1) * r)
                rest[:, cols] = z[three, cols] + block

        spread(earlier, r, put, rows=(3,))
        vec[0:1, :] = own[base + 2 : base + 3, :] + row_times(b1, full[...], r)
        vec[1:2, :] = earlier[base + 2 : base + 3, :]

    to_far[0:r, :] = rest[:, 0:r]
    to_far[r : 2 * r, :] = rest[:, r : 2 * r]
    out = vec[1:2, :] + row_times(vec[0:1, :], mh[...].astype(F32) + ml[...].astype(F32), r)
    to_far[2 * r :, :] = jnp.broadcast_to(out[:, 3 * r :], (8, r))
    for i in range(4):
        short[i : i + 1, :] = out[:, i * r : (i + 1) * r]
    short[4:8, :] = jnp.zeros((4, r), F32)


def rest_kernel(earlier, th, tl, full, z, uh, ul, short, keep, to_core, rest):
    q, _, c = place_of()
    r = earlier.shape[1] // 4

    @pl.when(c == 0)
    def _():
        rest[...] = dot3(th[0 : 2 * r, :], tl[0 : 2 * r, :], uh[...], ul[...]) + full[0 : 2 * r, :]

    @pl.when(c == 1)
    def _():
        def put(i, j, block):
            rows = slice(i * r, (i + 1) * r)
            cols = slice(j * r, (j + 1) * r)
            rest[rows, cols] = z[rows, cols] + block

        spread(earlier, r, put, rows=(0, 1))

    put_rows(keep, rest[0:r, :], q, r)
    put_rows(to_core, rest[r : 2 * r, :], q, r)
    to_core[4 * r :, :] = jnp.broadcast_to(short[1:2, :], (8, r))


def turn_kernel(from_chip, diagonal_block, mirrored):
    r = diagonal_block.shape[0]
    first, second = unfold(from_chip[0:r, :], from_chip[4 * r : 4 * r + 1, :], r)
    diagonal_block[...] = first
    mirrored[0:r, :] = from_chip[3 * r : 4 * r, :].T
    mirrored[r : 2 * r, :] = second


def panel_copies(panel, target, element, r):
    return [
        (panel.at[pl.ds(g * r, r), :], target.at[element, :, pl.ds(g * r, r)]) for g in range(4)
    ]


def block_copies(blocks, target, element, r):
    return [(source, target.at[element, :, lanes(at, r)]) for source, at in blocks]


def fill_kernel(
    keep,
    from_core,
    dyn_own,
    dyn_recv,
    diagonal_block,
    from_chip,
    dyn_out,
    cov_out,
    cost_out,
    sems,
):
    q, y, c = place_of()
    r = dyn_own.shape[0]
    dyn = [(dyn_own, dyn_out.at[y]), (dyn_recv, dyn_out.at[1 - y])]
    blocks = [(diagonal_block, q)] + [
        (from_chip.at[pl.ds(at * r, r), :], q ^ bit) for at, bit in ((1, 2), (2, 3), (3, 1))
    ]

    def write(mine, other):
        copy_all(
            dyn
            + panel_copies(keep, mine, y, r)
            + panel_copies(from_core, other, y, r)
            + block_copies(blocks, mine, 1 - y, r),
            sems,
        )

    @pl.when(c == 0)
    def _():
        write(cov_out, cost_out)

    @pl.when(c == 1)
    def _():
        write(cost_out, cov_out)


def place_kernel(
    cov_in,
    cost_in,
    short,
    chip_short,
    from_core,
    mirrored,
    panel,
    cov_out,
    cost_out,
    drift_out,
    eta_out,
    lines,
    sems,
):
    del cov_in, cost_in
    q, y, c = place_of()
    first = c == 0
    r = short.shape[1]
    mine, other = short[0:1, :], from_core[4 * r : 4 * r + 1, :]
    chip, far = chip_short[2:3, :], panel[2 * r : 2 * r + 1, :]
    for at, (one, two, three, four) in enumerate(
        ((mine, other, chip, far), (other, mine, far, chip))
    ):
        lines[at, pl.ds(y, 1), :] = jnp.where(first, one, two)
        lines[at, pl.ds(1 - y, 1), :] = jnp.where(first, three, four)
    vectors = [(lines.at[0], drift_out), (lines.at[1], eta_out)]
    near, far = pl.ds(0, r), pl.ds(r, r)
    blocks = [
        (panel.at[near, :], q ^ 3),
        (panel.at[far, :], q ^ 2),
        (mirrored.at[near, :], q ^ 1),
        (mirrored.at[far, :], q),
    ]

    @pl.when(first)
    def _():
        copy_all(vectors + block_copies(blocks, cost_out, 1 - y, r), sems)

    @pl.when(c == 1)
    def _():
        copy_all(vectors + block_copies(blocks, cov_out, 1 - y, r), sems)


IN_HBM, IN_VMEM = 0, 1


def kernel(body, operands, shapes, scratch=(), aliases=None):
    specs = {
        IN_HBM: pl.BlockSpec(memory_space=pltpu.HBM),
        IN_VMEM: pl.BlockSpec(memory_space=pltpu.VMEM),
    }
    call = pl.pallas_call(
        body,
        in_specs=[specs[where] for where, _ in operands],
        out_specs=[specs[where] for where, _ in shapes],
        out_shape=[
            pltpu.VMEM(s.shape, s.dtype) if where == IN_VMEM else s for where, s in shapes
        ],
        scratch_shapes=list(scratch),
        input_output_aliases=aliases or {},
        compiler_params=pltpu.CompilerParams(vmem_limit_bytes=20 * 2**20),
    )
    kept = {IN_HBM: pltpu.HBM, IN_VMEM: pltpu.VMEM}
    return call(
        *(
            pltpu.with_memory_space_constraint(x, kept[where]) if where in kept else x
            for where, x in operands
        )
    )


def per_device_split(blocks, pattern, drift, cov, cost, eta):
    elements, r, n = cov.shape
    bs = blocks.shape[2] // 3
    tms, cols = lax.axis_size("tm"), lax.axis_size("col")

    def swap(value, bit):
        return lax.ppermute(value, "col", [(i, i ^ bit) for i in range(cols)])

    def later(value, distance):
        return lax.ppermute(value, "tm", [(i, i + distance) for i in range(tms - distance)])

    def hbm(*arrays):
        return [(IN_HBM, x) for x in arrays]

    def vmem(*arrays):
        return [(IN_VMEM, x) for x in arrays]

    def shape(*dims):
        return jax.ShapeDtypeStruct(dims, F32)

    def half(*dims):
        return jax.ShapeDtypeStruct(dims, BF16)

    def square(dtype):
        return pltpu.VMEM((n, n), dtype)

    def sems(count):
        return pltpu.SemaphoreType.DMA((count,))

    turned = jnp.swapaxes(blocks, 1, 2)
    before = later(turned, 1)
    to_core, to_chip, to_far, panel, vecs = kernel(
        send_kernel,
        hbm(cov, cost, drift, eta),
        vmem(shape(r + 8, 3 * r), shape(r + 8, 2 * r), shape(r + 8, r), shape(r, n), shape(8, r)),
        [pltpu.VMEM(drift.shape, F32), pltpu.VMEM(eta.shape, F32), sems(12)],
    )
    from_core = swap(to_core, 1)
    from_chip = swap(to_chip, 2)
    from_far = swap(to_far, 3)
    (own_near,) = kernel(pack_near_kernel, vmem(panel, from_core), vmem(shape(r, 6 * r)))
    near = later(own_near, 1)
    (own_far,) = kernel(
        pack_far_kernel, vmem(vecs, from_core, from_chip, from_far), vmem(shape(r + 8, 2 * r))
    )
    far = later(own_far, 1)
    (picked,) = kernel(pick_kernel, vmem(turned, before), vmem(shape(6 * bs, r)))
    other = swap(picked, 2)
    (halves,) = kernel(halves_kernel, vmem(turned, before, other), vmem(shape(12 * bs, r)))
    core_halves = swap(halves, 1)
    far_halves = later(halves, 2)
    m1 = kernel(
        functools.partial(prepare_kernel, bs),
        vmem(pattern, halves, core_halves),
        vmem(*[half(n, n)] * 4),
        [square(F32)],
    )
    (level1,) = kernel(
        level1_kernel,
        vmem(own_near, own_far, near, far, *m1),
        vmem(shape(2 * r + 8, n)),
        [pltpu.VMEM((n + 16, n), BF16)] * 2 + [pltpu.VMEM((2 * r + 16, n), BF16)] * 2,
    )
    earlier = later(level1, 2)
    *a01, t = kernel(
        functools.partial(early_kernel, bs),
        vmem(pattern, halves, core_halves),
        vmem(*[half(n, n)] * 4, shape(n, 2 * r)),
    )
    far_core_halves = swap(far_halves, 1)
    dyn_own, dyn_send, a2, *a23 = kernel(
        functools.partial(rows_kernel, bs),
        vmem(pattern, far_halves, far_core_halves, t),
        vmem(shape(r, n), shape(r, n), shape(n, n), *[half(n, n)] * 4),
    )
    dyn_recv = swap(dyn_send, 2)
    m2 = kernel(product_kernel, vmem(*a01, *a23), vmem(*[half(n, n)] * 4), [square(F32)])
    full, z = kernel(
        ahead_kernel, vmem(level1, *m2), vmem(shape(n, n), shape(n, n)), [square(BF16)] * 2
    )
    to_chip, *u = kernel(
        level2_kernel,
        vmem(level1, earlier, *m2, full, z),
        vmem(shape(n + 8, r), half(n, n), half(n, n)),
        [square(BF16)] * 2 + [pltpu.VMEM((2 * r, n), F32)],
    )
    from_chip = swap(to_chip, 2)
    to_far, short = kernel(
        far_rows_kernel,
        vmem(level1, earlier, *m2, a2, full, z, *u),
        vmem(shape(2 * r + 8, r), shape(8, r)),
        [pltpu.VMEM((8, n), F32), pltpu.VMEM((r, 2 * r), F32)],
    )
    chip_short = swap(short, 2)
    from_far = swap(to_far, 3)
    keep, to_core = kernel(
        rest_kernel,
        vmem(earlier, *m2[2:], full, z, *u, short),
        vmem(shape(n, r), shape(n + 8, r)),
        [pltpu.VMEM((2 * r, n), F32)],
    )
    from_core = swap(to_core, 1)
    diagonal_block, mirrored = kernel(
        turn_kernel, vmem(from_chip), vmem(shape(r, r), shape(2 * r, r))
    )
    mirrored = swap(mirrored, 1)
    whole, line = shape(elements, r, n), shape(elements, r)
    dyn_out, cov_out, cost_out = kernel(
        fill_kernel,
        vmem(keep, from_core, dyn_own, dyn_recv, diagonal_block, from_chip),
        hbm(whole, whole, whole),
        [sems(14)],
    )
    cov_out, cost_out, drift_out, eta_out = kernel(
        place_kernel,
        hbm(cov_out, cost_out) + vmem(short, chip_short, from_core, mirrored, from_far),
        hbm(whole, whole, line, line),
        [pltpu.VMEM((2, elements, r), F32), sems(6)],
        {0: 0, 1: 1},
    )
    return dyn_out, drift_out, cov_out, cost_out, eta_out


def takes_split(elements, r, bs, cols):
    return elements == 2 and cols == 4 and r % 128 == 0 and r % bs == 0 and bs % 8 == 0


def per_device(blocks, pattern, drift, cov, cost, eta):
    elements, r, _ = cov.shape
    bs = blocks.shape[2] // 3
    if takes_split(elements, r, bs, lax.axis_size("col")):
        return per_device_split(blocks, pattern, drift, cov, cost, eta)
    return per_device_general(blocks, pattern, drift, cov, cost, eta)


def solution(mesh):
    return jax.shard_map(
        per_device,
        mesh=mesh,
        in_specs=(
            P("tm", "col", None),
            P(),
            P("tm", "col"),
            P("tm", "col", None),
            P("tm", "col", None),
            P("tm", "col"),
        ),
        out_specs=(
            P("tm", "col", None),
            P("tm", "col"),
            P("tm", "col", None),
            P("tm", "col", None),
            P("tm", "col"),
        ),
        check_vma=False,
    )
```

```python
import functools

import jax
import jax.numpy as jnp
from jax import lax
from jax.experimental import pallas as pl
from jax.experimental.pallas import tpu as pltpu
from jax.sharding import PartitionSpec as P


HIGH = lax.Precision.HIGHEST
F32 = jnp.float32
BF16 = jnp.bfloat16


def shifted(block, axis, distance):
    devices = range(lax.axis_size(axis))
    route = [(i - distance, i) for i in devices if i - distance in devices]
    return lax.ppermute(block, axis, route)


def product(form, left, right):
    return jnp.einsum(form, left, right, precision=HIGH)


def densify(row_blocks, row_ids, pattern, block_size):
    block_count = pattern.shape[0]
    row_block = row_ids // block_size
    chooser = (row_block[:, None] == jnp.arange(block_count, dtype=jnp.int32)[None, :]).astype(
        jnp.int32
    )
    columns = jnp.sum(chooser[:, :, None] * pattern[None, :, :], axis=1)
    matches = (
        columns[:, :, None] == jnp.arange(block_count, dtype=jnp.int32)[None, None, :]
    ).astype(jnp.float32)
    pieces = row_blocks.reshape(row_blocks.shape[:-1] + (3, 1, block_size))
    filled = jnp.sum(matches[:, :, :, None] * pieces, axis=-3)
    return filled.reshape(row_blocks.shape[:-1] + (block_count * block_size,))


def combine_rows(
    dyn_prev_full,
    dyn_own_full,
    dyn_own,
    drift_prev_full,
    drift_own,
    cov_prev,
    cov_own,
    cost_prev,
    cost_own,
    eta_prev,
    eta_own,
    first_row,
):
    height = dyn_own.shape[1]
    dyn_res = product("tij,tjk->tik", dyn_own, dyn_prev_full)
    drift_res = product("tij,tj->ti", dyn_own, drift_prev_full) + drift_own
    carried = eta_own + product("tij,tj->ti", cost_own, drift_prev_full)
    value_rows = product("tij,tjk->tik", cost_own, dyn_prev_full)
    prev_columns = lax.dynamic_slice_in_dim(dyn_prev_full, first_row, height, 2)
    cov_full, carried_full, value_full = (
        lax.all_gather(cov_prev, "col", axis=1, tiled=True),
        lax.all_gather(carried, "col", axis=1, tiled=True),
        lax.all_gather(value_rows, "col", axis=1, tiled=True),
    )
    cost_res = cost_prev + product("tki,tkj->tij", prev_columns, value_full)
    cov_res = (
        product("tik,tjk->tij", product("tij,tjk->tik", dyn_own, cov_full), dyn_own_full) + cov_own
    )
    eta_res = eta_prev + product("tki,tk->ti", prev_columns, carried_full)
    return (dyn_res, drift_res, cov_res, cost_res, eta_res)


def choose(flag, combined, kept):
    return tuple(jnp.where(flag, new, old) for new, old in zip(combined, kept))


def per_device_general(blocks, pattern, drift, cov, cost, eta):
    height = cov.shape[1]
    modes = cov.shape[2]
    block_size = blocks.shape[2] // 3
    first_row = lax.axis_index("col") * height
    own_ids = first_row + jnp.arange(height, dtype=jnp.int32)
    all_ids = jnp.arange(modes, dtype=jnp.int32)
    position = lax.axis_index("tm")
    dyn_own = densify(blocks, own_ids, pattern, block_size)
    received = shifted((blocks, drift, cov, cost, eta), "tm", 1)
    blocks_prev, blocks_own, drift_prev_full = (
        lax.all_gather(received[0], "col", axis=1, tiled=True),
        lax.all_gather(blocks, "col", axis=1, tiled=True),
        lax.all_gather(received[1], "col", axis=1, tiled=True),
    )
    merged = combine_rows(
        densify(blocks_prev, all_ids, pattern, block_size),
        densify(blocks_own, all_ids, pattern, block_size),
        dyn_own,
        drift_prev_full,
        drift,
        received[2],
        cov,
        received[3],
        cost,
        received[4],
        eta,
        first_row,
    )
    current = choose(position >= 1, merged, (dyn_own, drift, cov, cost, eta))
    received = shifted(current, "tm", 2)
    dyn_prev_full = lax.all_gather(received[0], "col", axis=1, tiled=True)
    dyn_own_full = lax.all_gather(current[0], "col", axis=1, tiled=True)
    drift_prev_full = lax.all_gather(received[1], "col", axis=1, tiled=True)
    merged = combine_rows(
        dyn_prev_full,
        dyn_own_full,
        current[0],
        drift_prev_full,
        current[1],
        received[2],
        current[2],
        received[3],
        current[3],
        received[4],
        current[4],
        first_row,
    )
    return choose(position >= 2, merged, current)


def split(x):
    hi = x.astype(BF16)
    lo = (x - hi.astype(F32)).astype(BF16)
    return hi, lo


def dot(a, b):
    return jnp.dot(a, b, preferred_element_type=F32)


def dot3(ah, al, bh, bl):
    return dot(ah, bh) + (dot(ah, bl) + dot(al, bh))


def triangle(r):
    rows = lax.broadcasted_iota(jnp.int32, (r, r), 0)
    cols = lax.broadcasted_iota(jnp.int32, (r, r), 1)
    return rows, cols


def fold(first, second, r):
    rows, cols = triangle(r)
    return jnp.where(rows >= cols, first, second)


def diagonal(block, r):
    rows, cols = triangle(r)
    return jnp.sum(jnp.where(rows == cols, block, 0.0), axis=0, keepdims=True)


def unfold(folded, second_diag, r):
    rows, cols = triangle(r)
    turned = folded.T
    first = jnp.where(rows >= cols, folded, turned)
    second = jnp.where(rows < cols, folded, turned)
    second = jnp.where(rows == cols, jnp.broadcast_to(second_diag, (r, r)), second)
    return first, second


UPPER = ((0, 1), (0, 2), (0, 3), (1, 2), (1, 3), (2, 3))


def spread(packed, r, put, rows=(0, 1, 2, 3)):
    panel0, panel1, diags = packed[0:r], packed[r : 2 * r], packed[2 * r : 2 * r + 1]
    for at, (panel, pair) in enumerate(((panel0, (0, 1)), (panel1, (2, 3)))):
        if pair[0] in rows or pair[1] in rows:
            blocks = unfold(panel[:, 0:r], diags[:, at * r : (at + 1) * r], r)
            for i, block in zip(pair, blocks):
                if i in rows:
                    put(i, i, block)
    for at, (i, j) in enumerate(UPPER):
        panel = panel0 if at < 3 else panel1
        block = panel[:, (at % 3 + 1) * r : (at % 3 + 2) * r]
        if i in rows:
            put(i, j, block)
        if j in rows:
            put(j, i, block.T)


def column(row, r):
    rows, cols = triangle(r)
    pieces = []
    for at in range(row.shape[1] // r):
        piece = jnp.broadcast_to(row[:, at * r : (at + 1) * r], (r, r))
        pieces.append(jnp.sum(jnp.where(rows == cols, piece, 0.0), axis=1, keepdims=True))
    return jnp.concatenate(pieces, axis=0)


def row_times(row, matrix, r):
    return jnp.sum(column(row, r) * matrix, axis=0, keepdims=True)


def place_of():
    q = lax.axis_index("col")
    return q, q >> 1, q & 1


def has(distance):
    return (lax.axis_index("tm") >= distance).astype(jnp.int32)


def lanes(index, r):
    return pl.ds(pl.multiple_of(index * r, r), r)


def copy_all(pairs, sems):
    copies = [
        pltpu.make_async_copy(source, target, sems.at[i]) for i, (source, target) in enumerate(pairs)
    ]
    for copy in copies:
        copy.start()
    for copy in copies:
        copy.wait()


def send_kernel(
    cov, cost, drift, eta, to_core, to_chip, to_far, panel, vecs, b_in, e_in, sems
):
    q, y, c = place_of()
    r = to_far.shape[1]

    def load(mine, theirs):
        pairs = []
        for j in range(2, 4):
            source = mine.at[1 - y, :, lanes((q ^ 2) ^ j, r)]
            pairs.append((source, to_chip.at[pl.ds(0, r), pl.ds((j - 2) * r, r)]))
        pairs.append((theirs.at[1 - y, :, lanes(q, r)], to_far.at[pl.ds(0, r), :]))
        for j in range(1, 4):
            source = theirs.at[y, :, lanes((q ^ 1) ^ j, r)]
            pairs.append((source, to_core.at[pl.ds(0, r), pl.ds((j - 1) * r, r)]))
        for j in range(4):
            pairs.append((mine.at[y, :, lanes(q ^ j, r)], panel.at[:, pl.ds(j * r, r)]))
        pairs.append((drift, b_in))
        pairs.append((eta, e_in))
        copy_all(pairs, sems)

    @pl.when(c == 0)
    def _():
        load(cov, cost)

    @pl.when(c == 1)
    def _():
        load(cost, cov)

    b, e = b_in[pl.ds(y, 1), :], e_in[pl.ds(y, 1), :]
    vecs[...] = jnp.zeros(vecs.shape, F32)
    vecs[0:1, :] = b
    vecs[1:2, :] = e
    to_core[r : r + 8, :] = jnp.zeros((8, 3 * r), F32)
    to_core[r : r + 1, 0:r] = b
    to_core[r : r + 1, r : 2 * r] = e
    b, e = b_in[pl.ds(1 - y, 1), :], e_in[pl.ds(1 - y, 1), :]
    to_chip[r : r + 8, :] = jnp.zeros((8, 2 * r), F32)
    to_chip[r : r + 1, 0:r] = b
    to_chip[r : r + 1, r : 2 * r] = e
    to_far[r : r + 8, :] = jnp.zeros((8, r), F32)
    to_far[r : r + 1, :] = b
    to_far[r + 1 : r + 2, :] = e


def pack_near_kernel(panel, from_core, packed):
    r = panel.shape[0]
    packed[:, 0:r] = fold(panel[:, 0:r], from_core[0:r, 0:r], r)
    packed[:, r : 4 * r] = panel[:, r:]
    packed[:, 4 * r :] = from_core[0:r, r : 3 * r]


def pack_far_kernel(vecs, from_core, from_chip, from_far, packed):
    r = vecs.shape[1]
    k33 = from_far[0:r, :]
    packed[0:r, 0:r] = fold(from_chip[0:r, 0:r], k33, r)
    packed[0:r, r:] = from_chip[0:r, r : 2 * r]
    packed[r : r + 1, 0:r] = diagonal(from_core[0:r, 0:r], r)
    packed[r : r + 1, r:] = diagonal(k33, r)
    b = (
        vecs[0:1, :],
        from_core[r : r + 1, 0:r],
        from_chip[r : r + 1, 0:r],
        from_far[r : r + 1, :],
    )
    e = (
        vecs[1:2, :],
        from_core[r : r + 1, r : 2 * r],
        from_chip[r : r + 1, r : 2 * r],
        from_far[r + 1 : r + 2, :],
    )
    for j in range(4):
        at = slice(j % 2 * r, (j % 2 + 1) * r)
        packed[r + 1 + j // 2 : r + 2 + j // 2, at] = b[j]
        packed[r + 3 + j // 2 : r + 4 + j // 2, at] = e[j]
    packed[r + 5 : r + 8, :] = jnp.zeros((3, 2 * r), F32)


def far_row(packed, r, at):
    return jnp.concatenate(
        [packed[r + at : r + at + 1, :], packed[r + at + 1 : r + at + 2, :]], axis=1
    )


def pick_kernel(turned, before, out):
    y = place_of()[1]
    height = turned.shape[1]
    out[0:height, :] = turned[1 - y]
    out[height:, :] = before[1 - y]


def halves_kernel(turned, before, other, out):
    y = place_of()[1]
    height = turned.shape[1]
    out[0:height, :] = turned[y]
    out[height : 2 * height, :] = other[0:height, :]
    out[2 * height : 3 * height, :] = before[y]
    out[3 * height :, :] = other[height:, :]


def dense_turned(put, pattern, own_half, core_half, flag, n, r, bs):
    q = place_of()[0]
    lane = lax.broadcasted_iota(jnp.int32, (bs, r), 1) // bs
    rows = lax.broadcasted_iota(jnp.int32, (bs, r), 0)
    cols = lax.broadcasted_iota(jnp.int32, (bs, r), 1)
    per = r // bs
    height = 3 * bs
    for j in range(4):
        half = own_half if j % 2 == 0 else core_half
        full = half[(j // 2) * height : (j // 2 + 1) * height, :]
        wanted = []
        for k in range(3):
            want = jnp.zeros((bs, r), jnp.int32)
            for h in range(per):
                block = pattern[pl.ds((q ^ j) * per + h, 1), :][:, k : k + 1] ^ (q * per)
                want = jnp.where(lane == h, jnp.broadcast_to(block, (bs, r)), want)
            wanted.append(jnp.where(flag == 1, want, -1))
        for block in range(n // bs):
            if j * r <= block * bs < (j + 1) * r:
                value = jnp.where(
                    jnp.logical_and(rows + block * bs == cols + j * r, flag == 0), 1.0, 0.0
                )
            else:
                value = jnp.zeros((bs, r), F32)
            for k in range(3):
                piece = full[k * bs : (k + 1) * bs, :]
                value = value + jnp.where(wanted[k] == block, piece, 0.0)
            put(slice(block * bs, (block + 1) * bs), slice(j * r, (j + 1) * r), value)


def put_split(hi_ref, lo_ref, rows, cols, value):
    hi, lo = split(value)
    hi_ref[rows, cols] = hi
    lo_ref[rows, cols] = lo


def transpose_split(hi_ref, lo_ref, source, r):
    n = source.shape[0]
    for i in range(n // r):
        for j in range(n // r):
            put_split(
                hi_ref,
                lo_ref,
                slice(j * r, (j + 1) * r),
                slice(i * r, (i + 1) * r),
                source[i * r : (i + 1) * r, j * r : (j + 1) * r].T,
            )


def straight_split(hi_ref, lo_ref, source, r):
    n = source.shape[0]
    for i in range(n // r):
        put_split(
            hi_ref, lo_ref, slice(i * r, (i + 1) * r), slice(None), source[i * r : (i + 1) * r, :]
        )


def prepare_kernel(bs, pattern, halves, core_halves, mh, ml, th, tl, dense):
    c, has1 = place_of()[2], has(1)
    n = dense.shape[0]
    r = halves.shape[1]
    half = halves.shape[0] // 2
    first = c == 0
    own_half = jnp.where(first, halves[0:half, :], halves[half:, :])
    core_half = jnp.where(first, core_halves[0:half, :], core_halves[half:, :])
    flag = jnp.where(first, 1, has1)

    def put(row, col, value):
        dense[row, col] = value

    dense_turned(put, pattern, own_half, core_half, flag, n, r, bs)

    @pl.when(first)
    def _():
        straight_split(mh, ml, dense, r)
        transpose_split(th, tl, dense, r)

    @pl.when(jnp.logical_not(first))
    def _():
        straight_split(th, tl, dense, r)
        transpose_split(mh, ml, dense, r)


def level1_kernel(own_near, own_far, near, far, mh, ml, th, tl, out, xh, xl, sh, sl):
    c = place_of()[2]
    r = own_near.shape[0]
    n = 4 * r
    extra = slice(n, n + 16)
    first = c == 0
    came = jnp.where(has(1) == 1, near[...], 0.0)
    xn = jnp.where(first, came, own_near[...])
    xf = jnp.where(first, far[...], own_far[...])
    x = jnp.concatenate(
        [
            xn[:, 0 : 4 * r],
            jnp.concatenate([xf[0:r, 0:r], xn[:, 4 * r :], xf[0:r, r:]], axis=1),
            jnp.concatenate([xf[r : r + 1, :], xf[r : r + 1, :]], axis=1),
        ],
        axis=0,
    )

    def put(i, j, block):
        put_split(xh, xl, slice(i * r, (i + 1) * r), slice(j * r, (j + 1) * r), block)

    spread(x, r, put)
    b_before, b_own = far_row(far, r, 1), far_row(own_far, r, 1)
    e_before, e_own = far_row(far, r, 3), far_row(own_far, r, 3)
    row = jnp.broadcast_to(jnp.where(first, b_before, e_own), (16, n))
    put_split(xh, xl, extra, slice(None), row)
    u = dot3(xh[...], xl[...], mh[...], ml[...])
    uh, ul = split(u[0:n, :])
    sh[0 : 2 * r, :] = th[0 : 2 * r, :]
    sl[0 : 2 * r, :] = tl[0 : 2 * r, :]
    row = jnp.broadcast_to(jnp.where(first, 0.0, b_before), (16, n))
    put_split(sh, sl, slice(2 * r, 2 * r + 16), slice(None), row)
    top = dot3(sh[...], sl[...], uh, ul)
    low = dot3(th[2 * r :, :], tl[2 * r :, :], uh[:, 2 * r :], ul[:, 2 * r :])
    vec = jnp.where(first, b_own, e_before) + u[n : n + 1, :] + top[2 * r : 2 * r + 1, :]
    dn = jnp.where(first, own_near[...], came)
    df = jnp.where(first, own_far[...], far[...])
    z11 = top[r : 2 * r, r : 2 * r]
    z33 = low[r : 2 * r, r : 2 * r]
    out[0:r, 0:r] = fold(top[0:r, 0:r], z11, r) + dn[:, 0:r]
    out[0:r, r:] = top[0:r, r:] + dn[:, r : 4 * r]
    out[r : 2 * r, 0:r] = fold(low[0:r, 0:r], z33, r) + df[0:r, 0:r]
    out[r : 2 * r, r : 3 * r] = top[r : 2 * r, 2 * r :] + dn[:, 4 * r :]
    out[r : 2 * r, 3 * r :] = low[0:r, r : 2 * r] + df[0:r, r:]
    base = 2 * r
    out[base : base + 1, 0:r] = diagonal(z11, r) + df[r : r + 1, 0:r]
    out[base : base + 1, r : 2 * r] = diagonal(z33, r) + df[r : r + 1, r:]
    out[base : base + 1, 2 * r :] = jnp.zeros((1, 2 * r), F32)
    out[base + 1 : base + 2, :] = b_own
    out[base + 2 : base + 3, :] = vec
    out[base + 3 : base + 4, :] = b_before
    out[base + 4 : base + 8, :] = jnp.zeros((4, 4 * r), F32)


def early_kernel(bs, pattern, halves, core_halves, a0h, a0l, a1h, a1l, t):
    n = a0h.shape[0]
    r = halves.shape[1]
    half = halves.shape[0] // 2
    for at, flag, hi, lo in ((0, 1, a0h, a0l), (1, has(1), a1h, a1l)):
        rows = slice(at * half, (at + 1) * half)
        put = functools.partial(put_split, hi, lo)
        dense_turned(put, pattern, halves[rows, :], core_halves[rows, :], flag, n, r, bs)

    def wanted(ref):
        return jnp.concatenate([ref[:, 0:r], ref[:, 2 * r : 3 * r]], axis=1)

    t[...] = dot3(a1h[...], a1l[...], wanted(a0h), wanted(a0l))


def rows_kernel(
    bs, pattern, halves, core_halves, t, dyn_own, dyn_send, a2, a2h, a2l, a3h, a3l
):
    q, _, _ = place_of()
    n = a2.shape[0]
    r = halves.shape[1]
    half = halves.shape[0] // 2

    def put2(row, col, value):
        put_split(a2h, a2l, row, col, value)
        a2[row, col] = value

    def put3(row, col, value):
        put_split(a3h, a3l, row, col, value)

    for at, flag, put in ((0, has(2), put2), (1, has(3), put3)):
        rows = slice(at * half, (at + 1) * half)
        dense_turned(put, pattern, halves[rows, :], core_halves[rows, :], flag, n, r, bs)
    rows = dot3(a2h[...], a2l[...], *split(t[...]))
    rows = dot3(a3h[...], a3l[...], *split(rows))
    for j in range(4):
        at = lanes(q ^ j, r)
        dyn_own[:, at] = rows[j * r : (j + 1) * r, 0:r].T
        dyn_send[:, at] = rows[j * r : (j + 1) * r, r : 2 * r].T


def product_kernel(
    a0h, a0l, a1h, a1l, a2h, a2l, a3h, a3l, mh, ml, th, tl, product_ref
):
    first = place_of()[2] == 0
    r = a0h.shape[0] // 4

    @pl.when(first)
    def _():
        product_ref[...] = dot3(a1h[...], a1l[...], a0h[...], a0l[...])
        straight_split(mh, ml, product_ref, r)
        transpose_split(th, tl, product_ref, r)

    @pl.when(jnp.logical_not(first))
    def _():
        product_ref[...] = dot3(a3h[...], a3l[...], a2h[...], a2l[...])
        straight_split(th, tl, product_ref, r)
        transpose_split(mh, ml, product_ref, r)


def ahead_kernel(own, mh, ml, th, tl, full, z, xh, xl):
    r = own.shape[1] // 4

    def put(i, j, block):
        full[i * r : (i + 1) * r, j * r : (j + 1) * r] = block

    spread(own, r, put)

    @pl.when(place_of()[2] == 1)
    def _():
        straight_split(xh, xl, full, r)
        u = dot3(xh[...], xl[...], mh[...], ml[...])
        z[...] = dot3(th[...], tl[...], *split(u))


def put_rows(ref, value, q, r):
    for j in range(4):
        ref[lanes(q ^ j, r), :] = value[:, j * r : (j + 1) * r]


CROSSING = ((2, 0), (2, 1), (2, 3))


def level2_kernel(own, earlier, mh, ml, th, tl, full, z, to_chip, uh, ul, xh, xl, rest):
    c = place_of()[2]
    r = own.shape[1] // 4
    two, three = slice(2 * r, 3 * r), slice(3 * r, 4 * r)

    @pl.when(c == 0)
    def _():
        def put(i, j, block):
            put_split(xh, xl, slice(i * r, (i + 1) * r), slice(j * r, (j + 1) * r), block)

        spread(earlier, r, put)
        hi, lo = split(dot3(xh[...], xl[...], mh[...], ml[...]))
        uh[...] = hi
        ul[...] = lo
        rest[:, 2 * r :] = dot3(th[2 * r :, :], tl[2 * r :, :], hi[:, 2 * r :], lo[:, 2 * r :])
        rest[0:r, 0 : 2 * r] = dot3(th[two, :], tl[two, :], hi[:, 0 : 2 * r], lo[:, 0 : 2 * r])
        rest[:, 2 * r :] = rest[:, 2 * r :] + full[2 * r :, 2 * r :]
        rest[0:r, 0 : 2 * r] = rest[0:r, 0 : 2 * r] + full[two, 0 : 2 * r]

    @pl.when(c == 1)
    def _():
        def put(i, j, block):
            if (i, j) in CROSSING or i == j:
                rows = slice((i - 2) * r, (i - 1) * r)
                cols = slice(j * r, (j + 1) * r)
                rest[rows, cols] = z[i * r : (i + 1) * r, cols] + block

        spread(earlier, r, put, rows=(2, 3))

    z33 = rest[r : 2 * r, three]
    to_chip[0:r, :] = fold(rest[0:r, two], z33, r)
    for at, (_, j) in enumerate(CROSSING):
        to_chip[(at + 1) * r : (at + 2) * r, :] = rest[0:r, j * r : (j + 1) * r]
    to_chip[4 * r :, :] = jnp.broadcast_to(diagonal(z33, r), (8, r))


def far_rows_kernel(
    own, earlier, mh, ml, th, tl, a2, full, z, uh, ul, to_far, short, vec, rest
):
    c = place_of()[2]
    r = own.shape[1] // 4
    base = 2 * r
    three = slice(3 * r, 4 * r)
    b1 = earlier[base + 1 : base + 2, :] + row_times(earlier[base + 3 : base + 4, :], a2[...], r)

    @pl.when(c == 0)
    def _():
        value = dot3(th[three, :], tl[three, :], uh[:, 0 : 2 * r], ul[:, 0 : 2 * r])
        rest[...] = value + full[three, 0 : 2 * r]
        vec[0:1, :] = b1
        vec[1:2, :] = own[base + 2 : base + 3, :]

    @pl.when(c == 1)
    def _():
        def put(i, j, block):
            if j < 2:
                cols = slice(j * r, (j + 1) * r)
                rest[:, cols] = z[three, cols] + block

        spread(earlier, r, put, rows=(3,))
        vec[0:1, :] = own[base + 2 : base + 3, :] + row_times(b1, full[...], r)
        vec[1:2, :] = earlier[base + 2 : base + 3, :]

    to_far[0:r, :] = rest[:, 0:r]
    to_far[r : 2 * r, :] = rest[:, r : 2 * r]
    out = vec[1:2, :] + row_times(vec[0:1, :], mh[...].astype(F32) + ml[...].astype(F32), r)
    to_far[2 * r :, :] = jnp.broadcast_to(out[:, 3 * r :], (8, r))
    for i in range(4):
        short[i : i + 1, :] = out[:, i * r : (i + 1) * r]
    short[4:8, :] = jnp.zeros((4, r), F32)


def rest_kernel(earlier, th, tl, full, z, uh, ul, short, keep, to_core, rest):
    q, _, c = place_of()
    r = earlier.shape[1] // 4

    @pl.when(c == 0)
    def _():
        rest[...] = dot3(th[0 : 2 * r, :], tl[0 : 2 * r, :], uh[...], ul[...]) + full[0 : 2 * r, :]

    @pl.when(c == 1)
    def _():
        def put(i, j, block):
            rows = slice(i * r, (i + 1) * r)
            cols = slice(j * r, (j + 1) * r)
            rest[rows, cols] = z[rows, cols] + block

        spread(earlier, r, put, rows=(0, 1))

    put_rows(keep, rest[0:r, :], q, r)
    put_rows(to_core, rest[r : 2 * r, :], q, r)
    to_core[4 * r :, :] = jnp.broadcast_to(short[1:2, :], (8, r))


def turn_kernel(from_chip, diagonal_block, mirrored):
    r = diagonal_block.shape[0]
    first, second = unfold(from_chip[0:r, :], from_chip[4 * r : 4 * r + 1, :], r)
    diagonal_block[...] = first
    mirrored[0:r, :] = from_chip[3 * r : 4 * r, :].T
    mirrored[r : 2 * r, :] = second


def panel_copies(panel, target, element, r):
    return [
        (panel.at[pl.ds(g * r, r), :], target.at[element, :, pl.ds(g * r, r)]) for g in range(4)
    ]


def block_copies(blocks, target, element, r):
    return [(source, target.at[element, :, lanes(at, r)]) for source, at in blocks]


def fill_kernel(
    keep,
    from_core,
    dyn_own,
    dyn_recv,
    diagonal_block,
    from_chip,
    dyn_out,
    cov_out,
    cost_out,
    sems,
):
    q, y, c = place_of()
    r = dyn_own.shape[0]
    dyn = [(dyn_own, dyn_out.at[y]), (dyn_recv, dyn_out.at[1 - y])]
    blocks = [(diagonal_block, q)] + [
        (from_chip.at[pl.ds(at * r, r), :], q ^ bit) for at, bit in ((1, 2), (2, 3), (3, 1))
    ]

    def write(mine, other):
        copy_all(
            dyn
            + panel_copies(keep, mine, y, r)
            + panel_copies(from_core, other, y, r)
            + block_copies(blocks, mine, 1 - y, r),
            sems,
        )

    @pl.when(c == 0)
    def _():
        write(cov_out, cost_out)

    @pl.when(c == 1)
    def _():
        write(cost_out, cov_out)


def place_kernel(
    cov_in,
    cost_in,
    short,
    chip_short,
    from_core,
    mirrored,
    panel,
    cov_out,
    cost_out,
    drift_out,
    eta_out,
    lines,
    sems,
):
    del cov_in, cost_in
    q, y, c = place_of()
    first = c == 0
    r = short.shape[1]
    mine, other = short[0:1, :], from_core[4 * r : 4 * r + 1, :]
    chip, far = chip_short[2:3, :], panel[2 * r : 2 * r + 1, :]
    for at, (one, two, three, four) in enumerate(
        ((mine, other, chip, far), (other, mine, far, chip))
    ):
        lines[at, pl.ds(y, 1), :] = jnp.where(first, one, two)
        lines[at, pl.ds(1 - y, 1), :] = jnp.where(first, three, four)
    vectors = [(lines.at[0], drift_out), (lines.at[1], eta_out)]
    near, far = pl.ds(0, r), pl.ds(r, r)
    blocks = [
        (panel.at[near, :], q ^ 3),
        (panel.at[far, :], q ^ 2),
        (mirrored.at[near, :], q ^ 1),
        (mirrored.at[far, :], q),
    ]

    @pl.when(first)
    def _():
        copy_all(vectors + block_copies(blocks, cost_out, 1 - y, r), sems)

    @pl.when(c == 1)
    def _():
        copy_all(vectors + block_copies(blocks, cov_out, 1 - y, r), sems)


IN_HBM, IN_VMEM = 0, 1


def kernel(body, operands, shapes, scratch=(), aliases=None):
    specs = {
        IN_HBM: pl.BlockSpec(memory_space=pltpu.HBM),
        IN_VMEM: pl.BlockSpec(memory_space=pltpu.VMEM),
    }
    call = pl.pallas_call(
        body,
        in_specs=[specs[where] for where, _ in operands],
        out_specs=[specs[where] for where, _ in shapes],
        out_shape=[
            pltpu.VMEM(s.shape, s.dtype) if where == IN_VMEM else s for where, s in shapes
        ],
        scratch_shapes=list(scratch),
        input_output_aliases=aliases or {},
        compiler_params=pltpu.CompilerParams(vmem_limit_bytes=20 * 2**20),
    )
    kept = {IN_HBM: pltpu.HBM, IN_VMEM: pltpu.VMEM}
    return call(
        *(
            pltpu.with_memory_space_constraint(x, kept[where]) if where in kept else x
            for where, x in operands
        )
    )


def per_device_split(blocks, pattern, drift, cov, cost, eta):
    elements, r, n = cov.shape
    bs = blocks.shape[2] // 3
    tms, cols = lax.axis_size("tm"), lax.axis_size("col")

    def swap(value, bit):
        return lax.ppermute(value, "col", [(i, i ^ bit) for i in range(cols)])

    def later(value, distance, cyclic=False):
        count = tms if cyclic else tms - distance
        return lax.ppermute(value, "tm", [(i, (i + distance) % tms) for i in range(count)])

    def hbm(*arrays):
        return [(IN_HBM, x) for x in arrays]

    def vmem(*arrays):
        return [(IN_VMEM, x) for x in arrays]

    def shape(*dims):
        return jax.ShapeDtypeStruct(dims, F32)

    def half(*dims):
        return jax.ShapeDtypeStruct(dims, BF16)

    def square(dtype):
        return pltpu.VMEM((n, n), dtype)

    def sems(count):
        return pltpu.SemaphoreType.DMA((count,))

    turned = jnp.swapaxes(blocks, 1, 2)
    before = later(turned, 1, cyclic=True)
    to_core, to_chip, to_far, panel, vecs = kernel(
        send_kernel,
        hbm(cov, cost, drift, eta),
        vmem(shape(r + 8, 3 * r), shape(r + 8, 2 * r), shape(r + 8, r), shape(r, n), shape(8, r)),
        [pltpu.VMEM(drift.shape, F32), pltpu.VMEM(eta.shape, F32), sems(12)],
    )
    from_core = swap(to_core, 1)
    from_chip = swap(to_chip, 2)
    from_far = swap(to_far, 3)
    (own_near,) = kernel(pack_near_kernel, vmem(panel, from_core), vmem(shape(r, 6 * r)))
    near = later(own_near, 1, cyclic=True)
    (own_far,) = kernel(
        pack_far_kernel, vmem(vecs, from_core, from_chip, from_far), vmem(shape(r + 8, 2 * r))
    )
    far = later(own_far, 1)
    (picked,) = kernel(pick_kernel, vmem(turned, before), vmem(shape(6 * bs, r)))
    other = swap(picked, 2)
    (halves,) = kernel(halves_kernel, vmem(turned, before, other), vmem(shape(12 * bs, r)))
    core_halves = swap(halves, 1)
    far_halves = later(halves, 2, cyclic=True)
    m1 = kernel(
        functools.partial(prepare_kernel, bs),
        vmem(pattern, halves, core_halves),
        vmem(*[half(n, n)] * 4),
        [square(F32)],
    )
    (level1,) = kernel(
        level1_kernel,
        vmem(own_near, own_far, near, far, *m1),
        vmem(shape(2 * r + 8, n)),
        [pltpu.VMEM((n + 16, n), BF16)] * 2 + [pltpu.VMEM((2 * r + 16, n), BF16)] * 2,
    )
    earlier = later(level1, 2)
    *a01, t = kernel(
        functools.partial(early_kernel, bs),
        vmem(pattern, halves, core_halves),
        vmem(*[half(n, n)] * 4, shape(n, 2 * r)),
    )
    far_core_halves = swap(far_halves, 1)
    dyn_own, dyn_send, a2, *a23 = kernel(
        functools.partial(rows_kernel, bs),
        vmem(pattern, far_halves, far_core_halves, t),
        vmem(shape(r, n), shape(r, n), shape(n, n), *[half(n, n)] * 4),
    )
    dyn_recv = swap(dyn_send, 2)
    m2 = kernel(product_kernel, vmem(*a01, *a23), vmem(*[half(n, n)] * 4), [square(F32)])
    full, z = kernel(
        ahead_kernel, vmem(level1, *m2), vmem(shape(n, n), shape(n, n)), [square(BF16)] * 2
    )
    to_chip, *u = kernel(
        level2_kernel,
        vmem(level1, earlier, *m2, full, z),
        vmem(shape(n + 8, r), half(n, n), half(n, n)),
        [square(BF16)] * 2 + [pltpu.VMEM((2 * r, n), F32)],
    )
    from_chip = swap(to_chip, 2)
    to_far, short = kernel(
        far_rows_kernel,
        vmem(level1, earlier, *m2, a2, full, z, *u),
        vmem(shape(2 * r + 8, r), shape(8, r)),
        [pltpu.VMEM((8, n), F32), pltpu.VMEM((r, 2 * r), F32)],
    )
    chip_short = swap(short, 2)
    from_far = swap(to_far, 3)
    keep, to_core = kernel(
        rest_kernel,
        vmem(earlier, *m2[2:], full, z, *u, short),
        vmem(shape(n, r), shape(n + 8, r)),
        [pltpu.VMEM((2 * r, n), F32)],
    )
    from_core = swap(to_core, 1)
    diagonal_block, mirrored = kernel(
        turn_kernel, vmem(from_chip), vmem(shape(r, r), shape(2 * r, r))
    )
    mirrored = swap(mirrored, 1)
    whole, line = shape(elements, r, n), shape(elements, r)
    dyn_out, cov_out, cost_out = kernel(
        fill_kernel,
        vmem(keep, from_core, dyn_own, dyn_recv, diagonal_block, from_chip),
        hbm(whole, whole, whole),
        [sems(14)],
    )
    cov_out, cost_out, drift_out, eta_out = kernel(
        place_kernel,
        hbm(cov_out, cost_out) + vmem(short, chip_short, from_core, mirrored, from_far),
        hbm(whole, whole, line, line),
        [pltpu.VMEM((2, elements, r), F32), sems(6)],
        {0: 0, 1: 1},
    )
    return dyn_out, drift_out, cov_out, cost_out, eta_out


def takes_split(elements, r, bs, cols):
    return elements == 2 and cols == 4 and r % 128 == 0 and r % bs == 0 and bs % 8 == 0


def per_device(blocks, pattern, drift, cov, cost, eta):
    elements, r, _ = cov.shape
    bs = blocks.shape[2] // 3
    if takes_split(elements, r, bs, lax.axis_size("col")):
        return per_device_split(blocks, pattern, drift, cov, cost, eta)
    return per_device_general(blocks, pattern, drift, cov, cost, eta)


def solution(mesh):
    return jax.shard_map(
        per_device,
        mesh=mesh,
        in_specs=(
            P("tm", "col", None),
            P(),
            P("tm", "col"),
            P("tm", "col", None),
            P("tm", "col", None),
            P("tm", "col"),
        ),
        out_specs=(
            P("tm", "col", None),
            P("tm", "col"),
            P("tm", "col", None),
            P("tm", "col", None),
            P("tm", "col"),
        ),
        check_vma=False,
    )
```

```python
import functools

import jax
import jax.numpy as jnp
from jax import lax
from jax.experimental import pallas as pl
from jax.experimental.pallas import tpu as pltpu
from jax.sharding import PartitionSpec as P


HIGH = lax.Precision.HIGHEST
F32 = jnp.float32
BF16 = jnp.bfloat16


def shifted(block, axis, distance):
    devices = range(lax.axis_size(axis))
    route = [(i - distance, i) for i in devices if i - distance in devices]
    return lax.ppermute(block, axis, route)


def product(form, left, right):
    return jnp.einsum(form, left, right, precision=HIGH)


def densify(row_blocks, row_ids, pattern, block_size):
    block_count = pattern.shape[0]
    row_block = row_ids // block_size
    chooser = (row_block[:, None] == jnp.arange(block_count, dtype=jnp.int32)[None, :]).astype(
        jnp.int32
    )
    columns = jnp.sum(chooser[:, :, None] * pattern[None, :, :], axis=1)
    matches = (
        columns[:, :, None] == jnp.arange(block_count, dtype=jnp.int32)[None, None, :]
    ).astype(jnp.float32)
    pieces = row_blocks.reshape(row_blocks.shape[:-1] + (3, 1, block_size))
    filled = jnp.sum(matches[:, :, :, None] * pieces, axis=-3)
    return filled.reshape(row_blocks.shape[:-1] + (block_count * block_size,))


def combine_rows(
    dyn_prev_full,
    dyn_own_full,
    dyn_own,
    drift_prev_full,
    drift_own,
    cov_prev,
    cov_own,
    cost_prev,
    cost_own,
    eta_prev,
    eta_own,
    first_row,
):
    height = dyn_own.shape[1]
    dyn_res = product("tij,tjk->tik", dyn_own, dyn_prev_full)
    drift_res = product("tij,tj->ti", dyn_own, drift_prev_full) + drift_own
    carried = eta_own + product("tij,tj->ti", cost_own, drift_prev_full)
    value_rows = product("tij,tjk->tik", cost_own, dyn_prev_full)
    prev_columns = lax.dynamic_slice_in_dim(dyn_prev_full, first_row, height, 2)
    cov_full, carried_full, value_full = (
        lax.all_gather(cov_prev, "col", axis=1, tiled=True),
        lax.all_gather(carried, "col", axis=1, tiled=True),
        lax.all_gather(value_rows, "col", axis=1, tiled=True),
    )
    cost_res = cost_prev + product("tki,tkj->tij", prev_columns, value_full)
    cov_res = (
        product("tik,tjk->tij", product("tij,tjk->tik", dyn_own, cov_full), dyn_own_full) + cov_own
    )
    eta_res = eta_prev + product("tki,tk->ti", prev_columns, carried_full)
    return (dyn_res, drift_res, cov_res, cost_res, eta_res)


def choose(flag, combined, kept):
    return tuple(jnp.where(flag, new, old) for new, old in zip(combined, kept))


def per_device_general(blocks, pattern, drift, cov, cost, eta):
    height = cov.shape[1]
    modes = cov.shape[2]
    block_size = blocks.shape[2] // 3
    first_row = lax.axis_index("col") * height
    own_ids = first_row + jnp.arange(height, dtype=jnp.int32)
    all_ids = jnp.arange(modes, dtype=jnp.int32)
    position = lax.axis_index("tm")
    dyn_own = densify(blocks, own_ids, pattern, block_size)
    received = shifted((blocks, drift, cov, cost, eta), "tm", 1)
    blocks_prev, blocks_own, drift_prev_full = (
        lax.all_gather(received[0], "col", axis=1, tiled=True),
        lax.all_gather(blocks, "col", axis=1, tiled=True),
        lax.all_gather(received[1], "col", axis=1, tiled=True),
    )
    merged = combine_rows(
        densify(blocks_prev, all_ids, pattern, block_size),
        densify(blocks_own, all_ids, pattern, block_size),
        dyn_own,
        drift_prev_full,
        drift,
        received[2],
        cov,
        received[3],
        cost,
        received[4],
        eta,
        first_row,
    )
    current = choose(position >= 1, merged, (dyn_own, drift, cov, cost, eta))
    received = shifted(current, "tm", 2)
    dyn_prev_full = lax.all_gather(received[0], "col", axis=1, tiled=True)
    dyn_own_full = lax.all_gather(current[0], "col", axis=1, tiled=True)
    drift_prev_full = lax.all_gather(received[1], "col", axis=1, tiled=True)
    merged = combine_rows(
        dyn_prev_full,
        dyn_own_full,
        current[0],
        drift_prev_full,
        current[1],
        received[2],
        current[2],
        received[3],
        current[3],
        received[4],
        current[4],
        first_row,
    )
    return choose(position >= 2, merged, current)


def split(x):
    hi = x.astype(BF16)
    lo = (x - hi.astype(F32)).astype(BF16)
    return hi, lo


def dot(a, b):
    return jnp.dot(a, b, preferred_element_type=F32)


def dot3(ah, al, bh, bl):
    return dot(ah, bh) + (dot(ah, bl) + dot(al, bh))


def triangle(r):
    rows = lax.broadcasted_iota(jnp.int32, (r, r), 0)
    cols = lax.broadcasted_iota(jnp.int32, (r, r), 1)
    return rows, cols


def fold(first, second, r):
    rows, cols = triangle(r)
    return jnp.where(rows >= cols, first, second)


def diagonal(block, r):
    rows, cols = triangle(r)
    return jnp.sum(jnp.where(rows == cols, block, 0.0), axis=0, keepdims=True)


def unfold(folded, second_diag, r):
    rows, cols = triangle(r)
    turned = folded.T
    first = jnp.where(rows >= cols, folded, turned)
    second = jnp.where(rows < cols, folded, turned)
    second = jnp.where(rows == cols, jnp.broadcast_to(second_diag, (r, r)), second)
    return first, second


UPPER = ((0, 1), (0, 2), (0, 3), (1, 2), (1, 3), (2, 3))


def spread(packed, r, put, rows=(0, 1, 2, 3)):
    panel0, panel1, diags = packed[0:r], packed[r : 2 * r], packed[2 * r : 2 * r + 1]
    for at, (panel, pair) in enumerate(((panel0, (0, 1)), (panel1, (2, 3)))):
        if pair[0] in rows or pair[1] in rows:
            blocks = unfold(panel[:, 0:r], diags[:, at * r : (at + 1) * r], r)
            for i, block in zip(pair, blocks):
                if i in rows:
                    put(i, i, block)
    for at, (i, j) in enumerate(UPPER):
        panel = panel0 if at < 3 else panel1
        block = panel[:, (at % 3 + 1) * r : (at % 3 + 2) * r]
        if i in rows:
            put(i, j, block)
        if j in rows:
            put(j, i, block.T)


def column(row, r):
    rows, cols = triangle(r)
    pieces = []
    for at in range(row.shape[1] // r):
        piece = jnp.broadcast_to(row[:, at * r : (at + 1) * r], (r, r))
        pieces.append(jnp.sum(jnp.where(rows == cols, piece, 0.0), axis=1, keepdims=True))
    return jnp.concatenate(pieces, axis=0)


def row_times(row, matrix, r):
    return jnp.sum(column(row, r) * matrix, axis=0, keepdims=True)


def place_of():
    q = lax.axis_index("col")
    return q, q >> 1, q & 1


def has(distance):
    return (lax.axis_index("tm") >= distance).astype(jnp.int32)


def lanes(index, r):
    return pl.ds(pl.multiple_of(index * r, r), r)


def copy_all(pairs, sems):
    copies = [
        pltpu.make_async_copy(source, target, sems.at[i]) for i, (source, target) in enumerate(pairs)
    ]
    for copy in copies:
        copy.start()
    for copy in copies:
        copy.wait()


def send_kernel(
    cov, cost, drift, eta, to_core, to_chip, to_far, panel, vecs, b_in, e_in, sems
):
    q, y, c = place_of()
    r = to_far.shape[1]

    def load(mine, theirs):
        pairs = []
        for j in range(2, 4):
            source = mine.at[1 - y, :, lanes((q ^ 2) ^ j, r)]
            pairs.append((source, to_chip.at[pl.ds(0, r), pl.ds((j - 2) * r, r)]))
        pairs.append((theirs.at[1 - y, :, lanes(q, r)], to_far.at[pl.ds(0, r), :]))
        for j in range(1, 4):
            source = theirs.at[y, :, lanes((q ^ 1) ^ j, r)]
            pairs.append((source, to_core.at[pl.ds(0, r), pl.ds((j - 1) * r, r)]))
        for j in range(4):
            pairs.append((mine.at[y, :, lanes(q ^ j, r)], panel.at[:, pl.ds(j * r, r)]))
        pairs.append((drift, b_in))
        pairs.append((eta, e_in))
        copy_all(pairs, sems)

    @pl.when(c == 0)
    def _():
        load(cov, cost)

    @pl.when(c == 1)
    def _():
        load(cost, cov)

    b, e = b_in[pl.ds(y, 1), :], e_in[pl.ds(y, 1), :]
    vecs[...] = jnp.zeros(vecs.shape, F32)
    vecs[0:1, :] = b
    vecs[1:2, :] = e
    to_core[r : r + 8, :] = jnp.zeros((8, 3 * r), F32)
    to_core[r : r + 1, 0:r] = b
    to_core[r : r + 1, r : 2 * r] = e
    b, e = b_in[pl.ds(1 - y, 1), :], e_in[pl.ds(1 - y, 1), :]
    to_chip[r : r + 8, :] = jnp.zeros((8, 2 * r), F32)
    to_chip[r : r + 1, 0:r] = b
    to_chip[r : r + 1, r : 2 * r] = e
    to_far[r : r + 8, :] = jnp.zeros((8, r), F32)
    to_far[r : r + 1, :] = b
    to_far[r + 1 : r + 2, :] = e


def pack_near_kernel(panel, from_core, packed):
    r = panel.shape[0]
    packed[:, 0:r] = fold(panel[:, 0:r], from_core[0:r, 0:r], r)
    packed[:, r : 4 * r] = panel[:, r:]
    packed[:, 4 * r :] = from_core[0:r, r : 3 * r]


def pack_far_kernel(vecs, from_core, from_chip, from_far, packed):
    r = vecs.shape[1]
    k33 = from_far[0:r, :]
    packed[0:r, 0:r] = fold(from_chip[0:r, 0:r], k33, r)
    packed[0:r, r:] = from_chip[0:r, r : 2 * r]
    packed[r : r + 1, 0:r] = diagonal(from_core[0:r, 0:r], r)
    packed[r : r + 1, r:] = diagonal(k33, r)
    b = (
        vecs[0:1, :],
        from_core[r : r + 1, 0:r],
        from_chip[r : r + 1, 0:r],
        from_far[r : r + 1, :],
    )
    e = (
        vecs[1:2, :],
        from_core[r : r + 1, r : 2 * r],
        from_chip[r : r + 1, r : 2 * r],
        from_far[r + 1 : r + 2, :],
    )
    for j in range(4):
        at = slice(j % 2 * r, (j % 2 + 1) * r)
        packed[r + 1 + j // 2 : r + 2 + j // 2, at] = b[j]
        packed[r + 3 + j // 2 : r + 4 + j // 2, at] = e[j]
    packed[r + 5 : r + 8, :] = jnp.zeros((3, 2 * r), F32)


def far_row(packed, r, at):
    return jnp.concatenate(
        [packed[r + at : r + at + 1, :], packed[r + at + 1 : r + at + 2, :]], axis=1
    )


def pick_kernel(turned, before, out):
    y = place_of()[1]
    height = turned.shape[1]
    out[0:height, :] = turned[1 - y]
    out[height:, :] = before[1 - y]


def halves_kernel(turned, before, other, out):
    y = place_of()[1]
    height = turned.shape[1]
    out[0:height, :] = turned[y]
    out[height : 2 * height, :] = other[0:height, :]
    out[2 * height : 3 * height, :] = before[y]
    out[3 * height :, :] = other[height:, :]


def dense_turned(put, pattern, own_half, core_half, flag, n, r, bs):
    q = place_of()[0]
    sub = 8
    lane = lax.broadcasted_iota(jnp.int32, (sub, r), 1) // bs
    rows = lax.broadcasted_iota(jnp.int32, (bs, r), 0)
    cols = lax.broadcasted_iota(jnp.int32, (bs, r), 1)
    per = r // bs
    height = 3 * bs
    for j in range(4):
        half = own_half if j % 2 == 0 else core_half
        pieces, wanted = [], []
        for k in range(3):
            at = (j // 2) * height + k * bs
            pieces.append(half[at : at + bs, :].reshape(bs // sub, sub, r))
            want = jnp.zeros((sub, r), jnp.int32)
            for h in range(per):
                block = pattern[pl.ds((q ^ j) * per + h, 1), :][:, k : k + 1] ^ (q * per)
                want = jnp.where(lane == h, jnp.broadcast_to(block, (sub, r)), want)
            wanted.append(jnp.where(flag == 1, want, -1))
        for block in range(n // bs):
            if j * r <= block * bs < (j + 1) * r:
                value = jnp.where(
                    jnp.logical_and(rows + block * bs == cols + j * r, flag == 0), 1.0, 0.0
                ).reshape(bs // sub, sub, r)
            else:
                value = jnp.zeros((bs // sub, sub, r), F32)
            for k in range(3):
                value = jnp.where((wanted[k] == block)[None], pieces[k], value)
            put(
                slice(block * bs, (block + 1) * bs),
                slice(j * r, (j + 1) * r),
                value.reshape(bs, r),
            )


def put_split(hi_ref, lo_ref, rows, cols, value):
    hi, lo = split(value)
    hi_ref[rows, cols] = hi
    lo_ref[rows, cols] = lo


def transpose_split(hi_ref, lo_ref, source, r):
    n = source.shape[0]
    for i in range(n // r):
        for j in range(n // r):
            put_split(
                hi_ref,
                lo_ref,
                slice(j * r, (j + 1) * r),
                slice(i * r, (i + 1) * r),
                source[i * r : (i + 1) * r, j * r : (j + 1) * r].T,
            )


def straight_split(hi_ref, lo_ref, source, r):
    n = source.shape[0]
    for i in range(n // r):
        put_split(
            hi_ref, lo_ref, slice(i * r, (i + 1) * r), slice(None), source[i * r : (i + 1) * r, :]
        )


def prepare_kernel(bs, pattern, halves, core_halves, mh, ml, th, tl, dense):
    c, has1 = place_of()[2], has(1)
    n = dense.shape[0]
    r = halves.shape[1]
    half = halves.shape[0] // 2
    first = c == 0
    own_half = jnp.where(first, halves[0:half, :], halves[half:, :])
    core_half = jnp.where(first, core_halves[0:half, :], core_halves[half:, :])
    flag = jnp.where(first, 1, has1)

    def put(row, col, value):
        dense[row, col] = value

    dense_turned(put, pattern, own_half, core_half, flag, n, r, bs)

    @pl.when(first)
    def _():
        straight_split(mh, ml, dense, r)
        transpose_split(th, tl, dense, r)

    @pl.when(jnp.logical_not(first))
    def _():
        straight_split(th, tl, dense, r)
        transpose_split(mh, ml, dense, r)


def level1_kernel(own_near, own_far, near, far, mh, ml, th, tl, out, xh, xl, sh, sl):
    c = place_of()[2]
    r = own_near.shape[0]
    n = 4 * r
    extra = slice(n, n + 16)
    first = c == 0
    came = jnp.where(has(1) == 1, near[...], 0.0)
    xn = jnp.where(first, came, own_near[...])
    xf = jnp.where(first, far[...], own_far[...])
    x = jnp.concatenate(
        [
            xn[:, 0 : 4 * r],
            jnp.concatenate([xf[0:r, 0:r], xn[:, 4 * r :], xf[0:r, r:]], axis=1),
            jnp.concatenate([xf[r : r + 1, :], xf[r : r + 1, :]], axis=1),
        ],
        axis=0,
    )

    def put(i, j, block):
        put_split(xh, xl, slice(i * r, (i + 1) * r), slice(j * r, (j + 1) * r), block)

    spread(x, r, put)
    b_before, b_own = far_row(far, r, 1), far_row(own_far, r, 1)
    e_before, e_own = far_row(far, r, 3), far_row(own_far, r, 3)
    row = jnp.broadcast_to(jnp.where(first, b_before, e_own), (16, n))
    put_split(xh, xl, extra, slice(None), row)
    u = dot3(xh[...], xl[...], mh[...], ml[...])
    uh, ul = split(u[0:n, :])
    sh[0 : 2 * r, :] = th[0 : 2 * r, :]
    sl[0 : 2 * r, :] = tl[0 : 2 * r, :]
    row = jnp.broadcast_to(jnp.where(first, 0.0, b_before), (16, n))
    put_split(sh, sl, slice(2 * r, 2 * r + 16), slice(None), row)
    top = dot3(sh[...], sl[...], uh, ul)
    low = dot3(th[2 * r :, :], tl[2 * r :, :], uh[:, 2 * r :], ul[:, 2 * r :])
    vec = jnp.where(first, b_own, e_before) + u[n : n + 1, :] + top[2 * r : 2 * r + 1, :]
    dn = jnp.where(first, own_near[...], came)
    df = jnp.where(first, own_far[...], far[...])
    z11 = top[r : 2 * r, r : 2 * r]
    z33 = low[r : 2 * r, r : 2 * r]
    out[0:r, 0:r] = fold(top[0:r, 0:r], z11, r) + dn[:, 0:r]
    out[0:r, r:] = top[0:r, r:] + dn[:, r : 4 * r]
    out[r : 2 * r, 0:r] = fold(low[0:r, 0:r], z33, r) + df[0:r, 0:r]
    out[r : 2 * r, r : 3 * r] = top[r : 2 * r, 2 * r :] + dn[:, 4 * r :]
    out[r : 2 * r, 3 * r :] = low[0:r, r : 2 * r] + df[0:r, r:]
    base = 2 * r
    out[base : base + 1, 0:r] = diagonal(z11, r) + df[r : r + 1, 0:r]
    out[base : base + 1, r : 2 * r] = diagonal(z33, r) + df[r : r + 1, r:]
    out[base : base + 1, 2 * r :] = jnp.zeros((1, 2 * r), F32)
    out[base + 1 : base + 2, :] = b_own
    out[base + 2 : base + 3, :] = vec
    out[base + 3 : base + 4, :] = b_before
    out[base + 4 : base + 8, :] = jnp.zeros((4, 4 * r), F32)


def early_kernel(bs, pattern, halves, core_halves, a0h, a0l, a1h, a1l, t):
    n = a0h.shape[0]
    r = halves.shape[1]
    half = halves.shape[0] // 2
    for at, flag, hi, lo in ((0, 1, a0h, a0l), (1, has(1), a1h, a1l)):
        rows = slice(at * half, (at + 1) * half)
        put = functools.partial(put_split, hi, lo)
        dense_turned(put, pattern, halves[rows, :], core_halves[rows, :], flag, n, r, bs)

    def wanted(ref):
        return jnp.concatenate([ref[:, 0:r], ref[:, 2 * r : 3 * r]], axis=1)

    t[...] = dot3(a1h[...], a1l[...], wanted(a0h), wanted(a0l))


def rows_kernel(
    bs, pattern, halves, core_halves, t, dyn_own, dyn_send, a2, a2h, a2l, a3h, a3l
):
    q, _, _ = place_of()
    n = a2.shape[0]
    r = halves.shape[1]
    half = halves.shape[0] // 2

    def put2(row, col, value):
        put_split(a2h, a2l, row, col, value)
        a2[row, col] = value

    def put3(row, col, value):
        put_split(a3h, a3l, row, col, value)

    for at, flag, put in ((0, has(2), put2), (1, has(3), put3)):
        rows = slice(at * half, (at + 1) * half)
        dense_turned(put, pattern, halves[rows, :], core_halves[rows, :], flag, n, r, bs)
    rows = dot3(a2h[...], a2l[...], *split(t[...]))
    rows = dot3(a3h[...], a3l[...], *split(rows))
    for j in range(4):
        at = lanes(q ^ j, r)
        dyn_own[:, at] = rows[j * r : (j + 1) * r, 0:r].T
        dyn_send[:, at] = rows[j * r : (j + 1) * r, r : 2 * r].T


def product_kernel(
    a0h, a0l, a1h, a1l, a2h, a2l, a3h, a3l, mh, ml, th, tl, product_ref
):
    first = place_of()[2] == 0
    r = a0h.shape[0] // 4

    @pl.when(first)
    def _():
        product_ref[...] = dot3(a1h[...], a1l[...], a0h[...], a0l[...])
        straight_split(mh, ml, product_ref, r)
        transpose_split(th, tl, product_ref, r)

    @pl.when(jnp.logical_not(first))
    def _():
        product_ref[...] = dot3(a3h[...], a3l[...], a2h[...], a2l[...])
        straight_split(th, tl, product_ref, r)
        transpose_split(mh, ml, product_ref, r)


def ahead_kernel(own, mh, ml, th, tl, full, z, xh, xl):
    r = own.shape[1] // 4

    def put(i, j, block):
        full[i * r : (i + 1) * r, j * r : (j + 1) * r] = block

    spread(own, r, put)

    @pl.when(place_of()[2] == 1)
    def _():
        straight_split(xh, xl, full, r)
        u = dot3(xh[...], xl[...], mh[...], ml[...])
        z[...] = dot3(th[...], tl[...], *split(u))


def put_rows(ref, value, q, r):
    for j in range(4):
        ref[lanes(q ^ j, r), :] = value[:, j * r : (j + 1) * r]


CROSSING = ((2, 0), (2, 1), (2, 3))


def level2_kernel(own, earlier, mh, ml, th, tl, full, z, to_chip, uh, ul, xh, xl, rest):
    c = place_of()[2]
    r = own.shape[1] // 4
    two, three = slice(2 * r, 3 * r), slice(3 * r, 4 * r)

    @pl.when(c == 0)
    def _():
        def put(i, j, block):
            put_split(xh, xl, slice(i * r, (i + 1) * r), slice(j * r, (j + 1) * r), block)

        spread(earlier, r, put)
        hi, lo = split(dot3(xh[...], xl[...], mh[...], ml[...]))
        uh[...] = hi
        ul[...] = lo
        rest[:, 2 * r :] = dot3(th[2 * r :, :], tl[2 * r :, :], hi[:, 2 * r :], lo[:, 2 * r :])
        rest[0:r, 0 : 2 * r] = dot3(th[two, :], tl[two, :], hi[:, 0 : 2 * r], lo[:, 0 : 2 * r])
        rest[:, 2 * r :] = rest[:, 2 * r :] + full[2 * r :, 2 * r :]
        rest[0:r, 0 : 2 * r] = rest[0:r, 0 : 2 * r] + full[two, 0 : 2 * r]

    @pl.when(c == 1)
    def _():
        def put(i, j, block):
            if (i, j) in CROSSING or i == j:
                rows = slice((i - 2) * r, (i - 1) * r)
                cols = slice(j * r, (j + 1) * r)
                rest[rows, cols] = z[i * r : (i + 1) * r, cols] + block

        spread(earlier, r, put, rows=(2, 3))

    z33 = rest[r : 2 * r, three]
    to_chip[0:r, :] = fold(rest[0:r, two], z33, r)
    for at, (_, j) in enumerate(CROSSING):
        to_chip[(at + 1) * r : (at + 2) * r, :] = rest[0:r, j * r : (j + 1) * r]
    to_chip[4 * r :, :] = jnp.broadcast_to(diagonal(z33, r), (8, r))


def far_rows_kernel(
    own, earlier, mh, ml, th, tl, a2, full, z, uh, ul, to_far, short, vec, rest
):
    c = place_of()[2]
    r = own.shape[1] // 4
    base = 2 * r
    three = slice(3 * r, 4 * r)
    b1 = earlier[base + 1 : base + 2, :] + row_times(earlier[base + 3 : base + 4, :], a2[...], r)

    @pl.when(c == 0)
    def _():
        value = dot3(th[three, :], tl[three, :], uh[:, 0 : 2 * r], ul[:, 0 : 2 * r])
        rest[...] = value + full[three, 0 : 2 * r]
        vec[0:1, :] = b1
        vec[1:2, :] = own[base + 2 : base + 3, :]

    @pl.when(c == 1)
    def _():
        def put(i, j, block):
            if j < 2:
                cols = slice(j * r, (j + 1) * r)
                rest[:, cols] = z[three, cols] + block

        spread(earlier, r, put, rows=(3,))
        vec[0:1, :] = own[base + 2 : base + 3, :] + row_times(b1, full[...], r)
        vec[1:2, :] = earlier[base + 2 : base + 3, :]

    to_far[0:r, :] = rest[:, 0:r]
    to_far[r : 2 * r, :] = rest[:, r : 2 * r]
    out = vec[1:2, :] + row_times(vec[0:1, :], mh[...].astype(F32) + ml[...].astype(F32), r)
    to_far[2 * r :, :] = jnp.broadcast_to(out[:, 3 * r :], (8, r))
    for i in range(4):
        short[i : i + 1, :] = out[:, i * r : (i + 1) * r]
    short[4:8, :] = jnp.zeros((4, r), F32)


def rest_kernel(earlier, th, tl, full, z, uh, ul, short, keep, to_core, rest):
    q, _, c = place_of()
    r = earlier.shape[1] // 4

    @pl.when(c == 0)
    def _():
        rest[...] = dot3(th[0 : 2 * r, :], tl[0 : 2 * r, :], uh[...], ul[...]) + full[0 : 2 * r, :]

    @pl.when(c == 1)
    def _():
        def put(i, j, block):
            rows = slice(i * r, (i + 1) * r)
            cols = slice(j * r, (j + 1) * r)
            rest[rows, cols] = z[rows, cols] + block

        spread(earlier, r, put, rows=(0, 1))

    put_rows(keep, rest[0:r, :], q, r)
    put_rows(to_core, rest[r : 2 * r, :], q, r)
    to_core[4 * r :, :] = jnp.broadcast_to(short[1:2, :], (8, r))


def turn_kernel(from_chip, diagonal_block, mirrored):
    r = diagonal_block.shape[0]
    first, second = unfold(from_chip[0:r, :], from_chip[4 * r : 4 * r + 1, :], r)
    diagonal_block[...] = first
    mirrored[0:r, :] = from_chip[3 * r : 4 * r, :].T
    mirrored[r : 2 * r, :] = second


def panel_copies(panel, target, element, r):
    return [
        (panel.at[pl.ds(g * r, r), :], target.at[element, :, pl.ds(g * r, r)]) for g in range(4)
    ]


def block_copies(blocks, target, element, r):
    return [(source, target.at[element, :, lanes(at, r)]) for source, at in blocks]


def fill_kernel(
    keep,
    from_core,
    dyn_own,
    dyn_recv,
    diagonal_block,
    from_chip,
    dyn_out,
    cov_out,
    cost_out,
    sems,
):
    q, y, c = place_of()
    r = dyn_own.shape[0]
    dyn = [(dyn_own, dyn_out.at[y]), (dyn_recv, dyn_out.at[1 - y])]
    blocks = [(diagonal_block, q)] + [
        (from_chip.at[pl.ds(at * r, r), :], q ^ bit) for at, bit in ((1, 2), (2, 3), (3, 1))
    ]

    def write(mine, other):
        copy_all(
            dyn
            + panel_copies(keep, mine, y, r)
            + panel_copies(from_core, other, y, r)
            + block_copies(blocks, mine, 1 - y, r),
            sems,
        )

    @pl.when(c == 0)
    def _():
        write(cov_out, cost_out)

    @pl.when(c == 1)
    def _():
        write(cost_out, cov_out)


def place_kernel(
    cov_in,
    cost_in,
    short,
    chip_short,
    from_core,
    mirrored,
    panel,
    cov_out,
    cost_out,
    drift_out,
    eta_out,
    lines,
    sems,
):
    del cov_in, cost_in
    q, y, c = place_of()
    first = c == 0
    r = short.shape[1]
    mine, other = short[0:1, :], from_core[4 * r : 4 * r + 1, :]
    chip, far = chip_short[2:3, :], panel[2 * r : 2 * r + 1, :]
    for at, (one, two, three, four) in enumerate(
        ((mine, other, chip, far), (other, mine, far, chip))
    ):
        lines[at, pl.ds(y, 1), :] = jnp.where(first, one, two)
        lines[at, pl.ds(1 - y, 1), :] = jnp.where(first, three, four)
    vectors = [(lines.at[0], drift_out), (lines.at[1], eta_out)]
    near, far = pl.ds(0, r), pl.ds(r, r)
    blocks = [
        (panel.at[near, :], q ^ 3),
        (panel.at[far, :], q ^ 2),
        (mirrored.at[near, :], q ^ 1),
        (mirrored.at[far, :], q),
    ]

    @pl.when(first)
    def _():
        copy_all(vectors + block_copies(blocks, cost_out, 1 - y, r), sems)

    @pl.when(c == 1)
    def _():
        copy_all(vectors + block_copies(blocks, cov_out, 1 - y, r), sems)


IN_HBM, IN_VMEM = 0, 1


def kernel(body, operands, shapes, scratch=(), aliases=None):
    specs = {
        IN_HBM: pl.BlockSpec(memory_space=pltpu.HBM),
        IN_VMEM: pl.BlockSpec(memory_space=pltpu.VMEM),
    }
    call = pl.pallas_call(
        body,
        in_specs=[specs[where] for where, _ in operands],
        out_specs=[specs[where] for where, _ in shapes],
        out_shape=[
            pltpu.VMEM(s.shape, s.dtype) if where == IN_VMEM else s for where, s in shapes
        ],
        scratch_shapes=list(scratch),
        input_output_aliases=aliases or {},
        compiler_params=pltpu.CompilerParams(vmem_limit_bytes=20 * 2**20),
    )
    kept = {IN_HBM: pltpu.HBM, IN_VMEM: pltpu.VMEM}
    return call(
        *(
            pltpu.with_memory_space_constraint(x, kept[where]) if where in kept else x
            for where, x in operands
        )
    )


def per_device_split(blocks, pattern, drift, cov, cost, eta):
    elements, r, n = cov.shape
    bs = blocks.shape[2] // 3
    tms, cols = lax.axis_size("tm"), lax.axis_size("col")

    def swap(value, bit):
        return lax.ppermute(value, "col", [(i, i ^ bit) for i in range(cols)])

    def later(value, distance, cyclic=False):
        count = tms if cyclic else tms - distance
        return lax.ppermute(value, "tm", [(i, (i + distance) % tms) for i in range(count)])

    def hbm(*arrays):
        return [(IN_HBM, x) for x in arrays]

    def vmem(*arrays):
        return [(IN_VMEM, x) for x in arrays]

    def shape(*dims):
        return jax.ShapeDtypeStruct(dims, F32)

    def half(*dims):
        return jax.ShapeDtypeStruct(dims, BF16)

    def square(dtype):
        return pltpu.VMEM((n, n), dtype)

    def sems(count):
        return pltpu.SemaphoreType.DMA((count,))

    turned = jnp.swapaxes(blocks, 1, 2)
    before = later(turned, 1, cyclic=True)
    to_core, to_chip, to_far, panel, vecs = kernel(
        send_kernel,
        hbm(cov, cost, drift, eta),
        vmem(shape(r + 8, 3 * r), shape(r + 8, 2 * r), shape(r + 8, r), shape(r, n), shape(8, r)),
        [pltpu.VMEM(drift.shape, F32), pltpu.VMEM(eta.shape, F32), sems(12)],
    )
    from_core = swap(to_core, 1)
    from_chip = swap(to_chip, 2)
    from_far = swap(to_far, 3)
    (own_near,) = kernel(pack_near_kernel, vmem(panel, from_core), vmem(shape(r, 6 * r)))
    near = later(own_near, 1, cyclic=True)
    (own_far,) = kernel(
        pack_far_kernel, vmem(vecs, from_core, from_chip, from_far), vmem(shape(r + 8, 2 * r))
    )
    far = later(own_far, 1)
    (picked,) = kernel(pick_kernel, vmem(turned, before), vmem(shape(6 * bs, r)))
    other = swap(picked, 2)
    (halves,) = kernel(halves_kernel, vmem(turned, before, other), vmem(shape(12 * bs, r)))
    core_halves = swap(halves, 1)
    far_halves = later(halves, 2, cyclic=True)
    m1 = kernel(
        functools.partial(prepare_kernel, bs),
        vmem(pattern, halves, core_halves),
        vmem(*[half(n, n)] * 4),
        [square(F32)],
    )
    (level1,) = kernel(
        level1_kernel,
        vmem(own_near, own_far, near, far, *m1),
        vmem(shape(2 * r + 8, n)),
        [pltpu.VMEM((n + 16, n), BF16)] * 2 + [pltpu.VMEM((2 * r + 16, n), BF16)] * 2,
    )
    earlier = later(level1, 2)
    *a01, t = kernel(
        functools.partial(early_kernel, bs),
        vmem(pattern, halves, core_halves),
        vmem(*[half(n, n)] * 4, shape(n, 2 * r)),
    )
    far_core_halves = swap(far_halves, 1)
    dyn_own, dyn_send, a2, *a23 = kernel(
        functools.partial(rows_kernel, bs),
        vmem(pattern, far_halves, far_core_halves, t),
        vmem(shape(r, n), shape(r, n), shape(n, n), *[half(n, n)] * 4),
    )
    dyn_recv = swap(dyn_send, 2)
    m2 = kernel(product_kernel, vmem(*a01, *a23), vmem(*[half(n, n)] * 4), [square(F32)])
    full, z = kernel(
        ahead_kernel, vmem(level1, *m2), vmem(shape(n, n), shape(n, n)), [square(BF16)] * 2
    )
    to_chip, *u = kernel(
        level2_kernel,
        vmem(level1, earlier, *m2, full, z),
        vmem(shape(n + 8, r), half(n, n), half(n, n)),
        [square(BF16)] * 2 + [pltpu.VMEM((2 * r, n), F32)],
    )
    from_chip = swap(to_chip, 2)
    to_far, short = kernel(
        far_rows_kernel,
        vmem(level1, earlier, *m2, a2, full, z, *u),
        vmem(shape(2 * r + 8, r), shape(8, r)),
        [pltpu.VMEM((8, n), F32), pltpu.VMEM((r, 2 * r), F32)],
    )
    chip_short = swap(short, 2)
    from_far = swap(to_far, 3)
    keep, to_core = kernel(
        rest_kernel,
        vmem(earlier, *m2[2:], full, z, *u, short),
        vmem(shape(n, r), shape(n + 8, r)),
        [pltpu.VMEM((2 * r, n), F32)],
    )
    from_core = swap(to_core, 1)
    diagonal_block, mirrored = kernel(
        turn_kernel, vmem(from_chip), vmem(shape(r, r), shape(2 * r, r))
    )
    mirrored = swap(mirrored, 1)
    whole, line = shape(elements, r, n), shape(elements, r)
    dyn_out, cov_out, cost_out = kernel(
        fill_kernel,
        vmem(keep, from_core, dyn_own, dyn_recv, diagonal_block, from_chip),
        hbm(whole, whole, whole),
        [sems(14)],
    )
    cov_out, cost_out, drift_out, eta_out = kernel(
        place_kernel,
        hbm(cov_out, cost_out) + vmem(short, chip_short, from_core, mirrored, from_far),
        hbm(whole, whole, line, line),
        [pltpu.VMEM((2, elements, r), F32), sems(6)],
        {0: 0, 1: 1},
    )
    return dyn_out, drift_out, cov_out, cost_out, eta_out


def takes_split(elements, r, bs, cols):
    return elements == 2 and cols == 4 and r % 128 == 0 and r % bs == 0 and bs % 8 == 0


def per_device(blocks, pattern, drift, cov, cost, eta):
    elements, r, _ = cov.shape
    bs = blocks.shape[2] // 3
    if takes_split(elements, r, bs, lax.axis_size("col")):
        return per_device_split(blocks, pattern, drift, cov, cost, eta)
    return per_device_general(blocks, pattern, drift, cov, cost, eta)


def solution(mesh):
    return jax.shard_map(
        per_device,
        mesh=mesh,
        in_specs=(
            P("tm", "col", None),
            P(),
            P("tm", "col"),
            P("tm", "col", None),
            P("tm", "col", None),
            P("tm", "col"),
        ),
        out_specs=(
            P("tm", "col", None),
            P("tm", "col"),
            P("tm", "col", None),
            P("tm", "col", None),
            P("tm", "col"),
        ),
        check_vma=False,
    )
```

```python
import functools

import jax
import jax.numpy as jnp
from jax import lax
from jax.experimental import pallas as pl
from jax.experimental.pallas import tpu as pltpu
from jax.sharding import PartitionSpec as P


HIGH = lax.Precision.HIGHEST
F32 = jnp.float32
BF16 = jnp.bfloat16


def shifted(block, axis, distance):
    devices = range(lax.axis_size(axis))
    route = [(i - distance, i) for i in devices if i - distance in devices]
    return lax.ppermute(block, axis, route)


def product(form, left, right):
    return jnp.einsum(form, left, right, precision=HIGH)


def densify(row_blocks, row_ids, pattern, block_size):
    block_count = pattern.shape[0]
    row_block = row_ids // block_size
    chooser = (row_block[:, None] == jnp.arange(block_count, dtype=jnp.int32)[None, :]).astype(
        jnp.int32
    )
    columns = jnp.sum(chooser[:, :, None] * pattern[None, :, :], axis=1)
    matches = (
        columns[:, :, None] == jnp.arange(block_count, dtype=jnp.int32)[None, None, :]
    ).astype(jnp.float32)
    pieces = row_blocks.reshape(row_blocks.shape[:-1] + (3, 1, block_size))
    filled = jnp.sum(matches[:, :, :, None] * pieces, axis=-3)
    return filled.reshape(row_blocks.shape[:-1] + (block_count * block_size,))


def combine_rows(
    dyn_prev_full,
    dyn_own_full,
    dyn_own,
    drift_prev_full,
    drift_own,
    cov_prev,
    cov_own,
    cost_prev,
    cost_own,
    eta_prev,
    eta_own,
    first_row,
):
    height = dyn_own.shape[1]
    dyn_res = product("tij,tjk->tik", dyn_own, dyn_prev_full)
    drift_res = product("tij,tj->ti", dyn_own, drift_prev_full) + drift_own
    carried = eta_own + product("tij,tj->ti", cost_own, drift_prev_full)
    value_rows = product("tij,tjk->tik", cost_own, dyn_prev_full)
    prev_columns = lax.dynamic_slice_in_dim(dyn_prev_full, first_row, height, 2)
    cov_full, carried_full, value_full = (
        lax.all_gather(cov_prev, "col", axis=1, tiled=True),
        lax.all_gather(carried, "col", axis=1, tiled=True),
        lax.all_gather(value_rows, "col", axis=1, tiled=True),
    )
    cost_res = cost_prev + product("tki,tkj->tij", prev_columns, value_full)
    cov_res = (
        product("tik,tjk->tij", product("tij,tjk->tik", dyn_own, cov_full), dyn_own_full) + cov_own
    )
    eta_res = eta_prev + product("tki,tk->ti", prev_columns, carried_full)
    return (dyn_res, drift_res, cov_res, cost_res, eta_res)


def choose(flag, combined, kept):
    return tuple(jnp.where(flag, new, old) for new, old in zip(combined, kept))


def per_device_general(blocks, pattern, drift, cov, cost, eta):
    height = cov.shape[1]
    modes = cov.shape[2]
    block_size = blocks.shape[2] // 3
    first_row = lax.axis_index("col") * height
    own_ids = first_row + jnp.arange(height, dtype=jnp.int32)
    all_ids = jnp.arange(modes, dtype=jnp.int32)
    position = lax.axis_index("tm")
    dyn_own = densify(blocks, own_ids, pattern, block_size)
    received = shifted((blocks, drift, cov, cost, eta), "tm", 1)
    blocks_prev, blocks_own, drift_prev_full = (
        lax.all_gather(received[0], "col", axis=1, tiled=True),
        lax.all_gather(blocks, "col", axis=1, tiled=True),
        lax.all_gather(received[1], "col", axis=1, tiled=True),
    )
    merged = combine_rows(
        densify(blocks_prev, all_ids, pattern, block_size),
        densify(blocks_own, all_ids, pattern, block_size),
        dyn_own,
        drift_prev_full,
        drift,
        received[2],
        cov,
        received[3],
        cost,
        received[4],
        eta,
        first_row,
    )
    current = choose(position >= 1, merged, (dyn_own, drift, cov, cost, eta))
    received = shifted(current, "tm", 2)
    dyn_prev_full = lax.all_gather(received[0], "col", axis=1, tiled=True)
    dyn_own_full = lax.all_gather(current[0], "col", axis=1, tiled=True)
    drift_prev_full = lax.all_gather(received[1], "col", axis=1, tiled=True)
    merged = combine_rows(
        dyn_prev_full,
        dyn_own_full,
        current[0],
        drift_prev_full,
        current[1],
        received[2],
        current[2],
        received[3],
        current[3],
        received[4],
        current[4],
        first_row,
    )
    return choose(position >= 2, merged, current)


def split(x):
    hi = x.astype(BF16)
    lo = (x - hi.astype(F32)).astype(BF16)
    return hi, lo


def dot(a, b):
    return jnp.dot(a, b, preferred_element_type=F32)


def dot3(ah, al, bh, bl):
    return dot(ah, bh) + (dot(ah, bl) + dot(al, bh))


def triangle(r):
    rows = lax.broadcasted_iota(jnp.int32, (r, r), 0)
    cols = lax.broadcasted_iota(jnp.int32, (r, r), 1)
    return rows, cols


def fold(first, second, r):
    rows, cols = triangle(r)
    return jnp.where(rows >= cols, first, second)


def diagonal(block, r):
    rows, cols = triangle(r)
    return jnp.sum(jnp.where(rows == cols, block, 0.0), axis=0, keepdims=True)


def unfold(folded, second_diag, r):
    rows, cols = triangle(r)
    turned = folded.T
    first = jnp.where(rows >= cols, folded, turned)
    second = jnp.where(rows < cols, folded, turned)
    second = jnp.where(rows == cols, jnp.broadcast_to(second_diag, (r, r)), second)
    return first, second


UPPER = ((0, 1), (0, 2), (0, 3), (1, 2), (1, 3), (2, 3))


def spread(packed, r, put, rows=(0, 1, 2, 3)):
    panel0, panel1, diags = packed[0:r], packed[r : 2 * r], packed[2 * r : 2 * r + 1]
    for at, (panel, pair) in enumerate(((panel0, (0, 1)), (panel1, (2, 3)))):
        if pair[0] in rows or pair[1] in rows:
            blocks = unfold(panel[:, 0:r], diags[:, at * r : (at + 1) * r], r)
            for i, block in zip(pair, blocks):
                if i in rows:
                    put(i, i, block)
    for at, (i, j) in enumerate(UPPER):
        panel = panel0 if at < 3 else panel1
        block = panel[:, (at % 3 + 1) * r : (at % 3 + 2) * r]
        if i in rows:
            put(i, j, block)
        if j in rows:
            put(j, i, block.T)


def column(row, r):
    rows, cols = triangle(r)
    pieces = []
    for at in range(row.shape[1] // r):
        piece = jnp.broadcast_to(row[:, at * r : (at + 1) * r], (r, r))
        pieces.append(jnp.sum(jnp.where(rows == cols, piece, 0.0), axis=1, keepdims=True))
    return jnp.concatenate(pieces, axis=0)


def row_times(row, matrix, r):
    return jnp.sum(column(row, r) * matrix, axis=0, keepdims=True)


def place_of():
    q = lax.axis_index("col")
    return q, q >> 1, q & 1


def has(distance):
    return (lax.axis_index("tm") >= distance).astype(jnp.int32)


def lanes(index, r):
    return pl.ds(pl.multiple_of(index * r, r), r)


def copy_all(pairs, sems):
    copies = [
        pltpu.make_async_copy(source, target, sems.at[i]) for i, (source, target) in enumerate(pairs)
    ]
    for copy in copies:
        copy.start()
    for copy in copies:
        copy.wait()


def send_kernel(
    cov, cost, drift, eta, to_core, to_chip, to_far, panel, vecs, b_in, e_in, sems
):
    q, y, c = place_of()
    r = to_far.shape[1]

    def load(mine, theirs):
        pairs = []
        for j in range(2, 4):
            source = mine.at[1 - y, :, lanes((q ^ 2) ^ j, r)]
            pairs.append((source, to_chip.at[pl.ds(0, r), pl.ds((j - 2) * r, r)]))
        pairs.append((theirs.at[1 - y, :, lanes(q, r)], to_far.at[pl.ds(0, r), :]))
        for j in range(1, 4):
            source = theirs.at[y, :, lanes((q ^ 1) ^ j, r)]
            pairs.append((source, to_core.at[pl.ds(0, r), pl.ds((j - 1) * r, r)]))
        for j in range(4):
            pairs.append((mine.at[y, :, lanes(q ^ j, r)], panel.at[:, pl.ds(j * r, r)]))
        pairs.append((drift, b_in))
        pairs.append((eta, e_in))
        copy_all(pairs, sems)

    @pl.when(c == 0)
    def _():
        load(cov, cost)

    @pl.when(c == 1)
    def _():
        load(cost, cov)

    b, e = b_in[pl.ds(y, 1), :], e_in[pl.ds(y, 1), :]
    vecs[...] = jnp.zeros(vecs.shape, F32)
    vecs[0:1, :] = b
    vecs[1:2, :] = e
    to_core[r : r + 8, :] = jnp.zeros((8, 3 * r), F32)
    to_core[r : r + 1, 0:r] = b
    to_core[r : r + 1, r : 2 * r] = e
    b, e = b_in[pl.ds(1 - y, 1), :], e_in[pl.ds(1 - y, 1), :]
    to_chip[r : r + 8, :] = jnp.zeros((8, 2 * r), F32)
    to_chip[r : r + 1, 0:r] = b
    to_chip[r : r + 1, r : 2 * r] = e
    to_far[r : r + 8, :] = jnp.zeros((8, r), F32)
    to_far[r : r + 1, :] = b
    to_far[r + 1 : r + 2, :] = e


def pack_near_kernel(panel, from_core, packed):
    r = panel.shape[0]
    packed[:, 0:r] = fold(panel[:, 0:r], from_core[0:r, 0:r], r)
    packed[:, r : 4 * r] = panel[:, r:]
    packed[:, 4 * r :] = from_core[0:r, r : 3 * r]


def pack_far_kernel(vecs, from_core, from_chip, from_far, packed):
    r = vecs.shape[1]
    k33 = from_far[0:r, :]
    packed[0:r, 0:r] = fold(from_chip[0:r, 0:r], k33, r)
    packed[0:r, r:] = from_chip[0:r, r : 2 * r]
    packed[r : r + 1, 0:r] = diagonal(from_core[0:r, 0:r], r)
    packed[r : r + 1, r:] = diagonal(k33, r)
    b = (
        vecs[0:1, :],
        from_core[r : r + 1, 0:r],
        from_chip[r : r + 1, 0:r],
        from_far[r : r + 1, :],
    )
    e = (
        vecs[1:2, :],
        from_core[r : r + 1, r : 2 * r],
        from_chip[r : r + 1, r : 2 * r],
        from_far[r + 1 : r + 2, :],
    )
    for j in range(4):
        at = slice(j % 2 * r, (j % 2 + 1) * r)
        packed[r + 1 + j // 2 : r + 2 + j // 2, at] = b[j]
        packed[r + 3 + j // 2 : r + 4 + j // 2, at] = e[j]
    packed[r + 5 : r + 8, :] = jnp.zeros((3, 2 * r), F32)


def far_row(packed, r, at):
    return jnp.concatenate(
        [packed[r + at : r + at + 1, :], packed[r + at + 1 : r + at + 2, :]], axis=1
    )


def pick_kernel(turned, before, out):
    y = place_of()[1]
    height = turned.shape[1]
    out[0:height, :] = turned[1 - y]
    out[height:, :] = before[1 - y]


def halves_kernel(turned, before, other, own, earlier):
    y = place_of()[1]
    height = turned.shape[1]
    own[0:height, :] = turned[y]
    own[height:, :] = other[0:height, :]
    earlier[0:height, :] = before[y]
    earlier[height:, :] = other[height:, :]


def dense_turned(put, pattern, own_half, core_half, flag, n, r, bs):
    q = place_of()[0]
    sub = 8
    lane = lax.broadcasted_iota(jnp.int32, (sub, r), 1) // bs
    rows = lax.broadcasted_iota(jnp.int32, (bs, r), 0)
    cols = lax.broadcasted_iota(jnp.int32, (bs, r), 1)
    per = r // bs
    height = 3 * bs
    for j in range(4):
        half = own_half if j % 2 == 0 else core_half
        pieces, wanted = [], []
        for k in range(3):
            at = (j // 2) * height + k * bs
            pieces.append(half[at : at + bs, :].reshape(bs // sub, sub, r))
            want = jnp.zeros((sub, r), jnp.int32)
            for h in range(per):
                block = pattern[pl.ds((q ^ j) * per + h, 1), :][:, k : k + 1] ^ (q * per)
                want = jnp.where(lane == h, jnp.broadcast_to(block, (sub, r)), want)
            wanted.append(jnp.where(flag == 1, want, -1))
        for block in range(n // bs):
            if j * r <= block * bs < (j + 1) * r:
                value = jnp.where(
                    jnp.logical_and(rows + block * bs == cols + j * r, flag == 0), 1.0, 0.0
                ).reshape(bs // sub, sub, r)
            else:
                value = jnp.zeros((bs // sub, sub, r), F32)
            for k in range(3):
                value = jnp.where((wanted[k] == block)[None], pieces[k], value)
            put(
                slice(block * bs, (block + 1) * bs),
                slice(j * r, (j + 1) * r),
                value.reshape(bs, r),
            )


def put_split(hi_ref, lo_ref, rows, cols, value):
    hi, lo = split(value)
    hi_ref[rows, cols] = hi
    lo_ref[rows, cols] = lo


def transpose_split(hi_ref, lo_ref, source, r):
    n = source.shape[0]
    for i in range(n // r):
        for j in range(n // r):
            put_split(
                hi_ref,
                lo_ref,
                slice(j * r, (j + 1) * r),
                slice(i * r, (i + 1) * r),
                source[i * r : (i + 1) * r, j * r : (j + 1) * r].T,
            )


def straight_split(hi_ref, lo_ref, source, r):
    n = source.shape[0]
    for i in range(n // r):
        put_split(
            hi_ref, lo_ref, slice(i * r, (i + 1) * r), slice(None), source[i * r : (i + 1) * r, :]
        )


def prepare_kernel(bs, pattern, own, own_core, before, before_core, mh, ml, th, tl, dense):
    c, has1 = place_of()[2], has(1)
    n = dense.shape[0]
    r = own.shape[1]
    first = c == 0
    own_half = jnp.where(first, own[...], before[...])
    core_half = jnp.where(first, own_core[...], before_core[...])
    flag = jnp.where(first, 1, has1)

    def put(row, col, value):
        dense[row, col] = value

    dense_turned(put, pattern, own_half, core_half, flag, n, r, bs)

    @pl.when(first)
    def _():
        straight_split(mh, ml, dense, r)
        transpose_split(th, tl, dense, r)

    @pl.when(jnp.logical_not(first))
    def _():
        straight_split(th, tl, dense, r)
        transpose_split(mh, ml, dense, r)


def level1_kernel(own_near, own_far, near, far, mh, ml, th, tl, out, xh, xl, sh, sl):
    c = place_of()[2]
    r = own_near.shape[0]
    n = 4 * r
    extra = slice(n, n + 16)
    first = c == 0
    came = jnp.where(has(1) == 1, near[...], 0.0)
    xn = jnp.where(first, came, own_near[...])
    xf = jnp.where(first, far[...], own_far[...])
    x = jnp.concatenate(
        [
            xn[:, 0 : 4 * r],
            jnp.concatenate([xf[0:r, 0:r], xn[:, 4 * r :], xf[0:r, r:]], axis=1),
            jnp.concatenate([xf[r : r + 1, :], xf[r : r + 1, :]], axis=1),
        ],
        axis=0,
    )

    def put(i, j, block):
        put_split(xh, xl, slice(i * r, (i + 1) * r), slice(j * r, (j + 1) * r), block)

    spread(x, r, put)
    b_before, b_own = far_row(far, r, 1), far_row(own_far, r, 1)
    e_before, e_own = far_row(far, r, 3), far_row(own_far, r, 3)
    row = jnp.broadcast_to(jnp.where(first, b_before, e_own), (16, n))
    put_split(xh, xl, extra, slice(None), row)
    u = dot3(xh[...], xl[...], mh[...], ml[...])
    uh, ul = split(u[0:n, :])
    sh[0 : 2 * r, :] = th[0 : 2 * r, :]
    sl[0 : 2 * r, :] = tl[0 : 2 * r, :]
    row = jnp.broadcast_to(jnp.where(first, 0.0, b_before), (16, n))
    put_split(sh, sl, slice(2 * r, 2 * r + 16), slice(None), row)
    top = dot3(sh[...], sl[...], uh, ul)
    low = dot3(th[2 * r :, :], tl[2 * r :, :], uh[:, 2 * r :], ul[:, 2 * r :])
    vec = jnp.where(first, b_own, e_before) + u[n : n + 1, :] + top[2 * r : 2 * r + 1, :]
    dn = jnp.where(first, own_near[...], came)
    df = jnp.where(first, own_far[...], far[...])
    z11 = top[r : 2 * r, r : 2 * r]
    z33 = low[r : 2 * r, r : 2 * r]
    out[0:r, 0:r] = fold(top[0:r, 0:r], z11, r) + dn[:, 0:r]
    out[0:r, r:] = top[0:r, r:] + dn[:, r : 4 * r]
    out[r : 2 * r, 0:r] = fold(low[0:r, 0:r], z33, r) + df[0:r, 0:r]
    out[r : 2 * r, r : 3 * r] = top[r : 2 * r, 2 * r :] + dn[:, 4 * r :]
    out[r : 2 * r, 3 * r :] = low[0:r, r : 2 * r] + df[0:r, r:]
    base = 2 * r
    out[base : base + 1, 0:r] = diagonal(z11, r) + df[r : r + 1, 0:r]
    out[base : base + 1, r : 2 * r] = diagonal(z33, r) + df[r : r + 1, r:]
    out[base : base + 1, 2 * r :] = jnp.zeros((1, 2 * r), F32)
    out[base + 1 : base + 2, :] = b_own
    out[base + 2 : base + 3, :] = vec
    out[base + 3 : base + 4, :] = b_before
    out[base + 4 : base + 8, :] = jnp.zeros((4, 4 * r), F32)


def early_kernel(bs, pattern, own, own_core, before, before_core, a0h, a0l, a1h, a1l, t):
    n = a0h.shape[0]
    r = own.shape[1]
    for flag, mine, theirs, hi, lo in (
        (1, own, own_core, a0h, a0l),
        (has(1), before, before_core, a1h, a1l),
    ):
        put = functools.partial(put_split, hi, lo)
        dense_turned(put, pattern, mine[...], theirs[...], flag, n, r, bs)

    def wanted(ref):
        return jnp.concatenate([ref[:, 0:r], ref[:, 2 * r : 3 * r]], axis=1)

    t[...] = dot3(a1h[...], a1l[...], wanted(a0h), wanted(a0l))


def third_kernel(bs, pattern, mine, theirs, t, out, a2, a2h, a2l):
    n = a2.shape[0]
    r = mine.shape[1]

    def put(row, col, value):
        put_split(a2h, a2l, row, col, value)
        a2[row, col] = value

    dense_turned(put, pattern, mine[...], theirs[...], has(2), n, r, bs)
    out[...] = dot3(a2h[...], a2l[...], *split(t[...]))


def rows_kernel(bs, pattern, mine, theirs, t, dyn_own, dyn_send, a3h, a3l):
    q, _, _ = place_of()
    n = a3h.shape[0]
    r = mine.shape[1]
    put = functools.partial(put_split, a3h, a3l)
    dense_turned(put, pattern, mine[...], theirs[...], has(3), n, r, bs)
    rows = dot3(a3h[...], a3l[...], *split(t[...]))
    for j in range(4):
        at = lanes(q ^ j, r)
        dyn_own[:, at] = rows[j * r : (j + 1) * r, 0:r].T
        dyn_send[:, at] = rows[j * r : (j + 1) * r, r : 2 * r].T


def product_kernel(
    a0h, a0l, a1h, a1l, a2h, a2l, a3h, a3l, mh, ml, th, tl, product_ref
):
    first = place_of()[2] == 0
    r = a0h.shape[0] // 4

    @pl.when(first)
    def _():
        product_ref[...] = dot3(a1h[...], a1l[...], a0h[...], a0l[...])
        straight_split(mh, ml, product_ref, r)
        transpose_split(th, tl, product_ref, r)

    @pl.when(jnp.logical_not(first))
    def _():
        product_ref[...] = dot3(a3h[...], a3l[...], a2h[...], a2l[...])
        straight_split(th, tl, product_ref, r)
        transpose_split(mh, ml, product_ref, r)


def ahead_kernel(own, mh, ml, th, tl, full, z, xh, xl):
    r = own.shape[1] // 4

    def put(i, j, block):
        full[i * r : (i + 1) * r, j * r : (j + 1) * r] = block

    spread(own, r, put)

    @pl.when(place_of()[2] == 1)
    def _():
        straight_split(xh, xl, full, r)
        u = dot3(xh[...], xl[...], mh[...], ml[...])
        z[...] = dot3(th[...], tl[...], *split(u))


def put_rows(ref, value, q, r):
    for j in range(4):
        ref[lanes(q ^ j, r), :] = value[:, j * r : (j + 1) * r]


def came(earlier):
    return jnp.where(has(2) == 1, earlier[...], 0.0)


CROSSING = ((2, 0), (2, 1), (2, 3))


def level2_kernel(own, earlier, mh, ml, th, tl, full, z, to_chip, uh, ul, xh, xl, rest):
    c = place_of()[2]
    r = own.shape[1] // 4
    earlier = came(earlier)
    two, three = slice(2 * r, 3 * r), slice(3 * r, 4 * r)

    @pl.when(c == 0)
    def _():
        def put(i, j, block):
            put_split(xh, xl, slice(i * r, (i + 1) * r), slice(j * r, (j + 1) * r), block)

        spread(earlier, r, put)
        hi, lo = split(dot3(xh[...], xl[...], mh[...], ml[...]))
        uh[...] = hi
        ul[...] = lo
        rest[:, 2 * r :] = dot3(th[2 * r :, :], tl[2 * r :, :], hi[:, 2 * r :], lo[:, 2 * r :])
        rest[0:r, 0 : 2 * r] = dot3(th[two, :], tl[two, :], hi[:, 0 : 2 * r], lo[:, 0 : 2 * r])
        rest[:, 2 * r :] = rest[:, 2 * r :] + full[2 * r :, 2 * r :]
        rest[0:r, 0 : 2 * r] = rest[0:r, 0 : 2 * r] + full[two, 0 : 2 * r]

    @pl.when(c == 1)
    def _():
        def put(i, j, block):
            if (i, j) in CROSSING or i == j:
                rows = slice((i - 2) * r, (i - 1) * r)
                cols = slice(j * r, (j + 1) * r)
                rest[rows, cols] = z[i * r : (i + 1) * r, cols] + block

        spread(earlier, r, put, rows=(2, 3))

    z33 = rest[r : 2 * r, three]
    to_chip[0:r, :] = fold(rest[0:r, two], z33, r)
    for at, (_, j) in enumerate(CROSSING):
        to_chip[(at + 1) * r : (at + 2) * r, :] = rest[0:r, j * r : (j + 1) * r]
    to_chip[4 * r :, :] = jnp.broadcast_to(diagonal(z33, r), (8, r))


def far_rows_kernel(
    own, earlier, mh, ml, th, tl, a2, full, z, uh, ul, to_far, short, vec, rest
):
    c = place_of()[2]
    r = own.shape[1] // 4
    earlier = came(earlier)
    base = 2 * r
    three = slice(3 * r, 4 * r)
    b1 = earlier[base + 1 : base + 2, :] + row_times(earlier[base + 3 : base + 4, :], a2[...], r)

    @pl.when(c == 0)
    def _():
        value = dot3(th[three, :], tl[three, :], uh[:, 0 : 2 * r], ul[:, 0 : 2 * r])
        rest[...] = value + full[three, 0 : 2 * r]
        vec[0:1, :] = b1
        vec[1:2, :] = own[base + 2 : base + 3, :]

    @pl.when(c == 1)
    def _():
        def put(i, j, block):
            if j < 2:
                cols = slice(j * r, (j + 1) * r)
                rest[:, cols] = z[three, cols] + block

        spread(earlier, r, put, rows=(3,))
        vec[0:1, :] = own[base + 2 : base + 3, :] + row_times(b1, full[...], r)
        vec[1:2, :] = earlier[base + 2 : base + 3, :]

    to_far[0:r, :] = rest[:, 0:r]
    to_far[r : 2 * r, :] = rest[:, r : 2 * r]
    out = vec[1:2, :] + row_times(vec[0:1, :], mh[...].astype(F32) + ml[...].astype(F32), r)
    to_far[2 * r :, :] = jnp.broadcast_to(out[:, 3 * r :], (8, r))
    for i in range(4):
        short[i : i + 1, :] = out[:, i * r : (i + 1) * r]
    short[4:8, :] = jnp.zeros((4, r), F32)


def rest_kernel(earlier, th, tl, full, z, uh, ul, short, keep, to_core, rest):
    q, _, c = place_of()
    r = earlier.shape[1] // 4
    earlier = came(earlier)

    @pl.when(c == 0)
    def _():
        rest[...] = dot3(th[0 : 2 * r, :], tl[0 : 2 * r, :], uh[...], ul[...]) + full[0 : 2 * r, :]

    @pl.when(c == 1)
    def _():
        def put(i, j, block):
            rows = slice(i * r, (i + 1) * r)
            cols = slice(j * r, (j + 1) * r)
            rest[rows, cols] = z[rows, cols] + block

        spread(earlier, r, put, rows=(0, 1))

    put_rows(keep, rest[0:r, :], q, r)
    put_rows(to_core, rest[r : 2 * r, :], q, r)
    to_core[4 * r :, :] = jnp.broadcast_to(short[1:2, :], (8, r))


def turn_kernel(from_chip, diagonal_block, mirrored):
    r = diagonal_block.shape[0]
    first, second = unfold(from_chip[0:r, :], from_chip[4 * r : 4 * r + 1, :], r)
    diagonal_block[...] = first
    mirrored[0:r, :] = from_chip[3 * r : 4 * r, :].T
    mirrored[r : 2 * r, :] = second


def panel_copies(panel, target, element, r):
    return [
        (panel.at[pl.ds(g * r, r), :], target.at[element, :, pl.ds(g * r, r)]) for g in range(4)
    ]


def block_copies(blocks, target, element, r):
    return [(source, target.at[element, :, lanes(at, r)]) for source, at in blocks]


def fill_kernel(
    keep,
    from_core,
    dyn_own,
    dyn_recv,
    diagonal_block,
    from_chip,
    dyn_out,
    cov_out,
    cost_out,
    sems,
):
    q, y, c = place_of()
    r = dyn_own.shape[0]
    dyn = [(dyn_own, dyn_out.at[y]), (dyn_recv, dyn_out.at[1 - y])]
    blocks = [(diagonal_block, q)] + [
        (from_chip.at[pl.ds(at * r, r), :], q ^ bit) for at, bit in ((1, 2), (2, 3), (3, 1))
    ]

    def write(mine, other):
        copy_all(
            dyn
            + panel_copies(keep, mine, y, r)
            + panel_copies(from_core, other, y, r)
            + block_copies(blocks, mine, 1 - y, r),
            sems,
        )

    @pl.when(c == 0)
    def _():
        write(cov_out, cost_out)

    @pl.when(c == 1)
    def _():
        write(cost_out, cov_out)


def place_kernel(
    cov_in,
    cost_in,
    short,
    chip_short,
    from_core,
    mirrored,
    panel,
    cov_out,
    cost_out,
    drift_out,
    eta_out,
    lines,
    sems,
):
    del cov_in, cost_in
    q, y, c = place_of()
    first = c == 0
    r = short.shape[1]
    mine, other = short[0:1, :], from_core[4 * r : 4 * r + 1, :]
    chip, far = chip_short[2:3, :], panel[2 * r : 2 * r + 1, :]
    for at, (one, two, three, four) in enumerate(
        ((mine, other, chip, far), (other, mine, far, chip))
    ):
        lines[at, pl.ds(y, 1), :] = jnp.where(first, one, two)
        lines[at, pl.ds(1 - y, 1), :] = jnp.where(first, three, four)
    vectors = [(lines.at[0], drift_out), (lines.at[1], eta_out)]
    near, far = pl.ds(0, r), pl.ds(r, r)
    blocks = [
        (panel.at[near, :], q ^ 3),
        (panel.at[far, :], q ^ 2),
        (mirrored.at[near, :], q ^ 1),
        (mirrored.at[far, :], q),
    ]

    @pl.when(first)
    def _():
        copy_all(vectors + block_copies(blocks, cost_out, 1 - y, r), sems)

    @pl.when(c == 1)
    def _():
        copy_all(vectors + block_copies(blocks, cov_out, 1 - y, r), sems)


IN_HBM, IN_VMEM = 0, 1


def kernel(body, operands, shapes, scratch=(), aliases=None):
    specs = {
        IN_HBM: pl.BlockSpec(memory_space=pltpu.HBM),
        IN_VMEM: pl.BlockSpec(memory_space=pltpu.VMEM),
    }
    call = pl.pallas_call(
        body,
        in_specs=[specs[where] for where, _ in operands],
        out_specs=[specs[where] for where, _ in shapes],
        out_shape=[
            pltpu.VMEM(s.shape, s.dtype) if where == IN_VMEM else s for where, s in shapes
        ],
        scratch_shapes=list(scratch),
        input_output_aliases=aliases or {},
        compiler_params=pltpu.CompilerParams(vmem_limit_bytes=20 * 2**20),
    )
    kept = {IN_HBM: pltpu.HBM, IN_VMEM: pltpu.VMEM}
    return call(
        *(
            pltpu.with_memory_space_constraint(x, kept[where]) if where in kept else x
            for where, x in operands
        )
    )


def per_device_split(blocks, pattern, drift, cov, cost, eta):
    elements, r, n = cov.shape
    bs = blocks.shape[2] // 3
    tms, cols = lax.axis_size("tm"), lax.axis_size("col")

    def swap(value, bit):
        return lax.ppermute(value, "col", [(i, i ^ bit) for i in range(cols)])

    def later(value, distance, cyclic=False):
        count = tms if cyclic else tms - distance
        return lax.ppermute(value, "tm", [(i, (i + distance) % tms) for i in range(count)])

    def hbm(*arrays):
        return [(IN_HBM, x) for x in arrays]

    def vmem(*arrays):
        return [(IN_VMEM, x) for x in arrays]

    def shape(*dims):
        return jax.ShapeDtypeStruct(dims, F32)

    def half(*dims):
        return jax.ShapeDtypeStruct(dims, BF16)

    def square(dtype):
        return pltpu.VMEM((n, n), dtype)

    def sems(count):
        return pltpu.SemaphoreType.DMA((count,))

    turned = jnp.swapaxes(blocks, 1, 2)
    before = later(turned, 1, cyclic=True)
    to_core, to_chip, to_far, panel, vecs = kernel(
        send_kernel,
        hbm(cov, cost, drift, eta),
        vmem(shape(r + 8, 3 * r), shape(r + 8, 2 * r), shape(r + 8, r), shape(r, n), shape(8, r)),
        [pltpu.VMEM(drift.shape, F32), pltpu.VMEM(eta.shape, F32), sems(12)],
    )
    from_core = swap(to_core, 1)
    from_chip = swap(to_chip, 2)
    from_far = swap(to_far, 3)
    (own_near,) = kernel(pack_near_kernel, vmem(panel, from_core), vmem(shape(r, 6 * r)))
    near = later(own_near, 1, cyclic=True)
    (own_far,) = kernel(
        pack_far_kernel, vmem(vecs, from_core, from_chip, from_far), vmem(shape(r + 8, 2 * r))
    )
    far = later(own_far, 1)
    (picked,) = kernel(pick_kernel, vmem(turned, before), vmem(shape(6 * bs, r)))
    other = swap(picked, 2)
    own_half, before_half = kernel(
        halves_kernel, vmem(turned, before, other), vmem(shape(6 * bs, r), shape(6 * bs, r))
    )
    pairs = (own_half, swap(own_half, 1), before_half, swap(before_half, 1))
    third = later(own_half, 2, cyclic=True)
    fourth = later(before_half, 2, cyclic=True)
    m1 = kernel(
        functools.partial(prepare_kernel, bs),
        vmem(pattern, *pairs),
        vmem(*[half(n, n)] * 4),
        [square(F32)],
    )
    (level1,) = kernel(
        level1_kernel,
        vmem(own_near, own_far, near, far, *m1),
        vmem(shape(2 * r + 8, n)),
        [pltpu.VMEM((n + 16, n), BF16)] * 2 + [pltpu.VMEM((2 * r + 16, n), BF16)] * 2,
    )
    earlier = later(level1, 2, cyclic=True)
    *a01, t = kernel(
        functools.partial(early_kernel, bs),
        vmem(pattern, *pairs),
        vmem(*[half(n, n)] * 4, shape(n, 2 * r)),
    )
    t, a2, *a2_split = kernel(
        functools.partial(third_kernel, bs),
        vmem(pattern, third, swap(third, 1), t),
        vmem(shape(n, 2 * r), shape(n, n), half(n, n), half(n, n)),
    )
    dyn_own, dyn_send, *a3_split = kernel(
        functools.partial(rows_kernel, bs),
        vmem(pattern, fourth, swap(fourth, 1), t),
        vmem(shape(r, n), shape(r, n), half(n, n), half(n, n)),
    )
    a23 = (*a2_split, *a3_split)
    dyn_recv = swap(dyn_send, 2)
    m2 = kernel(product_kernel, vmem(*a01, *a23), vmem(*[half(n, n)] * 4), [square(F32)])
    full, z = kernel(
        ahead_kernel, vmem(level1, *m2), vmem(shape(n, n), shape(n, n)), [square(BF16)] * 2
    )
    to_chip, *u = kernel(
        level2_kernel,
        vmem(level1, earlier, *m2, full, z),
        vmem(shape(n + 8, r), half(n, n), half(n, n)),
        [square(BF16)] * 2 + [pltpu.VMEM((2 * r, n), F32)],
    )
    from_chip = swap(to_chip, 2)
    to_far, short = kernel(
        far_rows_kernel,
        vmem(level1, earlier, *m2, a2, full, z, *u),
        vmem(shape(2 * r + 8, r), shape(8, r)),
        [pltpu.VMEM((8, n), F32), pltpu.VMEM((r, 2 * r), F32)],
    )
    chip_short = swap(short, 2)
    from_far = swap(to_far, 3)
    keep, to_core = kernel(
        rest_kernel,
        vmem(earlier, *m2[2:], full, z, *u, short),
        vmem(shape(n, r), shape(n + 8, r)),
        [pltpu.VMEM((2 * r, n), F32)],
    )
    from_core = swap(to_core, 1)
    diagonal_block, mirrored = kernel(
        turn_kernel, vmem(from_chip), vmem(shape(r, r), shape(2 * r, r))
    )
    mirrored = swap(mirrored, 1)
    whole, line = shape(elements, r, n), shape(elements, r)
    dyn_out, cov_out, cost_out = kernel(
        fill_kernel,
        vmem(keep, from_core, dyn_own, dyn_recv, diagonal_block, from_chip),
        hbm(whole, whole, whole),
        [sems(14)],
    )
    cov_out, cost_out, drift_out, eta_out = kernel(
        place_kernel,
        hbm(cov_out, cost_out) + vmem(short, chip_short, from_core, mirrored, from_far),
        hbm(whole, whole, line, line),
        [pltpu.VMEM((2, elements, r), F32), sems(6)],
        {0: 0, 1: 1},
    )
    return dyn_out, drift_out, cov_out, cost_out, eta_out


def takes_split(elements, r, bs, cols):
    return elements == 2 and cols == 4 and r % 128 == 0 and r % bs == 0 and bs % 8 == 0


def per_device(blocks, pattern, drift, cov, cost, eta):
    elements, r, _ = cov.shape
    bs = blocks.shape[2] // 3
    if takes_split(elements, r, bs, lax.axis_size("col")):
        return per_device_split(blocks, pattern, drift, cov, cost, eta)
    return per_device_general(blocks, pattern, drift, cov, cost, eta)


def solution(mesh):
    return jax.shard_map(
        per_device,
        mesh=mesh,
        in_specs=(
            P("tm", "col", None),
            P(),
            P("tm", "col"),
            P("tm", "col", None),
            P("tm", "col", None),
            P("tm", "col"),
        ),
        out_specs=(
            P("tm", "col", None),
            P("tm", "col"),
            P("tm", "col", None),
            P("tm", "col", None),
            P("tm", "col"),
        ),
        check_vma=False,
    )
```

```python
import functools

import jax
import jax.numpy as jnp
from jax import lax
from jax.experimental import pallas as pl
from jax.experimental.pallas import tpu as pltpu
from jax.sharding import PartitionSpec as P


HIGH = lax.Precision.HIGHEST
F32 = jnp.float32
BF16 = jnp.bfloat16


def shifted(block, axis, distance):
    devices = range(lax.axis_size(axis))
    route = [(i - distance, i) for i in devices if i - distance in devices]
    return lax.ppermute(block, axis, route)


def product(form, left, right):
    return jnp.einsum(form, left, right, precision=HIGH)


def densify(row_blocks, row_ids, pattern, block_size):
    block_count = pattern.shape[0]
    row_block = row_ids // block_size
    chooser = (row_block[:, None] == jnp.arange(block_count, dtype=jnp.int32)[None, :]).astype(
        jnp.int32
    )
    columns = jnp.sum(chooser[:, :, None] * pattern[None, :, :], axis=1)
    matches = (
        columns[:, :, None] == jnp.arange(block_count, dtype=jnp.int32)[None, None, :]
    ).astype(jnp.float32)
    pieces = row_blocks.reshape(row_blocks.shape[:-1] + (3, 1, block_size))
    filled = jnp.sum(matches[:, :, :, None] * pieces, axis=-3)
    return filled.reshape(row_blocks.shape[:-1] + (block_count * block_size,))


def combine_rows(
    dyn_prev_full,
    dyn_own_full,
    dyn_own,
    drift_prev_full,
    drift_own,
    cov_prev,
    cov_own,
    cost_prev,
    cost_own,
    eta_prev,
    eta_own,
    first_row,
):
    height = dyn_own.shape[1]
    dyn_res = product("tij,tjk->tik", dyn_own, dyn_prev_full)
    drift_res = product("tij,tj->ti", dyn_own, drift_prev_full) + drift_own
    carried = eta_own + product("tij,tj->ti", cost_own, drift_prev_full)
    value_rows = product("tij,tjk->tik", cost_own, dyn_prev_full)
    prev_columns = lax.dynamic_slice_in_dim(dyn_prev_full, first_row, height, 2)
    cov_full, carried_full, value_full = (
        lax.all_gather(cov_prev, "col", axis=1, tiled=True),
        lax.all_gather(carried, "col", axis=1, tiled=True),
        lax.all_gather(value_rows, "col", axis=1, tiled=True),
    )
    cost_res = cost_prev + product("tki,tkj->tij", prev_columns, value_full)
    cov_res = (
        product("tik,tjk->tij", product("tij,tjk->tik", dyn_own, cov_full), dyn_own_full) + cov_own
    )
    eta_res = eta_prev + product("tki,tk->ti", prev_columns, carried_full)
    return (dyn_res, drift_res, cov_res, cost_res, eta_res)


def choose(flag, combined, kept):
    return tuple(jnp.where(flag, new, old) for new, old in zip(combined, kept))


def per_device_general(blocks, pattern, drift, cov, cost, eta):
    height = cov.shape[1]
    modes = cov.shape[2]
    block_size = blocks.shape[2] // 3
    first_row = lax.axis_index("col") * height
    own_ids = first_row + jnp.arange(height, dtype=jnp.int32)
    all_ids = jnp.arange(modes, dtype=jnp.int32)
    position = lax.axis_index("tm")
    dyn_own = densify(blocks, own_ids, pattern, block_size)
    received = shifted((blocks, drift, cov, cost, eta), "tm", 1)
    blocks_prev, blocks_own, drift_prev_full = (
        lax.all_gather(received[0], "col", axis=1, tiled=True),
        lax.all_gather(blocks, "col", axis=1, tiled=True),
        lax.all_gather(received[1], "col", axis=1, tiled=True),
    )
    merged = combine_rows(
        densify(blocks_prev, all_ids, pattern, block_size),
        densify(blocks_own, all_ids, pattern, block_size),
        dyn_own,
        drift_prev_full,
        drift,
        received[2],
        cov,
        received[3],
        cost,
        received[4],
        eta,
        first_row,
    )
    current = choose(position >= 1, merged, (dyn_own, drift, cov, cost, eta))
    received = shifted(current, "tm", 2)
    dyn_prev_full = lax.all_gather(received[0], "col", axis=1, tiled=True)
    dyn_own_full = lax.all_gather(current[0], "col", axis=1, tiled=True)
    drift_prev_full = lax.all_gather(received[1], "col", axis=1, tiled=True)
    merged = combine_rows(
        dyn_prev_full,
        dyn_own_full,
        current[0],
        drift_prev_full,
        current[1],
        received[2],
        current[2],
        received[3],
        current[3],
        received[4],
        current[4],
        first_row,
    )
    return choose(position >= 2, merged, current)


def split(x):
    hi = x.astype(BF16)
    lo = (x - hi.astype(F32)).astype(BF16)
    return hi, lo


def dot(a, b):
    return jnp.dot(a, b, preferred_element_type=F32)


def dot3(ah, al, bh, bl):
    return dot(ah, bh) + (dot(ah, bl) + dot(al, bh))


def triangle(r):
    rows = lax.broadcasted_iota(jnp.int32, (r, r), 0)
    cols = lax.broadcasted_iota(jnp.int32, (r, r), 1)
    return rows, cols


def fold(first, second, r):
    rows, cols = triangle(r)
    return jnp.where(rows >= cols, first, second)


def diagonal(block, r):
    rows, cols = triangle(r)
    return jnp.sum(jnp.where(rows == cols, block, 0.0), axis=0, keepdims=True)


def unfold(folded, second_diag, r):
    rows, cols = triangle(r)
    turned = folded.T
    first = jnp.where(rows >= cols, folded, turned)
    second = jnp.where(rows < cols, folded, turned)
    second = jnp.where(rows == cols, jnp.broadcast_to(second_diag, (r, r)), second)
    return first, second


UPPER = ((0, 1), (0, 2), (0, 3), (1, 2), (1, 3), (2, 3))


def spread(packed, r, put, rows=(0, 1, 2, 3)):
    panel0, panel1, diags = packed[0:r], packed[r : 2 * r], packed[2 * r : 2 * r + 1]
    for at, (panel, pair) in enumerate(((panel0, (0, 1)), (panel1, (2, 3)))):
        if pair[0] in rows or pair[1] in rows:
            blocks = unfold(panel[:, 0:r], diags[:, at * r : (at + 1) * r], r)
            for i, block in zip(pair, blocks):
                if i in rows:
                    put(i, i, block)
    for at, (i, j) in enumerate(UPPER):
        panel = panel0 if at < 3 else panel1
        block = panel[:, (at % 3 + 1) * r : (at % 3 + 2) * r]
        if i in rows:
            put(i, j, block)
        if j in rows:
            put(j, i, block.T)


def column(row, r):
    rows, cols = triangle(r)
    pieces = []
    for at in range(row.shape[1] // r):
        piece = jnp.broadcast_to(row[:, at * r : (at + 1) * r], (r, r))
        pieces.append(jnp.sum(jnp.where(rows == cols, piece, 0.0), axis=1, keepdims=True))
    return jnp.concatenate(pieces, axis=0)


def row_times(row, matrix, r):
    return jnp.sum(column(row, r) * matrix, axis=0, keepdims=True)


def place_of():
    q = lax.axis_index("col")
    return q, q >> 1, q & 1


def has(distance):
    return (lax.axis_index("tm") >= distance).astype(jnp.int32)


def lanes(index, r):
    return pl.ds(pl.multiple_of(index * r, r), r)


def copy_all(pairs, sems):
    copies = [
        pltpu.make_async_copy(source, target, sems.at[i]) for i, (source, target) in enumerate(pairs)
    ]
    for copy in copies:
        copy.start()
    for copy in copies:
        copy.wait()


def send_kernel(
    cov, cost, drift, eta, to_core, to_chip, to_far, panel, vecs, b_in, e_in, sems
):
    q, y, c = place_of()
    r = to_far.shape[1]

    def load(mine, theirs):
        pairs = []
        for j in range(2, 4):
            source = mine.at[1 - y, :, lanes((q ^ 2) ^ j, r)]
            pairs.append((source, to_chip.at[pl.ds(0, r), pl.ds((j - 2) * r, r)]))
        pairs.append((theirs.at[1 - y, :, lanes(q, r)], to_far.at[pl.ds(0, r), :]))
        for j in range(1, 4):
            source = theirs.at[y, :, lanes((q ^ 1) ^ j, r)]
            pairs.append((source, to_core.at[pl.ds(0, r), pl.ds((j - 1) * r, r)]))
        for j in range(4):
            pairs.append((mine.at[y, :, lanes(q ^ j, r)], panel.at[:, pl.ds(j * r, r)]))
        pairs.append((drift, b_in))
        pairs.append((eta, e_in))
        copy_all(pairs, sems)

    @pl.when(c == 0)
    def _():
        load(cov, cost)

    @pl.when(c == 1)
    def _():
        load(cost, cov)

    b, e = b_in[pl.ds(y, 1), :], e_in[pl.ds(y, 1), :]
    vecs[...] = jnp.zeros(vecs.shape, F32)
    vecs[0:1, :] = b
    vecs[1:2, :] = e
    to_core[r : r + 8, :] = jnp.zeros((8, 3 * r), F32)
    to_core[r : r + 1, 0:r] = b
    to_core[r : r + 1, r : 2 * r] = e
    b, e = b_in[pl.ds(1 - y, 1), :], e_in[pl.ds(1 - y, 1), :]
    to_chip[r : r + 8, :] = jnp.zeros((8, 2 * r), F32)
    to_chip[r : r + 1, 0:r] = b
    to_chip[r : r + 1, r : 2 * r] = e
    to_far[r : r + 8, :] = jnp.zeros((8, r), F32)
    to_far[r : r + 1, :] = b
    to_far[r + 1 : r + 2, :] = e


def pack_near_kernel(panel, from_core, packed):
    r = panel.shape[0]
    packed[:, 0:r] = fold(panel[:, 0:r], from_core[0:r, 0:r], r)
    packed[:, r : 4 * r] = panel[:, r:]
    packed[:, 4 * r :] = from_core[0:r, r : 3 * r]


def pack_far_kernel(vecs, from_core, from_chip, from_far, packed):
    r = vecs.shape[1]
    k33 = from_far[0:r, :]
    packed[0:r, 0:r] = fold(from_chip[0:r, 0:r], k33, r)
    packed[0:r, r:] = from_chip[0:r, r : 2 * r]
    packed[r : r + 1, 0:r] = diagonal(from_core[0:r, 0:r], r)
    packed[r : r + 1, r:] = diagonal(k33, r)
    b = (
        vecs[0:1, :],
        from_core[r : r + 1, 0:r],
        from_chip[r : r + 1, 0:r],
        from_far[r : r + 1, :],
    )
    e = (
        vecs[1:2, :],
        from_core[r : r + 1, r : 2 * r],
        from_chip[r : r + 1, r : 2 * r],
        from_far[r + 1 : r + 2, :],
    )
    for j in range(4):
        at = slice(j % 2 * r, (j % 2 + 1) * r)
        packed[r + 1 + j // 2 : r + 2 + j // 2, at] = b[j]
        packed[r + 3 + j // 2 : r + 4 + j // 2, at] = e[j]
    packed[r + 5 : r + 8, :] = jnp.zeros((3, 2 * r), F32)


def far_row(packed, r, at):
    return jnp.concatenate(
        [packed[r + at : r + at + 1, :], packed[r + at + 1 : r + at + 2, :]], axis=1
    )


def pick_kernel(turned, before, out):
    y = place_of()[1]
    height = turned.shape[1]
    out[0:height, :] = turned[1 - y]
    out[height:, :] = before[1 - y]


def halves_kernel(turned, before, other, own, earlier):
    y = place_of()[1]
    height = turned.shape[1]
    own[0:height, :] = turned[y]
    own[height:, :] = other[0:height, :]
    earlier[0:height, :] = before[y]
    earlier[height:, :] = other[height:, :]


def dense_turned(put, pattern, own_half, core_half, flag, n, r, bs):
    q = place_of()[0]
    sub = 8
    lane = lax.broadcasted_iota(jnp.int32, (sub, r), 1) // bs
    rows = lax.broadcasted_iota(jnp.int32, (bs, r), 0)
    cols = lax.broadcasted_iota(jnp.int32, (bs, r), 1)
    per = r // bs
    height = 3 * bs
    for j in range(4):
        half = own_half if j % 2 == 0 else core_half
        pieces, wanted = [], []
        for k in range(3):
            at = (j // 2) * height + k * bs
            pieces.append(half[at : at + bs, :].reshape(bs // sub, sub, r))
            want = jnp.zeros((sub, r), jnp.int32)
            for h in range(per):
                block = pattern[pl.ds((q ^ j) * per + h, 1), :][:, k : k + 1] ^ (q * per)
                want = jnp.where(lane == h, jnp.broadcast_to(block, (sub, r)), want)
            wanted.append(jnp.where(flag == 1, want, -1))
        for block in range(n // bs):
            if j * r <= block * bs < (j + 1) * r:
                value = jnp.where(
                    jnp.logical_and(rows + block * bs == cols + j * r, flag == 0), 1.0, 0.0
                ).reshape(bs // sub, sub, r)
            else:
                value = jnp.zeros((bs // sub, sub, r), F32)
            for k in range(3):
                value = jnp.where((wanted[k] == block)[None], pieces[k], value)
            put(
                slice(block * bs, (block + 1) * bs),
                slice(j * r, (j + 1) * r),
                value.reshape(bs, r),
            )


def put_split(hi_ref, lo_ref, rows, cols, value):
    hi, lo = split(value)
    hi_ref[rows, cols] = hi
    lo_ref[rows, cols] = lo


def transpose_split(hi_ref, lo_ref, source, r):
    n = source.shape[0]
    for i in range(n // r):
        for j in range(n // r):
            put_split(
                hi_ref,
                lo_ref,
                slice(j * r, (j + 1) * r),
                slice(i * r, (i + 1) * r),
                source[i * r : (i + 1) * r, j * r : (j + 1) * r].T,
            )


def straight_split(hi_ref, lo_ref, source, r):
    n = source.shape[0]
    for i in range(n // r):
        put_split(
            hi_ref, lo_ref, slice(i * r, (i + 1) * r), slice(None), source[i * r : (i + 1) * r, :]
        )


def prepare_kernel(bs, pattern, own, own_core, before, before_core, mh, ml, th, tl, dense):
    c, has1 = place_of()[2], has(1)
    n = dense.shape[0]
    r = own.shape[1]
    first = c == 0
    own_half = jnp.where(first, own[...], before[...])
    core_half = jnp.where(first, own_core[...], before_core[...])
    flag = jnp.where(first, 1, has1)

    def put(row, col, value):
        dense[row, col] = value

    dense_turned(put, pattern, own_half, core_half, flag, n, r, bs)

    @pl.when(first)
    def _():
        straight_split(mh, ml, dense, r)
        transpose_split(th, tl, dense, r)

    @pl.when(jnp.logical_not(first))
    def _():
        straight_split(th, tl, dense, r)
        transpose_split(mh, ml, dense, r)


def level1_kernel(own_near, own_far, near, far, mh, ml, th, tl, out, xh, xl, sh, sl):
    c = place_of()[2]
    r = own_near.shape[0]
    n = 4 * r
    extra = slice(n, n + 16)
    first = c == 0
    came = jnp.where(has(1) == 1, near[...], 0.0)
    xn = jnp.where(first, came, own_near[...])
    xf = jnp.where(first, far[...], own_far[...])
    x = jnp.concatenate(
        [
            xn[:, 0 : 4 * r],
            jnp.concatenate([xf[0:r, 0:r], xn[:, 4 * r :], xf[0:r, r:]], axis=1),
            jnp.concatenate([xf[r : r + 1, :], xf[r : r + 1, :]], axis=1),
        ],
        axis=0,
    )

    def put(i, j, block):
        put_split(xh, xl, slice(i * r, (i + 1) * r), slice(j * r, (j + 1) * r), block)

    spread(x, r, put)
    b_before, b_own = far_row(far, r, 1), far_row(own_far, r, 1)
    e_before, e_own = far_row(far, r, 3), far_row(own_far, r, 3)
    row = jnp.broadcast_to(jnp.where(first, b_before, e_own), (16, n))
    put_split(xh, xl, extra, slice(None), row)
    u = dot3(xh[...], xl[...], mh[...], ml[...])
    uh, ul = split(u[0:n, :])
    sh[0 : 2 * r, :] = th[0 : 2 * r, :]
    sl[0 : 2 * r, :] = tl[0 : 2 * r, :]
    row = jnp.broadcast_to(jnp.where(first, 0.0, b_before), (16, n))
    put_split(sh, sl, slice(2 * r, 2 * r + 16), slice(None), row)
    top = dot3(sh[...], sl[...], uh, ul)
    low = dot3(th[2 * r :, :], tl[2 * r :, :], uh[:, 2 * r :], ul[:, 2 * r :])
    vec = jnp.where(first, b_own, e_before) + u[n : n + 1, :] + top[2 * r : 2 * r + 1, :]
    dn = jnp.where(first, own_near[...], came)
    df = jnp.where(first, own_far[...], far[...])
    z11 = top[r : 2 * r, r : 2 * r]
    z33 = low[r : 2 * r, r : 2 * r]
    out[0:r, 0:r] = fold(top[0:r, 0:r], z11, r) + dn[:, 0:r]
    out[0:r, r:] = top[0:r, r:] + dn[:, r : 4 * r]
    out[r : 2 * r, 0:r] = fold(low[0:r, 0:r], z33, r) + df[0:r, 0:r]
    out[r : 2 * r, r : 3 * r] = top[r : 2 * r, 2 * r :] + dn[:, 4 * r :]
    out[r : 2 * r, 3 * r :] = low[0:r, r : 2 * r] + df[0:r, r:]
    base = 2 * r
    out[base : base + 1, 0:r] = diagonal(z11, r) + df[r : r + 1, 0:r]
    out[base : base + 1, r : 2 * r] = diagonal(z33, r) + df[r : r + 1, r:]
    out[base : base + 1, 2 * r :] = jnp.zeros((1, 2 * r), F32)
    out[base + 1 : base + 2, :] = b_own
    out[base + 2 : base + 3, :] = vec
    out[base + 3 : base + 4, :] = b_before
    out[base + 4 : base + 8, :] = jnp.zeros((4, 4 * r), F32)


def early_kernel(bs, pattern, own, own_core, before, before_core, a0h, a0l, a1h, a1l, t):
    n = a0h.shape[0]
    r = own.shape[1]
    for flag, mine, theirs, hi, lo in (
        (1, own, own_core, a0h, a0l),
        (has(1), before, before_core, a1h, a1l),
    ):
        put = functools.partial(put_split, hi, lo)
        dense_turned(put, pattern, mine[...], theirs[...], flag, n, r, bs)

    def wanted(ref):
        return jnp.concatenate([ref[:, 0:r], ref[:, 2 * r : 3 * r]], axis=1)

    t[...] = dot3(a1h[...], a1l[...], wanted(a0h), wanted(a0l))


def third_kernel(bs, pattern, mine, theirs, t, out, a2, a2h, a2l):
    n = a2.shape[0]
    r = mine.shape[1]

    def put(row, col, value):
        put_split(a2h, a2l, row, col, value)
        a2[row, col] = value

    dense_turned(put, pattern, mine[...], theirs[...], has(2), n, r, bs)
    out[...] = dot3(a2h[...], a2l[...], *split(t[...]))


def rows_kernel(bs, pattern, mine, theirs, t, dyn_own, dyn_send, a3h, a3l):
    q, _, _ = place_of()
    n = a3h.shape[0]
    r = mine.shape[1]
    put = functools.partial(put_split, a3h, a3l)
    dense_turned(put, pattern, mine[...], theirs[...], has(3), n, r, bs)
    rows = dot3(a3h[...], a3l[...], *split(t[...]))
    for j in range(4):
        at = lanes(q ^ j, r)
        dyn_own[:, at] = rows[j * r : (j + 1) * r, 0:r].T
        dyn_send[:, at] = rows[j * r : (j + 1) * r, r : 2 * r].T


def product_kernel(
    a0h, a0l, a1h, a1l, a2h, a2l, a3h, a3l, mh, ml, th, tl, product_ref
):
    first = place_of()[2] == 0
    r = a0h.shape[0] // 4

    @pl.when(first)
    def _():
        product_ref[...] = dot3(a1h[...], a1l[...], a0h[...], a0l[...])
        straight_split(mh, ml, product_ref, r)
        transpose_split(th, tl, product_ref, r)

    @pl.when(jnp.logical_not(first))
    def _():
        product_ref[...] = dot3(a3h[...], a3l[...], a2h[...], a2l[...])
        straight_split(th, tl, product_ref, r)
        transpose_split(mh, ml, product_ref, r)


def ahead_kernel(own, mh, ml, th, tl, full, z, xh, xl):
    r = own.shape[1] // 4

    def put(i, j, block):
        full[i * r : (i + 1) * r, j * r : (j + 1) * r] = block

    spread(own, r, put)

    @pl.when(place_of()[2] == 1)
    def _():
        straight_split(xh, xl, full, r)
        u = dot3(xh[...], xl[...], mh[...], ml[...])
        z[...] = dot3(th[...], tl[...], *split(u))


def put_rows(ref, value, q, r):
    for j in range(4):
        ref[lanes(q ^ j, r), :] = value[:, j * r : (j + 1) * r]


CROSSING = ((2, 0), (2, 1), (2, 3))


def level2_kernel(own, earlier, mh, ml, th, tl, full, z, to_chip, uh, ul, xh, xl, rest):
    c = place_of()[2]
    r = own.shape[1] // 4
    two, three = slice(2 * r, 3 * r), slice(3 * r, 4 * r)

    @pl.when(c == 0)
    def _():
        def put(i, j, block):
            put_split(xh, xl, slice(i * r, (i + 1) * r), slice(j * r, (j + 1) * r), block)

        spread(earlier, r, put)
        hi, lo = split(dot3(xh[...], xl[...], mh[...], ml[...]))
        uh[...] = hi
        ul[...] = lo
        rest[:, 2 * r :] = dot3(th[2 * r :, :], tl[2 * r :, :], hi[:, 2 * r :], lo[:, 2 * r :])
        rest[0:r, 0 : 2 * r] = dot3(th[two, :], tl[two, :], hi[:, 0 : 2 * r], lo[:, 0 : 2 * r])
        rest[:, 2 * r :] = rest[:, 2 * r :] + full[2 * r :, 2 * r :]
        rest[0:r, 0 : 2 * r] = rest[0:r, 0 : 2 * r] + full[two, 0 : 2 * r]

    @pl.when(c == 1)
    def _():
        def put(i, j, block):
            if (i, j) in CROSSING or i == j:
                rows = slice((i - 2) * r, (i - 1) * r)
                cols = slice(j * r, (j + 1) * r)
                rest[rows, cols] = z[i * r : (i + 1) * r, cols] + block

        spread(earlier, r, put, rows=(2, 3))

    z33 = rest[r : 2 * r, three]
    to_chip[0:r, :] = fold(rest[0:r, two], z33, r)
    for at, (_, j) in enumerate(CROSSING):
        to_chip[(at + 1) * r : (at + 2) * r, :] = rest[0:r, j * r : (j + 1) * r]
    to_chip[4 * r :, :] = jnp.broadcast_to(diagonal(z33, r), (8, r))


def far_rows_kernel(
    own, earlier, mh, ml, th, tl, a2, full, z, uh, ul, to_far, short, vec, rest
):
    c = place_of()[2]
    r = own.shape[1] // 4
    base = 2 * r
    three = slice(3 * r, 4 * r)
    b1 = earlier[base + 1 : base + 2, :] + row_times(earlier[base + 3 : base + 4, :], a2[...], r)

    @pl.when(c == 0)
    def _():
        value = dot3(th[three, :], tl[three, :], uh[:, 0 : 2 * r], ul[:, 0 : 2 * r])
        rest[...] = value + full[three, 0 : 2 * r]
        vec[0:1, :] = b1
        vec[1:2, :] = own[base + 2 : base + 3, :]

    @pl.when(c == 1)
    def _():
        def put(i, j, block):
            if j < 2:
                cols = slice(j * r, (j + 1) * r)
                rest[:, cols] = z[three, cols] + block

        spread(earlier, r, put, rows=(3,))
        vec[0:1, :] = own[base + 2 : base + 3, :] + row_times(b1, full[...], r)
        vec[1:2, :] = earlier[base + 2 : base + 3, :]

    to_far[0:r, :] = rest[:, 0:r]
    to_far[r : 2 * r, :] = rest[:, r : 2 * r]
    out = vec[1:2, :] + row_times(vec[0:1, :], mh[...].astype(F32) + ml[...].astype(F32), r)
    to_far[2 * r :, :] = jnp.broadcast_to(out[:, 3 * r :], (8, r))
    for i in range(4):
        short[i : i + 1, :] = out[:, i * r : (i + 1) * r]
    short[4:8, :] = jnp.zeros((4, r), F32)


def rest_kernel(earlier, th, tl, full, z, uh, ul, short, keep, to_core, rest):
    q, _, c = place_of()
    r = earlier.shape[1] // 4

    @pl.when(c == 0)
    def _():
        rest[...] = dot3(th[0 : 2 * r, :], tl[0 : 2 * r, :], uh[...], ul[...]) + full[0 : 2 * r, :]

    @pl.when(c == 1)
    def _():
        def put(i, j, block):
            rows = slice(i * r, (i + 1) * r)
            cols = slice(j * r, (j + 1) * r)
            rest[rows, cols] = z[rows, cols] + block

        spread(earlier, r, put, rows=(0, 1))

    put_rows(keep, rest[0:r, :], q, r)
    put_rows(to_core, rest[r : 2 * r, :], q, r)
    to_core[4 * r :, :] = jnp.broadcast_to(short[1:2, :], (8, r))


def turn_kernel(from_chip, diagonal_block, mirrored):
    r = diagonal_block.shape[0]
    first, second = unfold(from_chip[0:r, :], from_chip[4 * r : 4 * r + 1, :], r)
    diagonal_block[...] = first
    mirrored[0:r, :] = from_chip[3 * r : 4 * r, :].T
    mirrored[r : 2 * r, :] = second


def panel_copies(panel, target, element, r):
    return [
        (panel.at[pl.ds(g * r, r), :], target.at[element, :, pl.ds(g * r, r)]) for g in range(4)
    ]


def block_copies(blocks, target, element, r):
    return [(source, target.at[element, :, lanes(at, r)]) for source, at in blocks]


def fill_kernel(
    keep,
    from_core,
    dyn_own,
    dyn_recv,
    diagonal_block,
    from_chip,
    dyn_out,
    cov_out,
    cost_out,
    sems,
):
    q, y, c = place_of()
    r = dyn_own.shape[0]
    dyn = [(dyn_own, dyn_out.at[y]), (dyn_recv, dyn_out.at[1 - y])]
    blocks = [(diagonal_block, q)] + [
        (from_chip.at[pl.ds(at * r, r), :], q ^ bit) for at, bit in ((1, 2), (2, 3), (3, 1))
    ]

    def write(mine, other):
        copy_all(
            dyn
            + panel_copies(keep, mine, y, r)
            + panel_copies(from_core, other, y, r)
            + block_copies(blocks, mine, 1 - y, r),
            sems,
        )

    @pl.when(c == 0)
    def _():
        write(cov_out, cost_out)

    @pl.when(c == 1)
    def _():
        write(cost_out, cov_out)


def place_kernel(
    cov_in,
    cost_in,
    short,
    chip_short,
    from_core,
    mirrored,
    panel,
    cov_out,
    cost_out,
    drift_out,
    eta_out,
    lines,
    sems,
):
    del cov_in, cost_in
    q, y, c = place_of()
    first = c == 0
    r = short.shape[1]
    mine, other = short[0:1, :], from_core[4 * r : 4 * r + 1, :]
    chip, far = chip_short[2:3, :], panel[2 * r : 2 * r + 1, :]
    for at, (one, two, three, four) in enumerate(
        ((mine, other, chip, far), (other, mine, far, chip))
    ):
        lines[at, pl.ds(y, 1), :] = jnp.where(first, one, two)
        lines[at, pl.ds(1 - y, 1), :] = jnp.where(first, three, four)
    vectors = [(lines.at[0], drift_out), (lines.at[1], eta_out)]
    near, far = pl.ds(0, r), pl.ds(r, r)
    blocks = [
        (panel.at[near, :], q ^ 3),
        (panel.at[far, :], q ^ 2),
        (mirrored.at[near, :], q ^ 1),
        (mirrored.at[far, :], q),
    ]

    @pl.when(first)
    def _():
        copy_all(vectors + block_copies(blocks, cost_out, 1 - y, r), sems)

    @pl.when(c == 1)
    def _():
        copy_all(vectors + block_copies(blocks, cov_out, 1 - y, r), sems)


IN_HBM, IN_VMEM = 0, 1


def kernel(body, operands, shapes, scratch=(), aliases=None):
    specs = {
        IN_HBM: pl.BlockSpec(memory_space=pltpu.HBM),
        IN_VMEM: pl.BlockSpec(memory_space=pltpu.VMEM),
    }
    call = pl.pallas_call(
        body,
        in_specs=[specs[where] for where, _ in operands],
        out_specs=[specs[where] for where, _ in shapes],
        out_shape=[
            pltpu.VMEM(s.shape, s.dtype) if where == IN_VMEM else s for where, s in shapes
        ],
        scratch_shapes=list(scratch),
        input_output_aliases=aliases or {},
        compiler_params=pltpu.CompilerParams(vmem_limit_bytes=20 * 2**20),
    )
    kept = {IN_HBM: pltpu.HBM, IN_VMEM: pltpu.VMEM}
    return call(
        *(
            pltpu.with_memory_space_constraint(x, kept[where]) if where in kept else x
            for where, x in operands
        )
    )


def per_device_split(blocks, pattern, drift, cov, cost, eta):
    elements, r, n = cov.shape
    bs = blocks.shape[2] // 3
    tms, cols = lax.axis_size("tm"), lax.axis_size("col")

    def swap(value, bit):
        return lax.ppermute(value, "col", [(i, i ^ bit) for i in range(cols)])

    def later(value, distance, cyclic=False):
        count = tms if cyclic else tms - distance
        return lax.ppermute(value, "tm", [(i, (i + distance) % tms) for i in range(count)])

    def hbm(*arrays):
        return [(IN_HBM, x) for x in arrays]

    def vmem(*arrays):
        return [(IN_VMEM, x) for x in arrays]

    def shape(*dims):
        return jax.ShapeDtypeStruct(dims, F32)

    def half(*dims):
        return jax.ShapeDtypeStruct(dims, BF16)

    def square(dtype):
        return pltpu.VMEM((n, n), dtype)

    def sems(count):
        return pltpu.SemaphoreType.DMA((count,))

    turned = jnp.swapaxes(blocks, 1, 2)
    before = later(turned, 1, cyclic=True)
    to_core, to_chip, to_far, panel, vecs = kernel(
        send_kernel,
        hbm(cov, cost, drift, eta),
        vmem(shape(r + 8, 3 * r), shape(r + 8, 2 * r), shape(r + 8, r), shape(r, n), shape(8, r)),
        [pltpu.VMEM(drift.shape, F32), pltpu.VMEM(eta.shape, F32), sems(12)],
    )
    from_core = swap(to_core, 1)
    from_chip = swap(to_chip, 2)
    from_far = swap(to_far, 3)
    (own_near,) = kernel(pack_near_kernel, vmem(panel, from_core), vmem(shape(r, 6 * r)))
    near = later(own_near, 1, cyclic=True)
    (own_far,) = kernel(
        pack_far_kernel, vmem(vecs, from_core, from_chip, from_far), vmem(shape(r + 8, 2 * r))
    )
    far = later(own_far, 1)
    (picked,) = kernel(pick_kernel, vmem(turned, before), vmem(shape(6 * bs, r)))
    other = swap(picked, 2)
    own_half, before_half = kernel(
        halves_kernel, vmem(turned, before, other), vmem(shape(6 * bs, r), shape(6 * bs, r))
    )
    pairs = (own_half, swap(own_half, 1), before_half, swap(before_half, 1))
    third = later(own_half, 2, cyclic=True)
    fourth = later(before_half, 2, cyclic=True)
    m1 = kernel(
        functools.partial(prepare_kernel, bs),
        vmem(pattern, *pairs),
        vmem(*[half(n, n)] * 4),
        [square(F32)],
    )
    (level1,) = kernel(
        level1_kernel,
        vmem(own_near, own_far, near, far, *m1),
        vmem(shape(2 * r + 8, n)),
        [pltpu.VMEM((n + 16, n), BF16)] * 2 + [pltpu.VMEM((2 * r + 16, n), BF16)] * 2,
    )
    earlier = later(level1, 2)
    *a01, t = kernel(
        functools.partial(early_kernel, bs),
        vmem(pattern, *pairs),
        vmem(*[half(n, n)] * 4, shape(n, 2 * r)),
    )
    t, a2, *a2_split = kernel(
        functools.partial(third_kernel, bs),
        vmem(pattern, third, swap(third, 1), t),
        vmem(shape(n, 2 * r), shape(n, n), half(n, n), half(n, n)),
    )
    dyn_own, dyn_send, *a3_split = kernel(
        functools.partial(rows_kernel, bs),
        vmem(pattern, fourth, swap(fourth, 1), t),
        vmem(shape(r, n), shape(r, n), half(n, n), half(n, n)),
    )
    a23 = (*a2_split, *a3_split)
    dyn_recv = swap(dyn_send, 2)
    m2 = kernel(product_kernel, vmem(*a01, *a23), vmem(*[half(n, n)] * 4), [square(F32)])
    full, z = kernel(
        ahead_kernel, vmem(level1, *m2), vmem(shape(n, n), shape(n, n)), [square(BF16)] * 2
    )
    to_chip, *u = kernel(
        level2_kernel,
        vmem(level1, earlier, *m2, full, z),
        vmem(shape(n + 8, r), half(n, n), half(n, n)),
        [square(BF16)] * 2 + [pltpu.VMEM((2 * r, n), F32)],
    )
    from_chip = swap(to_chip, 2)
    to_far, short = kernel(
        far_rows_kernel,
        vmem(level1, earlier, *m2, a2, full, z, *u),
        vmem(shape(2 * r + 8, r), shape(8, r)),
        [pltpu.VMEM((8, n), F32), pltpu.VMEM((r, 2 * r), F32)],
    )
    chip_short = swap(short, 2)
    from_far = swap(to_far, 3)
    keep, to_core = kernel(
        rest_kernel,
        vmem(earlier, *m2[2:], full, z, *u, short),
        vmem(shape(n, r), shape(n + 8, r)),
        [pltpu.VMEM((2 * r, n), F32)],
    )
    from_core = swap(to_core, 1)
    diagonal_block, mirrored = kernel(
        turn_kernel, vmem(from_chip), vmem(shape(r, r), shape(2 * r, r))
    )
    mirrored = swap(mirrored, 1)
    whole, line = shape(elements, r, n), shape(elements, r)
    dyn_out, cov_out, cost_out = kernel(
        fill_kernel,
        vmem(keep, from_core, dyn_own, dyn_recv, diagonal_block, from_chip),
        hbm(whole, whole, whole),
        [sems(14)],
    )
    cov_out, cost_out, drift_out, eta_out = kernel(
        place_kernel,
        hbm(cov_out, cost_out) + vmem(short, chip_short, from_core, mirrored, from_far),
        hbm(whole, whole, line, line),
        [pltpu.VMEM((2, elements, r), F32), sems(6)],
        {0: 0, 1: 1},
    )
    return dyn_out, drift_out, cov_out, cost_out, eta_out


def takes_split(elements, r, bs, cols):
    return elements == 2 and cols == 4 and r % 128 == 0 and r % bs == 0 and bs % 8 == 0


def per_device(blocks, pattern, drift, cov, cost, eta):
    elements, r, _ = cov.shape
    bs = blocks.shape[2] // 3
    if takes_split(elements, r, bs, lax.axis_size("col")):
        return per_device_split(blocks, pattern, drift, cov, cost, eta)
    return per_device_general(blocks, pattern, drift, cov, cost, eta)


def solution(mesh):
    return jax.shard_map(
        per_device,
        mesh=mesh,
        in_specs=(
            P("tm", "col", None),
            P(),
            P("tm", "col"),
            P("tm", "col", None),
            P("tm", "col", None),
            P("tm", "col"),
        ),
        out_specs=(
            P("tm", "col", None),
            P("tm", "col"),
            P("tm", "col", None),
            P("tm", "col", None),
            P("tm", "col"),
        ),
        check_vma=False,
    )
```

```python
import functools

import jax
import jax.numpy as jnp
from jax import lax
from jax.experimental import pallas as pl
from jax.experimental.pallas import tpu as pltpu
from jax.sharding import PartitionSpec as P


HIGH = lax.Precision.HIGHEST
F32 = jnp.float32
BF16 = jnp.bfloat16


def shifted(block, axis, distance):
    devices = range(lax.axis_size(axis))
    route = [(i - distance, i) for i in devices if i - distance in devices]
    return lax.ppermute(block, axis, route)


def product(form, left, right):
    return jnp.einsum(form, left, right, precision=HIGH)


def densify(row_blocks, row_ids, pattern, block_size):
    block_count = pattern.shape[0]
    row_block = row_ids // block_size
    chooser = (row_block[:, None] == jnp.arange(block_count, dtype=jnp.int32)[None, :]).astype(
        jnp.int32
    )
    columns = jnp.sum(chooser[:, :, None] * pattern[None, :, :], axis=1)
    matches = (
        columns[:, :, None] == jnp.arange(block_count, dtype=jnp.int32)[None, None, :]
    ).astype(jnp.float32)
    pieces = row_blocks.reshape(row_blocks.shape[:-1] + (3, 1, block_size))
    filled = jnp.sum(matches[:, :, :, None] * pieces, axis=-3)
    return filled.reshape(row_blocks.shape[:-1] + (block_count * block_size,))


def combine_rows(
    dyn_prev_full,
    dyn_own_full,
    dyn_own,
    drift_prev_full,
    drift_own,
    cov_prev,
    cov_own,
    cost_prev,
    cost_own,
    eta_prev,
    eta_own,
    first_row,
):
    height = dyn_own.shape[1]
    dyn_res = product("tij,tjk->tik", dyn_own, dyn_prev_full)
    drift_res = product("tij,tj->ti", dyn_own, drift_prev_full) + drift_own
    carried = eta_own + product("tij,tj->ti", cost_own, drift_prev_full)
    value_rows = product("tij,tjk->tik", cost_own, dyn_prev_full)
    prev_columns = lax.dynamic_slice_in_dim(dyn_prev_full, first_row, height, 2)
    cov_full, carried_full, value_full = (
        lax.all_gather(cov_prev, "col", axis=1, tiled=True),
        lax.all_gather(carried, "col", axis=1, tiled=True),
        lax.all_gather(value_rows, "col", axis=1, tiled=True),
    )
    cost_res = cost_prev + product("tki,tkj->tij", prev_columns, value_full)
    cov_res = (
        product("tik,tjk->tij", product("tij,tjk->tik", dyn_own, cov_full), dyn_own_full) + cov_own
    )
    eta_res = eta_prev + product("tki,tk->ti", prev_columns, carried_full)
    return (dyn_res, drift_res, cov_res, cost_res, eta_res)


def choose(flag, combined, kept):
    return tuple(jnp.where(flag, new, old) for new, old in zip(combined, kept))


def per_device_general(blocks, pattern, drift, cov, cost, eta):
    height = cov.shape[1]
    modes = cov.shape[2]
    block_size = blocks.shape[2] // 3
    first_row = lax.axis_index("col") * height
    own_ids = first_row + jnp.arange(height, dtype=jnp.int32)
    all_ids = jnp.arange(modes, dtype=jnp.int32)
    position = lax.axis_index("tm")
    dyn_own = densify(blocks, own_ids, pattern, block_size)
    received = shifted((blocks, drift, cov, cost, eta), "tm", 1)
    blocks_prev, blocks_own, drift_prev_full = (
        lax.all_gather(received[0], "col", axis=1, tiled=True),
        lax.all_gather(blocks, "col", axis=1, tiled=True),
        lax.all_gather(received[1], "col", axis=1, tiled=True),
    )
    merged = combine_rows(
        densify(blocks_prev, all_ids, pattern, block_size),
        densify(blocks_own, all_ids, pattern, block_size),
        dyn_own,
        drift_prev_full,
        drift,
        received[2],
        cov,
        received[3],
        cost,
        received[4],
        eta,
        first_row,
    )
    current = choose(position >= 1, merged, (dyn_own, drift, cov, cost, eta))
    received = shifted(current, "tm", 2)
    dyn_prev_full = lax.all_gather(received[0], "col", axis=1, tiled=True)
    dyn_own_full = lax.all_gather(current[0], "col", axis=1, tiled=True)
    drift_prev_full = lax.all_gather(received[1], "col", axis=1, tiled=True)
    merged = combine_rows(
        dyn_prev_full,
        dyn_own_full,
        current[0],
        drift_prev_full,
        current[1],
        received[2],
        current[2],
        received[3],
        current[3],
        received[4],
        current[4],
        first_row,
    )
    return choose(position >= 2, merged, current)


def split(x):
    hi = x.astype(BF16)
    lo = (x - hi.astype(F32)).astype(BF16)
    return hi, lo


def dot(a, b):
    return jnp.dot(a, b, preferred_element_type=F32)


def dot3(ah, al, bh, bl):
    return dot(ah, bh) + (dot(ah, bl) + dot(al, bh))


def triangle(r):
    rows = lax.broadcasted_iota(jnp.int32, (r, r), 0)
    cols = lax.broadcasted_iota(jnp.int32, (r, r), 1)
    return rows, cols


def fold(first, second, r):
    rows, cols = triangle(r)
    return jnp.where(rows >= cols, first, second)


def diagonal(block, r):
    rows, cols = triangle(r)
    return jnp.sum(jnp.where(rows == cols, block, 0.0), axis=0, keepdims=True)


def unfold(folded, second_diag, r):
    rows, cols = triangle(r)
    turned = folded.T
    first = jnp.where(rows >= cols, folded, turned)
    second = jnp.where(rows < cols, folded, turned)
    second = jnp.where(rows == cols, jnp.broadcast_to(second_diag, (r, r)), second)
    return first, second


UPPER = ((0, 1), (0, 2), (0, 3), (1, 2), (1, 3), (2, 3))


def spread(packed, r, put, rows=(0, 1, 2, 3)):
    panel0, panel1, diags = packed[0:r], packed[r : 2 * r], packed[2 * r : 2 * r + 1]
    for at, (panel, pair) in enumerate(((panel0, (0, 1)), (panel1, (2, 3)))):
        if pair[0] in rows or pair[1] in rows:
            blocks = unfold(panel[:, 0:r], diags[:, at * r : (at + 1) * r], r)
            for i, block in zip(pair, blocks):
                if i in rows:
                    put(i, i, block)
    for at, (i, j) in enumerate(UPPER):
        panel = panel0 if at < 3 else panel1
        block = panel[:, (at % 3 + 1) * r : (at % 3 + 2) * r]
        if i in rows:
            put(i, j, block)
        if j in rows:
            put(j, i, block.T)


def column(row, r):
    rows, cols = triangle(r)
    pieces = []
    for at in range(row.shape[1] // r):
        piece = jnp.broadcast_to(row[:, at * r : (at + 1) * r], (r, r))
        pieces.append(jnp.sum(jnp.where(rows == cols, piece, 0.0), axis=1, keepdims=True))
    return jnp.concatenate(pieces, axis=0)


def row_times(row, matrix, r):
    return jnp.sum(column(row, r) * matrix, axis=0, keepdims=True)


def place_of():
    q = lax.axis_index("col")
    return q, q >> 1, q & 1


def has(distance):
    return (lax.axis_index("tm") >= distance).astype(jnp.int32)


def lanes(index, r):
    return pl.ds(pl.multiple_of(index * r, r), r)


def copy_all(pairs, sems):
    copies = [
        pltpu.make_async_copy(source, target, sems.at[i]) for i, (source, target) in enumerate(pairs)
    ]
    for copy in copies:
        copy.start()
    for copy in copies:
        copy.wait()


def send_kernel(
    cov, cost, drift, eta, to_core, to_chip, to_far, panel, vecs, b_in, e_in, sems
):
    q, y, c = place_of()
    r = to_far.shape[1]

    def load(mine, theirs):
        pairs = []
        for j in range(2, 4):
            source = mine.at[1 - y, :, lanes((q ^ 2) ^ j, r)]
            pairs.append((source, to_chip.at[pl.ds(0, r), pl.ds((j - 2) * r, r)]))
        pairs.append((theirs.at[1 - y, :, lanes(q, r)], to_far.at[pl.ds(0, r), :]))
        for j in range(1, 4):
            source = theirs.at[y, :, lanes((q ^ 1) ^ j, r)]
            pairs.append((source, to_core.at[pl.ds(0, r), pl.ds((j - 1) * r, r)]))
        for j in range(4):
            pairs.append((mine.at[y, :, lanes(q ^ j, r)], panel.at[:, pl.ds(j * r, r)]))
        pairs.append((drift, b_in))
        pairs.append((eta, e_in))
        copy_all(pairs, sems)

    @pl.when(c == 0)
    def _():
        load(cov, cost)

    @pl.when(c == 1)
    def _():
        load(cost, cov)

    b, e = b_in[pl.ds(y, 1), :], e_in[pl.ds(y, 1), :]
    vecs[...] = jnp.zeros(vecs.shape, F32)
    vecs[0:1, :] = b
    vecs[1:2, :] = e
    to_core[r : r + 8, :] = jnp.zeros((8, 3 * r), F32)
    to_core[r : r + 1, 0:r] = b
    to_core[r : r + 1, r : 2 * r] = e
    b, e = b_in[pl.ds(1 - y, 1), :], e_in[pl.ds(1 - y, 1), :]
    to_chip[r : r + 8, :] = jnp.zeros((8, 2 * r), F32)
    to_chip[r : r + 1, 0:r] = b
    to_chip[r : r + 1, r : 2 * r] = e
    to_far[r : r + 8, :] = jnp.zeros((8, r), F32)
    to_far[r : r + 1, :] = b
    to_far[r + 1 : r + 2, :] = e


def pack_near_kernel(panel, from_core, packed):
    r = panel.shape[0]
    packed[:, 0:r] = fold(panel[:, 0:r], from_core[0:r, 0:r], r)
    packed[:, r : 4 * r] = panel[:, r:]
    packed[:, 4 * r :] = from_core[0:r, r : 3 * r]


def pack_far_kernel(vecs, from_core, from_chip, from_far, packed):
    r = vecs.shape[1]
    k33 = from_far[0:r, :]
    packed[0:r, 0:r] = fold(from_chip[0:r, 0:r], k33, r)
    packed[0:r, r:] = from_chip[0:r, r : 2 * r]
    packed[r : r + 1, 0:r] = diagonal(from_core[0:r, 0:r], r)
    packed[r : r + 1, r:] = diagonal(k33, r)
    b = (
        vecs[0:1, :],
        from_core[r : r + 1, 0:r],
        from_chip[r : r + 1, 0:r],
        from_far[r : r + 1, :],
    )
    e = (
        vecs[1:2, :],
        from_core[r : r + 1, r : 2 * r],
        from_chip[r : r + 1, r : 2 * r],
        from_far[r + 1 : r + 2, :],
    )
    for j in range(4):
        at = slice(j % 2 * r, (j % 2 + 1) * r)
        packed[r + 1 + j // 2 : r + 2 + j // 2, at] = b[j]
        packed[r + 3 + j // 2 : r + 4 + j // 2, at] = e[j]
    packed[r + 5 : r + 8, :] = jnp.zeros((3, 2 * r), F32)


def far_row(packed, r, at):
    return jnp.concatenate(
        [packed[r + at : r + at + 1, :], packed[r + at + 1 : r + at + 2, :]], axis=1
    )


def pick_kernel(turned, before, out):
    y = place_of()[1]
    height = turned.shape[1]
    out[0:height, :] = turned[1 - y]
    out[height:, :] = before[1 - y]


def halves_kernel(turned, before, other, own, earlier):
    y = place_of()[1]
    height = turned.shape[1]
    own[0:height, :] = turned[y]
    own[height:, :] = other[0:height, :]
    earlier[0:height, :] = before[y]
    earlier[height:, :] = other[height:, :]


def dense_turned(put, pattern, own_half, core_half, flag, n, r, bs):
    q = place_of()[0]
    sub = 8
    lane = lax.broadcasted_iota(jnp.int32, (sub, r), 1) // bs
    rows = lax.broadcasted_iota(jnp.int32, (bs, r), 0)
    cols = lax.broadcasted_iota(jnp.int32, (bs, r), 1)
    per = r // bs
    height = 3 * bs
    for j in range(4):
        half = own_half if j % 2 == 0 else core_half
        pieces, wanted = [], []
        for k in range(3):
            at = (j // 2) * height + k * bs
            pieces.append(half[at : at + bs, :].reshape(bs // sub, sub, r))
            want = jnp.zeros((sub, r), jnp.int32)
            for h in range(per):
                block = pattern[pl.ds((q ^ j) * per + h, 1), :][:, k : k + 1] ^ (q * per)
                want = jnp.where(lane == h, jnp.broadcast_to(block, (sub, r)), want)
            wanted.append(jnp.where(flag == 1, want, -1))
        for block in range(n // bs):
            if j * r <= block * bs < (j + 1) * r:
                value = jnp.where(
                    jnp.logical_and(rows + block * bs == cols + j * r, flag == 0), 1.0, 0.0
                ).reshape(bs // sub, sub, r)
            else:
                value = jnp.zeros((bs // sub, sub, r), F32)
            for k in range(3):
                value = jnp.where((wanted[k] == block)[None], pieces[k], value)
            put(
                slice(block * bs, (block + 1) * bs),
                slice(j * r, (j + 1) * r),
                value.reshape(bs, r),
            )


def put_split(hi_ref, lo_ref, rows, cols, value):
    hi, lo = split(value)
    hi_ref[rows, cols] = hi
    lo_ref[rows, cols] = lo


def transpose_split(hi_ref, lo_ref, source, r):
    n = source.shape[0]
    for i in range(n // r):
        for j in range(n // r):
            put_split(
                hi_ref,
                lo_ref,
                slice(j * r, (j + 1) * r),
                slice(i * r, (i + 1) * r),
                source[i * r : (i + 1) * r, j * r : (j + 1) * r].T,
            )


def straight_split(hi_ref, lo_ref, source, r):
    n = source.shape[0]
    for i in range(n // r):
        put_split(
            hi_ref, lo_ref, slice(i * r, (i + 1) * r), slice(None), source[i * r : (i + 1) * r, :]
        )


def prepare_kernel(bs, pattern, own, own_core, before, before_core, mh, ml, th, tl, dense):
    c, has1 = place_of()[2], has(1)
    n = dense.shape[0]
    r = own.shape[1]
    first = c == 0
    own_half = jnp.where(first, own[...], before[...])
    core_half = jnp.where(first, own_core[...], before_core[...])
    flag = jnp.where(first, 1, has1)

    def put(row, col, value):
        dense[row, col] = value

    dense_turned(put, pattern, own_half, core_half, flag, n, r, bs)

    @pl.when(first)
    def _():
        straight_split(mh, ml, dense, r)
        transpose_split(th, tl, dense, r)

    @pl.when(jnp.logical_not(first))
    def _():
        straight_split(th, tl, dense, r)
        transpose_split(mh, ml, dense, r)


def level1_kernel(own_near, own_far, near, far, mh, ml, th, tl, out, xh, xl, sh, sl):
    c = place_of()[2]
    r = own_near.shape[0]
    n = 4 * r
    extra = slice(n, n + 16)
    first = c == 0
    came = jnp.where(has(1) == 1, near[...], 0.0)
    xn = jnp.where(first, came, own_near[...])
    xf = jnp.where(first, far[...], own_far[...])
    x = jnp.concatenate(
        [
            xn[:, 0 : 4 * r],
            jnp.concatenate([xf[0:r, 0:r], xn[:, 4 * r :], xf[0:r, r:]], axis=1),
            jnp.concatenate([xf[r : r + 1, :], xf[r : r + 1, :]], axis=1),
        ],
        axis=0,
    )

    def put(i, j, block):
        put_split(xh, xl, slice(i * r, (i + 1) * r), slice(j * r, (j + 1) * r), block)

    spread(x, r, put)
    b_before, b_own = far_row(far, r, 1), far_row(own_far, r, 1)
    e_before, e_own = far_row(far, r, 3), far_row(own_far, r, 3)
    row = jnp.broadcast_to(jnp.where(first, b_before, e_own), (16, n))
    put_split(xh, xl, extra, slice(None), row)
    u = dot3(xh[...], xl[...], mh[...], ml[...])
    uh, ul = split(u[0:n, :])
    sh[0 : 2 * r, :] = th[0 : 2 * r, :]
    sl[0 : 2 * r, :] = tl[0 : 2 * r, :]
    row = jnp.broadcast_to(jnp.where(first, 0.0, b_before), (16, n))
    put_split(sh, sl, slice(2 * r, 2 * r + 16), slice(None), row)
    top = dot3(sh[...], sl[...], uh, ul)
    low = dot3(th[2 * r :, :], tl[2 * r :, :], uh[:, 2 * r :], ul[:, 2 * r :])
    vec = jnp.where(first, b_own, e_before) + u[n : n + 1, :] + top[2 * r : 2 * r + 1, :]
    dn = jnp.where(first, own_near[...], came)
    df = jnp.where(first, own_far[...], far[...])
    z11 = top[r : 2 * r, r : 2 * r]
    z33 = low[r : 2 * r, r : 2 * r]
    out[0:r, 0:r] = fold(top[0:r, 0:r], z11, r) + dn[:, 0:r]
    out[0:r, r:] = top[0:r, r:] + dn[:, r : 4 * r]
    out[r : 2 * r, 0:r] = fold(low[0:r, 0:r], z33, r) + df[0:r, 0:r]
    out[r : 2 * r, r : 3 * r] = top[r : 2 * r, 2 * r :] + dn[:, 4 * r :]
    out[r : 2 * r, 3 * r :] = low[0:r, r : 2 * r] + df[0:r, r:]
    base = 2 * r
    out[base : base + 1, 0:r] = diagonal(z11, r) + df[r : r + 1, 0:r]
    out[base : base + 1, r : 2 * r] = diagonal(z33, r) + df[r : r + 1, r:]
    out[base : base + 1, 2 * r :] = jnp.zeros((1, 2 * r), F32)
    out[base + 1 : base + 2, :] = b_own
    out[base + 2 : base + 3, :] = vec
    out[base + 3 : base + 4, :] = b_before
    out[base + 4 : base + 8, :] = jnp.zeros((4, 4 * r), F32)


def early_kernel(bs, pattern, own, own_core, before, before_core, a0h, a0l, a1h, a1l, t):
    n = a0h.shape[0]
    r = own.shape[1]
    for flag, mine, theirs, hi, lo in (
        (1, own, own_core, a0h, a0l),
        (has(1), before, before_core, a1h, a1l),
    ):
        put = functools.partial(put_split, hi, lo)
        dense_turned(put, pattern, mine[...], theirs[...], flag, n, r, bs)

    def wanted(ref):
        return jnp.concatenate([ref[:, 0:r], ref[:, 2 * r : 3 * r]], axis=1)

    t[...] = dot3(a1h[...], a1l[...], wanted(a0h), wanted(a0l))


def third_kernel(bs, pattern, mine, theirs, t, out, a2, a2h, a2l):
    n = a2.shape[0]
    r = mine.shape[1]

    def put(row, col, value):
        put_split(a2h, a2l, row, col, value)
        a2[row, col] = value

    dense_turned(put, pattern, mine[...], theirs[...], has(2), n, r, bs)
    out[...] = dot3(a2h[...], a2l[...], *split(t[...]))


def rows_kernel(bs, pattern, mine, theirs, t, dyn_own, dyn_send, a3h, a3l):
    q, _, _ = place_of()
    n = a3h.shape[0]
    r = mine.shape[1]
    put = functools.partial(put_split, a3h, a3l)
    dense_turned(put, pattern, mine[...], theirs[...], has(3), n, r, bs)
    rows = dot3(a3h[...], a3l[...], *split(t[...]))
    for j in range(4):
        at = lanes(q ^ j, r)
        dyn_own[:, at] = rows[j * r : (j + 1) * r, 0:r].T
        dyn_send[:, at] = rows[j * r : (j + 1) * r, r : 2 * r].T


def product_kernel(
    a0h, a0l, a1h, a1l, a2h, a2l, a3h, a3l, mh, ml, th, tl, product_ref
):
    first = place_of()[2] == 0
    r = a0h.shape[0] // 4

    @pl.when(first)
    def _():
        product_ref[...] = dot3(a1h[...], a1l[...], a0h[...], a0l[...])
        straight_split(mh, ml, product_ref, r)
        transpose_split(th, tl, product_ref, r)

    @pl.when(jnp.logical_not(first))
    def _():
        product_ref[...] = dot3(a3h[...], a3l[...], a2h[...], a2l[...])
        straight_split(th, tl, product_ref, r)
        transpose_split(mh, ml, product_ref, r)


def ahead_kernel(own, mh, ml, th, tl, full, z, xh, xl):
    r = own.shape[1] // 4

    def put(i, j, block):
        full[i * r : (i + 1) * r, j * r : (j + 1) * r] = block

    spread(own, r, put)

    @pl.when(place_of()[2] == 1)
    def _():
        straight_split(xh, xl, full, r)
        u = dot3(xh[...], xl[...], mh[...], ml[...])
        z[...] = dot3(th[...], tl[...], *split(u))


def put_rows(ref, value, q, r):
    for j in range(4):
        ref[lanes(q ^ j, r), :] = value[:, j * r : (j + 1) * r]


CROSSING = ((2, 0), (2, 1), (2, 3))


def level2_kernel(own, earlier, mh, ml, th, tl, full, z, to_chip, vh, vl, xh, xl, rest):
    c = place_of()[2]
    r = own.shape[1] // 4
    two, three = slice(2 * r, 3 * r), slice(3 * r, 4 * r)

    @pl.when(c == 0)
    def _():
        def put(i, j, block):
            put_split(xh, xl, slice(i * r, (i + 1) * r), slice(j * r, (j + 1) * r), block)

        spread(earlier, r, put)
        hi, lo = split(dot3(th[2 * r :, :], tl[2 * r :, :], xh[...], xl[...]))
        vh[...] = hi
        vl[...] = lo
        rest[:, 2 * r :] = dot3(hi, lo, mh[:, 2 * r :], ml[:, 2 * r :])
        rest[0:r, 0 : 2 * r] = dot3(hi[0:r, :], lo[0:r, :], mh[:, 0 : 2 * r], ml[:, 0 : 2 * r])
        rest[:, 2 * r :] = rest[:, 2 * r :] + full[2 * r :, 2 * r :]
        rest[0:r, 0 : 2 * r] = rest[0:r, 0 : 2 * r] + full[two, 0 : 2 * r]

    @pl.when(c == 1)
    def _():
        def put(i, j, block):
            if (i, j) in CROSSING or i == j:
                rows = slice((i - 2) * r, (i - 1) * r)
                cols = slice(j * r, (j + 1) * r)
                rest[rows, cols] = z[i * r : (i + 1) * r, cols] + block

        spread(earlier, r, put, rows=(2, 3))

    z33 = rest[r : 2 * r, three]
    to_chip[0:r, :] = fold(rest[0:r, two], z33, r)
    for at, (_, j) in enumerate(CROSSING):
        to_chip[(at + 1) * r : (at + 2) * r, :] = rest[0:r, j * r : (j + 1) * r]
    to_chip[4 * r :, :] = jnp.broadcast_to(diagonal(z33, r), (8, r))


def far_rows_kernel(
    own, earlier, mh, ml, a2, full, z, vh, vl, to_far, short, vec, rest
):
    c = place_of()[2]
    r = own.shape[1] // 4
    base = 2 * r
    three = slice(3 * r, 4 * r)
    b1 = earlier[base + 1 : base + 2, :] + row_times(earlier[base + 3 : base + 4, :], a2[...], r)

    @pl.when(c == 0)
    def _():
        value = dot3(vh[r:, :], vl[r:, :], mh[:, 0 : 2 * r], ml[:, 0 : 2 * r])
        rest[...] = value + full[three, 0 : 2 * r]
        vec[0:1, :] = b1
        vec[1:2, :] = own[base + 2 : base + 3, :]

    @pl.when(c == 1)
    def _():
        def put(i, j, block):
            if j < 2:
                cols = slice(j * r, (j + 1) * r)
                rest[:, cols] = z[three, cols] + block

        spread(earlier, r, put, rows=(3,))
        vec[0:1, :] = own[base + 2 : base + 3, :] + row_times(b1, full[...], r)
        vec[1:2, :] = earlier[base + 2 : base + 3, :]

    to_far[0:r, :] = rest[:, 0:r]
    to_far[r : 2 * r, :] = rest[:, r : 2 * r]
    out = vec[1:2, :] + row_times(vec[0:1, :], mh[...].astype(F32) + ml[...].astype(F32), r)
    to_far[2 * r :, :] = jnp.broadcast_to(out[:, 3 * r :], (8, r))
    for i in range(4):
        short[i : i + 1, :] = out[:, i * r : (i + 1) * r]
    short[4:8, :] = jnp.zeros((4, r), F32)


def rest_kernel(earlier, mh, ml, th, tl, full, z, xh, xl, short, keep, to_core, rest):
    q, _, c = place_of()
    r = earlier.shape[1] // 4

    @pl.when(c == 0)
    def _():
        hi, lo = split(dot3(th[0 : 2 * r, :], tl[0 : 2 * r, :], xh[...], xl[...]))
        rest[...] = dot3(hi, lo, mh[...], ml[...]) + full[0 : 2 * r, :]

    @pl.when(c == 1)
    def _():
        def put(i, j, block):
            rows = slice(i * r, (i + 1) * r)
            cols = slice(j * r, (j + 1) * r)
            rest[rows, cols] = z[rows, cols] + block

        spread(earlier, r, put, rows=(0, 1))

    put_rows(keep, rest[0:r, :], q, r)
    put_rows(to_core, rest[r : 2 * r, :], q, r)
    to_core[4 * r :, :] = jnp.broadcast_to(short[1:2, :], (8, r))


def turn_kernel(from_chip, diagonal_block, mirrored):
    r = diagonal_block.shape[0]
    first, second = unfold(from_chip[0:r, :], from_chip[4 * r : 4 * r + 1, :], r)
    diagonal_block[...] = first
    mirrored[0:r, :] = from_chip[3 * r : 4 * r, :].T
    mirrored[r : 2 * r, :] = second


def panel_copies(panel, target, element, r):
    return [
        (panel.at[pl.ds(g * r, r), :], target.at[element, :, pl.ds(g * r, r)]) for g in range(4)
    ]


def block_copies(blocks, target, element, r):
    return [(source, target.at[element, :, lanes(at, r)]) for source, at in blocks]


def fill_kernel(
    keep,
    from_core,
    dyn_own,
    dyn_recv,
    diagonal_block,
    from_chip,
    dyn_out,
    cov_out,
    cost_out,
    sems,
):
    q, y, c = place_of()
    r = dyn_own.shape[0]
    dyn = [(dyn_own, dyn_out.at[y]), (dyn_recv, dyn_out.at[1 - y])]
    blocks = [(diagonal_block, q)] + [
        (from_chip.at[pl.ds(at * r, r), :], q ^ bit) for at, bit in ((1, 2), (2, 3), (3, 1))
    ]

    def write(mine, other):
        copy_all(
            dyn
            + panel_copies(keep, mine, y, r)
            + panel_copies(from_core, other, y, r)
            + block_copies(blocks, mine, 1 - y, r),
            sems,
        )

    @pl.when(c == 0)
    def _():
        write(cov_out, cost_out)

    @pl.when(c == 1)
    def _():
        write(cost_out, cov_out)


def place_kernel(
    cov_in,
    cost_in,
    short,
    chip_short,
    from_core,
    mirrored,
    panel,
    cov_out,
    cost_out,
    drift_out,
    eta_out,
    lines,
    sems,
):
    del cov_in, cost_in
    q, y, c = place_of()
    first = c == 0
    r = short.shape[1]
    mine, other = short[0:1, :], from_core[4 * r : 4 * r + 1, :]
    chip, far = chip_short[2:3, :], panel[2 * r : 2 * r + 1, :]
    for at, (one, two, three, four) in enumerate(
        ((mine, other, chip, far), (other, mine, far, chip))
    ):
        lines[at, pl.ds(y, 1), :] = jnp.where(first, one, two)
        lines[at, pl.ds(1 - y, 1), :] = jnp.where(first, three, four)
    vectors = [(lines.at[0], drift_out), (lines.at[1], eta_out)]
    near, far = pl.ds(0, r), pl.ds(r, r)
    blocks = [
        (panel.at[near, :], q ^ 3),
        (panel.at[far, :], q ^ 2),
        (mirrored.at[near, :], q ^ 1),
        (mirrored.at[far, :], q),
    ]

    @pl.when(first)
    def _():
        copy_all(vectors + block_copies(blocks, cost_out, 1 - y, r), sems)

    @pl.when(c == 1)
    def _():
        copy_all(vectors + block_copies(blocks, cov_out, 1 - y, r), sems)


IN_HBM, IN_VMEM = 0, 1


def kernel(body, operands, shapes, scratch=(), aliases=None):
    specs = {
        IN_HBM: pl.BlockSpec(memory_space=pltpu.HBM),
        IN_VMEM: pl.BlockSpec(memory_space=pltpu.VMEM),
    }
    call = pl.pallas_call(
        body,
        in_specs=[specs[where] for where, _ in operands],
        out_specs=[specs[where] for where, _ in shapes],
        out_shape=[
            pltpu.VMEM(s.shape, s.dtype) if where == IN_VMEM else s for where, s in shapes
        ],
        scratch_shapes=list(scratch),
        input_output_aliases=aliases or {},
        compiler_params=pltpu.CompilerParams(vmem_limit_bytes=20 * 2**20),
    )
    kept = {IN_HBM: pltpu.HBM, IN_VMEM: pltpu.VMEM}
    return call(
        *(
            pltpu.with_memory_space_constraint(x, kept[where]) if where in kept else x
            for where, x in operands
        )
    )


def per_device_split(blocks, pattern, drift, cov, cost, eta):
    elements, r, n = cov.shape
    bs = blocks.shape[2] // 3
    tms, cols = lax.axis_size("tm"), lax.axis_size("col")

    def swap(value, bit):
        return lax.ppermute(value, "col", [(i, i ^ bit) for i in range(cols)])

    def later(value, distance, cyclic=False):
        count = tms if cyclic else tms - distance
        return lax.ppermute(value, "tm", [(i, (i + distance) % tms) for i in range(count)])

    def hbm(*arrays):
        return [(IN_HBM, x) for x in arrays]

    def vmem(*arrays):
        return [(IN_VMEM, x) for x in arrays]

    def shape(*dims):
        return jax.ShapeDtypeStruct(dims, F32)

    def half(*dims):
        return jax.ShapeDtypeStruct(dims, BF16)

    def square(dtype):
        return pltpu.VMEM((n, n), dtype)

    def sems(count):
        return pltpu.SemaphoreType.DMA((count,))

    turned = jnp.swapaxes(blocks, 1, 2)
    before = later(turned, 1, cyclic=True)
    to_core, to_chip, to_far, panel, vecs = kernel(
        send_kernel,
        hbm(cov, cost, drift, eta),
        vmem(shape(r + 8, 3 * r), shape(r + 8, 2 * r), shape(r + 8, r), shape(r, n), shape(8, r)),
        [pltpu.VMEM(drift.shape, F32), pltpu.VMEM(eta.shape, F32), sems(12)],
    )
    from_core = swap(to_core, 1)
    from_chip = swap(to_chip, 2)
    from_far = swap(to_far, 3)
    (own_near,) = kernel(pack_near_kernel, vmem(panel, from_core), vmem(shape(r, 6 * r)))
    near = later(own_near, 1, cyclic=True)
    (own_far,) = kernel(
        pack_far_kernel, vmem(vecs, from_core, from_chip, from_far), vmem(shape(r + 8, 2 * r))
    )
    far = later(own_far, 1)
    (picked,) = kernel(pick_kernel, vmem(turned, before), vmem(shape(6 * bs, r)))
    other = swap(picked, 2)
    own_half, before_half = kernel(
        halves_kernel, vmem(turned, before, other), vmem(shape(6 * bs, r), shape(6 * bs, r))
    )
    pairs = (own_half, swap(own_half, 1), before_half, swap(before_half, 1))
    third = later(own_half, 2, cyclic=True)
    fourth = later(before_half, 2)
    m1 = kernel(
        functools.partial(prepare_kernel, bs),
        vmem(pattern, *pairs),
        vmem(*[half(n, n)] * 4),
        [square(F32)],
    )
    (level1,) = kernel(
        level1_kernel,
        vmem(own_near, own_far, near, far, *m1),
        vmem(shape(2 * r + 8, n)),
        [pltpu.VMEM((n + 16, n), BF16)] * 2 + [pltpu.VMEM((2 * r + 16, n), BF16)] * 2,
    )
    earlier = later(level1, 2)
    *a01, t = kernel(
        functools.partial(early_kernel, bs),
        vmem(pattern, *pairs),
        vmem(*[half(n, n)] * 4, shape(n, 2 * r)),
    )
    t, a2, *a2_split = kernel(
        functools.partial(third_kernel, bs),
        vmem(pattern, third, swap(third, 1), t),
        vmem(shape(n, 2 * r), shape(n, n), half(n, n), half(n, n)),
    )
    dyn_own, dyn_send, *a3_split = kernel(
        functools.partial(rows_kernel, bs),
        vmem(pattern, fourth, swap(fourth, 1), t),
        vmem(shape(r, n), shape(r, n), half(n, n), half(n, n)),
    )
    a23 = (*a2_split, *a3_split)
    dyn_recv = swap(dyn_send, 2)
    m2 = kernel(product_kernel, vmem(*a01, *a23), vmem(*[half(n, n)] * 4), [square(F32)])
    full, z = kernel(
        ahead_kernel, vmem(level1, *m2), vmem(shape(n, n), shape(n, n)), [square(BF16)] * 2
    )
    to_chip, vh, vl, *x = kernel(
        level2_kernel,
        vmem(level1, earlier, *m2, full, z),
        vmem(shape(n + 8, r), *[half(2 * r, n)] * 2, *[half(n, n)] * 2),
        [pltpu.VMEM((2 * r, n), F32)],
    )
    from_chip = swap(to_chip, 2)
    to_far, short = kernel(
        far_rows_kernel,
        vmem(level1, earlier, *m2[:2], a2, full, z, vh, vl),
        vmem(shape(2 * r + 8, r), shape(8, r)),
        [pltpu.VMEM((8, n), F32), pltpu.VMEM((r, 2 * r), F32)],
    )
    chip_short = swap(short, 2)
    from_far = swap(to_far, 3)
    keep, to_core = kernel(
        rest_kernel,
        vmem(earlier, *m2, full, z, *x, short),
        vmem(shape(n, r), shape(n + 8, r)),
        [pltpu.VMEM((2 * r, n), F32)],
    )
    from_core = swap(to_core, 1)
    diagonal_block, mirrored = kernel(
        turn_kernel, vmem(from_chip), vmem(shape(r, r), shape(2 * r, r))
    )
    mirrored = swap(mirrored, 1)
    whole, line = shape(elements, r, n), shape(elements, r)
    dyn_out, cov_out, cost_out = kernel(
        fill_kernel,
        vmem(keep, from_core, dyn_own, dyn_recv, diagonal_block, from_chip),
        hbm(whole, whole, whole),
        [sems(14)],
    )
    cov_out, cost_out, drift_out, eta_out = kernel(
        place_kernel,
        hbm(cov_out, cost_out) + vmem(short, chip_short, from_core, mirrored, from_far),
        hbm(whole, whole, line, line),
        [pltpu.VMEM((2, elements, r), F32), sems(6)],
        {0: 0, 1: 1},
    )
    return dyn_out, drift_out, cov_out, cost_out, eta_out


def takes_split(elements, r, bs, cols):
    return elements == 2 and cols == 4 and r % 128 == 0 and r % bs == 0 and bs % 8 == 0


def per_device(blocks, pattern, drift, cov, cost, eta):
    elements, r, _ = cov.shape
    bs = blocks.shape[2] // 3
    if takes_split(elements, r, bs, lax.axis_size("col")):
        return per_device_split(blocks, pattern, drift, cov, cost, eta)
    return per_device_general(blocks, pattern, drift, cov, cost, eta)


def solution(mesh):
    return jax.shard_map(
        per_device,
        mesh=mesh,
        in_specs=(
            P("tm", "col", None),
            P(),
            P("tm", "col"),
            P("tm", "col", None),
            P("tm", "col", None),
            P("tm", "col"),
        ),
        out_specs=(
            P("tm", "col", None),
            P("tm", "col"),
            P("tm", "col", None),
            P("tm", "col", None),
            P("tm", "col"),
        ),
        check_vma=False,
    )
```

```python
import functools

import jax
import jax.numpy as jnp
from jax import lax
from jax.experimental import pallas as pl
from jax.experimental.pallas import tpu as pltpu
from jax.sharding import PartitionSpec as P


HIGH = lax.Precision.HIGHEST
F32 = jnp.float32
BF16 = jnp.bfloat16


def shifted(block, axis, distance):
    devices = range(lax.axis_size(axis))
    route = [(i - distance, i) for i in devices if i - distance in devices]
    return lax.ppermute(block, axis, route)


def product(form, left, right):
    return jnp.einsum(form, left, right, precision=HIGH)


def densify(row_blocks, row_ids, pattern, block_size):
    block_count = pattern.shape[0]
    row_block = row_ids // block_size
    chooser = (row_block[:, None] == jnp.arange(block_count, dtype=jnp.int32)[None, :]).astype(
        jnp.int32
    )
    columns = jnp.sum(chooser[:, :, None] * pattern[None, :, :], axis=1)
    matches = (
        columns[:, :, None] == jnp.arange(block_count, dtype=jnp.int32)[None, None, :]
    ).astype(jnp.float32)
    pieces = row_blocks.reshape(row_blocks.shape[:-1] + (3, 1, block_size))
    filled = jnp.sum(matches[:, :, :, None] * pieces, axis=-3)
    return filled.reshape(row_blocks.shape[:-1] + (block_count * block_size,))


def combine_rows(
    dyn_prev_full,
    dyn_own_full,
    dyn_own,
    drift_prev_full,
    drift_own,
    cov_prev,
    cov_own,
    cost_prev,
    cost_own,
    eta_prev,
    eta_own,
    first_row,
):
    height = dyn_own.shape[1]
    dyn_res = product("tij,tjk->tik", dyn_own, dyn_prev_full)
    drift_res = product("tij,tj->ti", dyn_own, drift_prev_full) + drift_own
    carried = eta_own + product("tij,tj->ti", cost_own, drift_prev_full)
    value_rows = product("tij,tjk->tik", cost_own, dyn_prev_full)
    prev_columns = lax.dynamic_slice_in_dim(dyn_prev_full, first_row, height, 2)
    cov_full, carried_full, value_full = (
        lax.all_gather(cov_prev, "col", axis=1, tiled=True),
        lax.all_gather(carried, "col", axis=1, tiled=True),
        lax.all_gather(value_rows, "col", axis=1, tiled=True),
    )
    cost_res = cost_prev + product("tki,tkj->tij", prev_columns, value_full)
    cov_res = (
        product("tik,tjk->tij", product("tij,tjk->tik", dyn_own, cov_full), dyn_own_full) + cov_own
    )
    eta_res = eta_prev + product("tki,tk->ti", prev_columns, carried_full)
    return (dyn_res, drift_res, cov_res, cost_res, eta_res)


def choose(flag, combined, kept):
    return tuple(jnp.where(flag, new, old) for new, old in zip(combined, kept))


def per_device_general(blocks, pattern, drift, cov, cost, eta):
    height = cov.shape[1]
    modes = cov.shape[2]
    block_size = blocks.shape[2] // 3
    first_row = lax.axis_index("col") * height
    own_ids = first_row + jnp.arange(height, dtype=jnp.int32)
    all_ids = jnp.arange(modes, dtype=jnp.int32)
    position = lax.axis_index("tm")
    dyn_own = densify(blocks, own_ids, pattern, block_size)
    received = shifted((blocks, drift, cov, cost, eta), "tm", 1)
    blocks_prev, blocks_own, drift_prev_full = (
        lax.all_gather(received[0], "col", axis=1, tiled=True),
        lax.all_gather(blocks, "col", axis=1, tiled=True),
        lax.all_gather(received[1], "col", axis=1, tiled=True),
    )
    merged = combine_rows(
        densify(blocks_prev, all_ids, pattern, block_size),
        densify(blocks_own, all_ids, pattern, block_size),
        dyn_own,
        drift_prev_full,
        drift,
        received[2],
        cov,
        received[3],
        cost,
        received[4],
        eta,
        first_row,
    )
    current = choose(position >= 1, merged, (dyn_own, drift, cov, cost, eta))
    received = shifted(current, "tm", 2)
    dyn_prev_full = lax.all_gather(received[0], "col", axis=1, tiled=True)
    dyn_own_full = lax.all_gather(current[0], "col", axis=1, tiled=True)
    drift_prev_full = lax.all_gather(received[1], "col", axis=1, tiled=True)
    merged = combine_rows(
        dyn_prev_full,
        dyn_own_full,
        current[0],
        drift_prev_full,
        current[1],
        received[2],
        current[2],
        received[3],
        current[3],
        received[4],
        current[4],
        first_row,
    )
    return choose(position >= 2, merged, current)


def split(x):
    hi = x.astype(BF16)
    lo = (x - hi.astype(F32)).astype(BF16)
    return hi, lo


def dot(a, b):
    return jnp.dot(a, b, preferred_element_type=F32)


def dot3(ah, al, bh, bl):
    return dot(ah, bh) + (dot(ah, bl) + dot(al, bh))


def triangle(r):
    rows = lax.broadcasted_iota(jnp.int32, (r, r), 0)
    cols = lax.broadcasted_iota(jnp.int32, (r, r), 1)
    return rows, cols


def fold(first, second, r):
    rows, cols = triangle(r)
    return jnp.where(rows >= cols, first, second)


def diagonal(block, r):
    rows, cols = triangle(r)
    return jnp.sum(jnp.where(rows == cols, block, 0.0), axis=0, keepdims=True)


def unfold(folded, second_diag, r):
    rows, cols = triangle(r)
    turned = folded.T
    first = jnp.where(rows >= cols, folded, turned)
    second = jnp.where(rows < cols, folded, turned)
    second = jnp.where(rows == cols, jnp.broadcast_to(second_diag, (r, r)), second)
    return first, second


UPPER = ((0, 1), (0, 2), (0, 3), (1, 2), (1, 3), (2, 3))


def spread(packed, r, put, rows=(0, 1, 2, 3)):
    panel0, panel1, diags = packed[0:r], packed[r : 2 * r], packed[2 * r : 2 * r + 1]
    for at, (panel, pair) in enumerate(((panel0, (0, 1)), (panel1, (2, 3)))):
        if pair[0] in rows or pair[1] in rows:
            blocks = unfold(panel[:, 0:r], diags[:, at * r : (at + 1) * r], r)
            for i, block in zip(pair, blocks):
                if i in rows:
                    put(i, i, block)
    for at, (i, j) in enumerate(UPPER):
        panel = panel0 if at < 3 else panel1
        block = panel[:, (at % 3 + 1) * r : (at % 3 + 2) * r]
        if i in rows:
            put(i, j, block)
        if j in rows:
            put(j, i, block.T)


def column(row, r):
    rows, cols = triangle(r)
    pieces = []
    for at in range(row.shape[1] // r):
        piece = jnp.broadcast_to(row[:, at * r : (at + 1) * r], (r, r))
        pieces.append(jnp.sum(jnp.where(rows == cols, piece, 0.0), axis=1, keepdims=True))
    return jnp.concatenate(pieces, axis=0)


def row_times(row, matrix, r):
    return jnp.sum(column(row, r) * matrix, axis=0, keepdims=True)


def place_of():
    q = lax.axis_index("col")
    return q, q >> 1, q & 1


def has(distance):
    return (lax.axis_index("tm") >= distance).astype(jnp.int32)


def lanes(index, r):
    return pl.ds(pl.multiple_of(index * r, r), r)


def copy_all(pairs, sems):
    copies = [
        pltpu.make_async_copy(source, target, sems.at[i]) for i, (source, target) in enumerate(pairs)
    ]
    for copy in copies:
        copy.start()
    for copy in copies:
        copy.wait()


def send_kernel(
    cov, cost, drift, eta, to_core, to_chip, to_far, panel, vecs, b_in, e_in, sems
):
    q, y, c = place_of()
    r = to_far.shape[1]

    def load(mine, theirs):
        pairs = []
        for j in range(2, 4):
            source = mine.at[1 - y, :, lanes((q ^ 2) ^ j, r)]
            pairs.append((source, to_chip.at[pl.ds(0, r), pl.ds((j - 2) * r, r)]))
        pairs.append((theirs.at[1 - y, :, lanes(q, r)], to_far.at[pl.ds(0, r), :]))
        for j in range(1, 4):
            source = theirs.at[y, :, lanes((q ^ 1) ^ j, r)]
            pairs.append((source, to_core.at[pl.ds(0, r), pl.ds((j - 1) * r, r)]))
        for j in range(4):
            pairs.append((mine.at[y, :, lanes(q ^ j, r)], panel.at[:, pl.ds(j * r, r)]))
        pairs.append((drift, b_in))
        pairs.append((eta, e_in))
        copy_all(pairs, sems)

    @pl.when(c == 0)
    def _():
        load(cov, cost)

    @pl.when(c == 1)
    def _():
        load(cost, cov)

    b, e = b_in[pl.ds(y, 1), :], e_in[pl.ds(y, 1), :]
    vecs[...] = jnp.zeros(vecs.shape, F32)
    vecs[0:1, :] = b
    vecs[1:2, :] = e
    to_core[r : r + 8, :] = jnp.zeros((8, 3 * r), F32)
    to_core[r : r + 1, 0:r] = b
    to_core[r : r + 1, r : 2 * r] = e
    b, e = b_in[pl.ds(1 - y, 1), :], e_in[pl.ds(1 - y, 1), :]
    to_chip[r : r + 8, :] = jnp.zeros((8, 2 * r), F32)
    to_chip[r : r + 1, 0:r] = b
    to_chip[r : r + 1, r : 2 * r] = e
    to_far[r : r + 8, :] = jnp.zeros((8, r), F32)
    to_far[r : r + 1, :] = b
    to_far[r + 1 : r + 2, :] = e


def pack_near_kernel(panel, from_core, packed):
    r = panel.shape[0]
    packed[:, 0:r] = fold(panel[:, 0:r], from_core[0:r, 0:r], r)
    packed[:, r : 4 * r] = panel[:, r:]
    packed[:, 4 * r :] = from_core[0:r, r : 3 * r]


def pack_far_kernel(vecs, from_core, from_chip, from_far, packed):
    r = vecs.shape[1]
    k33 = from_far[0:r, :]
    packed[0:r, 0:r] = fold(from_chip[0:r, 0:r], k33, r)
    packed[0:r, r:] = from_chip[0:r, r : 2 * r]
    packed[r : r + 1, 0:r] = diagonal(from_core[0:r, 0:r], r)
    packed[r : r + 1, r:] = diagonal(k33, r)
    b = (
        vecs[0:1, :],
        from_core[r : r + 1, 0:r],
        from_chip[r : r + 1, 0:r],
        from_far[r : r + 1, :],
    )
    e = (
        vecs[1:2, :],
        from_core[r : r + 1, r : 2 * r],
        from_chip[r : r + 1, r : 2 * r],
        from_far[r + 1 : r + 2, :],
    )
    for j in range(4):
        at = slice(j % 2 * r, (j % 2 + 1) * r)
        packed[r + 1 + j // 2 : r + 2 + j // 2, at] = b[j]
        packed[r + 3 + j // 2 : r + 4 + j // 2, at] = e[j]
    packed[r + 5 : r + 8, :] = jnp.zeros((3, 2 * r), F32)


def far_row(packed, r, at):
    return jnp.concatenate(
        [packed[r + at : r + at + 1, :], packed[r + at + 1 : r + at + 2, :]], axis=1
    )


def pick_kernel(turned, before, out):
    y = place_of()[1]
    height = turned.shape[1]
    out[0:height, :] = turned[1 - y]
    out[height:, :] = before[1 - y]


def halves_kernel(turned, before, other, own, earlier):
    y = place_of()[1]
    height = turned.shape[1]
    own[0:height, :] = turned[y]
    own[height:, :] = other[0:height, :]
    earlier[0:height, :] = before[y]
    earlier[height:, :] = other[height:, :]


def dense_turned(put, pattern, own_half, core_half, flag, n, r, bs):
    q = place_of()[0]
    sub = 8
    lane = lax.broadcasted_iota(jnp.int32, (sub, r), 1) // bs
    rows = lax.broadcasted_iota(jnp.int32, (bs, r), 0)
    cols = lax.broadcasted_iota(jnp.int32, (bs, r), 1)
    per = r // bs
    height = 3 * bs
    for j in range(4):
        half = own_half if j % 2 == 0 else core_half
        pieces, wanted = [], []
        for k in range(3):
            at = (j // 2) * height + k * bs
            pieces.append(half[at : at + bs, :].reshape(bs // sub, sub, r))
            want = jnp.zeros((sub, r), jnp.int32)
            for h in range(per):
                block = pattern[pl.ds((q ^ j) * per + h, 1), :][:, k : k + 1] ^ (q * per)
                want = jnp.where(lane == h, jnp.broadcast_to(block, (sub, r)), want)
            wanted.append(jnp.where(flag == 1, want, -1))
        for block in range(n // bs):
            if j * r <= block * bs < (j + 1) * r:
                value = jnp.where(
                    jnp.logical_and(rows + block * bs == cols + j * r, flag == 0), 1.0, 0.0
                ).reshape(bs // sub, sub, r)
            else:
                value = jnp.zeros((bs // sub, sub, r), F32)
            for k in range(3):
                value = jnp.where((wanted[k] == block)[None], pieces[k], value)
            put(
                slice(block * bs, (block + 1) * bs),
                slice(j * r, (j + 1) * r),
                value.reshape(bs, r),
            )


def put_split(hi_ref, lo_ref, rows, cols, value):
    hi, lo = split(value)
    hi_ref[rows, cols] = hi
    lo_ref[rows, cols] = lo


def transpose_split(hi_ref, lo_ref, source, r):
    n = source.shape[0]
    for i in range(n // r):
        for j in range(n // r):
            put_split(
                hi_ref,
                lo_ref,
                slice(j * r, (j + 1) * r),
                slice(i * r, (i + 1) * r),
                source[i * r : (i + 1) * r, j * r : (j + 1) * r].T,
            )


def straight_split(hi_ref, lo_ref, source, r):
    n = source.shape[0]
    for i in range(n // r):
        put_split(
            hi_ref, lo_ref, slice(i * r, (i + 1) * r), slice(None), source[i * r : (i + 1) * r, :]
        )


def prepare_kernel(bs, pattern, own, own_core, before, before_core, mh, ml, th, tl, dense):
    c, has1 = place_of()[2], has(1)
    n = dense.shape[0]
    r = own.shape[1]
    first = c == 0
    own_half = jnp.where(first, own[...], before[...])
    core_half = jnp.where(first, own_core[...], before_core[...])
    flag = jnp.where(first, 1, has1)

    def put(row, col, value):
        dense[row, col] = value

    dense_turned(put, pattern, own_half, core_half, flag, n, r, bs)

    @pl.when(first)
    def _():
        straight_split(mh, ml, dense, r)
        transpose_split(th, tl, dense, r)

    @pl.when(jnp.logical_not(first))
    def _():
        straight_split(th, tl, dense, r)
        transpose_split(mh, ml, dense, r)


def level1_kernel(own_near, own_far, near, far, mh, ml, th, tl, out, xh, xl, sh, sl):
    c = place_of()[2]
    r = own_near.shape[0]
    n = 4 * r
    extra = slice(n, n + 16)
    first = c == 0
    came = jnp.where(has(1) == 1, near[...], 0.0)
    far = jnp.where(has(1) == 1, far[...], 0.0)
    xn = jnp.where(first, came, own_near[...])
    xf = jnp.where(first, far[...], own_far[...])
    x = jnp.concatenate(
        [
            xn[:, 0 : 4 * r],
            jnp.concatenate([xf[0:r, 0:r], xn[:, 4 * r :], xf[0:r, r:]], axis=1),
            jnp.concatenate([xf[r : r + 1, :], xf[r : r + 1, :]], axis=1),
        ],
        axis=0,
    )

    def put(i, j, block):
        put_split(xh, xl, slice(i * r, (i + 1) * r), slice(j * r, (j + 1) * r), block)

    spread(x, r, put)
    b_before, b_own = far_row(far, r, 1), far_row(own_far, r, 1)
    e_before, e_own = far_row(far, r, 3), far_row(own_far, r, 3)
    row = jnp.broadcast_to(jnp.where(first, b_before, e_own), (16, n))
    put_split(xh, xl, extra, slice(None), row)
    u = dot3(xh[...], xl[...], mh[...], ml[...])
    uh, ul = split(u[0:n, :])
    sh[0 : 2 * r, :] = th[0 : 2 * r, :]
    sl[0 : 2 * r, :] = tl[0 : 2 * r, :]
    row = jnp.broadcast_to(jnp.where(first, 0.0, b_before), (16, n))
    put_split(sh, sl, slice(2 * r, 2 * r + 16), slice(None), row)
    top = dot3(sh[...], sl[...], uh, ul)
    low = dot3(th[2 * r :, :], tl[2 * r :, :], uh[:, 2 * r :], ul[:, 2 * r :])
    vec = jnp.where(first, b_own, e_before) + u[n : n + 1, :] + top[2 * r : 2 * r + 1, :]
    dn = jnp.where(first, own_near[...], came)
    df = jnp.where(first, own_far[...], far[...])
    z11 = top[r : 2 * r, r : 2 * r]
    z33 = low[r : 2 * r, r : 2 * r]
    out[0:r, 0:r] = fold(top[0:r, 0:r], z11, r) + dn[:, 0:r]
    out[0:r, r:] = top[0:r, r:] + dn[:, r : 4 * r]
    out[r : 2 * r, 0:r] = fold(low[0:r, 0:r], z33, r) + df[0:r, 0:r]
    out[r : 2 * r, r : 3 * r] = top[r : 2 * r, 2 * r :] + dn[:, 4 * r :]
    out[r : 2 * r, 3 * r :] = low[0:r, r : 2 * r] + df[0:r, r:]
    base = 2 * r
    out[base : base + 1, 0:r] = diagonal(z11, r) + df[r : r + 1, 0:r]
    out[base : base + 1, r : 2 * r] = diagonal(z33, r) + df[r : r + 1, r:]
    out[base : base + 1, 2 * r :] = jnp.zeros((1, 2 * r), F32)
    out[base + 1 : base + 2, :] = b_own
    out[base + 2 : base + 3, :] = vec
    out[base + 3 : base + 4, :] = b_before
    out[base + 4 : base + 8, :] = jnp.zeros((4, 4 * r), F32)


def early_kernel(bs, pattern, own, own_core, before, before_core, a0h, a0l, a1h, a1l, t):
    n = a0h.shape[0]
    r = own.shape[1]
    for flag, mine, theirs, hi, lo in (
        (1, own, own_core, a0h, a0l),
        (has(1), before, before_core, a1h, a1l),
    ):
        put = functools.partial(put_split, hi, lo)
        dense_turned(put, pattern, mine[...], theirs[...], flag, n, r, bs)

    def wanted(ref):
        return jnp.concatenate([ref[:, 0:r], ref[:, 2 * r : 3 * r]], axis=1)

    t[...] = dot3(a1h[...], a1l[...], wanted(a0h), wanted(a0l))


def third_kernel(bs, pattern, mine, theirs, t, out, a2, a2h, a2l):
    n = a2.shape[0]
    r = mine.shape[1]

    def put(row, col, value):
        put_split(a2h, a2l, row, col, value)
        a2[row, col] = value

    dense_turned(put, pattern, mine[...], theirs[...], has(2), n, r, bs)
    out[...] = dot3(a2h[...], a2l[...], *split(t[...]))


def rows_kernel(bs, pattern, mine, theirs, t, dyn_own, dyn_send, a3h, a3l):
    q, _, _ = place_of()
    n = a3h.shape[0]
    r = mine.shape[1]
    put = functools.partial(put_split, a3h, a3l)
    dense_turned(put, pattern, mine[...], theirs[...], has(3), n, r, bs)
    rows = dot3(a3h[...], a3l[...], *split(t[...]))
    for j in range(4):
        at = lanes(q ^ j, r)
        dyn_own[:, at] = rows[j * r : (j + 1) * r, 0:r].T
        dyn_send[:, at] = rows[j * r : (j + 1) * r, r : 2 * r].T


def product_kernel(
    a0h, a0l, a1h, a1l, a2h, a2l, a3h, a3l, mh, ml, th, tl, product_ref
):
    first = place_of()[2] == 0
    r = a0h.shape[0] // 4

    @pl.when(first)
    def _():
        product_ref[...] = dot3(a1h[...], a1l[...], a0h[...], a0l[...])
        straight_split(mh, ml, product_ref, r)
        transpose_split(th, tl, product_ref, r)

    @pl.when(jnp.logical_not(first))
    def _():
        product_ref[...] = dot3(a3h[...], a3l[...], a2h[...], a2l[...])
        straight_split(th, tl, product_ref, r)
        transpose_split(mh, ml, product_ref, r)


def ahead_kernel(own, mh, ml, th, tl, full, z, xh, xl):
    r = own.shape[1] // 4

    def put(i, j, block):
        full[i * r : (i + 1) * r, j * r : (j + 1) * r] = block

    spread(own, r, put)

    @pl.when(place_of()[2] == 1)
    def _():
        straight_split(xh, xl, full, r)
        u = dot3(xh[...], xl[...], mh[...], ml[...])
        z[...] = dot3(th[...], tl[...], *split(u))


def put_rows(ref, value, q, r):
    for j in range(4):
        ref[lanes(q ^ j, r), :] = value[:, j * r : (j + 1) * r]


CROSSING = ((2, 0), (2, 1), (2, 3))


def level2_kernel(own, earlier, mh, ml, th, tl, full, z, to_chip, uh, ul, xh, xl, rest):
    c = place_of()[2]
    r = own.shape[1] // 4
    two, three = slice(2 * r, 3 * r), slice(3 * r, 4 * r)

    @pl.when(c == 0)
    def _():
        def put(i, j, block):
            put_split(xh, xl, slice(i * r, (i + 1) * r), slice(j * r, (j + 1) * r), block)

        spread(earlier, r, put)
        hi, lo = split(dot3(xh[...], xl[...], mh[...], ml[...]))
        uh[...] = hi
        ul[...] = lo
        rest[:, 2 * r :] = dot3(th[2 * r :, :], tl[2 * r :, :], hi[:, 2 * r :], lo[:, 2 * r :])
        rest[0:r, 0 : 2 * r] = dot3(th[two, :], tl[two, :], hi[:, 0 : 2 * r], lo[:, 0 : 2 * r])
        rest[:, 2 * r :] = rest[:, 2 * r :] + full[2 * r :, 2 * r :]
        rest[0:r, 0 : 2 * r] = rest[0:r, 0 : 2 * r] + full[two, 0 : 2 * r]

    @pl.when(c == 1)
    def _():
        def put(i, j, block):
            if (i, j) in CROSSING or i == j:
                rows = slice((i - 2) * r, (i - 1) * r)
                cols = slice(j * r, (j + 1) * r)
                rest[rows, cols] = z[i * r : (i + 1) * r, cols] + block

        spread(earlier, r, put, rows=(2, 3))

    z33 = rest[r : 2 * r, three]
    to_chip[0:r, :] = fold(rest[0:r, two], z33, r)
    for at, (_, j) in enumerate(CROSSING):
        to_chip[(at + 1) * r : (at + 2) * r, :] = rest[0:r, j * r : (j + 1) * r]
    to_chip[4 * r :, :] = jnp.broadcast_to(diagonal(z33, r), (8, r))


def far_rows_kernel(
    own, earlier, mh, ml, th, tl, a2, full, z, uh, ul, to_far, short, vec, rest
):
    c = place_of()[2]
    r = own.shape[1] // 4
    base = 2 * r
    three = slice(3 * r, 4 * r)
    b1 = earlier[base + 1 : base + 2, :] + row_times(earlier[base + 3 : base + 4, :], a2[...], r)

    @pl.when(c == 0)
    def _():
        value = dot3(th[three, :], tl[three, :], uh[:, 0 : 2 * r], ul[:, 0 : 2 * r])
        rest[...] = value + full[three, 0 : 2 * r]
        vec[0:1, :] = b1
        vec[1:2, :] = own[base + 2 : base + 3, :]

    @pl.when(c == 1)
    def _():
        def put(i, j, block):
            if j < 2:
                cols = slice(j * r, (j + 1) * r)
                rest[:, cols] = z[three, cols] + block

        spread(earlier, r, put, rows=(3,))
        vec[0:1, :] = own[base + 2 : base + 3, :] + row_times(b1, full[...], r)
        vec[1:2, :] = earlier[base + 2 : base + 3, :]

    to_far[0:r, :] = rest[:, 0:r]
    to_far[r : 2 * r, :] = rest[:, r : 2 * r]
    out = vec[1:2, :] + row_times(vec[0:1, :], mh[...].astype(F32) + ml[...].astype(F32), r)
    to_far[2 * r :, :] = jnp.broadcast_to(out[:, 3 * r :], (8, r))
    for i in range(4):
        short[i : i + 1, :] = out[:, i * r : (i + 1) * r]
    short[4:8, :] = jnp.zeros((4, r), F32)


def rest_kernel(earlier, th, tl, full, z, uh, ul, short, keep, to_core, rest):
    q, _, c = place_of()
    r = earlier.shape[1] // 4

    @pl.when(c == 0)
    def _():
        rest[...] = dot3(th[0 : 2 * r, :], tl[0 : 2 * r, :], uh[...], ul[...]) + full[0 : 2 * r, :]

    @pl.when(c == 1)
    def _():
        def put(i, j, block):
            rows = slice(i * r, (i + 1) * r)
            cols = slice(j * r, (j + 1) * r)
            rest[rows, cols] = z[rows, cols] + block

        spread(earlier, r, put, rows=(0, 1))

    put_rows(keep, rest[0:r, :], q, r)
    put_rows(to_core, rest[r : 2 * r, :], q, r)
    to_core[4 * r :, :] = jnp.broadcast_to(short[1:2, :], (8, r))


def turn_kernel(from_chip, diagonal_block, mirrored):
    r = diagonal_block.shape[0]
    first, second = unfold(from_chip[0:r, :], from_chip[4 * r : 4 * r + 1, :], r)
    diagonal_block[...] = first
    mirrored[0:r, :] = from_chip[3 * r : 4 * r, :].T
    mirrored[r : 2 * r, :] = second


def panel_copies(panel, target, element, r):
    return [
        (panel.at[pl.ds(g * r, r), :], target.at[element, :, pl.ds(g * r, r)]) for g in range(4)
    ]


def block_copies(blocks, target, element, r):
    return [(source, target.at[element, :, lanes(at, r)]) for source, at in blocks]


def fill_kernel(
    keep,
    from_core,
    dyn_own,
    dyn_recv,
    diagonal_block,
    from_chip,
    dyn_out,
    cov_out,
    cost_out,
    sems,
):
    q, y, c = place_of()
    r = dyn_own.shape[0]
    dyn = [(dyn_own, dyn_out.at[y]), (dyn_recv, dyn_out.at[1 - y])]
    blocks = [(diagonal_block, q)] + [
        (from_chip.at[pl.ds(at * r, r), :], q ^ bit) for at, bit in ((1, 2), (2, 3), (3, 1))
    ]

    def write(mine, other):
        copy_all(
            dyn
            + panel_copies(keep, mine, y, r)
            + panel_copies(from_core, other, y, r)
            + block_copies(blocks, mine, 1 - y, r),
            sems,
        )

    @pl.when(c == 0)
    def _():
        write(cov_out, cost_out)

    @pl.when(c == 1)
    def _():
        write(cost_out, cov_out)


def place_kernel(
    cov_in,
    cost_in,
    short,
    chip_short,
    from_core,
    mirrored,
    panel,
    cov_out,
    cost_out,
    drift_out,
    eta_out,
    lines,
    sems,
):
    del cov_in, cost_in
    q, y, c = place_of()
    first = c == 0
    r = short.shape[1]
    mine, other = short[0:1, :], from_core[4 * r : 4 * r + 1, :]
    chip, far = chip_short[2:3, :], panel[2 * r : 2 * r + 1, :]
    for at, (one, two, three, four) in enumerate(
        ((mine, other, chip, far), (other, mine, far, chip))
    ):
        lines[at, pl.ds(y, 1), :] = jnp.where(first, one, two)
        lines[at, pl.ds(1 - y, 1), :] = jnp.where(first, three, four)
    vectors = [(lines.at[0], drift_out), (lines.at[1], eta_out)]
    near, far = pl.ds(0, r), pl.ds(r, r)
    blocks = [
        (panel.at[near, :], q ^ 3),
        (panel.at[far, :], q ^ 2),
        (mirrored.at[near, :], q ^ 1),
        (mirrored.at[far, :], q),
    ]

    @pl.when(first)
    def _():
        copy_all(vectors + block_copies(blocks, cost_out, 1 - y, r), sems)

    @pl.when(c == 1)
    def _():
        copy_all(vectors + block_copies(blocks, cov_out, 1 - y, r), sems)


IN_HBM, IN_VMEM = 0, 1


def kernel(body, operands, shapes, scratch=(), aliases=None):
    specs = {
        IN_HBM: pl.BlockSpec(memory_space=pltpu.HBM),
        IN_VMEM: pl.BlockSpec(memory_space=pltpu.VMEM),
    }
    call = pl.pallas_call(
        body,
        in_specs=[specs[where] for where, _ in operands],
        out_specs=[specs[where] for where, _ in shapes],
        out_shape=[
            pltpu.VMEM(s.shape, s.dtype) if where == IN_VMEM else s for where, s in shapes
        ],
        scratch_shapes=list(scratch),
        input_output_aliases=aliases or {},
        compiler_params=pltpu.CompilerParams(vmem_limit_bytes=20 * 2**20),
    )
    kept = {IN_HBM: pltpu.HBM, IN_VMEM: pltpu.VMEM}
    return call(
        *(
            pltpu.with_memory_space_constraint(x, kept[where]) if where in kept else x
            for where, x in operands
        )
    )


def per_device_split(blocks, pattern, drift, cov, cost, eta):
    elements, r, n = cov.shape
    bs = blocks.shape[2] // 3
    tms, cols = lax.axis_size("tm"), lax.axis_size("col")

    def swap(value, bit):
        return lax.ppermute(value, "col", [(i, i ^ bit) for i in range(cols)])

    def later(value, distance, cyclic=False):
        count = tms if cyclic else tms - distance
        return lax.ppermute(value, "tm", [(i, (i + distance) % tms) for i in range(count)])

    def hbm(*arrays):
        return [(IN_HBM, x) for x in arrays]

    def vmem(*arrays):
        return [(IN_VMEM, x) for x in arrays]

    def shape(*dims):
        return jax.ShapeDtypeStruct(dims, F32)

    def half(*dims):
        return jax.ShapeDtypeStruct(dims, BF16)

    def square(dtype):
        return pltpu.VMEM((n, n), dtype)

    def sems(count):
        return pltpu.SemaphoreType.DMA((count,))

    turned = jnp.swapaxes(blocks, 1, 2)
    before = later(turned, 1, cyclic=True)
    to_core, to_chip, to_far, panel, vecs = kernel(
        send_kernel,
        hbm(cov, cost, drift, eta),
        vmem(shape(r + 8, 3 * r), shape(r + 8, 2 * r), shape(r + 8, r), shape(r, n), shape(8, r)),
        [pltpu.VMEM(drift.shape, F32), pltpu.VMEM(eta.shape, F32), sems(12)],
    )
    from_core = swap(to_core, 1)
    from_chip = swap(to_chip, 2)
    from_far = swap(to_far, 3)
    (own_near,) = kernel(pack_near_kernel, vmem(panel, from_core), vmem(shape(r, 6 * r)))
    near = later(own_near, 1, cyclic=True)
    (own_far,) = kernel(
        pack_far_kernel, vmem(vecs, from_core, from_chip, from_far), vmem(shape(r + 8, 2 * r))
    )
    far = later(own_far, 1, cyclic=True)
    (picked,) = kernel(pick_kernel, vmem(turned, before), vmem(shape(6 * bs, r)))
    other = swap(picked, 2)
    own_half, before_half = kernel(
        halves_kernel, vmem(turned, before, other), vmem(shape(6 * bs, r), shape(6 * bs, r))
    )
    pairs = (own_half, swap(own_half, 1), before_half, swap(before_half, 1))
    third = later(own_half, 2, cyclic=True)
    fourth = later(before_half, 2)
    m1 = kernel(
        functools.partial(prepare_kernel, bs),
        vmem(pattern, *pairs),
        vmem(*[half(n, n)] * 4),
        [square(F32)],
    )
    (level1,) = kernel(
        level1_kernel,
        vmem(own_near, own_far, near, far, *m1),
        vmem(shape(2 * r + 8, n)),
        [pltpu.VMEM((n + 16, n), BF16)] * 2 + [pltpu.VMEM((2 * r + 16, n), BF16)] * 2,
    )
    earlier = later(level1, 2)
    *a01, t = kernel(
        functools.partial(early_kernel, bs),
        vmem(pattern, *pairs),
        vmem(*[half(n, n)] * 4, shape(n, 2 * r)),
    )
    t, a2, *a2_split = kernel(
        functools.partial(third_kernel, bs),
        vmem(pattern, third, swap(third, 1), t),
        vmem(shape(n, 2 * r), shape(n, n), half(n, n), half(n, n)),
    )
    dyn_own, dyn_send, *a3_split = kernel(
        functools.partial(rows_kernel, bs),
        vmem(pattern, fourth, swap(fourth, 1), t),
        vmem(shape(r, n), shape(r, n), half(n, n), half(n, n)),
    )
    a23 = (*a2_split, *a3_split)
    dyn_recv = swap(dyn_send, 2)
    m2 = kernel(product_kernel, vmem(*a01, *a23), vmem(*[half(n, n)] * 4), [square(F32)])
    full, z = kernel(
        ahead_kernel, vmem(level1, *m2), vmem(shape(n, n), shape(n, n)), [square(BF16)] * 2
    )
    to_chip, *u = kernel(
        level2_kernel,
        vmem(level1, earlier, *m2, full, z),
        vmem(shape(n + 8, r), half(n, n), half(n, n)),
        [square(BF16)] * 2 + [pltpu.VMEM((2 * r, n), F32)],
    )
    from_chip = swap(to_chip, 2)
    to_far, short = kernel(
        far_rows_kernel,
        vmem(level1, earlier, *m2, a2, full, z, *u),
        vmem(shape(2 * r + 8, r), shape(8, r)),
        [pltpu.VMEM((8, n), F32), pltpu.VMEM((r, 2 * r), F32)],
    )
    chip_short = swap(short, 2)
    from_far = swap(to_far, 3)
    keep, to_core = kernel(
        rest_kernel,
        vmem(earlier, *m2[2:], full, z, *u, short),
        vmem(shape(n, r), shape(n + 8, r)),
        [pltpu.VMEM((2 * r, n), F32)],
    )
    from_core = swap(to_core, 1)
    diagonal_block, mirrored = kernel(
        turn_kernel, vmem(from_chip), vmem(shape(r, r), shape(2 * r, r))
    )
    mirrored = swap(mirrored, 1)
    whole, line = shape(elements, r, n), shape(elements, r)
    dyn_out, cov_out, cost_out = kernel(
        fill_kernel,
        vmem(keep, from_core, dyn_own, dyn_recv, diagonal_block, from_chip),
        hbm(whole, whole, whole),
        [sems(14)],
    )
    cov_out, cost_out, drift_out, eta_out = kernel(
        place_kernel,
        hbm(cov_out, cost_out) + vmem(short, chip_short, from_core, mirrored, from_far),
        hbm(whole, whole, line, line),
        [pltpu.VMEM((2, elements, r), F32), sems(6)],
        {0: 0, 1: 1},
    )
    return dyn_out, drift_out, cov_out, cost_out, eta_out


def takes_split(elements, r, bs, cols):
    return elements == 2 and cols == 4 and r % 128 == 0 and r % bs == 0 and bs % 8 == 0


def per_device(blocks, pattern, drift, cov, cost, eta):
    elements, r, _ = cov.shape
    bs = blocks.shape[2] // 3
    if takes_split(elements, r, bs, lax.axis_size("col")):
        return per_device_split(blocks, pattern, drift, cov, cost, eta)
    return per_device_general(blocks, pattern, drift, cov, cost, eta)


def solution(mesh):
    return jax.shard_map(
        per_device,
        mesh=mesh,
        in_specs=(
            P("tm", "col", None),
            P(),
            P("tm", "col"),
            P("tm", "col", None),
            P("tm", "col", None),
            P("tm", "col"),
        ),
        out_specs=(
            P("tm", "col", None),
            P("tm", "col"),
            P("tm", "col", None),
            P("tm", "col", None),
            P("tm", "col"),
        ),
        check_vma=False,
    )
```
